32 devices in a mesh: dp: 8 (over z, y), fsdp: 4 (over x, core).
Axes of the slice: x: 2, y: 2, z: 4, core: 2. Of those that a mesh axis runs over, the one named last changes fastest.
Arguments:
- inputs: bfloat16 [32, 128, 768], P(('dp', 'fsdp')), may hold values from -6 to 6
- memory: bfloat16 [32, 512, 768], P(('dp', 'fsdp')), may hold values from -6 to 6
- out_cotangent: bfloat16 [32, 128, 768], P(('dp', 'fsdp')), may hold values from -6 to 6
- dec_lengths: int32 [32], P(('dp', 'fsdp')), may hold values from 32 to 128, as said below
- mem_lengths: int32 [32], P(('dp', 'fsdp')), may hold values from 128 to 512, as said below
- self_params: bfloat16 [2359296], P(('dp', 'fsdp'))
- cross_params: bfloat16 [2359296], P(('dp', 'fsdp'))
- ff_params: bfloat16 [4718592], P(('dp', 'fsdp'))
- gains: float32 [3, 768], replicated, may hold values from 0.1 to 1.9
- table: float32 [32, 12], replicated, may hold values from -4 to 4
Outputs:
- block_out: bfloat16 [32, 128, 768], P(('dp', 'fsdp'))
- input_grad: bfloat16 [32, 128, 768], P(('dp', 'fsdp'))
- memory_grad: bfloat16 [32, 512, 768], P(('dp', 'fsdp'))
- self_grad: float32 [2359296], P(('dp', 'fsdp'))
- cross_grad: float32 [2359296], P(('dp', 'fsdp'))
- ff_grad: float32 [4718592], P(('dp', 'fsdp'))
- gains_grad: float32 [3, 768], replicated
- table_grad: float32 [32, 12], replicated
The draws below stay inside these ranges and needn't reach their ends.
Inputs may be any that keep to these rules, and one draw needn't show every extreme that they name: `dec_lengths`: positions of a decoder slot from its length on are padding; some slot has exactly 128 tokens and some exactly 32. `mem_lengths`: encoder positions of a slot from its length on are padding; some slot has exactly 512 and some exactly 128.
All inputs are finite; a program needn't handle non-finite values.
Results may differ from the reference program's by a relative error of at most 0.03.
The reference program's roundings to bfloat16 on the way count: a program that leaves them out, or rounds other values in their place, can miss the bound.
Values may be sent and summed in bfloat16 or wider, within the bound.
A program may use at most 192 MiB of HBM per device.

```python
import jax
import jax.numpy as jnp
import numpy as np
from jax import lax

D = 768
FF = 2048
H = 12
DH = 64
NB = 32
MAXD = 128
L = 128
ME = 512
S_DEV = 1
SEQS = 32


def attention_matrices(key):
    scales = jnp.array([(16.0 * D) ** (-0.5), D ** (-0.5), D ** (-0.5), (D / 8.0) ** (-0.5)], jnp.float32)
    normal = jax.random.truncated_normal(key, -4.0, 4.0, (4, D * D), jnp.float32)
    return (normal * scales[:, None]).reshape(4 * D * D).astype(jnp.bfloat16)


def draw_self_params(key, part):
    return attention_matrices(jax.random.fold_in(key, 11))


def draw_cross_params(key, part):
    return attention_matrices(jax.random.fold_in(key, 12))


def draw_ff_params(key, part):
    scales = jnp.array([D ** (-0.5), D ** (-0.5), FF ** (-0.5)], jnp.float32)
    normal = jax.random.truncated_normal(jax.random.fold_in(key, 13), -4.0, 4.0, (3, D * FF), jnp.float32)
    return (normal * scales[:, None]).reshape(3 * D * FF).astype(jnp.bfloat16)


def slot_lengths(key, longest):
    values = jax.random.randint(key, (SEQS,), longest // 4, longest + 1)
    first = jax.random.randint(jax.random.fold_in(key, 1), (), 0, SEQS)
    second = (first + 1 + jax.random.randint(jax.random.fold_in(key, 2), (), 0, SEQS - 1)) % SEQS
    return values.at[first].set(longest).at[second].set(longest // 4).astype(jnp.int32)


def draw_dec_lengths(key, part):
    return slot_lengths(jax.random.fold_in(key, 21), L)


def draw_mem_lengths(key, part):
    return slot_lengths(jax.random.fold_in(key, 22), ME)


def block_scale(key, extent, pieces, least, top_value):
    level = 1.0
    for dim, parts in pieces:
        steps = jax.random.uniform(jax.random.fold_in(jax.random.fold_in(key, 6), dim), (parts,), jnp.float32, least / len(pieces), top_value / len(pieces))
        level = level * jnp.repeat(jnp.exp(steps), extent[dim] // parts).reshape((-1,) + (1,) * (len(extent) - 1 - dim))
    return level


def noise(rng, extent, spread, limit, shards=(), held_as=jnp.bfloat16):
    loudness = block_scale(rng, extent, shards, -0.22, 0.18) if shards else 1.0
    values = jax.random.normal(rng, extent, jnp.float32) * spread * loudness
    return jnp.minimum(jnp.maximum(values, -limit), limit).astype(held_as)


def setup_inputs(seed: int = 0) -> dict:
    key_list = jax.random.split(jax.random.key(seed), 11)
    return {
        "inputs": noise(key_list[0], (SEQS, L, D), 1.0, 6.0, ((0, 32),)),
        "memory": noise(key_list[1], (SEQS, ME, D), 1.0, 6.0, ((0, 32),)),
        "out_cotangent": noise(key_list[2], (SEQS, L, D), 1.0, 6.0, ((0, 32),)),
        "dec_lengths": draw_dec_lengths(jax.random.fold_in(key_list[10], 71), 0),
        "mem_lengths": draw_mem_lengths(jax.random.fold_in(key_list[10], 71), 0),
        "self_params": draw_self_params(jax.random.fold_in(key_list[10], 71), 0),
        "cross_params": draw_cross_params(jax.random.fold_in(key_list[10], 71), 0),
        "ff_params": draw_ff_params(jax.random.fold_in(key_list[10], 71), 0),
        "gains": jnp.clip(1.0 + 0.18 * jax.random.normal(key_list[8], (3, D), jnp.float32), 0.1, 1.9),
        "table": noise(key_list[9], (NB, H), 1.0, 4.0, (), jnp.float32),
    }


@jax.custom_vjp
def low(v):
    return lax.optimization_barrier(v.astype(jnp.bfloat16)).astype(jnp.float32)

@jax.custom_vjp
def low_back(v):
    return v

def low_keep(v):
    return (low(v), None)

def low_pass(kept, grad):
    return (grad,)

def back_keep(v):
    return (v, None)

def back_low(kept, grad):
    return (low(grad),)
low.defvjp(low_keep, low_pass)
low_back.defvjp(back_keep, back_low)
HIGHEST = lax.Precision.HIGHEST

def matmul_high(left, right):
    return jnp.matmul(left, right, precision=HIGHEST)

def both_ways(value):
    return low(low_back(value))

def rms_scale(value, gain):
    return value * lax.rsqrt(lax.optimization_barrier(jnp.mean(value * value, axis=-1, keepdims=True)) + 1e-06) * gain

def gelu_gate(gate_pre, up_pre):
    return jax.nn.gelu(gate_pre, approximate=True) * up_pre

def bucket_rows(start, count, length):
    half_count = NB // 2
    limits = np.ceil(half_count * (MAXD / half_count) ** (np.arange(1, half_count) / half_count)).astype(np.int32)
    query_pos = start + jnp.arange(count, dtype=jnp.int32)
    key_pos = jnp.arange(length, dtype=jnp.int32)
    distance = query_pos[:, None] - key_pos[None, :]
    beyond = half_count + lax.optimization_barrier(jnp.sum((distance[None] >= jnp.asarray(limits)[:, None, None]).astype(jnp.int32), axis=0))
    return jnp.where(distance < half_count, jnp.maximum(distance, 0), beyond).astype(jnp.int32)

def attend(queries, keys_in, values, score_bias, keep_mask):
    batch, q_len, _ = queries.shape
    k_len = keys_in.shape[1]
    q_heads = queries.reshape(batch, q_len, H, DH)
    k_heads = keys_in.reshape(batch, k_len, H, DH)
    v_heads = values.reshape(batch, k_len, H, DH)
    scores = low_back(jnp.einsum('bqhe,bkhe->bhqk', q_heads, k_heads, precision=HIGHEST) + score_bias)
    scores = jnp.where(keep_mask[:, None], scores, -1000000000.0)
    row_max = lax.optimization_barrier(jnp.max(scores, axis=-1, keepdims=True))
    exponent = jnp.exp(scores - row_max)
    softmax_low = low(exponent / lax.optimization_barrier(jnp.sum(exponent, axis=-1, keepdims=True)))
    head_mix = jnp.einsum('bhqk,bkhe->bqhe', softmax_low, v_heads, precision=HIGHEST)
    return both_ways(head_mix.reshape(batch, q_len, H * DH))

def layer(self_w, cross_w, ff_w, gain_w, table_w, tokens, encoded, keep_self, keep_cross, bucket):
    self_mats = self_w.reshape(4, D, D)
    cross_mats = cross_w.reshape(4, D, D)
    block_size = D * FF
    w_gate = ff_w[:block_size].reshape(D, FF)
    w_up = ff_w[block_size:2 * block_size].reshape(D, FF)
    w_down = ff_w[2 * block_size:].reshape(FF, D)
    norm_one = low(rms_scale(tokens, gain_w[0]))
    self_q = both_ways(matmul_high(norm_one, self_mats[0]))
    self_k = both_ways(matmul_high(norm_one, self_mats[1]))
    self_v = both_ways(matmul_high(norm_one, self_mats[2]))
    pos_bias = jnp.transpose(table_w[bucket], (2, 0, 1))
    self_mix = attend(self_q, self_k, self_v, pos_bias, keep_self)
    resid_one = tokens + low_back(matmul_high(self_mix, self_mats[3]))
    norm_two = low(rms_scale(resid_one, gain_w[1]))
    cross_q = both_ways(matmul_high(norm_two, cross_mats[0]))
    cross_k = both_ways(matmul_high(encoded, cross_mats[1]))
    cross_v = both_ways(matmul_high(encoded, cross_mats[2]))
    cross_mix = attend(cross_q, cross_k, cross_v, 0.0, keep_cross)
    resid_two = resid_one + low_back(matmul_high(cross_mix, cross_mats[3]))
    norm_three = low(rms_scale(resid_two, gain_w[2]))
    gate_pre = low_back(matmul_high(norm_three, w_gate))
    up_pre = low_back(matmul_high(norm_three, w_up))
    hidden = both_ways(gelu_gate(gate_pre, up_pre))
    return resid_two + low_back(matmul_high(hidden, w_down))

def reference(inputs, memory, out_cotangent, dec_lengths, mem_lengths, self_params, cross_params, ff_params, gains, table):
    groups = SEQS // S_DEV
    bucket = bucket_rows(0, L, L)
    query_pos = jnp.arange(L, dtype=jnp.int32)
    mem_pos = jnp.arange(ME, dtype=jnp.int32)
    params = (self_params.astype(jnp.float32), cross_params.astype(jnp.float32), ff_params.astype(jnp.float32), gains.astype(jnp.float32), table.astype(jnp.float32))

    def group_step(carry, slot_item):
        tokens, encoded, cotangent, dec_len, mem_len = slot_item
        keep_self = (query_pos[None, None, :] <= query_pos[None, :, None]) & (query_pos[None, None, :] < dec_len[:, None, None])
        keep_cross = jnp.broadcast_to(mem_pos[None, None, :] < mem_len[:, None, None], (S_DEV, L, ME))

        def forward(self_w, cross_w, ff_w, gain_w, table_w, token_f, encoded_f):
            return layer(self_w, cross_w, ff_w, gain_w, table_w, token_f, encoded_f, keep_self, keep_cross, bucket)
        block, pull_back = jax.vjp(forward, params[0], params[1], params[2], params[3], params[4], tokens.astype(jnp.float32), encoded.astype(jnp.float32))
        grad_list = pull_back(cotangent.astype(jnp.float32))
        summed = tuple((older + newer for older, newer in zip(carry, grad_list[:5])))
        return (summed, (block.astype(jnp.bfloat16), grad_list[5].astype(jnp.bfloat16), grad_list[6].astype(jnp.bfloat16)))
    start = tuple((jnp.zeros_like(param) for param in params))
    items = (inputs.reshape(groups, S_DEV, L, D), memory.reshape(groups, S_DEV, ME, D), out_cotangent.reshape(groups, S_DEV, L, D), dec_lengths.reshape(groups, S_DEV), mem_lengths.reshape(groups, S_DEV))
    sums, outputs = lax.scan(group_step, start, items)
    return (outputs[0].reshape(SEQS, L, D), outputs[1].reshape(SEQS, L, D), outputs[2].reshape(SEQS, ME, D), sums[0], sums[1], sums[2], sums[3], sums[4])
```

```python
import functools

import jax
import jax.numpy as jnp
import numpy as np
from jax import lax
from jax.experimental import pallas as pl
from jax.experimental.pallas import tpu as pltpu
from jax.sharding import PartitionSpec as P

D = 768
FF = 2048
H = 12
DH = 64
NB = 32
MAXD = 128
PAIRS = H // 2
MASKED = -1000000000.0
BF = jnp.bfloat16
F32 = jnp.float32
MESH = pl.DeviceIdType.MESH

AR = 96
AU = 288
FU = 576
GROUPS = (
    (2, 3), (2, 2), (2, 0), (2, 1),
    (1, 3), (1, 2), (1, 1), (1, 0),
    (0, 3), (0, 2), (0, 1), (0, 0),
)
UNIT = tuple(FU if t == 2 else AU for t, _ in GROUPS)
OWN = tuple(4 * sum(UNIT[:g]) for g in range(12))
OWN_ROWS = 4 * sum(UNIT)
LAND = tuple(3 * sum(UNIT[:g]) for g in range(12))
LAND_ROWS = 3 * sum(UNIT)
ZBASE = (0, 3 * AU, 6 * AU)
Z_ROWS = 6 * AU + 3 * FU
STAGE = 4 * FU


def limits():
    half = NB // 2
    return [
        int(v)
        for v in np.ceil(half * (MAXD / half) ** (np.arange(1, half) / half)).astype(np.int32)
    ]


def bucket_of(distance):
    half = NB // 2
    beyond = jnp.full(distance.shape, half, jnp.int32)
    for limit in limits():
        beyond = beyond + jnp.where(distance >= limit, 1, 0)
    return jnp.where(distance < half, jnp.maximum(distance, 0), beyond)


def nn(left, right):
    return jnp.dot(left, right, preferred_element_type=F32)


def nt(left, right):
    return lax.dot_general(left, right, (((1,), (1,)), ((), ())), preferred_element_type=F32)


def tn(left, right):
    return lax.dot_general(left, right, (((0,), (0,)), ((), ())), preferred_element_type=F32)


def al(value, step):
    return pl.multiple_of(value, step)


def rms(value, gain):
    r = lax.rsqrt(jnp.mean(value * value, axis=-1, keepdims=True) + 1e-06)
    return value * r * gain


def rms_back(value, gain, dz):
    r = lax.rsqrt(jnp.mean(value * value, axis=-1, keepdims=True) + 1e-06)
    inner = jnp.mean(value * gain * dz, axis=-1, keepdims=True)
    dv = r * gain * dz - value * (r * r * r) * inner
    dg = jnp.sum(value * r * dz, axis=0, keepdims=True)
    return dv, dg


class Layer:
    def __init__(self, refs):
        self.__dict__.update(refs)
        self.flat, self.dm = self.ps, self.n3
        dp = lax.axis_index("dp")
        fs = lax.axis_index("fsdp")
        self.z, self.y = dp // 2, dp % 2
        self.x, self.c = fs // 2, fs % 2
        self.shard = dp * 4 + fs

    def dev(self, z=None, fx=0, fy=0, fc=0):
        z = self.z if z is None else z
        y = (self.y + fy) % 2
        x = (self.x + fx) % 2
        c = (self.c + fc) % 2
        return (z * 2 + y, x * 2 + c)

    def chip(self, fx=0, fy=0):
        return ((self.y + fy) % 2) * 2 + (self.x + fx) % 2

    def shard_at(self, z, fx=0, fy=0, fc=0):
        return z * 8 + self.chip(fx, fy) * 2 + (self.c + fc) % 2

    def copy(self, src, dst, send, recv, device):
        return pltpu.make_async_remote_copy(
            src_ref=src, dst_ref=dst, send_sem=send, recv_sem=recv,
            device_id=device, device_id_type=MESH,
        )

    def piece(self, tensor, shard, half=None):
        rows = FU if tensor == 2 else AR
        ref = (self.ws, self.wc, self.wf)[tensor]
        start = shard * rows
        if half is not None:
            rows = rows // 2
            start = start + half * rows
        return ref.at[pl.ds(al(start, 16), rows), :]

    def gcopy(self, tensor, zs, kind):
        if kind == 0:
            part, dev = self.piece(tensor, self.shard_at(zs)), self.dev(fx=1)
        elif kind == 1:
            part, dev = self.piece(tensor, self.shard_at(zs)), self.dev(fy=1)
        elif kind == 2:
            part, dev = self.piece(tensor, self.shard_at(zs, fx=1), 0), self.dev(fy=1)
        elif kind == 3:
            part, dev = self.piece(tensor, self.shard_at(zs, fy=1), 1), self.dev(fx=1)
        else:
            fx, fy = ((0, 0), (1, 0), (0, 1), (1, 1))[kind - 4]
            part, dev = self.piece(tensor, self.shard_at(zs, fx, fy)), self.dev(fc=1)
        row = (tensor * 4 + zs) * 8 + kind
        return self.copy(part, part, self.gsend.at[row], self.grecv.at[row], dev)

    def start(self, tensor, zs, kind):
        self.gcopy(tensor, zs, kind).start()

    def arrive(self, tensor, zs, kind):
        if kind < 2:
            part = self.piece(tensor, self.shard_at(zs, fx=1 - kind, fy=kind))
        elif kind < 4:
            part = self.piece(tensor, self.shard_at(zs, 1, 1), kind - 2)
        else:
            fx, fy = ((0, 0), (1, 0), (0, 1), (1, 1))[kind - 4]
            part = self.piece(tensor, self.shard_at(zs, fx, fy, 1))
        row = (tensor * 4 + zs) * 8 + kind
        self.copy(
            part, part, self.gsend.at[row], self.grecv.at[row], self.dev(fc=1)).wait_recv()

    def z_arrive(self, tensor, k):
        part = self.piece(tensor, self.shard_at((self.z + 4 - k) % 4))
        row = tensor * 3 + k - 1
        self.copy(
            part, part, self.zsend.at[row], self.zrecv.at[row], self.dev(fc=1)).wait_recv()

    def zcopy(self, tensor, k):
        part = self.piece(tensor, self.shard)
        row = tensor * 3 + k - 1
        return self.copy(
            part, part, self.zsend.at[row], self.zrecv.at[row], self.dev(z=(self.z + k) % 4)
        )

    def z_sends(self, tensor):
        for k in (1, 3, 2):
            self.zcopy(tensor, k).start()

    def p1(self, tensor, zs, k=None):
        if k is None:
            for kk in (1, 2, 3):
                @pl.when((self.z + 4 - kk) % 4 == zs)
                def _(kk=kk):
                    self.z_arrive(tensor, kk)
        elif k:
            self.z_arrive(tensor, k)
        for kind in (0, 1, 4):
            self.start(tensor, zs, kind)

    def p2(self, tensor, zs):
        self.arrive(tensor, zs, 0)
        self.start(tensor, zs, 2)
        self.start(tensor, zs, 5)
        self.arrive(tensor, zs, 1)
        self.start(tensor, zs, 3)
        self.start(tensor, zs, 6)

    def p3(self, tensor, zs):
        self.arrive(tensor, zs, 2)
        self.arrive(tensor, zs, 3)
        self.start(tensor, zs, 7)

    def p4(self, tensor, zs):
        for kind in (4, 5, 6, 7):
            self.arrive(tensor, zs, kind)

    def sends_done(self, tensor):
        for zs in range(4):
            self.plane_sent(tensor, zs)
        for k in (1, 2, 3):
            self.zcopy(tensor, k).wait_send()

    def plane_sent(self, tensor, zs):
        for kind in range(8):
            self.gcopy(tensor, zs, kind).wait_send()

    def own_rows(self):
        for src, dst in ((self.sh_s, self.ws), (self.sh_c, self.wc)):
            self.flat[0:576, :] = src[...].astype(F32)
            row = al(self.shard * AR, 16)
            for t in range(6):
                dst[pl.ds(row, AR), 128 * t:128 * t + 128] = self.flat[
                    pl.ds(t, AR, stride=6), :].astype(BF)
        self.own_ff()

    def own_ff(self):
        self.flat[0:1152, :] = self.sh_f[...].astype(F32)
        base = self.shard * FU
        flat, wf = self.flat, self.wf

        def wide(rows):
            for u in range(4):
                for w in range(2):
                    top = flat[pl.ds(4 * u + w, rows, stride=16), :]
                    low = flat[pl.ds(4 * u + w + 2, rows, stride=16), :]
                    wf[pl.ds(al(base + 2 * rows * u, 16), 2 * rows), 128 * w:128 * w + 128] = (
                        jnp.concatenate([top, low], axis=0).astype(BF))

        def tall(first, rows, offset):
            for t in range(6):
                wf[pl.ds(al(base + offset + rows * (t // 2), 16), rows),
                   128 * (t % 2):128 * (t % 2) + 128] = flat[
                       pl.ds(first + t, rows, stride=6), :].astype(BF)

        @pl.when(self.shard < 21)
        def _():
            wide(72)

        @pl.when(self.shard == 21)
        def _():
            wide(24)
            tall(384, 128, 192)

        @pl.when(self.shard > 21)
        def _():
            tall(0, 192, 0)

    def build_wide(self, ch):
        rows1 = 24 if ch == 10 else 72

        def step(u, _):
            low = self.wf[pl.ds(al(1152 * ch + 144 * u, 16), 144), :].astype(F32)
            high = self.wf[
                pl.ds(al(1152 * ch + FU + 2 * rows1 * u, 16), 2 * rows1), :].astype(F32)
            for w in range(2):
                value = jnp.concatenate(
                    [low[72 * w:72 * w + 72], high[rows1 * w:rows1 * w + rows1]], axis=0)
                self.wgu[144 * ch:144 * ch + 72 + rows1,
                         pl.ds(al(512 * u + 256 * w, 256), 256)] = value.astype(BF)
            return 0

        lax.fori_loop(0, 4, step, 0)

    def build_tall(self, s):
        first, rows, offset = (0, 128, 192) if s == 21 else (192 * s - 4096, 192, 0)
        for p in range(3):
            self.wd[first:first + rows, 256 * p:256 * p + 256] = self.wf[
                FU * s + offset + rows * p:FU * s + offset + rows * p + rows, :]

    def build_plane(self, zs):
        if zs < 2:
            for ch in range(4 * zs, 4 * zs + 4):
                self.build_wide(ch)
        elif zs == 2:
            for ch in (8, 9, 10):
                self.build_wide(ch)
            for s in (21, 22, 23):
                self.build_tall(s)
        else:
            for s in range(24, 32):
                self.build_tall(s)

    def masks(self):
        lane = lax.broadcasted_iota(jnp.int32, (128, 128), 1)
        self.left = lane < DH

    def stack(self, pair):
        zero = jnp.zeros_like(pair)
        return jnp.concatenate(
            [jnp.where(self.left, pair, zero), jnp.where(self.left, zero, pair)], axis=0)

    def unstack(self, both):
        rows = both.shape[0] // 2
        return jnp.where(self.left, both[0:rows], both[rows:])

    def bias(self):
        lane = lax.broadcasted_iota(jnp.int32, (1, 128), 1)
        bucket = bucket_of((128 - lane) % 128)
        for h in range(H):
            row = jnp.zeros((1, 128), F32)
            for b in range(NB):
                row = jnp.where(bucket == b, self.table[b, h], row)
            full = jnp.broadcast_to(row, (128, 128))
            self.ps[128 * h:128 * h + 128, :] = pltpu.roll(
                full, 0, 1, stride=1, stride_axis=0)

    def project(self, left, ref, row, out):
        for p in range(3):
            out[:, 256 * p:256 * p + 256] = nn(
                left, ref[row:row + D, 256 * p:256 * p + 256]).astype(BF)

    def add_product(self, left, ref, row, base, out):
        for p in range(3):
            cols = slice(256 * p, 256 * p + 256)
            out[:, cols] = base[:, cols].astype(F32) + nn(left, ref[row:row + D, cols])

    def heads(self, p):
        return pl.ds(al(p * 256, 256), 256)

    def self_forward(self):
        x = self.x_in[...].astype(F32)
        self.n1[...] = rms(x, self.gains[0:1, :]).astype(BF)
        n1 = self.n1[...]
        for m, out in enumerate((self.q, self.k, self.v)):
            self.project(n1, self.ws, D * m, out)
        length = self.dl[0]
        row = lax.broadcasted_iota(jnp.int32, (256, 128), 0) % 128
        col = lax.broadcasted_iota(jnp.int32, (256, 128), 1)
        keep = (col <= row) & (col < length)

        def pair(p, _):
            cols = pl.ds(al(p * 128, 128), 128)
            s = nt(self.stack(self.q[:, cols]), self.k[:, cols]) + self.ps[self.heads(p), :]
            s = jnp.where(keep, s, MASKED)
            e = jnp.exp(s - jnp.max(s, axis=-1, keepdims=True))
            prob = e / jnp.sum(e, axis=-1, keepdims=True)
            self.ps[self.heads(p), :] = prob
            self.mix[:, cols] = self.unstack(nn(prob.astype(BF), self.v[:, cols])).astype(BF)
            return 0

        lax.fori_loop(0, PAIRS, pair, 0)
        self.add_product(self.mix[...], self.ws, 3 * D, self.x_in, self.r1)
        self.n2[...] = rms(self.r1[...], self.gains[1:2, :]).astype(BF)

    def cross_kv(self, m, out):
        for i in range(4):
            for p in range(3):
                out[128 * i:128 * i + 128, 256 * p:256 * p + 256] = nn(
                    self.mem[128 * i:128 * i + 128, :],
                    self.wc[D * m:D * m + D, 256 * p:256 * p + 256]).astype(BF)

    def cross_probs(self, p):
        cols = pl.ds(al(p * 128, 128), 128)
        col = lax.broadcasted_iota(jnp.int32, (256, self.mem.shape[0]), 1)
        s = nt(self.stack(self.cq[:, cols]), self.ck[:, cols])
        s = jnp.where(col < self.ml[0], s, MASKED)
        e = jnp.exp(s - jnp.max(s, axis=-1, keepdims=True))
        return e / jnp.sum(e, axis=-1, keepdims=True)

    def cross_forward(self):
        self.project(self.n2[...], self.wc, 0, self.cq)

        def pair(p, _):
            cols = pl.ds(al(p * 128, 128), 128)
            prob = self.cross_probs(p)
            self.cmix[:, cols] = self.unstack(nn(prob.astype(BF), self.cv[:, cols])).astype(BF)
            return 0

        lax.fori_loop(0, PAIRS, pair, 0)
        self.add_product(self.cmix[...], self.wc, 3 * D, self.r1, self.r2)
        self.n3[...] = rms(self.r2[...], self.gains[2:3, :]).astype(BF)

    def ff_forward(self):
        n3 = self.n3[...]
        c0 = float(np.sqrt(2.0 / np.pi))

        def chunk(i, _):
            cols = pl.ds(al(i * 256, 256), 256)
            a = nn(n3, self.wgu[0:D, cols])
            up = nn(n3, self.wgu[D:2 * D, cols])
            sq = a * a
            t = jnp.tanh(c0 * (a + 0.044715 * a * sq))
            gelu = 0.5 * a * (1.0 + t)
            slope = 0.5 * (1.0 + t) + 0.5 * a * (1.0 - t * t) * (c0 * (1.0 + 0.134145 * sq))
            self.ga[:, cols] = gelu
            self.ub[:, cols] = up * slope
            self.hid[:, cols] = (gelu * up).astype(BF)
            return 0

        lax.fori_loop(0, FF // 256, chunk, 0)

    def out_rows(self):
        hid = self.hid[...]
        for p in range(3):
            cols = slice(256 * p, 256 * p + 256)
            self.block[:, cols] = (self.r2[:, cols] + nn(hid, self.wd[:, cols])).astype(BF)

    def d_hidden(self):
        g = self.g[...]

        def chunk(i, _):
            at = al(i * 256, 256)
            cols = pl.ds(at, 256)
            dh = nt(g, self.wd[pl.ds(at, 256), :]).astype(BF).astype(F32)
            self.dg[:, cols] = (dh * self.ub[:, cols]).astype(BF)
            self.du[:, cols] = (dh * self.ga[:, cols]).astype(BF)
            return 0

        lax.fori_loop(0, FF // 256, chunk, 0)

    def place(self, g):
        own = OWN[g]
        out = OWN_ROWS + (g % 2) * STAGE
        return own + self.c * (out - own), out + self.c * (own - out)

    def grad_tall(self, g, ch, i):
        b0, b1 = self.place(g)
        gout = self.g[...]
        first = 384 * ch - 4096

        for p in range(3):
            both = nn(self.hidt[pl.ds(al(first, 16), 384), :], gout[:, 256 * p:256 * p + 256])
            self.gb[pl.ds(al(b0 + FU * i + 192 * p, 16), 192), :] = both[0:192].astype(BF)
            self.gb[pl.ds(al(b1 + FU * i + 192 * p, 16), 192), :] = both[192:].astype(BF)

    def grad_tall_part(self, base, i, first, rows, offset):
        for p in range(3):
            value = nn(self.hidt[first:first + rows, :], self.g[:, 256 * p:256 * p + 256])
            self.gb[pl.ds(al(base + FU * i + offset + rows * p, 16), rows), :] = value.astype(BF)

    def grad_wide(self, g, ch, i):
        b0, b1 = self.place(g)
        rows1 = 24 if ch == 10 else 72
        first, end = 144 * ch, 144 * ch + 72 + rows1

        def step(u, _):
            cols = pl.ds(al(512 * u, 512), 512)
            parts = []
            if first < D:
                parts.append(nn(self.n3t[first:min(end, D), :], self.dg[:, cols]))
            if end > D:
                parts.append(nn(self.n3t[max(first, D) - D:end - D, :], self.du[:, cols]))
            both = parts[0] if len(parts) == 1 else jnp.concatenate(parts, axis=0)
            for base, at, rows in ((b0, 0, 72), (b1, 72, rows1)):
                value = jnp.concatenate(
                    [both[at:at + rows, 0:256], both[at:at + rows, 256:512]], axis=0)
                self.gb[pl.ds(al(base + FU * i + 2 * rows * u, 16), 2 * rows), :] = (
                    value.astype(BF))
            return 0

        lax.fori_loop(0, 4, step, 0)

    def grad_ff(self, g):
        zb = GROUPS[g][1]
        if zb == 3:
            def step(i, _):
                self.grad_tall(g, 12 + i, i)
                return 0
            lax.fori_loop(0, 4, step, 0)
        elif zb == 2:
            b0, b1 = self.place(g)
            for i in range(3):
                self.grad_wide(g, 8 + i, i)
            self.grad_tall_part(b1, 2, 0, 128, 192)
            self.grad_tall_part(b0, 3, 128, 192, 0)
            self.grad_tall_part(b1, 3, 320, 192, 0)
        else:
            for i in range(4):
                self.grad_wide(g, 4 * zb + i, i)

    def grad_square(self, g, leftt, right):
        b0, b1 = self.place(g)

        def step(i, _):
            rows = leftt[pl.ds(al(192 * i, 16), 192), :]
            for p in range(3):
                both = nn(rows, right[:, 256 * p:256 * p + 256])
                self.gb[pl.ds(al(b0 + AU * i + 96 * p, 16), 96), :] = both[0:96].astype(BF)
                self.gb[pl.ds(al(b1 + AU * i + 96 * p, 16), 96), :] = both[96:].astype(BF)
            return 0

        lax.fori_loop(0, 4, step, 0)

    def back_product(self, terms, out):
        for p in range(3):
            total = None
            for d_ref, w_ref, row, width in terms:
                value = nt(d_ref[...], w_ref[row + 256 * p:row + 256 * p + 256, 0:width])
                total = value if total is None else total + value
            out[:, 256 * p:256 * p + 256] = total

    def norm_three_back(self):
        self.back_product(((self.dg, self.wgu, 0, FF), (self.du, self.wgu, D, FF)), self.dz)
        dv, dg = rms_back(self.r2[...], self.gains[2:3, :], self.dz[...])
        self.redg[2:3, :] = dg
        self.dr[...] = self.g[...].astype(F32) + dv
        self.drb[...] = self.dr[...].astype(BF)

    def cross_back(self):
        for p in range(3):
            self.dm[:, 256 * p:256 * p + 256] = nt(
                self.drb[...], self.wc[3 * D + 256 * p:3 * D + 256 * p + 256, :]).astype(BF)

        def pair(p, _):
            cols = pl.ds(al(p * 128, 128), 128)
            dms = self.stack(self.dm[:, cols])
            kp = self.ck[:, cols]
            qs = self.stack(self.cq[:, cols])
            prob = self.cross_probs(p)
            dp = nt(dms, self.cv[:, cols])
            ds = (prob * (dp - jnp.sum(prob * dp, axis=-1, keepdims=True))).astype(BF)
            self.cv[:, cols] = tn(prob.astype(BF), dms).astype(BF)
            self.cq[:, cols] = self.unstack(nn(ds, kp)).astype(BF)
            self.ck[:, cols] = tn(ds, qs).astype(BF)
            return 0

        lax.fori_loop(0, PAIRS, pair, 0)

    def memory_rows(self):
        for i in range(4):
            rows = slice(128 * i, 128 * i + 128)
            for p in range(3):
                wrow = 256 * p
                self.mgrad[rows, 256 * p:256 * p + 256] = (
                    nt(self.ck[rows, :], self.wc[D + wrow:D + wrow + 256, :])
                    + nt(self.cv[rows, :], self.wc[2 * D + wrow:2 * D + wrow + 256, :])
                ).astype(BF)

    def norm_two_back(self):
        self.back_product(((self.cq, self.wc, 0, D),), self.dz)
        dv, dg = rms_back(self.r1[...], self.gains[1:2, :], self.dz[...])
        self.redg[1:2, :] = dg
        self.dr[...] = self.dr[...] + dv
        self.drb[...] = self.dr[...].astype(BF)

    def self_back(self):
        for p in range(3):
            self.dm[:, 256 * p:256 * p + 256] = nt(
                self.drb[...], self.ws[3 * D + 256 * p:3 * D + 256 * p + 256, :]).astype(BF)

        def pair(p, _):
            cols = pl.ds(al(p * 128, 128), 128)
            dms = self.stack(self.dm[:, cols])
            kp = self.k[:, cols]
            qs = self.stack(self.q[:, cols])
            prob = self.ps[self.heads(p), :]
            dp = nt(dms, self.v[:, cols])
            ds = (prob * (dp - jnp.sum(prob * dp, axis=-1, keepdims=True))).astype(BF)
            self.ps[self.heads(p), :] = ds.astype(F32)
            self.v[:, cols] = tn(prob.astype(BF), dms).astype(BF)
            self.q[:, cols] = self.unstack(nn(ds, kp)).astype(BF)
            self.k[:, cols] = tn(ds, qs).astype(BF)
            return 0

        lax.fori_loop(0, PAIRS, pair, 0)

    def norm_one_back(self):
        self.back_product(
            ((self.q, self.ws, 0, D), (self.k, self.ws, D, D), (self.v, self.ws, 2 * D, D)),
            self.dz)
        dv, dg = rms_back(self.x_in[...].astype(F32), self.gains[0:1, :], self.dz[...])
        self.redg[0:1, :] = dg
        self.xgrad[...] = (self.dr[...] + dv).astype(BF)

    def table_back(self):
        row = lax.broadcasted_iota(jnp.int32, (128, 128), 0)
        col = lax.broadcasted_iota(jnp.int32, (128, 128), 1)
        flip = jnp.where(row + col == 127, 1.0, 0.0).astype(BF)
        self.diag[...] = jnp.zeros_like(self.diag)
        for p in range(PAIRS):
            back = nn(self.ps[256 * p:256 * p + 256, :].astype(BF), flip)
            for hh in range(2):
                turned = pltpu.roll(
                    back[128 * hh:128 * hh + 128], 0, 1, stride=1, stride_axis=0)
                self.diag[2 * p + hh:2 * p + hh + 1, :] = jnp.sum(turned, axis=0, keepdims=True)
        lane = lax.broadcasted_iota(jnp.int32, (NB, 128), 1)
        hot = jnp.where(
            bucket_of((lane + 1) % 128) == lax.broadcasted_iota(jnp.int32, (NB, 128), 0), 1.0, 0.0)
        self.redt[:, 0:16] = lax.dot_general(
            hot, self.diag[...], (((1,), (1,)), ((), ())),
            precision=lax.Precision.HIGHEST, preferred_element_type=F32)

    def ropy(self, src, dst, g, kind, device):
        row = g * 8 + kind
        return self.copy(src, dst, self.rsend.at[row], self.rrecv.at[row], device)

    def own(self, g, chip, half=None):
        unit = UNIT[g]
        start = OWN[g] + chip * unit
        if half is not None:
            unit = unit // 2
            start = start + half * unit
        return pl.ds(al(start, 16), unit)

    def land(self, g, which, half=None):
        unit = UNIT[g]
        start = LAND[g] + (0, unit // 2, unit, 2 * unit)[which]
        rows = unit // 2 if which < 2 else unit
        if half is not None:
            rows = unit // 2
            start = start + half * rows
        return pl.ds(start, rows)

    def scopy(self, g, kind):
        gb, lb = self.gb, self.lb
        if kind == 0:
            rows = 4 * UNIT[g]
            return self.ropy(
                gb.at[pl.ds(OWN_ROWS + (g % 2) * STAGE, rows), :],
                self.wf.at[pl.ds(OWN[g], rows), :], g, 0, self.dev(fc=1))
        src, dst, dev = {
            1: (self.own(g, self.chip(1, 1), 0), self.land(g, 0), self.dev(fx=1)),
            2: (self.own(g, self.chip(1, 1), 1), self.land(g, 1), self.dev(fy=1)),
            3: (self.own(g, self.chip(1, 0), 0), self.land(g, 2, 0), self.dev(fx=1)),
            4: (self.own(g, self.chip(1, 0), 1), self.land(g, 2, 1), self.dev(fx=1)),
            5: (self.own(g, self.chip(0, 1), 1), self.land(g, 3, 1), self.dev(fy=1)),
            6: (self.own(g, self.chip(0, 1), 0), self.land(g, 3, 0), self.dev(fy=1)),
        }[kind]
        return self.ropy(gb.at[src, :], lb.at[dst, :], g, kind, dev)

    def to_owner(self, g):
        t, zb = GROUPS[g]
        unit = UNIT[g]
        slot = (self.z + 3 - zb) % 4
        return self.copy(
            self.gb.at[self.own(g, self.chip()), :],
            self.zb.at[pl.ds(al(ZBASE[t] + slot * unit, 16), unit), :],
            self.rsend.at[g * 8 + 7], self.orecv.at[t * 3 + slot], self.dev(z=zb))

    def from_plane(self, g, slot):
        t, zb = GROUPS[g]
        unit = UNIT[g]
        return self.copy(
            self.gb.at[self.own(g, self.chip()), :],
            self.zb.at[pl.ds(ZBASE[t] + slot * unit, unit), :],
            self.rsend.at[g * 8 + 7], self.orecv.at[t * 3 + slot], self.dev(z=zb))

    def rs0(self, g):
        self.scopy(g, 0).start()

    def stage_free(self, g):
        if g >= 2:
            self.scopy(g - 2, 0).wait_send()

    def accumulate(self, dst, src_ref, src):
        self.gb[dst, :] = (
            self.gb[dst, :].astype(F32) + src_ref[src, :].astype(F32)).astype(BF)

    def rs1(self, g):
        self.scopy(g, 0).wait_recv()
        for fx, fy, kinds in ((1, 1, (1, 2)), (1, 0, (3,)), (0, 1, (5,)), (0, 0, ())):
            rows = self.own(g, self.chip(fx, fy))
            self.accumulate(rows, self.wf, rows)
            for kind in kinds:
                self.scopy(g, kind).start()

    def rs2(self, g):
        self.scopy(g, 1).wait_recv()
        self.accumulate(self.own(g, self.chip(0, 1), 0), self.lb, self.land(g, 0))
        self.scopy(g, 6).start()
        self.scopy(g, 2).wait_recv()
        self.accumulate(self.own(g, self.chip(1, 0), 1), self.lb, self.land(g, 1))
        self.scopy(g, 4).start()

    def rs3(self, g):
        for kind in (3, 5, 4, 6):
            self.scopy(g, kind).wait_recv()
        rows = self.own(g, self.chip())
        self.gb[rows, :] = (
            self.gb[rows, :].astype(F32) + self.lb[self.land(g, 2), :].astype(F32)
            + self.lb[self.land(g, 3), :].astype(F32)).astype(BF)

        @pl.when(self.z != GROUPS[g][1])
        def _():
            self.to_owner(g).start()

    def rs4(self, g):
        t, zb = GROUPS[g]
        unit = UNIT[g]

        @pl.when(self.z == zb)
        def _():
            for slot in range(3):
                self.from_plane(g, slot).wait_recv()
            rows = self.own(g, self.chip())

            def total(start, size, lanes):
                at = pl.ds(al(OWN[g] + self.chip() * unit + start, 16), size)
                value = self.gb[at, lanes].astype(F32)
                for slot in range(3):
                    value = value + self.zb[
                        pl.ds(ZBASE[t] + slot * unit + start, size), lanes].astype(F32)
                return value

            del rows
            if t < 2:
                out = (self.gs, self.gc)[t]
                for k in range(6):
                    out[pl.ds(k, AR, stride=6), :] = total(
                        96 * (k // 2), 96, slice(128 * (k % 2), 128 * (k % 2) + 128))
                return
            out = self.gf

            def wide(rows):
                for u in range(4):
                    for w in range(2):
                        v = total(2 * rows * u, 2 * rows, slice(128 * w, 128 * w + 128))
                        out[pl.ds(4 * u + w, rows, stride=16), :] = v[0:rows]
                        out[pl.ds(4 * u + w + 2, rows, stride=16), :] = v[rows:]

            def tall(first, rows, offset):
                for k in range(6):
                    out[pl.ds(first + k, rows, stride=6), :] = total(
                        offset + rows * (k // 2), rows, slice(128 * (k % 2), 128 * (k % 2) + 128))

            if zb < 2:
                wide(72)
            elif zb == 3:
                tall(0, 192, 0)
            else:
                @pl.when(self.shard < 21)
                def _():
                    wide(72)

                @pl.when(self.shard == 21)
                def _():
                    wide(24)
                    tall(384, 128, 192)

                @pl.when(self.shard > 21)
                def _():
                    tall(0, 192, 0)

    def group_sent(self, g):
        for kind in range(1, 7):
            self.scopy(g, kind).wait_send()

        @pl.when(self.z != GROUPS[g][1])
        def _():
            self.to_owner(g).wait_send()

    def small(self, step, which):
        dev = (
            self.dev(fc=1), self.dev(fx=1), self.dev(fy=1),
            self.dev(z=self.z + 1 - 2 * (self.z % 2)), self.dev(z=(self.z + 2) % 4),
        )[step]
        src, dst = ((self.redg, self.landg), (self.redt, self.landt))[which]
        row = step * 2 + which
        return self.copy(
            src.at[step], dst.at[step], self.ssend.at[row], self.srecv.at[row], dev)

    def small_start(self, step):
        for which in range(2):
            self.small(step, which).start()

    def small_add(self, step):
        for which in range(2):
            self.small(step, which).wait_recv()
        self.redg[step + 1] = self.redg[step] + self.landg[step]
        self.redt[step + 1] = self.redt[step] + self.landt[step]


NAMES = (
    "x_in", "mem", "g", "dl", "ml", "sh_s", "sh_c", "sh_f", "gains", "table",
    "block", "xgrad", "mgrad", "gs", "gc", "gf", "ggain", "gtable",
    "ws", "wc", "wf", "wgu", "wd", "gb", "lb", "zb",
    "n1", "q", "k", "v", "mix", "r1", "n2", "cq", "ck", "cv", "cmix", "r2", "n3",
    "ga", "ub", "hid", "hidt", "n3t", "dg", "du", "dz", "dr", "drb", "tt", "memt",
    "ps", "diag", "redga", "redta", "landg", "landt",
    "gsend", "grecv", "zsend", "zrecv", "rsend", "rrecv", "orecv", "ssend", "srecv", "free",
)


def kernel(*args):
    refs = dict(zip(NAMES, args))
    st = Layer(refs)
    st.redg, st.redt = st.redga.at[0], st.redta.at[0]

    barrier = pltpu.get_barrier_semaphore()
    others = [st.dev(fc=1), st.dev(fx=1), st.dev(fy=1)] + [
        st.dev(z=(st.z + k) % 4) for k in (1, 2, 3)]
    for other in others:
        pl.semaphore_signal(barrier, inc=1, device_id=other, device_id_type=MESH)
    st.own_rows()
    st.masks()
    pl.semaphore_wait(barrier, 6)

    st.z_sends(0)
    plane = [(st.z + 4 - k) % 4 for k in range(4)]
    st.p1(0, plane[0], 0)
    st.bias()
    st.p1(0, plane[1], 1)
    st.p2(0, plane[0])
    st.p1(0, plane[3], 3)
    st.p2(0, plane[1])
    st.p3(0, plane[0])
    st.p1(0, plane[2], 2)
    st.z_sends(1)
    st.p2(0, plane[3])
    st.p3(0, plane[1])
    st.p1(1, plane[0], 0)
    st.p2(0, plane[2])
    st.p3(0, plane[3])
    st.p1(1, plane[1], 1)
    st.p2(1, plane[0])
    st.p3(0, plane[2])
    for zs in range(4):
        st.p4(0, plane[zs])
    st.self_forward()
    st.p1(1, plane[3], 3)
    st.p2(1, plane[1])
    st.p3(1, plane[0])
    st.p1(1, plane[2], 2)
    st.z_sends(2)
    st.p2(1, plane[3])
    st.p3(1, plane[1])
    st.p1(2, 0)
    st.p2(1, plane[2])
    st.p3(1, plane[3])
    st.p1(2, 1)
    st.p2(2, 0)
    st.p3(1, plane[2])
    for zs in range(4):
        st.p4(1, plane[zs])
    st.cross_kv(1, st.ck)
    st.cross_kv(2, st.cv)
    st.p1(2, 2)
    st.p2(2, 1)
    st.p3(2, 0)
    st.cross_forward()
    st.p1(2, 3)
    st.p2(2, 2)
    st.p3(2, 1)
    st.p4(2, 0)
    st.build_plane(0)
    st.p4(2, 1)
    st.build_plane(1)
    st.p2(2, 3)
    st.p3(2, 2)
    st.p4(2, 2)
    st.build_plane(2)
    st.ff_forward()
    st.hidt[...] = st.hid[...].T
    st.p3(2, 3)
    st.p4(2, 3)
    st.build_plane(3)
    for t in range(3):
        st.sends_done(t)
    pl.semaphore_signal(st.free, inc=1, device_id=st.dev(fc=1), device_id_type=MESH)
    st.grad_ff(0)
    pl.semaphore_wait(st.free, 1)
    st.rs0(0)
    st.d_hidden()
    st.n3t[...] = st.n3[...].T
    st.grad_ff(1)
    st.rs0(1)
    st.rs1(0)
    st.out_rows()
    st.stage_free(2)
    st.grad_ff(2)
    st.rs0(2)
    st.rs1(1)
    st.rs2(0)
    st.stage_free(3)
    st.grad_ff(3)
    st.rs0(3)
    st.rs1(2)
    st.rs2(1)
    st.rs3(0)
    st.norm_three_back()
    st.tt[...] = st.cmix[...].T
    st.stage_free(4)
    st.grad_square(4, st.tt, st.drb)
    st.rs0(4)
    st.rs1(3)
    st.rs2(2)
    st.rs3(1)
    st.rs4(0)
    st.cross_back()
    st.memt[...] = st.mem[...].T
    st.stage_free(5)
    st.grad_square(5, st.memt, st.cv)
    st.rs0(5)
    st.rs1(4)
    st.rs2(3)
    st.rs3(2)
    st.rs4(1)
    st.stage_free(6)
    st.grad_square(6, st.memt, st.ck)
    st.rs0(6)
    st.rs1(5)
    st.rs2(4)
    st.rs3(3)
    st.rs4(2)
    st.tt[...] = st.n2[...].T
    st.stage_free(7)
    st.grad_square(7, st.tt, st.cq)
    st.rs0(7)
    st.norm_two_back()
    st.rs1(6)
    st.rs2(5)
    st.rs3(4)
    st.rs4(3)
    st.tt[...] = st.mix[...].T
    st.stage_free(8)
    st.grad_square(8, st.tt, st.drb)
    st.rs0(8)
    st.self_back()
    st.rs1(7)
    st.rs2(6)
    st.rs3(5)
    st.rs4(4)
    st.tt[...] = st.n1[...].T
    st.stage_free(9)
    st.grad_square(9, st.tt, st.v)
    st.rs0(9)
    st.rs1(8)
    st.rs2(7)
    st.rs3(6)
    st.rs4(5)
    st.stage_free(10)
    st.grad_square(10, st.tt, st.k)
    st.rs0(10)
    st.norm_one_back()
    st.table_back()
    st.redg, st.redt = st.redga, st.redta
    st.small_start(0)
    st.rs1(9)
    st.rs2(8)
    st.rs3(7)
    st.rs4(6)
    st.small_add(0)
    st.small_start(1)
    st.stage_free(11)
    st.grad_square(11, st.tt, st.q)
    st.rs0(11)
    st.rs1(10)
    st.rs2(9)
    st.rs3(8)
    st.rs4(7)
    st.small_add(1)
    st.small_start(2)
    st.rs1(11)
    st.rs2(10)
    st.rs3(9)
    st.rs4(8)
    st.memory_rows()
    st.small_add(2)
    st.small_start(3)
    st.rs2(11)
    st.rs3(10)
    st.rs4(9)
    st.small_add(3)
    st.small_start(4)
    st.rs3(11)
    st.rs4(10)
    st.small_add(4)
    st.ggain[...] = st.redga[5, 0:3, :]
    st.gtable[...] = st.redta[5, :, 0:H]
    st.rs4(11)
    for g in range(12):
        st.group_sent(g)
    st.scopy(10, 0).wait_send()
    st.scopy(11, 0).wait_send()
    for step in range(5):
        for which in range(2):
            st.small(step, which).wait_send()


def fused(inputs, memory, out_cotangent, dec_lengths, mem_lengths, self_params, cross_params,
          ff_params, gains, table):
    slots, length, width = inputs.shape
    mem_len = memory.shape[1]
    vm = pl.BlockSpec(memory_space=pltpu.VMEM)
    sm = pl.BlockSpec(memory_space=pltpu.SMEM)
    s = jax.ShapeDtypeStruct
    rows_s, rows_f = self_params.shape[0] // 128, ff_params.shape[0] // 128
    row = pltpu.VMEM((length, D), BF)
    rowf = pltpu.VMEM((length, D), F32)
    memory_row = pltpu.VMEM((mem_len, D), BF)
    dma = pltpu.SemaphoreType.DMA
    outs = pl.pallas_call(
        kernel,
        out_shape=(
            s((length, D), BF), s((length, D), BF), s((mem_len, D), BF),
            s((rows_s, 128), F32), s((rows_s, 128), F32), s((rows_f, 128), F32),
            s((3, D), F32), s((NB, H), F32),
        ),
        in_specs=[vm, vm, vm, sm, sm, vm, vm, vm, vm, sm],
        out_specs=[vm] * 8,
        scratch_shapes=[
            pltpu.VMEM((4 * D, D), BF), pltpu.VMEM((4 * D, D), BF),
            pltpu.VMEM((32 * FU, 256), BF),
            pltpu.VMEM((2 * D, FF), BF), pltpu.VMEM((FF, D), BF),
            pltpu.VMEM((OWN_ROWS + 2 * STAGE, 256), BF),
            pltpu.VMEM((LAND_ROWS, 256), BF), pltpu.VMEM((Z_ROWS, 256), BF),
            row, row, row, row, row, rowf, row, row, memory_row, memory_row, row, rowf, row,
            pltpu.VMEM((length, FF), F32), pltpu.VMEM((length, FF), F32),
            pltpu.VMEM((length, FF), BF), pltpu.VMEM((FF, length), BF),
            pltpu.VMEM((D, length), BF),
            pltpu.VMEM((length, FF), BF), pltpu.VMEM((length, FF), BF),
            rowf, rowf, row, pltpu.VMEM((D, length), BF), pltpu.VMEM((D, mem_len), BF),
            pltpu.VMEM((H * length, length), F32),
            pltpu.VMEM((16, 128), F32),
            pltpu.VMEM((6, 8, D), F32), pltpu.VMEM((6, NB, 128), F32),
            pltpu.VMEM((5, 8, D), F32), pltpu.VMEM((5, NB, 128), F32),
            dma((96,)), dma((96,)), dma((9,)), dma((9,)), dma((96,)), dma((96,)), dma((9,)),
            dma((10,)), dma((10,)), pltpu.SemaphoreType.REGULAR,
        ],
        compiler_params=pltpu.CompilerParams(
            collective_id=0, has_side_effects=True, vmem_limit_bytes=67000000),
        cost_estimate=pl.CostEstimate(
            flops=10_000_000_000, bytes_accessed=8_000_000, transcendentals=2_000_000),
    )(
        inputs.reshape(length, width), memory.reshape(mem_len, width),
        out_cotangent.reshape(length, width), dec_lengths, mem_lengths,
        self_params.reshape(rows_s, 128), cross_params.reshape(rows_s, 128),
        ff_params.reshape(rows_f, 128), gains, table,
    )
    return (
        outs[0].reshape(inputs.shape), outs[1].reshape(inputs.shape),
        outs[2].reshape(memory.shape), outs[3].reshape(-1), outs[4].reshape(-1),
        outs[5].reshape(-1), outs[6], outs[7],
    )


HIGHEST = lax.Precision.HIGHEST


def product(left, right):
    return jnp.dot(left, right, preferred_element_type=jnp.float32)


def product_t(left, right):
    return lax.dot_general(
        left, right, (((0,), (0,)), ((), ())), preferred_element_type=jnp.float32
    )


def product_nt(left, right):
    return lax.dot_general(
        left, right, (((1,), (1,)), ((), ())), preferred_element_type=jnp.float32
    )


def rms_scale(value, gain):
    return value * lax.rsqrt(jnp.mean(value * value, axis=-1, keepdims=True) + 1e-06) * gain


def gelu_gate(gate_pre, up_pre):
    return jax.nn.gelu(gate_pre, approximate=True) * up_pre


def bucket_rows(start, count, length):
    half_count = NB // 2
    limits = np.ceil(
        half_count * (MAXD / half_count) ** (np.arange(1, half_count) / half_count)
    ).astype(np.int32)
    query_pos = start + jnp.arange(count, dtype=jnp.int32)
    key_pos = jnp.arange(length, dtype=jnp.int32)
    distance = query_pos[:, None] - key_pos[None, :]
    beyond = half_count + jnp.sum(
        (distance[None] >= jnp.asarray(limits)[:, None, None]).astype(jnp.int32), axis=0
    )
    return jnp.where(distance < half_count, jnp.maximum(distance, 0), beyond)


def onehot_block(start, count, length):
    bucket = bucket_rows(start, count, length)
    hot_rows = jnp.arange(NB, dtype=jnp.int32)[:, None, None] == bucket[None]
    return hot_rows.astype(jnp.float32).reshape(NB, count * length)


def position_bias(table, length):
    block_rows = min(length, 128)
    block_count = length // block_rows

    def position_per_block(block):
        bucket_hot = onehot_block(block * block_rows, block_rows, length)
        return lax.dot_general(
            table,
            bucket_hot,
            (((0,), (0,)), ((), ())),
            precision=HIGHEST,
            preferred_element_type=jnp.float32,
        )

    pieces = lax.map(position_per_block, jnp.arange(block_count, dtype=jnp.int32))
    return (
        pieces.reshape(block_count, H, block_rows, length)
        .transpose(1, 0, 2, 3)
        .reshape(H, length, length)
    )


def table_gradient(score_sums, length):
    block_rows = min(length, 128)

    def table_per_block(carry, block):
        ds_piece = score_sums.reshape(H, block_rows * length)
        bucket_hot = onehot_block(block * block_rows, block_rows, length)
        return (
            carry
            + lax.dot_general(
                bucket_hot,
                ds_piece,
                (((1,), (1,)), ((), ())),
                precision=HIGHEST,
                preferred_element_type=jnp.float32,
            ),
            None,
        )

    result, _ = lax.scan(
        table_per_block,
        jnp.zeros((NB, H), jnp.float32),
        jnp.arange(length // block_rows, dtype=jnp.int32),
    )
    return result


def score_block(queries, keys_in, score_bias, keep_mask):
    q_len = queries.shape[0]
    k_len = keys_in.shape[0]
    raw_scores = (
        jnp.einsum(
            "qhe,khe->hqk",
            queries.reshape(q_len, H, DH),
            keys_in.reshape(k_len, H, DH),
            preferred_element_type=jnp.float32,
        )
        + score_bias
    )
    return jnp.where(keep_mask[None], raw_scores, MASKED)


def attend_forward(queries, keys_in, values, score_bias, keep_mask):
    q_len = queries.shape[0]
    k_len = keys_in.shape[0]
    raw_scores = score_block(queries, keys_in, score_bias, keep_mask)
    row_max = jnp.max(raw_scores, axis=2, keepdims=True)
    exponent = jnp.exp(raw_scores - row_max)
    row_sum = jnp.sum(exponent, axis=2, keepdims=True)
    softmax_low = (exponent / row_sum).astype(jnp.bfloat16)
    head_mix = jnp.einsum(
        "hqk,khe->qhe",
        softmax_low,
        values.reshape(k_len, H, DH),
        preferred_element_type=jnp.float32,
    )
    return (head_mix.reshape(q_len, H * DH).astype(jnp.bfloat16), row_max, row_sum)


def attend_backward(queries, keys_in, values, score_bias, keep_mask, row_max, row_sum, d_mix):
    q_len = queries.shape[0]
    k_len = keys_in.shape[0]
    raw_scores = score_block(queries, keys_in, score_bias, keep_mask)
    softmax_out = jnp.exp(raw_scores - row_max) / row_sum
    softmax_low = softmax_out.astype(jnp.bfloat16)
    mix_heads = d_mix.reshape(q_len, H, DH)
    q_heads = queries.reshape(q_len, H, DH)
    k_heads = keys_in.reshape(k_len, H, DH)
    v_heads = values.reshape(k_len, H, DH)
    d_softmax = jnp.einsum("qhe,khe->hqk", mix_heads, v_heads, preferred_element_type=jnp.float32)
    d_scores = (
        softmax_out * (d_softmax - jnp.sum(softmax_out * d_softmax, axis=2, keepdims=True))
    ).astype(jnp.bfloat16)
    d_values = (
        jnp.einsum("hqk,qhe->khe", softmax_low, mix_heads, preferred_element_type=jnp.float32)
        .reshape(k_len, H * DH)
        .astype(jnp.bfloat16)
    )
    d_queries = (
        jnp.einsum("hqk,khe->qhe", d_scores, k_heads, preferred_element_type=jnp.float32)
        .reshape(q_len, H * DH)
        .astype(jnp.bfloat16)
    )
    d_keys = (
        jnp.einsum("hqk,qhe->khe", d_scores, q_heads, preferred_element_type=jnp.float32)
        .reshape(k_len, H * DH)
        .astype(jnp.bfloat16)
    )
    return (d_queries, d_keys, d_values, d_scores)


def attend_slots(queries, keys_in, values, lengths, score_bias, base_mask):
    slot_count = lengths.shape[0]
    q_len = queries.shape[0] // slot_count
    k_len = keys_in.shape[0] // slot_count
    key_pos = jnp.arange(k_len, dtype=jnp.int32)

    def per_slot(slot_item):
        q_slot, k_slot, v_slot, slot_len = slot_item
        keep_mask = base_mask & (key_pos[None, :] < slot_len)
        return attend_forward(q_slot, k_slot, v_slot, score_bias, keep_mask)

    head_mix, row_max, row_sum = lax.map(
        per_slot,
        (
            queries.reshape(slot_count, q_len, -1),
            keys_in.reshape(slot_count, k_len, -1),
            values.reshape(slot_count, k_len, -1),
            lengths,
        ),
    )
    return (head_mix.reshape(slot_count * q_len, -1), row_max, row_sum)


def attend_back_slots(
    queries, keys_in, values, lengths, score_bias, base_mask, row_max, row_sum, d_mix, with_table
):
    slot_count = lengths.shape[0]
    q_len = queries.shape[0] // slot_count
    k_len = keys_in.shape[0] // slot_count
    key_pos = jnp.arange(k_len, dtype=jnp.int32)
    if with_table:
        start = jnp.zeros((H, q_len, k_len), jnp.float32)
    else:
        start = jnp.zeros((), jnp.float32)

    def per_slot(carry, slot_item):
        q_slot, k_slot, v_slot, slot_len, max_slot, sum_slot, dmix_slot = slot_item
        keep_mask = base_mask & (key_pos[None, :] < slot_len)
        d_queries, d_keys, d_values, d_scores = attend_backward(
            q_slot, k_slot, v_slot, score_bias, keep_mask, max_slot, sum_slot, dmix_slot
        )
        if with_table:
            carry = carry + d_scores.astype(jnp.float32)
        return (carry, (d_queries, d_keys, d_values))

    score_sums, grad_parts = lax.scan(
        per_slot,
        start,
        (
            queries.reshape(slot_count, q_len, -1),
            keys_in.reshape(slot_count, k_len, -1),
            values.reshape(slot_count, k_len, -1),
            lengths,
            row_max,
            row_sum,
            d_mix.reshape(slot_count, q_len, -1),
        ),
    )
    return (
        grad_parts[0].reshape(slot_count * q_len, -1),
        grad_parts[1].reshape(slot_count * k_len, -1),
        grad_parts[2].reshape(slot_count * k_len, -1),
        score_sums,
    )


def gather_weights(self_params, cross_params, ff_params):
    return (
        lax.all_gather(self_params, ("dp", "fsdp"), axis=0, tiled=True),
        lax.all_gather(cross_params, ("dp", "fsdp"), axis=0, tiled=True),
        lax.all_gather(ff_params, ("dp", "fsdp"), axis=0, tiled=True),
    )


def scatter_grads(self_full, cross_full, ff_full):
    wide_count = lax.axis_size("dp")
    spread = (
        lax.all_to_all(
            self_full.reshape(wide_count, -1).astype(jnp.bfloat16),
            "dp",
            split_axis=0,
            concat_axis=0,
            tiled=True,
        ).astype(jnp.float32),
        lax.all_to_all(
            cross_full.reshape(wide_count, -1).astype(jnp.bfloat16),
            "dp",
            split_axis=0,
            concat_axis=0,
            tiled=True,
        ).astype(jnp.float32),
        lax.all_to_all(
            ff_full.reshape(wide_count, -1).astype(jnp.bfloat16),
            "dp",
            split_axis=0,
            concat_axis=0,
            tiled=True,
        ).astype(jnp.float32),
    )
    self_block = jnp.sum(spread[0], axis=0)
    cross_block = jnp.sum(spread[1], axis=0)
    ff_block = jnp.sum(spread[2], axis=0)
    return (
        lax.psum_scatter(
            self_block.astype(jnp.bfloat16), "fsdp", scatter_dimension=0, tiled=True
        ).astype(jnp.float32),
        lax.psum_scatter(
            cross_block.astype(jnp.bfloat16), "fsdp", scatter_dimension=0, tiled=True
        ).astype(jnp.float32),
        lax.psum_scatter(
            ff_block.astype(jnp.bfloat16), "fsdp", scatter_dimension=0, tiled=True
        ).astype(jnp.float32),
    )


def unpack(weights):
    self_flat, cross_flat, ff_flat = weights
    self_mats = self_flat.reshape(4, D, D)
    cross_mats = cross_flat.reshape(4, D, D)
    block_size = D * FF
    return (
        self_mats[0],
        self_mats[1],
        self_mats[2],
        self_mats[3],
        cross_mats[0],
        cross_mats[1],
        cross_mats[2],
        cross_mats[3],
        ff_flat[:block_size].reshape(D, FF),
        ff_flat[block_size : 2 * block_size].reshape(D, FF),
        ff_flat[2 * block_size :].reshape(FF, D),
    )


def run_forward(
    weights, flat_in, flat_mem, gains, pos_bias, causal, open_mask, dec_lengths, mem_lengths
):
    w_sq, w_sk, w_sv, w_so, w_cq, w_ck, w_cv, w_co, w_gate, w_up, w_down = unpack(weights)
    norm_one = rms_scale(flat_in, gains[0]).astype(jnp.bfloat16)
    self_q = product(norm_one, w_sq).astype(jnp.bfloat16)
    self_k = product(norm_one, w_sk).astype(jnp.bfloat16)
    self_v = product(norm_one, w_sv).astype(jnp.bfloat16)
    self_mix, self_max, self_sum = attend_slots(
        self_q, self_k, self_v, dec_lengths, pos_bias, causal
    )
    resid_one = flat_in + product(self_mix, w_so)
    norm_two = rms_scale(resid_one, gains[1]).astype(jnp.bfloat16)
    cross_q = product(norm_two, w_cq).astype(jnp.bfloat16)
    cross_k = product(flat_mem, w_ck).astype(jnp.bfloat16)
    cross_v = product(flat_mem, w_cv).astype(jnp.bfloat16)
    cross_mix, cross_max, cross_sum = attend_slots(
        cross_q, cross_k, cross_v, mem_lengths, 0.0, open_mask
    )
    resid_two = resid_one + product(cross_mix, w_co)
    norm_three = rms_scale(resid_two, gains[2]).astype(jnp.bfloat16)
    gate_pre = product(norm_three, w_gate)
    up_pre = product(norm_three, w_up)
    hidden = gelu_gate(gate_pre, up_pre).astype(jnp.bfloat16)
    block = resid_two + product(hidden, w_down)
    return (
        norm_one,
        self_q,
        self_k,
        self_v,
        self_mix,
        self_max,
        self_sum,
        resid_one,
        norm_two,
        cross_q,
        cross_k,
        cross_v,
        cross_mix,
        cross_max,
        cross_sum,
        resid_two,
        norm_three,
        gate_pre,
        up_pre,
        hidden,
        block,
    )


def by_collectives(
    inputs,
    memory,
    out_cotangent,
    dec_lengths,
    mem_lengths,
    self_params,
    cross_params,
    ff_params,
    gains,
    table,
):
    slot_count, length, model_width = inputs.shape
    mem_len = memory.shape[1]
    row_count = slot_count * length
    pos_bias = position_bias(table, length)
    positions = jnp.arange(length, dtype=jnp.int32)
    causal = positions[None, :] <= positions[:, None]
    open_mask = jnp.ones((length, mem_len), dtype=bool)
    flat_in = inputs.reshape(row_count, model_width).astype(jnp.float32)
    flat_mem = memory.reshape(slot_count * mem_len, model_width)
    weights = gather_weights(self_params, cross_params, ff_params)
    first_pass = run_forward(
        weights, flat_in, flat_mem, gains, pos_bias, causal, open_mask, dec_lengths, mem_lengths
    )
    block_out = first_pass[20].astype(jnp.bfloat16).reshape(slot_count, length, model_width)
    again = gather_weights(self_params, cross_params, ff_params)
    w_sq, w_sk, w_sv, w_so, w_cq, w_ck, w_cv, w_co, w_gate, w_up, w_down = unpack(again)
    (
        norm_one,
        self_q,
        self_k,
        self_v,
        self_mix,
        self_max,
        self_sum,
        resid_one,
        norm_two,
        cross_q,
        cross_k,
        cross_v,
        cross_mix,
        cross_max,
        cross_sum,
        resid_two,
        norm_three,
        gate_pre,
        up_pre,
        hidden,
        _,
    ) = run_forward(
        again, flat_in, flat_mem, gains, pos_bias, causal, open_mask, dec_lengths, mem_lengths
    )
    d_out = out_cotangent.reshape(row_count, model_width)
    grad_down = product_t(hidden, d_out)
    d_hidden = product_nt(d_out, w_down).astype(jnp.bfloat16)
    _, pull_gate = jax.vjp(gelu_gate, gate_pre, up_pre)
    d_gate, d_up = pull_gate(d_hidden.astype(jnp.float32))
    d_gate = d_gate.astype(jnp.bfloat16)
    d_up = d_up.astype(jnp.bfloat16)
    grad_gate = product_t(norm_three, d_gate)
    grad_up = product_t(norm_three, d_up)
    d_norm_three = product_nt(d_gate, w_gate) + product_nt(d_up, w_up)
    _, pull_three = jax.vjp(rms_scale, resid_two, gains[2])
    d_from_three, grad_gain_three = pull_three(d_norm_three)
    d_resid_two = d_out.astype(jnp.float32) + d_from_three
    d_cross = d_resid_two.astype(jnp.bfloat16)
    grad_co = product_t(cross_mix, d_cross)
    d_cross_mix = product_nt(d_cross, w_co).astype(jnp.bfloat16)
    dq_cross, dk_cross, dv_cross, _ = attend_back_slots(
        cross_q,
        cross_k,
        cross_v,
        mem_lengths,
        0.0,
        open_mask,
        cross_max,
        cross_sum,
        d_cross_mix,
        False,
    )
    grad_cq = product_t(norm_two, dq_cross)
    grad_ck = product_t(flat_mem, dk_cross)
    grad_cv = product_t(flat_mem, dv_cross)
    memory_grad = (product_nt(dk_cross, w_ck) + product_nt(dv_cross, w_cv)).astype(jnp.bfloat16)
    _, pull_two = jax.vjp(rms_scale, resid_one, gains[1])
    d_from_two, grad_gain_two = pull_two(product_nt(dq_cross, w_cq))
    d_resid_one = d_resid_two + d_from_two
    d_self = d_resid_one.astype(jnp.bfloat16)
    grad_so = product_t(self_mix, d_self)
    d_self_mix = product_nt(d_self, w_so).astype(jnp.bfloat16)
    dq_self, dk_self, dv_self, score_sums = attend_back_slots(
        self_q, self_k, self_v, dec_lengths, pos_bias, causal, self_max, self_sum, d_self_mix, True
    )
    grad_sq = product_t(norm_one, dq_self)
    grad_sk = product_t(norm_one, dk_self)
    grad_sv = product_t(norm_one, dv_self)
    d_norm_one = product_nt(dq_self, w_sq) + product_nt(dk_self, w_sk) + product_nt(dv_self, w_sv)
    _, pull_one = jax.vjp(rms_scale, flat_in, gains[0])
    d_from_one, grad_gain_one = pull_one(d_norm_one)
    input_grad = (d_resid_one + d_from_one).astype(jnp.bfloat16)
    table_local = table_gradient(score_sums, length)
    self_full = jnp.stack([grad_sq, grad_sk, grad_sv, grad_so]).reshape(-1)
    cross_full = jnp.stack([grad_cq, grad_ck, grad_cv, grad_co]).reshape(-1)
    ff_full = jnp.concatenate([grad_gate.reshape(-1), grad_up.reshape(-1), grad_down.reshape(-1)])
    self_shard, cross_shard, ff_shard = scatter_grads(self_full, cross_full, ff_full)
    gain_local = jnp.stack([grad_gain_one, grad_gain_two, grad_gain_three])
    gain_total, table_total = lax.psum((gain_local, table_local), ("dp", "fsdp"))
    return (
        block_out,
        input_grad.reshape(slot_count, length, model_width),
        memory_grad.reshape(slot_count, mem_len, model_width),
        self_shard,
        cross_shard,
        ff_shard,
        gain_total,
        table_total,
    )


def solution(mesh):
    whole = ("dp", "fsdp")
    rows = P(whole, None, None)
    flat = P(whole)
    small = mesh.shape["dp"] == 8 and mesh.shape["fsdp"] == 4
    return jax.shard_map(
        fused if small else by_collectives,
        mesh=mesh,
        in_specs=(rows, rows, rows, flat, flat, flat, flat, flat, P(), P()),
        out_specs=(rows, rows, rows, flat, flat, flat, P(), P()),
        check_vma=False,
    )
```

```python
import functools

import jax
import jax.numpy as jnp
import numpy as np
from jax import lax
from jax.experimental import pallas as pl
from jax.experimental.pallas import tpu as pltpu
from jax.sharding import PartitionSpec as P

D = 768
FF = 2048
H = 12
DH = 64
NB = 32
MAXD = 128
PAIRS = H // 2
MASKED = -1000000000.0
BF = jnp.bfloat16
F32 = jnp.float32
MESH = pl.DeviceIdType.MESH

AR = 96
AU = 288
FU = 576
GROUPS = (
    (2, 3), (2, 2), (2, 0), (2, 1),
    (1, 3), (1, 2), (1, 1), (1, 0),
    (0, 3), (0, 0), (0, 2), (0, 1),
)
PAIR = (True,) * 2 + (False,) * 10
SHARED = (False, False, True)
UNIT = tuple(FU if t == 2 else AU for t, _ in GROUPS)
OWN = tuple(4 * sum(UNIT[:g]) for g in range(12))
OWN_ROWS = 4 * sum(UNIT)
LAND = tuple(3 * sum(UNIT[:g]) for g in range(12))
LAND_ROWS = 3 * sum(UNIT)
ZBASE = (0, 3 * AU, 6 * AU)
Z_ROWS = 6 * AU + 3 * FU
STAGE = 4 * FU
ROLES = ((1, 1), (1, 0), (0, 1), (0, 0))
SIB = (0, 12, 13, 14)


def limits():
    half = NB // 2
    return [
        int(v)
        for v in np.ceil(half * (MAXD / half) ** (np.arange(1, half) / half)).astype(np.int32)
    ]


def bucket_of(distance):
    half = NB // 2
    beyond = jnp.full(distance.shape, half, jnp.int32)
    for limit in limits():
        beyond = beyond + jnp.where(distance >= limit, 1, 0)
    return jnp.where(distance < half, jnp.maximum(distance, 0), beyond)


def nn(left, right):
    return jnp.dot(left, right, preferred_element_type=F32)


def nt(left, right):
    return lax.dot_general(left, right, (((1,), (1,)), ((), ())), preferred_element_type=F32)


def tn(left, right):
    return lax.dot_general(left, right, (((0,), (0,)), ((), ())), preferred_element_type=F32)


def al(value, step):
    return pl.multiple_of(value, step)


def rms(value, gain):
    r = lax.rsqrt(jnp.mean(value * value, axis=-1, keepdims=True) + 1e-06)
    return value * r * gain


def rms_back(value, gain, dz):
    r = lax.rsqrt(jnp.mean(value * value, axis=-1, keepdims=True) + 1e-06)
    inner = jnp.mean(value * gain * dz, axis=-1, keepdims=True)
    dv = r * gain * dz - value * (r * r * r) * inner
    dg = jnp.sum(value * r * dz, axis=0, keepdims=True)
    return dv, dg


class Layer:
    def __init__(self, refs):
        self.__dict__.update(refs)
        self.flat, self.dm = self.ps, self.n3
        dp = lax.axis_index("dp")
        fs = lax.axis_index("fsdp")
        self.z, self.y = dp // 2, dp % 2
        self.x, self.c = fs // 2, fs % 2
        self.shard = dp * 4 + fs

    def dev(self, z=None, fx=0, fy=0, fc=0):
        z = self.z if z is None else z
        y = (self.y + fy) % 2
        x = (self.x + fx) % 2
        c = (self.c + fc) % 2
        return (z * 2 + y, x * 2 + c)

    def chip(self, fx=0, fy=0):
        return ((self.y + fy) % 2) * 2 + (self.x + fx) % 2

    def shard_at(self, z, fx=0, fy=0, fc=0):
        return z * 8 + self.chip(fx, fy) * 2 + (self.c + fc) % 2

    def copy(self, src, dst, send, recv, device):
        return pltpu.make_async_remote_copy(
            src_ref=src, dst_ref=dst, send_sem=send, recv_sem=recv,
            device_id=device, device_id_type=MESH,
        )

    def piece(self, tensor, shard, half=None, par=None):
        rows = FU if tensor == 2 else AR
        ref = (self.ws, self.wc, self.wf)[tensor]
        start = shard * rows
        if half is None:
            return ref.at[pl.ds(al(start, 16), rows), :]
        rows = rows // 2
        start = pl.ds(al(start + half * rows, 16), rows)
        if not SHARED[tensor]:
            return ref.at[start, :]
        width = ref.shape[1] // 2
        return ref.at[start, pl.ds(al(par * width, 128), width)]

    def plane(self, tensor, k):
        return k if tensor == 2 else (self.z + 4 - k) % 4

    def gcopy(self, tensor, zs, kind, there=False):
        par = self.z % 2
        if kind < 2:
            spot, dev = (0, 0), ((1, 0), (0, 1))[kind]
            if there:
                spot = dev
            part, dev = self.piece(tensor, self.shard_at(zs, *spot)), self.dev(None, *dev)
        elif kind < 4:
            spot, dev = ((1, 0), (0, 1)) if kind == 2 else ((0, 1), (1, 0))
            if there:
                spot = (1, 1)
            part = self.piece(tensor, self.shard_at(zs, *spot), kind - 2, par)
            dev = self.dev(None, *dev)
        elif kind < 8:
            spot = ((0, 0), (1, 0), (0, 1), (1, 1))[kind - 4]
            part = self.piece(tensor, self.shard_at(zs, *spot, 1 if there else 0))
            dev = self.dev(fc=1)
        else:
            part = self.piece(
                tensor, self.shard_at(zs, 1, 1), kind - 8, 1 - par if there else par)
            dev = self.dev(z=self.z + 1 - 2 * par)
        row = (tensor * 4 + zs) * 10 + kind
        return self.copy(part, part, self.gsend.at[row], self.grecv.at[row], dev)

    def start(self, tensor, zs, *kinds):
        for kind in kinds:
            self.gcopy(tensor, zs, kind).start()

    def arrive(self, tensor, zs, *kinds):
        for kind in kinds:
            self.gcopy(tensor, zs, kind, True).wait_recv()

    def zcopy(self, tensor, k):
        part = self.piece(tensor, self.shard)
        row = tensor * 3 + k - 1
        return self.copy(
            part, part, self.zsend.at[row], self.zrecv.at[row], self.dev(z=(self.z + k) % 4))

    def z_arrive(self, tensor, k):
        part = self.piece(tensor, self.shard_at((self.z + 4 - k) % 4))
        row = tensor * 3 + k - 1
        self.copy(
            part, part, self.zsend.at[row], self.zrecv.at[row], self.dev(fc=1)).wait_recv()

    def own_z(self, tensor, k):
        self.zcopy(tensor, k).start()

    def own_xy(self, tensor):
        self.start(tensor, self.z, 0, 1, 4)

    def p1(self, tensor, k):
        if tensor < 2:
            self.z_arrive(tensor, k)
            self.start(tensor, self.plane(tensor, k), 0, 1, 4)
            return
        for up in (1, 2, 3):
            @pl.when((self.z + 4 - up) % 4 == k)
            def _(up=up):
                self.z_arrive(tensor, up)
                self.start(tensor, k, 0, 1, 4)

        @pl.when(self.z == k)
        def _():
            self.start(tensor, k, 0, 1, 4)

    def p2x(self, tensor, k):
        zs = self.plane(tensor, k)
        self.arrive(tensor, zs, 0)
        self.start(tensor, zs, 2, 5)

    def p2y(self, tensor, k):
        zs = self.plane(tensor, k)
        self.arrive(tensor, zs, 1)
        self.start(tensor, zs, 3, 6)

    def p3(self, tensor, k, half):
        zs = self.plane(tensor, k)
        self.arrive(tensor, zs, 2 + half)
        if SHARED[tensor]:
            self.start(tensor, zs, 8 + half)
        elif half:
            self.start(tensor, zs, 7)

    def p4(self, tensor, k):
        if SHARED[tensor]:
            zs = self.plane(tensor, k)
            self.arrive(tensor, zs, 8, 9)
            self.start(tensor, zs, 7)

    def p5(self, tensor, k):
        self.arrive(tensor, self.plane(tensor, k), 4, 5, 6, 7)

    def plane_sent(self, tensor, k):
        for kind in range(10 if SHARED[tensor] else 8):
            self.gcopy(tensor, self.plane(tensor, k), kind).wait_send()

    def z_sent(self, tensor):
        for k in (1, 2, 3):
            self.zcopy(tensor, k).wait_send()

    def credit(self, which):
        if which == 0:
            self.z_sent(2)
        for k in ((0,), (1, 2, 3))[which]:
            self.plane_sent(2, k)
        pl.semaphore_signal(
            self.free.at[which], inc=1, device_id=self.dev(fc=1), device_id_type=MESH)

    def own_square(self, tensor):
        src, dst = ((self.sh_s, self.ws), (self.sh_c, self.wc))[tensor]
        self.flat[0:576, :] = src[...].astype(F32)
        row = al(self.shard * AR, 16)
        for t in range(6):
            dst[pl.ds(row, AR), 128 * t:128 * t + 128] = self.flat[
                pl.ds(t, AR, stride=6), :].astype(BF)

    def own_ff(self):
        self.flat[0:1152, :] = self.sh_f[...].astype(F32)
        base = self.shard * FU
        flat, wf = self.flat, self.wf

        def wide(rows):
            for u in range(4):
                for w in range(2):
                    top = flat[pl.ds(4 * u + w, rows, stride=16), :]
                    low = flat[pl.ds(4 * u + w + 2, rows, stride=16), :]
                    wf[pl.ds(al(base + 2 * rows * u, 16), 2 * rows), 128 * w:128 * w + 128] = (
                        jnp.concatenate([top, low], axis=0).astype(BF))

        def tall(first, rows, offset):
            for t in range(6):
                wf[pl.ds(al(base + offset + rows * (t // 2), 16), rows),
                   128 * (t % 2):128 * (t % 2) + 128] = flat[
                       pl.ds(first + t, rows, stride=6), :].astype(BF)

        @pl.when(self.shard < 21)
        def _():
            wide(72)

        @pl.when(self.shard == 21)
        def _():
            wide(24)
            tall(384, 128, 192)

        @pl.when(self.shard > 21)
        def _():
            tall(0, 192, 0)

    def build_wide(self, ch):
        rows1 = 24 if ch == 10 else 72

        def step(u, _):
            low = self.wf[pl.ds(al(1152 * ch + 144 * u, 16), 144), :].astype(F32)
            high = self.wf[
                pl.ds(al(1152 * ch + FU + 2 * rows1 * u, 16), 2 * rows1), :].astype(F32)
            for w in range(2):
                value = jnp.concatenate(
                    [low[72 * w:72 * w + 72], high[rows1 * w:rows1 * w + rows1]], axis=0)
                self.wgu[144 * ch:144 * ch + 72 + rows1,
                         pl.ds(al(512 * u + 256 * w, 256), 256)] = value.astype(BF)
            return 0

        lax.fori_loop(0, 4, step, 0)

    def build_tall(self, s):
        first, rows, offset = (0, 128, 192) if s == 21 else (192 * s - 4096, 192, 0)
        for p in range(3):
            self.wd[first:first + rows, 256 * p:256 * p + 256] = self.wf[
                FU * s + offset + rows * p:FU * s + offset + rows * p + rows, :]

    def build_plane(self, zs):
        if zs < 2:
            for ch in range(4 * zs, 4 * zs + 4):
                self.build_wide(ch)
        elif zs == 2:
            for ch in (8, 9, 10):
                self.build_wide(ch)
            for s in (21, 22, 23):
                self.build_tall(s)
        else:
            for s in range(24, 32):
                self.build_tall(s)

    def masks(self):
        lane = lax.broadcasted_iota(jnp.int32, (128, 128), 1)
        self.left = lane < DH

    def stack(self, pair):
        zero = jnp.zeros_like(pair)
        return jnp.concatenate(
            [jnp.where(self.left, pair, zero), jnp.where(self.left, zero, pair)], axis=0)

    def unstack(self, both):
        rows = both.shape[0] // 2
        return jnp.where(self.left, both[0:rows], both[rows:])

    def bias(self):
        lane = lax.broadcasted_iota(jnp.int32, (1, 128), 1)
        bucket = bucket_of((128 - lane) % 128)
        for h in range(H):
            row = jnp.zeros((1, 128), F32)
            for b in range(NB):
                row = jnp.where(bucket == b, self.table[h, b], row)
            full = jnp.broadcast_to(row, (128, 128))
            self.ps[128 * h:128 * h + 128, :] = pltpu.roll(
                full, 0, 1, stride=1, stride_axis=0)

    def project(self, left, ref, row, out):
        for p in range(3):
            out[:, 256 * p:256 * p + 256] = nn(
                left, ref[row:row + D, 256 * p:256 * p + 256]).astype(BF)

    def add_product(self, left, ref, row, base, out):
        for p in range(3):
            cols = slice(256 * p, 256 * p + 256)
            out[:, cols] = base[:, cols].astype(F32) + nn(left, ref[row:row + D, cols])

    def heads(self, p):
        return pl.ds(al(p * 256, 256), 256)

    def self_forward(self):
        x = self.x_in[...].astype(F32)
        self.n1[...] = rms(x, self.gains[0:1, :]).astype(BF)
        n1 = self.n1[...]
        for m, out in enumerate((self.q, self.k, self.v)):
            self.project(n1, self.ws, D * m, out)
        length = self.dl[0]
        row = lax.broadcasted_iota(jnp.int32, (256, 128), 0) % 128
        col = lax.broadcasted_iota(jnp.int32, (256, 128), 1)
        keep = (col <= row) & (col < length)

        def pair(p, _):
            cols = pl.ds(al(p * 128, 128), 128)
            s = nt(self.stack(self.q[:, cols]), self.k[:, cols]) + self.ps[self.heads(p), :]
            s = jnp.where(keep, s, MASKED)
            e = jnp.exp(s - jnp.max(s, axis=-1, keepdims=True))
            prob = e / jnp.sum(e, axis=-1, keepdims=True)
            self.ps[self.heads(p), :] = prob
            self.mix[:, cols] = self.unstack(nn(prob.astype(BF), self.v[:, cols])).astype(BF)
            return 0

        lax.fori_loop(0, PAIRS, pair, 0)
        self.add_product(self.mix[...], self.ws, 3 * D, self.x_in, self.r1)
        self.n2[...] = rms(self.r1[...], self.gains[1:2, :]).astype(BF)

    def cross_kv(self, m):
        out = (self.ck, self.cv)[m - 1]
        for i in range(4):
            for p in range(3):
                out[128 * i:128 * i + 128, 256 * p:256 * p + 256] = nn(
                    self.mem[128 * i:128 * i + 128, :],
                    self.wc[D * m:D * m + D, 256 * p:256 * p + 256]).astype(BF)

    def cross_probs(self, p):
        cols = pl.ds(al(p * 128, 128), 128)
        col = lax.broadcasted_iota(jnp.int32, (256, self.mem.shape[0]), 1)
        s = nt(self.stack(self.cq[:, cols]), self.ck[:, cols])
        s = jnp.where(col < self.ml[0], s, MASKED)
        e = jnp.exp(s - jnp.max(s, axis=-1, keepdims=True))
        return e / jnp.sum(e, axis=-1, keepdims=True)

    def cross_forward(self, part):
        if part == 0:
            self.project(self.n2[...], self.wc, 0, self.cq)

        def pair(p, _):
            cols = pl.ds(al(p * 128, 128), 128)
            prob = self.cross_probs(p)
            self.cmix[:, cols] = self.unstack(nn(prob.astype(BF), self.cv[:, cols])).astype(BF)
            return 0

        lax.fori_loop(2 * part, 2 * part + 2, pair, 0)
        if part == 2:
            self.add_product(self.cmix[...], self.wc, 3 * D, self.r1, self.r2)
            self.n3[...] = rms(self.r2[...], self.gains[2:3, :]).astype(BF)

    def ff_gate(self):
        n3 = self.n3[...]
        c0 = float(np.sqrt(2.0 / np.pi))

        def chunk(i, _):
            cols = pl.ds(al(i * 256, 256), 256)
            a = nn(n3, self.wgu[0:D, cols])
            sq = a * a
            t = jnp.tanh(c0 * (a + 0.044715 * a * sq))
            self.ga[:, cols] = 0.5 * a * (1.0 + t)
            self.ub[:, cols] = 0.5 * (1.0 + t) + 0.5 * a * (1.0 - t * t) * (
                c0 * (1.0 + 0.134145 * sq))
            return 0

        lax.fori_loop(0, FF // 256, chunk, 0)

    def ff_up(self):
        n3 = self.n3[...]

        def chunk(i, _):
            cols = pl.ds(al(i * 256, 256), 256)
            up = nn(n3, self.wgu[D:2 * D, cols])
            self.ub[:, cols] = up * self.ub[:, cols]
            self.hid[:, cols] = (self.ga[:, cols] * up).astype(BF)
            return 0

        lax.fori_loop(0, FF // 256, chunk, 0)
        self.hidt[...] = self.hid[...].T

    def out_rows(self):
        hid = self.hid[...]
        for p in range(3):
            cols = slice(256 * p, 256 * p + 256)
            self.block[:, cols] = (self.r2[:, cols] + nn(hid, self.wd[:, cols])).astype(BF)

    def d_hidden(self, part):
        g = self.g[...]

        def chunk(i, _):
            at = al(i * 256, 256)
            cols = pl.ds(at, 256)
            dh = nt(g, self.wd[pl.ds(at, 256), :]).astype(BF).astype(F32)
            self.dg[:, cols] = (dh * self.ub[:, cols]).astype(BF)
            self.du[:, cols] = (dh * self.ga[:, cols]).astype(BF)
            return 0

        lax.fori_loop(4 * part, 4 * part + 4, chunk, 0)

    def place(self, g):
        own = OWN[g]
        out = OWN_ROWS + (g % 2) * STAGE
        return own + self.c * (out - own), out + self.c * (own - out)

    def grad_tall(self, g, i):
        b0, b1 = self.place(g)
        for p in range(3):
            both = nn(
                self.hidt[pl.ds(al(512 + 384 * i, 16), 384), :],
                self.g[:, 256 * p:256 * p + 256])
            self.gb[pl.ds(al(b0 + FU * i + 192 * p, 16), 192), :] = both[0:192].astype(BF)
            self.gb[pl.ds(al(b1 + FU * i + 192 * p, 16), 192), :] = both[192:].astype(BF)

    def grad_tall_part(self, base, i, first, rows, offset):
        for p in range(3):
            value = nn(self.hidt[first:first + rows, :], self.g[:, 256 * p:256 * p + 256])
            self.gb[pl.ds(al(base + FU * i + offset + rows * p, 16), rows), :] = value.astype(BF)

    def grad_wide(self, g, ch, i):
        b0, b1 = self.place(g)
        rows1 = 24 if ch == 10 else 72
        first, end = 144 * ch, 144 * ch + 72 + rows1

        def step(u, _):
            cols = pl.ds(al(512 * u, 512), 512)
            parts = []
            if first < D:
                parts.append(nn(self.n3t[first:min(end, D), :], self.dg[:, cols]))
            if end > D:
                parts.append(nn(self.n3t[max(first, D) - D:end - D, :], self.du[:, cols]))
            both = parts[0] if len(parts) == 1 else jnp.concatenate(parts, axis=0)
            for base, at, rows in ((b0, 0, 72), (b1, 72, rows1)):
                value = jnp.concatenate(
                    [both[at:at + rows, 0:256], both[at:at + rows, 256:512]], axis=0)
                self.gb[pl.ds(al(base + FU * i + 2 * rows * u, 16), 2 * rows), :] = (
                    value.astype(BF))
            return 0

        lax.fori_loop(0, 4, step, 0)

    def grad_ff(self, g):
        zb = GROUPS[g][1]
        if zb == 2:
            b0, b1 = self.place(g)
            for i in range(3):
                self.grad_wide(g, 8 + i, i)
            self.grad_tall_part(b1, 2, 0, 128, 192)
            self.grad_tall_part(b0, 3, 128, 192, 0)
            self.grad_tall_part(b1, 3, 320, 192, 0)
        else:
            for i in range(4):
                self.grad_wide(g, 4 * zb + i, i)

    def grad_square(self, g, i):
        t, zb = GROUPS[g]
        left = self.memt if t == 1 and zb in (1, 2) else self.tt
        right = ((self.q, self.k, self.v, self.drb), (self.cq, self.ck, self.cv, self.drb))[t][zb]
        b0, b1 = self.place(g)
        rows = left[pl.ds(al(192 * i, 16), 192), :]
        for p in range(3):
            both = nn(rows, right[:, 256 * p:256 * p + 256])
            self.gb[pl.ds(al(b0 + AU * i + 96 * p, 16), 96), :] = both[0:96].astype(BF)
            self.gb[pl.ds(al(b1 + AU * i + 96 * p, 16), 96), :] = both[96:].astype(BF)

    def turn(self, g):
        if g == 1:
            self.n3t[...] = self.n3[...].T
        elif g == 5:
            self.memt[...] = self.mem[...].T
        elif g in (4, 7, 8, 9):
            left = {4: self.cmix, 7: self.n2, 8: self.mix, 9: self.n1}[g]
            self.tt[...] = left[...].T

    def back_product(self, terms, out):
        for p in range(3):
            total = None
            for d_ref, w_ref, row, width in terms:
                value = nt(d_ref[...], w_ref[row + 256 * p:row + 256 * p + 256, 0:width])
                total = value if total is None else total + value
            out[:, 256 * p:256 * p + 256] = total

    def norm_three_back(self):
        self.back_product(((self.dg, self.wgu, 0, FF), (self.du, self.wgu, D, FF)), self.dz)
        dv, dg = rms_back(self.r2[...], self.gains[2:3, :], self.dz[...])
        self.redg[0, 2:3, :] = dg
        self.dr[...] = self.g[...].astype(F32) + dv
        self.drb[...] = self.dr[...].astype(BF)

    def cross_back(self, part):
        for p in range(3) if part == 0 else ():
            self.dm[:, 256 * p:256 * p + 256] = nt(
                self.drb[...], self.wc[3 * D + 256 * p:3 * D + 256 * p + 256, :]).astype(BF)

        def pair(p, _):
            cols = pl.ds(al(p * 128, 128), 128)
            dms = self.stack(self.dm[:, cols])
            kp = self.ck[:, cols]
            qs = self.stack(self.cq[:, cols])
            prob = self.cross_probs(p)
            dp = nt(dms, self.cv[:, cols])
            ds = (prob * (dp - jnp.sum(prob * dp, axis=-1, keepdims=True))).astype(BF)
            self.cv[:, cols] = tn(prob.astype(BF), dms).astype(BF)
            self.cq[:, cols] = self.unstack(nn(ds, kp)).astype(BF)
            self.ck[:, cols] = tn(ds, qs).astype(BF)
            return 0

        lax.fori_loop(2 * part, 2 * part + 2, pair, 0)

    def memory_rows(self, i):
        rows = slice(128 * i, 128 * i + 128)
        for p in range(3):
            wrow = 256 * p
            self.mgrad[rows, 256 * p:256 * p + 256] = (
                nt(self.ck[rows, :], self.wc[D + wrow:D + wrow + 256, :])
                + nt(self.cv[rows, :], self.wc[2 * D + wrow:2 * D + wrow + 256, :])
            ).astype(BF)

    def norm_two_back(self):
        self.back_product(((self.cq, self.wc, 0, D),), self.dz)
        dv, dg = rms_back(self.r1[...], self.gains[1:2, :], self.dz[...])
        self.redg[0, 1:2, :] = dg
        self.dr[...] = self.dr[...] + dv
        self.drb[...] = self.dr[...].astype(BF)

    def self_back(self, part):
        for p in range(3) if part == 0 else ():
            self.dm[:, 256 * p:256 * p + 256] = nt(
                self.drb[...], self.ws[3 * D + 256 * p:3 * D + 256 * p + 256, :]).astype(BF)

        def pair(p, _):
            cols = pl.ds(al(p * 128, 128), 128)
            dms = self.stack(self.dm[:, cols])
            kp = self.k[:, cols]
            qs = self.stack(self.q[:, cols])
            prob = self.ps[self.heads(p), :]
            dp = nt(dms, self.v[:, cols])
            ds = (prob * (dp - jnp.sum(prob * dp, axis=-1, keepdims=True))).astype(BF)
            self.ps[self.heads(p), :] = ds.astype(F32)
            self.v[:, cols] = tn(prob.astype(BF), dms).astype(BF)
            self.q[:, cols] = self.unstack(nn(ds, kp)).astype(BF)
            self.k[:, cols] = tn(ds, qs).astype(BF)
            return 0

        lax.fori_loop(3 * part, 3 * part + 3, pair, 0)

    def norm_one_back(self):
        self.back_product(
            ((self.q, self.ws, 0, D), (self.k, self.ws, D, D), (self.v, self.ws, 2 * D, D)),
            self.dz)
        dv, dg = rms_back(self.x_in[...].astype(F32), self.gains[0:1, :], self.dz[...])
        self.redg[0, 0:1, :] = dg
        self.xgrad[...] = (self.dr[...] + dv).astype(BF)

    def table_back(self):
        row = lax.broadcasted_iota(jnp.int32, (128, 128), 0)
        col = lax.broadcasted_iota(jnp.int32, (128, 128), 1)
        flip = jnp.where(row + col == 127, 1.0, 0.0).astype(BF)
        self.diag[...] = jnp.zeros_like(self.diag)
        for p in range(PAIRS):
            back = nn(self.ps[256 * p:256 * p + 256, :].astype(BF), flip)
            for hh in range(2):
                turned = pltpu.roll(
                    back[128 * hh:128 * hh + 128], 0, 1, stride=1, stride_axis=0)
                self.diag[2 * p + hh:2 * p + hh + 1, :] = jnp.sum(turned, axis=0, keepdims=True)
        lane = lax.broadcasted_iota(jnp.int32, (NB, 128), 1)
        hot = jnp.where(
            bucket_of((lane + 1) % 128) == lax.broadcasted_iota(jnp.int32, (NB, 128), 0), 1.0, 0.0)
        self.redt[0, :, 0:NB] = lax.dot_general(
            self.diag[...], hot, (((1,), (1,)), ((), ())),
            precision=lax.Precision.HIGHEST, preferred_element_type=F32)

    def own(self, g, chip, half=None):
        unit = UNIT[g]
        start = OWN[g] + chip * unit
        if half is not None:
            unit = unit // 2
            start = start + half * unit
        return pl.ds(al(start, 16), unit)

    def land(self, g, which, half=None):
        unit = UNIT[g]
        start = LAND[g] + (0, unit // 2, unit, 2 * unit)[which]
        rows = unit // 2 if which < 2 else unit
        if half is not None:
            rows = unit // 2
            start = start + half * rows
        return pl.ds(start, rows)

    def lanes(self, g, mine):
        if not PAIR[g]:
            return slice(None)
        par = self.z % 2
        return pl.ds(al((par if mine else 1 - par) * 128, 128), 128)

    def scopy(self, g, kind):
        gb, lb = self.gb, self.lb
        row = g * 15 + kind
        sems = self.rsend.at[row], self.rrecv.at[row]
        if kind in SIB:
            unit = UNIT[g]
            at = self.chip(*ROLES[SIB.index(kind)]) * unit
            return self.copy(
                gb.at[pl.ds(al(OWN_ROWS + (g % 2) * STAGE + at, 16), unit), :],
                self.wf.at[pl.ds(al(OWN[g] + at, 16), unit), :], *sems, self.dev(fc=1))
        spot, half, lanes, where, dev = {
            1: ((1, 1), 0, True, 0, (1, 0)),
            2: ((1, 1), 1, True, 1, (0, 1)),
            3: ((1, 0), 0, None, 2, (1, 0)),
            4: ((1, 0), 1, True, 2, (1, 0)),
            5: ((1, 0), 1, False, 2, (1, 0)),
            6: ((0, 1), 1, None, 3, (0, 1)),
            7: ((0, 1), 0, True, 3, (0, 1)),
            8: ((0, 1), 0, False, 3, (0, 1)),
            9: ((1, 1), 0, False, 0, None),
            10: ((1, 1), 1, False, 1, None),
        }[kind]
        src = self.own(g, self.chip(*spot), half)
        dst = self.land(g, where, half if where > 1 else None)
        lanes = slice(None) if lanes is None else self.lanes(g, lanes)
        put = self.lanes(g, True) if dev is None else lanes
        dev = self.dev(z=self.z + 1 - 2 * (self.z % 2)) if dev is None else self.dev(None, *dev)
        return self.copy(gb.at[src, lanes], lb.at[dst, put], *sems, dev)

    def came(self, g, *kinds):
        for kind in kinds:
            if kind in (9, 10):
                part = self.lb.at[self.land(g, kind - 9), self.lanes(g, False)]
                row = g * 15 + kind
                self.copy(
                    part, part, self.rsend.at[row], self.rrecv.at[row],
                    self.dev(fc=1)).wait_recv()
            else:
                self.scopy(g, kind).wait_recv()

    def go(self, g, *kinds):
        for kind in kinds:
            self.scopy(g, kind).start()

    def to_owner(self, g, slot=None):
        t, zb = GROUPS[g]
        unit = UNIT[g]
        if slot is None:
            slot = (self.z + 3 - zb) % 4
        return self.copy(
            self.gb.at[self.own(g, self.chip()), :],
            self.zb.at[pl.ds(al(ZBASE[t] + slot * unit, 16), unit), :],
            self.rsend.at[g * 15 + 11], self.orecv.at[t * 3 + slot], self.dev(z=zb))

    def ready(self, g):
        self.turn(g)
        if g >= 2:
            for role in range(4):
                self.scopy(g - 2, SIB[role]).wait_send()

    def allowed(self, g):
        if g in (0, 2):
            pl.semaphore_wait(self.free.at[g // 2], 1)

    def part(self, g, i):
        (self.grad_tall if g == 0 else self.grad_square)(g, i)

    def grad(self, g):
        self.ready(g)
        if 0 < g < 4:
            self.grad_ff(g)
        else:
            def step(i, _):
                self.part(g, i)
                return 0
            lax.fori_loop(0, 4, step, 0)
        self.allowed(g)
        self.go(g, *SIB)

    def grad_role(self, g, role):
        if role == 0:
            self.ready(g)
        self.part(g, self.chip(*ROLES[role]))
        if role == 0:
            self.allowed(g)
        self.go(g, SIB[role])

    def accumulate(self, dst, lanes, src_ref, src, from_lanes):
        self.gb[dst, lanes] = (
            self.gb[dst, lanes].astype(F32) + src_ref[src, from_lanes].astype(F32)).astype(BF)

    def rs1(self, g, role):
        self.came(g, SIB[role])
        rows = self.own(g, self.chip(*ROLES[role]))
        self.accumulate(rows, slice(None), self.wf, rows, slice(None))
        self.go(g, *(((9, 10), (3, 5), (6, 8), ()) if PAIR[g] else ((1, 2), (3,), (6,), ()))[role])

    def rs2(self, g, half):
        if PAIR[g]:
            self.came(g, 9 + half)
            self.accumulate(
                self.own(g, self.chip(1, 1), half), self.lanes(g, True),
                self.lb, self.land(g, half), self.lanes(g, False))
            self.go(g, 1 + half)

    def rs3(self, g, half):
        kind, spot, late = ((1, (0, 1), 7), (2, (1, 0), 4))[half]
        self.came(g, kind)
        self.accumulate(
            self.own(g, self.chip(*spot), half), self.lanes(g, True),
            self.lb, self.land(g, kind - 1), self.lanes(g, True))
        self.go(g, late)

    def rs4(self, g):
        self.came(g, *((3, 5, 6, 8, 4, 7) if PAIR[g] else (3, 6, 4, 7)))
        rows = self.own(g, self.chip())
        self.gb[rows, :] = (
            self.gb[rows, :].astype(F32) + self.lb[self.land(g, 2), :].astype(F32)
            + self.lb[self.land(g, 3), :].astype(F32)).astype(BF)

        @pl.when(self.z != GROUPS[g][1])
        def _():
            self.to_owner(g).start()

    def rs5(self, g):
        t, zb = GROUPS[g]
        unit = UNIT[g]

        @pl.when(self.z == zb)
        def _():
            for slot in range(3):
                self.to_owner(g, slot).wait_recv()

            def total(start, size, lanes):
                at = pl.ds(al(OWN[g] + self.chip() * unit + start, 16), size)
                value = self.gb[at, lanes].astype(F32)
                for slot in range(3):
                    value = value + self.zb[
                        pl.ds(ZBASE[t] + slot * unit + start, size), lanes].astype(F32)
                return value

            if t < 2:
                out = (self.gs, self.gc)[t]
                for k in range(6):
                    out[pl.ds(k, AR, stride=6), :] = total(
                        96 * (k // 2), 96, slice(128 * (k % 2), 128 * (k % 2) + 128))
                return
            out = self.gf

            def wide(rows):
                for u in range(4):
                    for w in range(2):
                        v = total(2 * rows * u, 2 * rows, slice(128 * w, 128 * w + 128))
                        out[pl.ds(4 * u + w, rows, stride=16), :] = v[0:rows]
                        out[pl.ds(4 * u + w + 2, rows, stride=16), :] = v[rows:]

            def tall(first, rows, offset):
                for k in range(6):
                    out[pl.ds(first + k, rows, stride=6), :] = total(
                        offset + rows * (k // 2), rows, slice(128 * (k % 2), 128 * (k % 2) + 128))

            if zb < 2:
                wide(72)
            elif zb == 3:
                tall(0, 192, 0)
            else:
                @pl.when(self.shard < 21)
                def _():
                    wide(72)

                @pl.when(self.shard == 21)
                def _():
                    wide(24)
                    tall(384, 128, 192)

                @pl.when(self.shard > 21)
                def _():
                    tall(0, 192, 0)

    def group_sent(self, g):
        for kind in range(1, 11):
            if PAIR[g] or kind not in (5, 8, 9, 10):
                self.scopy(g, kind).wait_send()

        @pl.when(self.z != GROUPS[g][1])
        def _():
            self.to_owner(g).wait_send()

    def small(self, step, which):
        dev = (
            self.dev(fc=1), self.dev(fx=1), self.dev(fy=1),
            self.dev(z=self.z + 1 - 2 * (self.z % 2)), self.dev(z=(self.z + 2) % 4),
        )[step]
        src, dst = ((self.redg, self.landg), (self.redt, self.landt))[which]
        row = step * 2 + which
        return self.copy(
            src.at[step], dst.at[step], self.ssend.at[row], self.srecv.at[row], dev)

    def small_start(self, step):
        for which in range(2):
            self.small(step, which).start()

    def small_add(self, step):
        for which in range(2):
            self.small(step, which).wait_recv()
        self.redg[step + 1] = self.redg[step] + self.landg[step]
        self.redt[step + 1] = self.redt[step] + self.landt[step]


    def finish(self):
        for tensor in (0, 1):
            self.z_sent(tensor)
            for k in range(4):
                self.plane_sent(tensor, k)
        for g in range(12):
            self.group_sent(g)
        for g in (10, 11):
            for role in range(4):
                self.scopy(g, SIB[role]).wait_send()
        self.ggain[...] = self.redga[5, 0:3, :]
        self.gtable[...] = self.redta[5, 0:H, 0:NB]
        for step in range(5):
            for which in range(2):
                self.small(step, which).wait_send()


K = Layer
SCHEDULE = (
    (K.own_z, 0, 1), (K.own_xy, 0), (K.own_square, 1), (K.own_z, 1, 1), (K.own_xy, 1),
    (K.p1, 0, 1), (K.own_z, 0, 3), (K.p2x, 0, 0), (K.own_z, 0, 2), (K.own_z, 1, 2),
    (K.p1, 1, 1), (K.p2x, 1, 0), (K.p2y, 1, 0), (K.p2y, 0, 0), (K.p2x, 0, 1), (K.p2y, 0, 1),
    (K.own_z, 1, 3), (K.p2y, 1, 1), (K.p1, 0, 3), (K.p3, 1, 0, 0), (K.p3, 0, 0, 0),
    (K.p1, 0, 2), (K.p3, 0, 0, 1), (K.own_ff,), (K.own_z, 2, 3), (K.own_z, 2, 1), (K.p2y, 0, 3),
    (K.p3, 0, 1, 0), (K.p2x, 0, 3), (K.p3, 0, 1, 1), (K.p2x, 1, 1), (K.p2y, 0, 2), (K.p4, 0, 0),
    (K.p1, 1, 3), (K.p3, 1, 0, 1), (K.p3, 0, 3, 0), (K.p4, 1, 0), (K.p1, 1, 2), (K.p3, 0, 3, 1),
    (K.p2y, 1, 3), (K.p3, 1, 1, 0), (K.bias,), (K.p2x, 1, 3), (K.p2x, 0, 2), (K.p2y, 1, 2),
    (K.p3, 1, 1, 1), (K.p3, 1, 3, 0), (K.p3, 1, 3, 1), (K.p5, 1, 0), (K.p2x, 1, 2),
    (K.own_z, 2, 2), (K.p4, 1, 1), (K.p3, 0, 2, 0), (K.p1, 2, 1), (K.p3, 0, 2, 1), (K.p4, 1, 3),
    (K.p3, 1, 2, 0), (K.p3, 1, 2, 1), (K.p4, 1, 2), (K.p5, 1, 2), (K.p5, 1, 3), (K.p1, 2, 0),
    (K.p2y, 2, 1), (K.p4, 0, 2), (K.p5, 1, 1), (K.cross_kv, 2), (K.p1, 2, 2), (K.p2x, 2, 0),
    (K.cross_kv, 1), (K.p2x, 2, 1), (K.p5, 0, 2), (K.p4, 0, 1), (K.p2y, 2, 0), (K.p4, 0, 3),
    (K.p5, 0, 3), (K.p5, 0, 0), (K.p5, 0, 1), (K.self_forward,), (K.cross_forward, 0),
    (K.p3, 2, 0, 0), (K.p2y, 2, 2), (K.p2x, 2, 2), (K.p3, 2, 1, 0), (K.p3, 2, 0, 1),
    (K.p1, 2, 3), (K.p3, 2, 1, 1), (K.cross_forward, 1), (K.p3, 2, 2, 0), (K.cross_forward, 2),
    (K.p4, 2, 0), (K.p3, 2, 2, 1), (K.p4, 2, 1), (K.p5, 2, 0), (K.build_plane, 0),
    (K.p2x, 2, 3), (K.p2y, 2, 3), (K.credit, 0), (K.p5, 2, 1), (K.build_plane, 1), (K.p4, 2, 2),
    (K.ff_gate,), (K.p3, 2, 3, 0), (K.p5, 2, 2), (K.build_plane, 2), (K.p3, 2, 3, 1),
    (K.ff_up,), (K.grad_role, 0, 0), (K.grad_role, 0, 1), (K.grad_role, 0, 2), (K.rs1, 0, 0),
    (K.p4, 2, 3), (K.rs1, 0, 1), (K.grad_role, 0, 3), (K.rs1, 0, 2), (K.p5, 2, 3),
    (K.build_plane, 3), (K.d_hidden, 0), (K.d_hidden, 1), (K.rs2, 0, 0), (K.rs2, 0, 1),
    (K.grad, 1), (K.rs1, 1, 0), (K.credit, 1), (K.rs1, 1, 1), (K.rs3, 0, 1), (K.rs3, 0, 0),
    (K.rs1, 1, 2), (K.grad, 2), (K.norm_three_back,), (K.rs1, 2, 0), (K.grad, 3), (K.rs2, 1, 0),
    (K.rs1, 2, 2), (K.rs2, 2, 0), (K.rs1, 2, 1), (K.grad_role, 4, 0), (K.grad_role, 4, 1),
    (K.grad_role, 4, 2), (K.rs1, 3, 0), (K.rs1, 0, 3), (K.rs2, 3, 1), (K.grad_role, 4, 3),
    (K.rs1, 2, 3), (K.rs2, 2, 1), (K.rs1, 4, 0), (K.rs3, 2, 0), (K.rs2, 4, 1),
    (K.cross_back, 0), (K.rs1, 3, 2), (K.rs2, 1, 1), (K.cross_back, 1), (K.rs3, 2, 1),
    (K.cross_back, 2), (K.rs2, 3, 0), (K.rs1, 4, 1), (K.rs3, 4, 1), (K.rs4, 0), (K.rs1, 3, 1),
    (K.rs3, 3, 0), (K.grad, 5), (K.grad, 6), (K.rs3, 1, 0), (K.rs3, 3, 1), (K.rs4, 2),
    (K.grad, 7), (K.rs1, 5, 0), (K.rs2, 5, 0), (K.norm_two_back,), (K.self_back, 0),
    (K.rs1, 1, 3), (K.rs1, 7, 2), (K.rs1, 3, 3), (K.rs1, 5, 2), (K.rs3, 1, 1), (K.rs1, 4, 2),
    (K.self_back, 1), (K.rs1, 6, 0), (K.grad, 8), (K.rs1, 5, 1), (K.norm_one_back,), (K.rs4, 1),
    (K.grad_role, 9, 0), (K.rs4, 3), (K.rs1, 7, 0), (K.rs2, 7, 1), (K.table_back,),
    (K.rs2, 4, 0), (K.small_start, 0), (K.rs1, 8, 0), (K.rs1, 7, 1), (K.rs1, 5, 3),
    (K.rs3, 5, 0), (K.grad_role, 9, 1), (K.small_add, 0), (K.grad_role, 9, 2), (K.rs1, 8, 3),
    (K.grad_role, 9, 3), (K.grad_role, 10, 0), (K.rs2, 6, 1), (K.grad_role, 10, 1),
    (K.grad_role, 10, 2), (K.small_start, 1), (K.rs1, 6, 2), (K.rs1, 9, 0), (K.rs2, 7, 0),
    (K.rs5, 2), (K.grad_role, 10, 3), (K.rs3, 7, 1), (K.rs1, 6, 1), (K.grad_role, 11, 0),
    (K.rs5, 0), (K.rs2, 6, 0), (K.out_rows,), (K.memory_rows, 3), (K.small_add, 1),
    (K.rs2, 5, 1), (K.rs1, 6, 3), (K.rs3, 5, 1), (K.small_start, 2), (K.rs2, 8, 1),
    (K.rs1, 9, 1), (K.rs3, 7, 0), (K.rs1, 10, 0), (K.grad_role, 11, 1), (K.rs3, 4, 0),
    (K.rs2, 9, 0), (K.rs2, 10, 1), (K.rs3, 6, 0), (K.rs1, 7, 3), (K.rs1, 9, 2), (K.rs1, 10, 2),
    (K.memory_rows, 1), (K.small_add, 2), (K.rs3, 6, 1), (K.rs1, 10, 1), (K.memory_rows, 0),
    (K.small_start, 3), (K.rs1, 11, 0), (K.rs2, 11, 0), (K.rs2, 8, 0), (K.rs4, 7),
    (K.rs2, 10, 0), (K.rs4, 5), (K.grad_role, 11, 2), (K.rs2, 9, 1), (K.rs1, 4, 3),
    (K.grad_role, 11, 3), (K.rs3, 10, 1), (K.rs3, 9, 1), (K.rs1, 10, 3), (K.rs1, 9, 3),
    (K.memory_rows, 2), (K.rs3, 9, 0), (K.rs1, 11, 3), (K.rs4, 4), (K.small_add, 3),
    (K.rs1, 8, 2), (K.rs3, 10, 0), (K.rs3, 8, 0), (K.rs1, 8, 1), (K.rs3, 8, 1), (K.rs5, 7),
    (K.small_start, 4), (K.rs1, 11, 2), (K.rs2, 11, 1), (K.rs1, 11, 1), (K.rs4, 6), (K.rs5, 4),
    (K.rs5, 3), (K.rs3, 11, 1), (K.rs4, 10), (K.rs3, 11, 0), (K.rs4, 9), (K.rs4, 11),
    (K.rs4, 8), (K.rs5, 8), (K.rs5, 5), (K.rs5, 10), (K.small_add, 4), (K.rs5, 6), (K.rs5, 11),
    (K.rs5, 1), (K.rs5, 9),
)

NAMES = (
    "x_in", "mem", "g", "dl", "ml", "sh_s", "sh_c", "sh_f", "gains", "table",
    "block", "xgrad", "mgrad", "gs", "gc", "gf", "ggain", "gtable",
    "ws", "wc", "wf", "wgu", "wd", "gb", "lb", "zb",
    "n1", "q", "k", "v", "mix", "r1", "n2", "cq", "ck", "cv", "cmix", "r2", "n3",
    "ga", "ub", "hid", "hidt", "n3t", "dg", "du", "dz", "dr", "drb", "tt", "memt",
    "ps", "diag", "redga", "redta", "landg", "landt",
    "gsend", "grecv", "zsend", "zrecv", "rsend", "rrecv", "orecv", "ssend", "srecv", "free",
)


def kernel(*args):
    st = Layer(dict(zip(NAMES, args)))
    st.redg, st.redt = st.redga, st.redta
    barrier = pltpu.get_barrier_semaphore()
    others = [st.dev(fc=1), st.dev(fx=1), st.dev(fy=1)] + [
        st.dev(z=(st.z + k) % 4) for k in (1, 2, 3)]
    for other in others:
        pl.semaphore_signal(barrier, inc=1, device_id=other, device_id_type=MESH)
    st.own_square(0)
    st.masks()
    pl.semaphore_wait(barrier, 6)
    for step, *numbers in SCHEDULE:
        step(st, *numbers)
    st.finish()


def settle_kernel(count, *refs):
    out = [pltpu.make_async_copy(refs[i], refs[count + i], refs[-1].at[i]) for i in range(count)]
    for one in out:
        one.start()
    for one in out:
        one.wait()


def settle(arrays):
    count = len(arrays)
    return pl.pallas_call(
        functools.partial(settle_kernel, count),
        out_shape=tuple(jax.ShapeDtypeStruct(v.shape, v.dtype) for v in arrays),
        in_specs=[pl.BlockSpec(memory_space=pltpu.VMEM)] * count,
        out_specs=tuple([pl.BlockSpec(memory_space=pl.ANY)] * count),
        scratch_shapes=[pltpu.SemaphoreType.DMA((count,))],
        compiler_params=pltpu.CompilerParams(vmem_limit_bytes=67000000),
    )(*arrays)


def fused(inputs, memory, out_cotangent, dec_lengths, mem_lengths, self_params, cross_params,
          ff_params, gains, table):
    slots, length, width = inputs.shape
    mem_len = memory.shape[1]
    vm = pl.BlockSpec(memory_space=pltpu.VMEM)
    sm = pl.BlockSpec(memory_space=pltpu.SMEM)
    s = jax.ShapeDtypeStruct
    rows_s, rows_f = self_params.shape[0] // 128, ff_params.shape[0] // 128
    row = pltpu.VMEM((length, D), BF)
    rowf = pltpu.VMEM((length, D), F32)
    memory_row = pltpu.VMEM((mem_len, D), BF)
    dma = pltpu.SemaphoreType.DMA
    outs = pl.pallas_call(
        kernel,
        out_shape=(
            s((length, D), BF), s((length, D), BF), s((mem_len, D), BF),
            s((rows_s, 128), F32), s((rows_s, 128), F32), s((rows_f, 128), F32),
            s((3, D), F32), s((H, NB), F32),
        ),
        in_specs=[vm, vm, vm, sm, sm, vm, vm, vm, vm, sm],
        out_specs=[vm] * 8,
        scratch_shapes=[
            pltpu.VMEM((4 * D, D), BF), pltpu.VMEM((4 * D, D), BF),
            pltpu.VMEM((32 * FU, 256), BF),
            pltpu.VMEM((2 * D, FF), BF), pltpu.VMEM((FF, D), BF),
            pltpu.VMEM((OWN_ROWS + 2 * STAGE, 256), BF),
            pltpu.VMEM((LAND_ROWS, 256), BF), pltpu.VMEM((Z_ROWS, 256), BF),
            row, row, row, row, row, rowf, row, row, memory_row, memory_row, row, rowf, row,
            pltpu.VMEM((length, FF), F32), pltpu.VMEM((length, FF), F32),
            pltpu.VMEM((length, FF), BF), pltpu.VMEM((FF, length), BF),
            pltpu.VMEM((D, length), BF),
            pltpu.VMEM((length, FF), BF), pltpu.VMEM((length, FF), BF),
            rowf, rowf, row, pltpu.VMEM((D, length), BF), pltpu.VMEM((D, mem_len), BF),
            pltpu.VMEM((H * length, length), F32),
            pltpu.VMEM((16, 128), F32),
            pltpu.VMEM((6, 8, D), F32), pltpu.VMEM((6, 16, 128), F32),
            pltpu.VMEM((5, 8, D), F32), pltpu.VMEM((5, 16, 128), F32),
            dma((120,)), dma((120,)), dma((9,)), dma((9,)), dma((180,)), dma((180,)), dma((9,)),
            dma((10,)), dma((10,)), pltpu.SemaphoreType.REGULAR((2,)),
        ],
        compiler_params=pltpu.CompilerParams(
            collective_id=0, has_side_effects=True, vmem_limit_bytes=67000000),
        cost_estimate=pl.CostEstimate(
            flops=10_000_000_000, bytes_accessed=8_000_000, transcendentals=2_000_000),
    )(
        inputs.reshape(length, width), memory.reshape(mem_len, width),
        out_cotangent.reshape(length, width), dec_lengths, mem_lengths,
        self_params.reshape(rows_s, 128), cross_params.reshape(rows_s, 128),
        ff_params.reshape(rows_f, 128), gains, table.T,
    )
    outs = settle(outs)
    return (
        outs[0].reshape(inputs.shape), outs[1].reshape(inputs.shape),
        outs[2].reshape(memory.shape), outs[3].reshape(-1), outs[4].reshape(-1),
        outs[5].reshape(-1), outs[6], outs[7].T,
    )


HIGHEST = lax.Precision.HIGHEST


def product(left, right):
    return jnp.dot(left, right, preferred_element_type=jnp.float32)


def product_t(left, right):
    return lax.dot_general(
        left, right, (((0,), (0,)), ((), ())), preferred_element_type=jnp.float32
    )


def product_nt(left, right):
    return lax.dot_general(
        left, right, (((1,), (1,)), ((), ())), preferred_element_type=jnp.float32
    )


def rms_scale(value, gain):
    return value * lax.rsqrt(jnp.mean(value * value, axis=-1, keepdims=True) + 1e-06) * gain


def gelu_gate(gate_pre, up_pre):
    return jax.nn.gelu(gate_pre, approximate=True) * up_pre


def bucket_rows(start, count, length):
    half_count = NB // 2
    limits = np.ceil(
        half_count * (MAXD / half_count) ** (np.arange(1, half_count) / half_count)
    ).astype(np.int32)
    query_pos = start + jnp.arange(count, dtype=jnp.int32)
    key_pos = jnp.arange(length, dtype=jnp.int32)
    distance = query_pos[:, None] - key_pos[None, :]
    beyond = half_count + jnp.sum(
        (distance[None] >= jnp.asarray(limits)[:, None, None]).astype(jnp.int32), axis=0
    )
    return jnp.where(distance < half_count, jnp.maximum(distance, 0), beyond)


def onehot_block(start, count, length):
    bucket = bucket_rows(start, count, length)
    hot_rows = jnp.arange(NB, dtype=jnp.int32)[:, None, None] == bucket[None]
    return hot_rows.astype(jnp.float32).reshape(NB, count * length)


def position_bias(table, length):
    block_rows = min(length, 128)
    block_count = length // block_rows

    def position_per_block(block):
        bucket_hot = onehot_block(block * block_rows, block_rows, length)
        return lax.dot_general(
            table,
            bucket_hot,
            (((0,), (0,)), ((), ())),
            precision=HIGHEST,
            preferred_element_type=jnp.float32,
        )

    pieces = lax.map(position_per_block, jnp.arange(block_count, dtype=jnp.int32))
    return (
        pieces.reshape(block_count, H, block_rows, length)
        .transpose(1, 0, 2, 3)
        .reshape(H, length, length)
    )


def table_gradient(score_sums, length):
    block_rows = min(length, 128)

    def table_per_block(carry, block):
        ds_piece = score_sums.reshape(H, block_rows * length)
        bucket_hot = onehot_block(block * block_rows, block_rows, length)
        return (
            carry
            + lax.dot_general(
                bucket_hot,
                ds_piece,
                (((1,), (1,)), ((), ())),
                precision=HIGHEST,
                preferred_element_type=jnp.float32,
            ),
            None,
        )

    result, _ = lax.scan(
        table_per_block,
        jnp.zeros((NB, H), jnp.float32),
        jnp.arange(length // block_rows, dtype=jnp.int32),
    )
    return result


def score_block(queries, keys_in, score_bias, keep_mask):
    q_len = queries.shape[0]
    k_len = keys_in.shape[0]
    raw_scores = (
        jnp.einsum(
            "qhe,khe->hqk",
            queries.reshape(q_len, H, DH),
            keys_in.reshape(k_len, H, DH),
            preferred_element_type=jnp.float32,
        )
        + score_bias
    )
    return jnp.where(keep_mask[None], raw_scores, MASKED)


def attend_forward(queries, keys_in, values, score_bias, keep_mask):
    q_len = queries.shape[0]
    k_len = keys_in.shape[0]
    raw_scores = score_block(queries, keys_in, score_bias, keep_mask)
    row_max = jnp.max(raw_scores, axis=2, keepdims=True)
    exponent = jnp.exp(raw_scores - row_max)
    row_sum = jnp.sum(exponent, axis=2, keepdims=True)
    softmax_low = (exponent / row_sum).astype(jnp.bfloat16)
    head_mix = jnp.einsum(
        "hqk,khe->qhe",
        softmax_low,
        values.reshape(k_len, H, DH),
        preferred_element_type=jnp.float32,
    )
    return (head_mix.reshape(q_len, H * DH).astype(jnp.bfloat16), row_max, row_sum)


def attend_backward(queries, keys_in, values, score_bias, keep_mask, row_max, row_sum, d_mix):
    q_len = queries.shape[0]
    k_len = keys_in.shape[0]
    raw_scores = score_block(queries, keys_in, score_bias, keep_mask)
    softmax_out = jnp.exp(raw_scores - row_max) / row_sum
    softmax_low = softmax_out.astype(jnp.bfloat16)
    mix_heads = d_mix.reshape(q_len, H, DH)
    q_heads = queries.reshape(q_len, H, DH)
    k_heads = keys_in.reshape(k_len, H, DH)
    v_heads = values.reshape(k_len, H, DH)
    d_softmax = jnp.einsum("qhe,khe->hqk", mix_heads, v_heads, preferred_element_type=jnp.float32)
    d_scores = (
        softmax_out * (d_softmax - jnp.sum(softmax_out * d_softmax, axis=2, keepdims=True))
    ).astype(jnp.bfloat16)
    d_values = (
        jnp.einsum("hqk,qhe->khe", softmax_low, mix_heads, preferred_element_type=jnp.float32)
        .reshape(k_len, H * DH)
        .astype(jnp.bfloat16)
    )
    d_queries = (
        jnp.einsum("hqk,khe->qhe", d_scores, k_heads, preferred_element_type=jnp.float32)
        .reshape(q_len, H * DH)
        .astype(jnp.bfloat16)
    )
    d_keys = (
        jnp.einsum("hqk,qhe->khe", d_scores, q_heads, preferred_element_type=jnp.float32)
        .reshape(k_len, H * DH)
        .astype(jnp.bfloat16)
    )
    return (d_queries, d_keys, d_values, d_scores)


def attend_slots(queries, keys_in, values, lengths, score_bias, base_mask):
    slot_count = lengths.shape[0]
    q_len = queries.shape[0] // slot_count
    k_len = keys_in.shape[0] // slot_count
    key_pos = jnp.arange(k_len, dtype=jnp.int32)

    def per_slot(slot_item):
        q_slot, k_slot, v_slot, slot_len = slot_item
        keep_mask = base_mask & (key_pos[None, :] < slot_len)
        return attend_forward(q_slot, k_slot, v_slot, score_bias, keep_mask)

    head_mix, row_max, row_sum = lax.map(
        per_slot,
        (
            queries.reshape(slot_count, q_len, -1),
            keys_in.reshape(slot_count, k_len, -1),
            values.reshape(slot_count, k_len, -1),
            lengths,
        ),
    )
    return (head_mix.reshape(slot_count * q_len, -1), row_max, row_sum)


def attend_back_slots(
    queries, keys_in, values, lengths, score_bias, base_mask, row_max, row_sum, d_mix, with_table
):
    slot_count = lengths.shape[0]
    q_len = queries.shape[0] // slot_count
    k_len = keys_in.shape[0] // slot_count
    key_pos = jnp.arange(k_len, dtype=jnp.int32)
    if with_table:
        start = jnp.zeros((H, q_len, k_len), jnp.float32)
    else:
        start = jnp.zeros((), jnp.float32)

    def per_slot(carry, slot_item):
        q_slot, k_slot, v_slot, slot_len, max_slot, sum_slot, dmix_slot = slot_item
        keep_mask = base_mask & (key_pos[None, :] < slot_len)
        d_queries, d_keys, d_values, d_scores = attend_backward(
            q_slot, k_slot, v_slot, score_bias, keep_mask, max_slot, sum_slot, dmix_slot
        )
        if with_table:
            carry = carry + d_scores.astype(jnp.float32)
        return (carry, (d_queries, d_keys, d_values))

    score_sums, grad_parts = lax.scan(
        per_slot,
        start,
        (
            queries.reshape(slot_count, q_len, -1),
            keys_in.reshape(slot_count, k_len, -1),
            values.reshape(slot_count, k_len, -1),
            lengths,
            row_max,
            row_sum,
            d_mix.reshape(slot_count, q_len, -1),
        ),
    )
    return (
        grad_parts[0].reshape(slot_count * q_len, -1),
        grad_parts[1].reshape(slot_count * k_len, -1),
        grad_parts[2].reshape(slot_count * k_len, -1),
        score_sums,
    )


def gather_weights(self_params, cross_params, ff_params):
    return (
        lax.all_gather(self_params, ("dp", "fsdp"), axis=0, tiled=True),
        lax.all_gather(cross_params, ("dp", "fsdp"), axis=0, tiled=True),
        lax.all_gather(ff_params, ("dp", "fsdp"), axis=0, tiled=True),
    )


def scatter_grads(self_full, cross_full, ff_full):
    wide_count = lax.axis_size("dp")
    spread = (
        lax.all_to_all(
            self_full.reshape(wide_count, -1).astype(jnp.bfloat16),
            "dp",
            split_axis=0,
            concat_axis=0,
            tiled=True,
        ).astype(jnp.float32),
        lax.all_to_all(
            cross_full.reshape(wide_count, -1).astype(jnp.bfloat16),
            "dp",
            split_axis=0,
            concat_axis=0,
            tiled=True,
        ).astype(jnp.float32),
        lax.all_to_all(
            ff_full.reshape(wide_count, -1).astype(jnp.bfloat16),
            "dp",
            split_axis=0,
            concat_axis=0,
            tiled=True,
        ).astype(jnp.float32),
    )
    self_block = jnp.sum(spread[0], axis=0)
    cross_block = jnp.sum(spread[1], axis=0)
    ff_block = jnp.sum(spread[2], axis=0)
    return (
        lax.psum_scatter(
            self_block.astype(jnp.bfloat16), "fsdp", scatter_dimension=0, tiled=True
        ).astype(jnp.float32),
        lax.psum_scatter(
            cross_block.astype(jnp.bfloat16), "fsdp", scatter_dimension=0, tiled=True
        ).astype(jnp.float32),
        lax.psum_scatter(
            ff_block.astype(jnp.bfloat16), "fsdp", scatter_dimension=0, tiled=True
        ).astype(jnp.float32),
    )


def unpack(weights):
    self_flat, cross_flat, ff_flat = weights
    self_mats = self_flat.reshape(4, D, D)
    cross_mats = cross_flat.reshape(4, D, D)
    block_size = D * FF
    return (
        self_mats[0],
        self_mats[1],
        self_mats[2],
        self_mats[3],
        cross_mats[0],
        cross_mats[1],
        cross_mats[2],
        cross_mats[3],
        ff_flat[:block_size].reshape(D, FF),
        ff_flat[block_size : 2 * block_size].reshape(D, FF),
        ff_flat[2 * block_size :].reshape(FF, D),
    )


def run_forward(
    weights, flat_in, flat_mem, gains, pos_bias, causal, open_mask, dec_lengths, mem_lengths
):
    w_sq, w_sk, w_sv, w_so, w_cq, w_ck, w_cv, w_co, w_gate, w_up, w_down = unpack(weights)
    norm_one = rms_scale(flat_in, gains[0]).astype(jnp.bfloat16)
    self_q = product(norm_one, w_sq).astype(jnp.bfloat16)
    self_k = product(norm_one, w_sk).astype(jnp.bfloat16)
    self_v = product(norm_one, w_sv).astype(jnp.bfloat16)
    self_mix, self_max, self_sum = attend_slots(
        self_q, self_k, self_v, dec_lengths, pos_bias, causal
    )
    resid_one = flat_in + product(self_mix, w_so)
    norm_two = rms_scale(resid_one, gains[1]).astype(jnp.bfloat16)
    cross_q = product(norm_two, w_cq).astype(jnp.bfloat16)
    cross_k = product(flat_mem, w_ck).astype(jnp.bfloat16)
    cross_v = product(flat_mem, w_cv).astype(jnp.bfloat16)
    cross_mix, cross_max, cross_sum = attend_slots(
        cross_q, cross_k, cross_v, mem_lengths, 0.0, open_mask
    )
    resid_two = resid_one + product(cross_mix, w_co)
    norm_three = rms_scale(resid_two, gains[2]).astype(jnp.bfloat16)
    gate_pre = product(norm_three, w_gate)
    up_pre = product(norm_three, w_up)
    hidden = gelu_gate(gate_pre, up_pre).astype(jnp.bfloat16)
    block = resid_two + product(hidden, w_down)
    return (
        norm_one,
        self_q,
        self_k,
        self_v,
        self_mix,
        self_max,
        self_sum,
        resid_one,
        norm_two,
        cross_q,
        cross_k,
        cross_v,
        cross_mix,
        cross_max,
        cross_sum,
        resid_two,
        norm_three,
        gate_pre,
        up_pre,
        hidden,
        block,
    )


def by_collectives(
    inputs,
    memory,
    out_cotangent,
    dec_lengths,
    mem_lengths,
    self_params,
    cross_params,
    ff_params,
    gains,
    table,
):
    slot_count, length, model_width = inputs.shape
    mem_len = memory.shape[1]
    row_count = slot_count * length
    pos_bias = position_bias(table, length)
    positions = jnp.arange(length, dtype=jnp.int32)
    causal = positions[None, :] <= positions[:, None]
    open_mask = jnp.ones((length, mem_len), dtype=bool)
    flat_in = inputs.reshape(row_count, model_width).astype(jnp.float32)
    flat_mem = memory.reshape(slot_count * mem_len, model_width)
    weights = gather_weights(self_params, cross_params, ff_params)
    first_pass = run_forward(
        weights, flat_in, flat_mem, gains, pos_bias, causal, open_mask, dec_lengths, mem_lengths
    )
    block_out = first_pass[20].astype(jnp.bfloat16).reshape(slot_count, length, model_width)
    again = gather_weights(self_params, cross_params, ff_params)
    w_sq, w_sk, w_sv, w_so, w_cq, w_ck, w_cv, w_co, w_gate, w_up, w_down = unpack(again)
    (
        norm_one,
        self_q,
        self_k,
        self_v,
        self_mix,
        self_max,
        self_sum,
        resid_one,
        norm_two,
        cross_q,
        cross_k,
        cross_v,
        cross_mix,
        cross_max,
        cross_sum,
        resid_two,
        norm_three,
        gate_pre,
        up_pre,
        hidden,
        _,
    ) = run_forward(
        again, flat_in, flat_mem, gains, pos_bias, causal, open_mask, dec_lengths, mem_lengths
    )
    d_out = out_cotangent.reshape(row_count, model_width)
    grad_down = product_t(hidden, d_out)
    d_hidden = product_nt(d_out, w_down).astype(jnp.bfloat16)
    _, pull_gate = jax.vjp(gelu_gate, gate_pre, up_pre)
    d_gate, d_up = pull_gate(d_hidden.astype(jnp.float32))
    d_gate = d_gate.astype(jnp.bfloat16)
    d_up = d_up.astype(jnp.bfloat16)
    grad_gate = product_t(norm_three, d_gate)
    grad_up = product_t(norm_three, d_up)
    d_norm_three = product_nt(d_gate, w_gate) + product_nt(d_up, w_up)
    _, pull_three = jax.vjp(rms_scale, resid_two, gains[2])
    d_from_three, grad_gain_three = pull_three(d_norm_three)
    d_resid_two = d_out.astype(jnp.float32) + d_from_three
    d_cross = d_resid_two.astype(jnp.bfloat16)
    grad_co = product_t(cross_mix, d_cross)
    d_cross_mix = product_nt(d_cross, w_co).astype(jnp.bfloat16)
    dq_cross, dk_cross, dv_cross, _ = attend_back_slots(
        cross_q,
        cross_k,
        cross_v,
        mem_lengths,
        0.0,
        open_mask,
        cross_max,
        cross_sum,
        d_cross_mix,
        False,
    )
    grad_cq = product_t(norm_two, dq_cross)
    grad_ck = product_t(flat_mem, dk_cross)
    grad_cv = product_t(flat_mem, dv_cross)
    memory_grad = (product_nt(dk_cross, w_ck) + product_nt(dv_cross, w_cv)).astype(jnp.bfloat16)
    _, pull_two = jax.vjp(rms_scale, resid_one, gains[1])
    d_from_two, grad_gain_two = pull_two(product_nt(dq_cross, w_cq))
    d_resid_one = d_resid_two + d_from_two
    d_self = d_resid_one.astype(jnp.bfloat16)
    grad_so = product_t(self_mix, d_self)
    d_self_mix = product_nt(d_self, w_so).astype(jnp.bfloat16)
    dq_self, dk_self, dv_self, score_sums = attend_back_slots(
        self_q, self_k, self_v, dec_lengths, pos_bias, causal, self_max, self_sum, d_self_mix, True
    )
    grad_sq = product_t(norm_one, dq_self)
    grad_sk = product_t(norm_one, dk_self)
    grad_sv = product_t(norm_one, dv_self)
    d_norm_one = product_nt(dq_self, w_sq) + product_nt(dk_self, w_sk) + product_nt(dv_self, w_sv)
    _, pull_one = jax.vjp(rms_scale, flat_in, gains[0])
    d_from_one, grad_gain_one = pull_one(d_norm_one)
    input_grad = (d_resid_one + d_from_one).astype(jnp.bfloat16)
    table_local = table_gradient(score_sums, length)
    self_full = jnp.stack([grad_sq, grad_sk, grad_sv, grad_so]).reshape(-1)
    cross_full = jnp.stack([grad_cq, grad_ck, grad_cv, grad_co]).reshape(-1)
    ff_full = jnp.concatenate([grad_gate.reshape(-1), grad_up.reshape(-1), grad_down.reshape(-1)])
    self_shard, cross_shard, ff_shard = scatter_grads(self_full, cross_full, ff_full)
    gain_local = jnp.stack([grad_gain_one, grad_gain_two, grad_gain_three])
    gain_total, table_total = lax.psum((gain_local, table_local), ("dp", "fsdp"))
    return (
        block_out,
        input_grad.reshape(slot_count, length, model_width),
        memory_grad.reshape(slot_count, mem_len, model_width),
        self_shard,
        cross_shard,
        ff_shard,
        gain_total,
        table_total,
    )


def solution(mesh):
    whole = ("dp", "fsdp")
    rows = P(whole, None, None)
    flat = P(whole)
    small = mesh.shape["dp"] == 8 and mesh.shape["fsdp"] == 4
    return jax.shard_map(
        fused if small else by_collectives,
        mesh=mesh,
        in_specs=(rows, rows, rows, flat, flat, flat, flat, flat, P(), P()),
        out_specs=(rows, rows, rows, flat, flat, flat, P(), P()),
        check_vma=False,
    )
```

```python
import functools

import jax
import jax.numpy as jnp
import numpy as np
from jax import lax
from jax.experimental import pallas as pl
from jax.experimental.pallas import tpu as pltpu
from jax.sharding import PartitionSpec as P

D = 768
FF = 2048
H = 12
DH = 64
NB = 32
MAXD = 128
PAIRS = H // 2
MASKED = -1000000000.0
BF = jnp.bfloat16
F32 = jnp.float32
MESH = pl.DeviceIdType.MESH

AR = 96
AU = 288
FU = 576
GROUPS = (
    (2, 3), (2, 2), (2, 0), (2, 1),
    (1, 3), (1, 2), (1, 1), (1, 0),
    (0, 3), (0, 0), (0, 2), (0, 1),
)
PAIR = (True,) * 4 + (False,) * 8
SHARED = (True, True, True)
UNIT = tuple(FU if t == 2 else AU for t, _ in GROUPS)
OWN = tuple(4 * sum(UNIT[:g]) for g in range(12))
OWN_ROWS = 4 * sum(UNIT)
LAND = tuple(3 * sum(UNIT[:g]) for g in range(12))
LAND_ROWS = 3 * sum(UNIT)
ZBASE = (0, 3 * AU, 6 * AU)
Z_ROWS = 6 * AU + 3 * FU
STAGE = 4 * FU
ROLES = ((1, 1), (1, 0), (0, 1), (0, 0))
SIB = (0, 12, 13, 14)


def limits():
    half = NB // 2
    return [
        int(v)
        for v in np.ceil(half * (MAXD / half) ** (np.arange(1, half) / half)).astype(np.int32)
    ]


def bucket_of(distance):
    half = NB // 2
    beyond = jnp.full(distance.shape, half, jnp.int32)
    for limit in limits():
        beyond = beyond + jnp.where(distance >= limit, 1, 0)
    return jnp.where(distance < half, jnp.maximum(distance, 0), beyond)


def nn(left, right):
    return jnp.dot(left, right, preferred_element_type=F32)


def nt(left, right):
    return lax.dot_general(left, right, (((1,), (1,)), ((), ())), preferred_element_type=F32)


def tn(left, right):
    return lax.dot_general(left, right, (((0,), (0,)), ((), ())), preferred_element_type=F32)


def al(value, step):
    return pl.multiple_of(value, step)


def rms(value, gain):
    r = lax.rsqrt(jnp.mean(value * value, axis=-1, keepdims=True) + 1e-06)
    return value * r * gain


def rms_back(value, gain, dz):
    r = lax.rsqrt(jnp.mean(value * value, axis=-1, keepdims=True) + 1e-06)
    inner = jnp.mean(value * gain * dz, axis=-1, keepdims=True)
    dv = r * gain * dz - value * (r * r * r) * inner
    dg = jnp.sum(value * r * dz, axis=0, keepdims=True)
    return dv, dg


class Layer:
    def __init__(self, refs):
        self.__dict__.update(refs)
        self.flat, self.dm = self.ps, self.n3
        dp = lax.axis_index("dp")
        fs = lax.axis_index("fsdp")
        self.z, self.y = dp // 2, dp % 2
        self.x, self.c = fs // 2, fs % 2
        self.shard = dp * 4 + fs

    def dev(self, z=None, fx=0, fy=0, fc=0):
        z = self.z if z is None else z
        y = (self.y + fy) % 2
        x = (self.x + fx) % 2
        c = (self.c + fc) % 2
        return (z * 2 + y, x * 2 + c)

    def chip(self, fx=0, fy=0):
        return ((self.y + fy) % 2) * 2 + (self.x + fx) % 2

    def shard_at(self, z, fx=0, fy=0, fc=0):
        return z * 8 + self.chip(fx, fy) * 2 + (self.c + fc) % 2

    def copy(self, src, dst, send, recv, device):
        return pltpu.make_async_remote_copy(
            src_ref=src, dst_ref=dst, send_sem=send, recv_sem=recv,
            device_id=device, device_id_type=MESH,
        )

    def piece(self, tensor, shard, half=None, par=None):
        rows = FU if tensor == 2 else AR
        ref = (self.ws, self.wc, self.wf)[tensor]
        start = shard * rows
        if half is None:
            return ref.at[pl.ds(al(start, 16), rows), :]
        rows = rows // 2
        start = pl.ds(al(start + half * rows, 16), rows)
        if not SHARED[tensor]:
            return ref.at[start, :]
        width = ref.shape[1] // 2
        return ref.at[start, pl.ds(al(par * width, 128), width)]

    def plane(self, tensor, k):
        if tensor == 2:
            return k
        far = self.z // 2
        return (self.z, self.z + 1 - 2 * (self.z % 2), 2 - far, 3 - 3 * far)[k]

    def gcopy(self, tensor, zs, kind, there=False):
        par = self.z % 2
        if kind < 2:
            spot, dev = (0, 0), ((1, 0), (0, 1))[kind]
            if there:
                spot = dev
            part, dev = self.piece(tensor, self.shard_at(zs, *spot)), self.dev(None, *dev)
        elif kind < 4:
            spot, dev = ((1, 0), (0, 1)) if kind == 2 else ((0, 1), (1, 0))
            if there:
                spot = (1, 1)
            part = self.piece(tensor, self.shard_at(zs, *spot), kind - 2, par)
            dev = self.dev(None, *dev)
        elif kind < 8:
            spot = ((0, 0), (1, 0), (0, 1), (1, 1))[kind - 4]
            part = self.piece(tensor, self.shard_at(zs, *spot, 1 if there else 0))
            dev = self.dev(fc=1)
        else:
            part = self.piece(
                tensor, self.shard_at(zs, 1, 1), kind - 8, 1 - par if there else par)
            dev = self.dev(z=self.z + 1 - 2 * par)
        row = (tensor * 4 + zs) * 10 + kind
        return self.copy(part, part, self.gsend.at[row], self.grecv.at[row], dev)

    def start(self, tensor, zs, *kinds):
        for kind in kinds:
            self.gcopy(tensor, zs, kind).start()

    def arrive(self, tensor, zs, *kinds):
        for kind in kinds:
            self.gcopy(tensor, zs, kind, True).wait_recv()

    def zcopy(self, tensor, zs, up):
        part = self.piece(tensor, self.shard_at(zs))
        row = tensor * 4 + zs
        return self.copy(
            part, part, self.zsend.at[2 * row + up], self.zrecv.at[row],
            self.dev(z=(self.z + (1 if up else 3)) % 4))

    def inner(self, up):
        return self.z < 3 if up else self.z > 0

    def own_z(self, tensor, up):
        @pl.when(self.inner(up))
        def _():
            self.zcopy(tensor, self.z, up).start()

    def z_arrive(self, tensor, zs):
        self.zcopy(tensor, zs, 0).wait_recv()
        for up in (0, 1):
            @pl.when((zs < self.z if up else zs > self.z) & self.inner(up))
            def _(up=up):
                self.zcopy(tensor, zs, up).start()
        self.start(tensor, zs, 0, 1, 4)

    def own_xy(self, tensor):
        self.start(tensor, self.z, 0, 1, 4)

    def p1(self, tensor, k):
        if tensor < 2:
            self.z_arrive(tensor, self.plane(tensor, k))
            return

        @pl.when(self.z == k)
        def _():
            self.start(tensor, k, 0, 1, 4)

        @pl.when(self.z != k)
        def _():
            self.z_arrive(tensor, k)

    def p2x(self, tensor, k):
        zs = self.plane(tensor, k)
        self.arrive(tensor, zs, 0)
        self.start(tensor, zs, 2, 5)

    def p2y(self, tensor, k):
        zs = self.plane(tensor, k)
        self.arrive(tensor, zs, 1)
        self.start(tensor, zs, 3, 6)

    def p3(self, tensor, k, half):
        zs = self.plane(tensor, k)
        self.arrive(tensor, zs, 2 + half)
        if SHARED[tensor]:
            self.start(tensor, zs, 8 + half)
        elif half:
            self.start(tensor, zs, 7)

    def p4(self, tensor, k):
        if SHARED[tensor]:
            zs = self.plane(tensor, k)
            self.arrive(tensor, zs, 8, 9)
            self.start(tensor, zs, 7)

    def p5(self, tensor, k):
        self.arrive(tensor, self.plane(tensor, k), 4, 5, 6, 7)

    def plane_sent(self, tensor, k):
        for kind in range(10 if SHARED[tensor] else 8):
            self.gcopy(tensor, self.plane(tensor, k), kind).wait_send()

    def z_sent(self, tensor, zs):
        for up in (0, 1):
            @pl.when((zs <= self.z if up else zs >= self.z) & self.inner(up))
            def _(up=up):
                self.zcopy(tensor, zs, up).wait_send()

    def credit(self, which):
        for k in ((0,), (1, 2, 3))[which]:
            self.plane_sent(2, k)
            self.z_sent(2, k)
        pl.semaphore_signal(
            self.free.at[which], inc=1, device_id=self.dev(fc=1), device_id_type=MESH)

    def own_square(self, tensor):
        src, dst = ((self.sh_s, self.ws), (self.sh_c, self.wc))[tensor]
        self.flat[0:576, :] = src[...].astype(F32)
        row = al(self.shard * AR, 16)
        for t in range(6):
            dst[pl.ds(row, AR), 128 * t:128 * t + 128] = self.flat[
                pl.ds(t, AR, stride=6), :].astype(BF)

    def own_ff(self):
        self.flat[0:1152, :] = self.sh_f[...].astype(F32)
        base = self.shard * FU
        flat, wf = self.flat, self.wf

        def wide(rows):
            for u in range(4):
                for w in range(2):
                    top = flat[pl.ds(4 * u + w, rows, stride=16), :]
                    low = flat[pl.ds(4 * u + w + 2, rows, stride=16), :]
                    wf[pl.ds(al(base + 2 * rows * u, 16), 2 * rows), 128 * w:128 * w + 128] = (
                        jnp.concatenate([top, low], axis=0).astype(BF))

        def tall(first, rows, offset):
            for t in range(6):
                wf[pl.ds(al(base + offset + rows * (t // 2), 16), rows),
                   128 * (t % 2):128 * (t % 2) + 128] = flat[
                       pl.ds(first + t, rows, stride=6), :].astype(BF)

        @pl.when(self.shard < 21)
        def _():
            wide(72)

        @pl.when(self.shard == 21)
        def _():
            wide(24)
            tall(384, 128, 192)

        @pl.when(self.shard > 21)
        def _():
            tall(0, 192, 0)

    def build_wide(self, ch):
        rows1 = 24 if ch == 10 else 72

        def step(u, _):
            low = self.wf[pl.ds(al(1152 * ch + 144 * u, 16), 144), :].astype(F32)
            high = self.wf[
                pl.ds(al(1152 * ch + FU + 2 * rows1 * u, 16), 2 * rows1), :].astype(F32)
            for w in range(2):
                value = jnp.concatenate(
                    [low[72 * w:72 * w + 72], high[rows1 * w:rows1 * w + rows1]], axis=0)
                self.wgu[144 * ch:144 * ch + 72 + rows1,
                         pl.ds(al(512 * u + 256 * w, 256), 256)] = value.astype(BF)
            return 0

        lax.fori_loop(0, 4, step, 0)

    def build_tall(self, s):
        first, rows, offset = (0, 128, 192) if s == 21 else (192 * s - 4096, 192, 0)
        for p in range(3):
            self.wd[first:first + rows, 256 * p:256 * p + 256] = self.wf[
                FU * s + offset + rows * p:FU * s + offset + rows * p + rows, :]

    def build_plane(self, zs):
        if zs < 2:
            for ch in range(4 * zs, 4 * zs + 4):
                self.build_wide(ch)
        elif zs == 2:
            for ch in (8, 9, 10):
                self.build_wide(ch)
            for s in (21, 22, 23):
                self.build_tall(s)
        else:
            for s in range(24, 32):
                self.build_tall(s)

    def masks(self):
        lane = lax.broadcasted_iota(jnp.int32, (128, 128), 1)
        self.left = lane < DH

    def stack(self, pair):
        zero = jnp.zeros_like(pair)
        return jnp.concatenate(
            [jnp.where(self.left, pair, zero), jnp.where(self.left, zero, pair)], axis=0)

    def unstack(self, both):
        rows = both.shape[0] // 2
        return jnp.where(self.left, both[0:rows], both[rows:])

    def bias(self):
        lane = lax.broadcasted_iota(jnp.int32, (1, 128), 1)
        bucket = bucket_of((128 - lane) % 128)
        for h in range(H):
            row = jnp.zeros((1, 128), F32)
            for b in range(NB):
                row = jnp.where(bucket == b, self.table[h, b], row)
            full = jnp.broadcast_to(row, (128, 128))
            self.ps[128 * h:128 * h + 128, :] = pltpu.roll(
                full, 0, 1, stride=1, stride_axis=0)

    def project(self, left, ref, row, out):
        for p in range(3):
            out[:, 256 * p:256 * p + 256] = nn(
                left, ref[row:row + D, 256 * p:256 * p + 256]).astype(BF)

    def add_product(self, left, ref, row, base, out):
        for p in range(3):
            cols = slice(256 * p, 256 * p + 256)
            out[:, cols] = base[:, cols].astype(F32) + nn(left, ref[row:row + D, cols])

    def heads(self, p):
        return pl.ds(al(p * 256, 256), 256)

    def self_forward(self):
        x = self.x_in[...].astype(F32)
        self.n1[...] = rms(x, self.gains[0:1, :]).astype(BF)
        n1 = self.n1[...]
        for m, out in enumerate((self.q, self.k, self.v)):
            self.project(n1, self.ws, D * m, out)
        length = self.dl[0]
        row = lax.broadcasted_iota(jnp.int32, (256, 128), 0) % 128
        col = lax.broadcasted_iota(jnp.int32, (256, 128), 1)
        keep = (col <= row) & (col < length)

        def pair(p, _):
            cols = pl.ds(al(p * 128, 128), 128)
            s = nt(self.stack(self.q[:, cols]), self.k[:, cols]) + self.ps[self.heads(p), :]
            s = jnp.where(keep, s, MASKED)
            e = jnp.exp(s - jnp.max(s, axis=-1, keepdims=True))
            prob = e / jnp.sum(e, axis=-1, keepdims=True)
            self.ps[self.heads(p), :] = prob
            self.mix[:, cols] = self.unstack(nn(prob.astype(BF), self.v[:, cols])).astype(BF)
            return 0

        lax.fori_loop(0, PAIRS, pair, 0)
        self.add_product(self.mix[...], self.ws, 3 * D, self.x_in, self.r1)
        self.n2[...] = rms(self.r1[...], self.gains[1:2, :]).astype(BF)

    def cross_kv(self, m):
        out = (self.ck, self.cv)[m - 1]
        for i in range(4):
            for p in range(3):
                out[128 * i:128 * i + 128, 256 * p:256 * p + 256] = nn(
                    self.mem[128 * i:128 * i + 128, :],
                    self.wc[D * m:D * m + D, 256 * p:256 * p + 256]).astype(BF)

    def cross_probs(self, p):
        cols = pl.ds(al(p * 128, 128), 128)
        col = lax.broadcasted_iota(jnp.int32, (256, self.mem.shape[0]), 1)
        s = nt(self.stack(self.cq[:, cols]), self.ck[:, cols])
        s = jnp.where(col < self.ml[0], s, MASKED)
        e = jnp.exp(s - jnp.max(s, axis=-1, keepdims=True))
        return e / jnp.sum(e, axis=-1, keepdims=True)

    def cross_forward(self, part):
        if part == 0:
            self.project(self.n2[...], self.wc, 0, self.cq)

        def pair(p, _):
            cols = pl.ds(al(p * 128, 128), 128)
            prob = self.cross_probs(p)
            self.cmix[:, cols] = self.unstack(nn(prob.astype(BF), self.cv[:, cols])).astype(BF)
            return 0

        lax.fori_loop(2 * part, 2 * part + 2, pair, 0)
        if part == 2:
            self.add_product(self.cmix[...], self.wc, 3 * D, self.r1, self.r2)
            self.n3[...] = rms(self.r2[...], self.gains[2:3, :]).astype(BF)

    def ff_gate(self):
        n3 = self.n3[...]
        c0 = float(np.sqrt(2.0 / np.pi))

        def chunk(i, _):
            cols = pl.ds(al(i * 256, 256), 256)
            a = nn(n3, self.wgu[0:D, cols])
            sq = a * a
            t = jnp.tanh(c0 * (a + 0.044715 * a * sq))
            self.ga[:, cols] = 0.5 * a * (1.0 + t)
            self.ub[:, cols] = 0.5 * (1.0 + t) + 0.5 * a * (1.0 - t * t) * (
                c0 * (1.0 + 0.134145 * sq))
            return 0

        lax.fori_loop(0, FF // 256, chunk, 0)

    def ff_up(self):
        n3 = self.n3[...]

        def chunk(i, _):
            cols = pl.ds(al(i * 256, 256), 256)
            up = nn(n3, self.wgu[D:2 * D, cols])
            self.ub[:, cols] = up * self.ub[:, cols]
            self.hid[:, cols] = (self.ga[:, cols] * up).astype(BF)
            return 0

        lax.fori_loop(0, FF // 256, chunk, 0)
        self.hidt[...] = self.hid[...].T

    def out_rows(self):
        hid = self.hid[...]
        for p in range(3):
            cols = slice(256 * p, 256 * p + 256)
            self.block[:, cols] = (self.r2[:, cols] + nn(hid, self.wd[:, cols])).astype(BF)

    def d_hidden(self, part):
        g = self.g[...]

        def chunk(i, _):
            at = al(i * 256, 256)
            cols = pl.ds(at, 256)
            dh = nt(g, self.wd[pl.ds(at, 256), :]).astype(BF).astype(F32)
            self.dg[:, cols] = (dh * self.ub[:, cols]).astype(BF)
            self.du[:, cols] = (dh * self.ga[:, cols]).astype(BF)
            return 0

        lax.fori_loop(4 * part, 4 * part + 4, chunk, 0)

    def place(self, g):
        own = OWN[g]
        out = OWN_ROWS + (g % 2) * STAGE
        return own + self.c * (out - own), out + self.c * (own - out)

    def grad_tall(self, g, i):
        b0, b1 = self.place(g)
        for p in range(3):
            both = nn(
                self.hidt[pl.ds(al(512 + 384 * i, 16), 384), :],
                self.g[:, 256 * p:256 * p + 256])
            self.gb[pl.ds(al(b0 + FU * i + 192 * p, 16), 192), :] = both[0:192].astype(BF)
            self.gb[pl.ds(al(b1 + FU * i + 192 * p, 16), 192), :] = both[192:].astype(BF)

    def grad_tall_part(self, base, i, first, rows, offset):
        for p in range(3):
            value = nn(self.hidt[first:first + rows, :], self.g[:, 256 * p:256 * p + 256])
            self.gb[pl.ds(al(base + FU * i + offset + rows * p, 16), rows), :] = value.astype(BF)

    def grad_wide(self, g, ch, i):
        b0, b1 = self.place(g)
        rows1 = 24 if ch == 10 else 72
        first, end = 144 * ch, 144 * ch + 72 + rows1

        def step(u, _):
            cols = pl.ds(al(512 * u, 512), 512)
            parts = []
            if first < D:
                parts.append(nn(self.n3t[first:min(end, D), :], self.dg[:, cols]))
            if end > D:
                parts.append(nn(self.n3t[max(first, D) - D:end - D, :], self.du[:, cols]))
            both = parts[0] if len(parts) == 1 else jnp.concatenate(parts, axis=0)
            for base, at, rows in ((b0, 0, 72), (b1, 72, rows1)):
                value = jnp.concatenate(
                    [both[at:at + rows, 0:256], both[at:at + rows, 256:512]], axis=0)
                self.gb[pl.ds(al(base + FU * i + 2 * rows * u, 16), 2 * rows), :] = (
                    value.astype(BF))
            return 0

        lax.fori_loop(0, 4, step, 0)

    def grad_ff(self, g):
        zb = GROUPS[g][1]
        if zb == 2:
            b0, b1 = self.place(g)
            for i in range(3):
                self.grad_wide(g, 8 + i, i)
            self.grad_tall_part(b1, 2, 0, 128, 192)
            self.grad_tall_part(b0, 3, 128, 192, 0)
            self.grad_tall_part(b1, 3, 320, 192, 0)
        else:
            for i in range(4):
                self.grad_wide(g, 4 * zb + i, i)

    def grad_square(self, g, i):
        t, zb = GROUPS[g]
        left = self.memt if t == 1 and zb in (1, 2) else self.tt
        right = ((self.q, self.k, self.v, self.drb), (self.cq, self.ck, self.cv, self.drb))[t][zb]
        b0, b1 = self.place(g)
        rows = left[pl.ds(al(192 * i, 16), 192), :]
        for p in range(3):
            both = nn(rows, right[:, 256 * p:256 * p + 256])
            self.gb[pl.ds(al(b0 + AU * i + 96 * p, 16), 96), :] = both[0:96].astype(BF)
            self.gb[pl.ds(al(b1 + AU * i + 96 * p, 16), 96), :] = both[96:].astype(BF)

    def turn(self, g):
        if g == 1:
            self.n3t[...] = self.n3[...].T
        elif g == 5:
            self.memt[...] = self.mem[...].T
        elif g in (4, 7, 8, 9):
            left = {4: self.cmix, 7: self.n2, 8: self.mix, 9: self.n1}[g]
            self.tt[...] = left[...].T

    def back_product(self, terms, out):
        for p in range(3):
            total = None
            for d_ref, w_ref, row, width in terms:
                value = nt(d_ref[...], w_ref[row + 256 * p:row + 256 * p + 256, 0:width])
                total = value if total is None else total + value
            out[:, 256 * p:256 * p + 256] = total

    def norm_three_back(self):
        self.back_product(((self.dg, self.wgu, 0, FF), (self.du, self.wgu, D, FF)), self.dz)
        dv, dg = rms_back(self.r2[...], self.gains[2:3, :], self.dz[...])
        self.redg[0, 2:3, :] = dg
        self.dr[...] = self.g[...].astype(F32) + dv
        self.drb[...] = self.dr[...].astype(BF)

    def cross_back(self, part):
        for p in range(3) if part == 0 else ():
            self.dm[:, 256 * p:256 * p + 256] = nt(
                self.drb[...], self.wc[3 * D + 256 * p:3 * D + 256 * p + 256, :]).astype(BF)

        def pair(p, _):
            cols = pl.ds(al(p * 128, 128), 128)
            dms = self.stack(self.dm[:, cols])
            kp = self.ck[:, cols]
            qs = self.stack(self.cq[:, cols])
            prob = self.cross_probs(p)
            dp = nt(dms, self.cv[:, cols])
            ds = (prob * (dp - jnp.sum(prob * dp, axis=-1, keepdims=True))).astype(BF)
            self.cv[:, cols] = tn(prob.astype(BF), dms).astype(BF)
            self.cq[:, cols] = self.unstack(nn(ds, kp)).astype(BF)
            self.ck[:, cols] = tn(ds, qs).astype(BF)
            return 0

        lax.fori_loop(2 * part, 2 * part + 2, pair, 0)

    def memory_rows(self, i):
        rows = slice(128 * i, 128 * i + 128)
        for p in range(3):
            wrow = 256 * p
            self.mgrad[rows, 256 * p:256 * p + 256] = (
                nt(self.ck[rows, :], self.wc[D + wrow:D + wrow + 256, :])
                + nt(self.cv[rows, :], self.wc[2 * D + wrow:2 * D + wrow + 256, :])
            ).astype(BF)

    def norm_two_back(self):
        self.back_product(((self.cq, self.wc, 0, D),), self.dz)
        dv, dg = rms_back(self.r1[...], self.gains[1:2, :], self.dz[...])
        self.redg[0, 1:2, :] = dg
        self.dr[...] = self.dr[...] + dv
        self.drb[...] = self.dr[...].astype(BF)

    def self_back(self, part):
        for p in range(3) if part == 0 else ():
            self.dm[:, 256 * p:256 * p + 256] = nt(
                self.drb[...], self.ws[3 * D + 256 * p:3 * D + 256 * p + 256, :]).astype(BF)

        def pair(p, _):
            cols = pl.ds(al(p * 128, 128), 128)
            dms = self.stack(self.dm[:, cols])
            kp = self.k[:, cols]
            qs = self.stack(self.q[:, cols])
            prob = self.ps[self.heads(p), :]
            dp = nt(dms, self.v[:, cols])
            ds = (prob * (dp - jnp.sum(prob * dp, axis=-1, keepdims=True))).astype(BF)
            self.ps[self.heads(p), :] = ds.astype(F32)
            self.v[:, cols] = tn(prob.astype(BF), dms).astype(BF)
            self.q[:, cols] = self.unstack(nn(ds, kp)).astype(BF)
            self.k[:, cols] = tn(ds, qs).astype(BF)
            return 0

        lax.fori_loop(3 * part, 3 * part + 3, pair, 0)

    def norm_one_back(self):
        self.back_product(
            ((self.q, self.ws, 0, D), (self.k, self.ws, D, D), (self.v, self.ws, 2 * D, D)),
            self.dz)
        dv, dg = rms_back(self.x_in[...].astype(F32), self.gains[0:1, :], self.dz[...])
        self.redg[0, 0:1, :] = dg
        self.xgrad[...] = (self.dr[...] + dv).astype(BF)

    def table_back(self):
        row = lax.broadcasted_iota(jnp.int32, (128, 128), 0)
        col = lax.broadcasted_iota(jnp.int32, (128, 128), 1)
        flip = jnp.where(row + col == 127, 1.0, 0.0).astype(BF)
        self.diag[...] = jnp.zeros_like(self.diag)
        for p in range(PAIRS):
            back = nn(self.ps[256 * p:256 * p + 256, :].astype(BF), flip)
            for hh in range(2):
                turned = pltpu.roll(
                    back[128 * hh:128 * hh + 128], 0, 1, stride=1, stride_axis=0)
                self.diag[2 * p + hh:2 * p + hh + 1, :] = jnp.sum(turned, axis=0, keepdims=True)
        lane = lax.broadcasted_iota(jnp.int32, (NB, 128), 1)
        hot = jnp.where(
            bucket_of((lane + 1) % 128) == lax.broadcasted_iota(jnp.int32, (NB, 128), 0), 1.0, 0.0)
        self.redt[0, :, 0:NB] = lax.dot_general(
            self.diag[...], hot, (((1,), (1,)), ((), ())),
            precision=lax.Precision.HIGHEST, preferred_element_type=F32)

    def own(self, g, chip, half=None):
        unit = UNIT[g]
        start = OWN[g] + chip * unit
        if half is not None:
            unit = unit // 2
            start = start + half * unit
        return pl.ds(al(start, 16), unit)

    def land(self, g, which, half=None):
        unit = UNIT[g]
        start = LAND[g] + (0, unit // 2, unit, 2 * unit)[which]
        rows = unit // 2 if which < 2 else unit
        if half is not None:
            rows = unit // 2
            start = start + half * rows
        return pl.ds(start, rows)

    def lanes(self, g, mine):
        if not PAIR[g]:
            return slice(None)
        par = self.z % 2
        return pl.ds(al((par if mine else 1 - par) * 128, 128), 128)

    def scopy(self, g, kind):
        gb, lb = self.gb, self.lb
        row = g * 15 + kind
        sems = self.rsend.at[row], self.rrecv.at[row]
        if kind in SIB:
            unit = UNIT[g]
            at = self.chip(*ROLES[SIB.index(kind)]) * unit
            return self.copy(
                gb.at[pl.ds(al(OWN_ROWS + (g % 2) * STAGE + at, 16), unit), :],
                self.wf.at[pl.ds(al(OWN[g] + at, 16), unit), :], *sems, self.dev(fc=1))
        spot, half, lanes, where, dev = {
            1: ((1, 1), 0, True, 0, (1, 0)),
            2: ((1, 1), 1, True, 1, (0, 1)),
            3: ((1, 0), 0, None, 2, (1, 0)),
            4: ((1, 0), 1, True, 2, (1, 0)),
            5: ((1, 0), 1, False, 2, (1, 0)),
            6: ((0, 1), 1, None, 3, (0, 1)),
            7: ((0, 1), 0, True, 3, (0, 1)),
            8: ((0, 1), 0, False, 3, (0, 1)),
            9: ((1, 1), 0, False, 0, None),
            10: ((1, 1), 1, False, 1, None),
        }[kind]
        src = self.own(g, self.chip(*spot), half)
        dst = self.land(g, where, half if where > 1 else None)
        lanes = slice(None) if lanes is None else self.lanes(g, lanes)
        put = self.lanes(g, True) if dev is None else lanes
        dev = self.dev(z=self.z + 1 - 2 * (self.z % 2)) if dev is None else self.dev(None, *dev)
        return self.copy(gb.at[src, lanes], lb.at[dst, put], *sems, dev)

    def came(self, g, *kinds):
        for kind in kinds:
            if kind in (9, 10):
                part = self.lb.at[self.land(g, kind - 9), self.lanes(g, False)]
                row = g * 15 + kind
                self.copy(
                    part, part, self.rsend.at[row], self.rrecv.at[row],
                    self.dev(fc=1)).wait_recv()
            else:
                self.scopy(g, kind).wait_recv()

    def go(self, g, *kinds):
        for kind in kinds:
            self.scopy(g, kind).start()

    def to_owner(self, g, slot=None):
        t, zb = GROUPS[g]
        unit = UNIT[g]
        if slot is None:
            slot = (self.z + 3 - zb) % 4
        return self.copy(
            self.gb.at[self.own(g, self.chip()), :],
            self.zb.at[pl.ds(al(ZBASE[t] + slot * unit, 16), unit), :],
            self.rsend.at[g * 15 + 11], self.orecv.at[t * 3 + slot], self.dev(z=zb))

    def ready(self, g):
        self.turn(g)
        if g >= 2:
            for role in range(4):
                self.scopy(g - 2, SIB[role]).wait_send()

    def allowed(self, g):
        if g in (0, 2):
            pl.semaphore_wait(self.free.at[g // 2], 1)

    def part(self, g, i):
        (self.grad_tall if g == 0 else self.grad_square)(g, i)

    def grad(self, g):
        self.ready(g)
        if 0 < g < 4:
            self.grad_ff(g)
        else:
            def step(i, _):
                self.part(g, i)
                return 0
            lax.fori_loop(0, 4, step, 0)
        self.allowed(g)
        self.go(g, *SIB)

    def grad_role(self, g, role):
        if role == 0:
            self.ready(g)
        self.part(g, self.chip(*ROLES[role]))
        if role == 0:
            self.allowed(g)
        self.go(g, SIB[role])

    def accumulate(self, dst, lanes, src_ref, src, from_lanes):
        self.gb[dst, lanes] = (
            self.gb[dst, lanes].astype(F32) + src_ref[src, from_lanes].astype(F32)).astype(BF)

    def rs1(self, g, role):
        self.came(g, SIB[role])
        rows = self.own(g, self.chip(*ROLES[role]))
        self.accumulate(rows, slice(None), self.wf, rows, slice(None))
        self.go(g, *(((9, 10), (3, 5), (6, 8), ()) if PAIR[g] else ((1, 2), (3,), (6,), ()))[role])

    def rs2(self, g, half):
        if PAIR[g]:
            self.came(g, 9 + half)
            self.accumulate(
                self.own(g, self.chip(1, 1), half), self.lanes(g, True),
                self.lb, self.land(g, half), self.lanes(g, False))
            self.go(g, 1 + half)

    def rs3(self, g, half):
        kind, spot, late = ((1, (0, 1), 7), (2, (1, 0), 4))[half]
        self.came(g, kind)
        self.accumulate(
            self.own(g, self.chip(*spot), half), self.lanes(g, True),
            self.lb, self.land(g, kind - 1), self.lanes(g, True))
        self.go(g, late)

    def rs4(self, g):
        self.came(g, *((3, 5, 6, 8, 4, 7) if PAIR[g] else (3, 6, 4, 7)))
        rows = self.own(g, self.chip())
        self.gb[rows, :] = (
            self.gb[rows, :].astype(F32) + self.lb[self.land(g, 2), :].astype(F32)
            + self.lb[self.land(g, 3), :].astype(F32)).astype(BF)

        @pl.when(self.z != GROUPS[g][1])
        def _():
            self.to_owner(g).start()

    def rs5(self, g):
        t, zb = GROUPS[g]
        unit = UNIT[g]

        @pl.when(self.z == zb)
        def _():
            for slot in range(3):
                self.to_owner(g, slot).wait_recv()

            def total(start, size, lanes):
                at = pl.ds(al(OWN[g] + self.chip() * unit + start, 16), size)
                value = self.gb[at, lanes].astype(F32)
                for slot in range(3):
                    value = value + self.zb[
                        pl.ds(ZBASE[t] + slot * unit + start, size), lanes].astype(F32)
                return value

            if t < 2:
                out = (self.gs, self.gc)[t]
                for k in range(6):
                    out[pl.ds(k, AR, stride=6), :] = total(
                        96 * (k // 2), 96, slice(128 * (k % 2), 128 * (k % 2) + 128))
                return
            out = self.gf

            def wide(rows):
                for u in range(4):
                    for w in range(2):
                        v = total(2 * rows * u, 2 * rows, slice(128 * w, 128 * w + 128))
                        out[pl.ds(4 * u + w, rows, stride=16), :] = v[0:rows]
                        out[pl.ds(4 * u + w + 2, rows, stride=16), :] = v[rows:]

            def tall(first, rows, offset):
                for k in range(6):
                    out[pl.ds(first + k, rows, stride=6), :] = total(
                        offset + rows * (k // 2), rows, slice(128 * (k % 2), 128 * (k % 2) + 128))

            if zb < 2:
                wide(72)
            elif zb == 3:
                tall(0, 192, 0)
            else:
                @pl.when(self.shard < 21)
                def _():
                    wide(72)

                @pl.when(self.shard == 21)
                def _():
                    wide(24)
                    tall(384, 128, 192)

                @pl.when(self.shard > 21)
                def _():
                    tall(0, 192, 0)

    def group_sent(self, g):
        for kind in range(1, 11):
            if PAIR[g] or kind not in (5, 8, 9, 10):
                self.scopy(g, kind).wait_send()

        @pl.when(self.z != GROUPS[g][1])
        def _():
            self.to_owner(g).wait_send()

    def small(self, step, which):
        dev = (
            self.dev(fc=1), self.dev(fx=1), self.dev(fy=1),
            self.dev(z=self.z + 1 - 2 * (self.z % 2)), self.dev(z=(self.z + 2) % 4),
        )[step]
        src, dst = ((self.redg, self.landg), (self.redt, self.landt))[which]
        row = step * 2 + which
        return self.copy(
            src.at[step], dst.at[step], self.ssend.at[row], self.srecv.at[row], dev)

    def small_start(self, step):
        for which in range(2):
            self.small(step, which).start()

    def small_add(self, step):
        for which in range(2):
            self.small(step, which).wait_recv()
        self.redg[step + 1] = self.redg[step] + self.landg[step]
        self.redt[step + 1] = self.redt[step] + self.landt[step]


    def finish(self):
        for tensor in (0, 1):
            for k in range(4):
                self.plane_sent(tensor, k)
                self.z_sent(tensor, k)
        for g in range(12):
            self.group_sent(g)
        for g in (10, 11):
            for role in range(4):
                self.scopy(g, SIB[role]).wait_send()
        self.ggain[...] = self.redga[5, 0:3, :]
        self.gtable[...] = self.redta[5, 0:H, 0:NB]
        for step in range(5):
            for which in range(2):
                self.small(step, which).wait_send()


K = Layer
SCHEDULE = (
    (K.own_xy, 0), (K.own_z, 0, 0), (K.own_z, 0, 1), (K.own_square, 1), (K.own_z, 1, 0),
    (K.own_ff,), (K.own_xy, 1), (K.own_z, 1, 1), (K.p2x, 0, 0), (K.p1, 0, 1), (K.p1, 0, 2),
    (K.p1, 1, 2), (K.p2y, 0, 0), (K.own_z, 2, 1), (K.p1, 1, 1), (K.p2y, 1, 0), (K.own_z, 2, 0),
    (K.p2x, 0, 2), (K.p2x, 0, 1), (K.p2x, 1, 0), (K.p2y, 0, 1), (K.p1, 0, 3), (K.p1, 1, 3),
    (K.p1, 2, 2), (K.p3, 1, 0, 0), (K.p2y, 1, 1), (K.p2x, 1, 1), (K.p1, 2, 1), (K.p3, 1, 0, 1),
    (K.p2y, 0, 2), (K.p3, 0, 0, 0), (K.p3, 0, 0, 1), (K.p2y, 1, 2), (K.p2x, 1, 2), (K.p1, 2, 0),
    (K.p3, 0, 1, 0), (K.p3, 1, 1, 0), (K.p3, 1, 1, 1), (K.p2y, 0, 3), (K.p3, 0, 1, 1),
    (K.p4, 0, 1), (K.p2y, 1, 3), (K.p2x, 0, 3), (K.p2y, 2, 2), (K.p2x, 2, 2), (K.p2x, 2, 1),
    (K.p2x, 1, 3), (K.p5, 0, 1), (K.p2y, 2, 1), (K.p3, 0, 2, 0), (K.p3, 0, 2, 1),
    (K.p3, 1, 2, 0), (K.p3, 1, 2, 1), (K.p1, 2, 3), (K.p3, 0, 3, 0), (K.p4, 0, 2),
    (K.p3, 0, 3, 1), (K.p3, 2, 2, 0), (K.p4, 0, 0), (K.p2x, 2, 0), (K.p2y, 2, 0), (K.p4, 1, 0),
    (K.p3, 1, 3, 0), (K.p5, 0, 2), (K.bias,), (K.p4, 0, 3), (K.p3, 1, 3, 1), (K.p4, 1, 2),
    (K.p5, 0, 0), (K.p3, 2, 1, 0), (K.p3, 2, 1, 1), (K.p3, 2, 2, 1), (K.p4, 1, 1), (K.p5, 1, 0),
    (K.p5, 0, 3), (K.p5, 1, 1), (K.self_forward,), (K.p4, 1, 3), (K.p3, 2, 0, 0), (K.p5, 1, 2),
    (K.p2x, 2, 3), (K.p2y, 2, 3), (K.p3, 2, 0, 1), (K.p4, 2, 1), (K.p5, 1, 3), (K.cross_kv, 2),
    (K.cross_kv, 1), (K.p4, 2, 2), (K.cross_forward, 0), (K.p5, 2, 1), (K.p3, 2, 3, 0),
    (K.cross_forward, 1), (K.p5, 2, 2), (K.build_plane, 1), (K.p3, 2, 3, 1), (K.p4, 2, 0),
    (K.cross_forward, 2), (K.build_plane, 2), (K.p5, 2, 0), (K.build_plane, 0), (K.ff_gate,),
    (K.ff_up,), (K.credit, 0), (K.p4, 2, 3), (K.grad_role, 0, 0), (K.grad_role, 0, 1),
    (K.grad_role, 0, 2), (K.grad_role, 0, 3), (K.p5, 2, 3), (K.rs1, 0, 0), (K.build_plane, 3),
    (K.d_hidden, 0), (K.rs1, 0, 2), (K.rs1, 0, 1), (K.d_hidden, 1), (K.grad, 1), (K.credit, 1),
    (K.rs2, 0, 1), (K.rs2, 0, 0), (K.grad, 2), (K.rs1, 1, 2), (K.rs1, 1, 1), (K.rs1, 1, 0),
    (K.grad, 3), (K.rs1, 2, 2), (K.rs1, 2, 0), (K.rs1, 2, 1), (K.norm_three_back,),
    (K.grad_role, 4, 0), (K.cross_back, 0), (K.rs2, 1, 1), (K.rs2, 1, 0), (K.rs2, 2, 0),
    (K.rs2, 2, 1), (K.rs3, 0, 1), (K.rs1, 1, 3), (K.rs1, 4, 0), (K.rs3, 0, 0),
    (K.grad_role, 4, 1), (K.cross_back, 1), (K.rs1, 3, 0), (K.cross_back, 2),
    (K.grad_role, 4, 2), (K.rs3, 2, 0), (K.grad_role, 4, 3), (K.rs3, 2, 1), (K.rs1, 3, 2),
    (K.rs1, 0, 3), (K.rs1, 2, 3), (K.rs1, 3, 1), (K.rs2, 3, 0), (K.rs3, 1, 1), (K.grad, 5),
    (K.rs3, 1, 0), (K.rs2, 3, 1), (K.rs4, 0), (K.grad, 6), (K.rs4, 2), (K.grad, 7),
    (K.rs1, 4, 2), (K.norm_two_back,), (K.rs1, 5, 0), (K.rs1, 4, 3), (K.grad, 8), (K.rs1, 6, 0),
    (K.self_back, 0), (K.rs3, 3, 0), (K.rs1, 8, 0), (K.rs1, 4, 1), (K.self_back, 1),
    (K.rs3, 3, 1), (K.grad_role, 9, 0), (K.grad_role, 9, 1), (K.rs2, 8, 0), (K.rs4, 1),
    (K.grad_role, 9, 2), (K.rs2, 4, 0), (K.grad_role, 9, 3), (K.rs2, 6, 0), (K.rs1, 7, 0),
    (K.table_back,), (K.rs2, 7, 0), (K.rs1, 8, 3), (K.rs3, 4, 0), (K.rs2, 7, 1), (K.rs2, 4, 1),
    (K.grad_role, 10, 0), (K.grad_role, 10, 1), (K.grad_role, 10, 2), (K.grad_role, 10, 3),
    (K.rs1, 8, 1), (K.rs1, 8, 2), (K.norm_one_back,), (K.rs1, 3, 3), (K.grad_role, 11, 0),
    (K.rs1, 10, 0), (K.rs2, 8, 1), (K.small_start, 0), (K.rs2, 6, 1), (K.rs4, 3),
    (K.small_add, 0), (K.small_start, 1), (K.rs3, 8, 1), (K.grad_role, 11, 1),
    (K.grad_role, 11, 2), (K.memory_rows, 0), (K.rs1, 11, 0), (K.rs2, 11, 1), (K.rs2, 11, 0),
    (K.rs3, 4, 1), (K.small_add, 1), (K.small_start, 2), (K.rs1, 9, 3), (K.rs3, 8, 0),
    (K.memory_rows, 3), (K.rs2, 10, 0), (K.out_rows,), (K.grad_role, 11, 3), (K.rs1, 11, 2),
    (K.rs1, 7, 1), (K.rs5, 2), (K.rs1, 7, 3), (K.rs3, 11, 0), (K.rs1, 6, 2), (K.rs1, 9, 2),
    (K.rs1, 7, 2), (K.rs1, 10, 2), (K.small_add, 2), (K.rs2, 10, 1), (K.small_start, 3),
    (K.rs1, 11, 1), (K.rs4, 8), (K.rs3, 7, 0), (K.rs3, 11, 1), (K.rs1, 11, 3),
    (K.memory_rows, 2), (K.rs3, 7, 1), (K.rs4, 4), (K.rs3, 10, 0), (K.rs1, 9, 0), (K.rs1, 6, 3),
    (K.rs3, 6, 0), (K.rs1, 10, 1), (K.rs4, 11), (K.rs1, 9, 1), (K.rs3, 10, 1), (K.rs1, 10, 3),
    (K.rs2, 9, 0), (K.rs1, 6, 1), (K.memory_rows, 1), (K.rs3, 9, 0), (K.rs3, 6, 1),
    (K.rs2, 9, 1), (K.rs5, 1), (K.small_add, 3), (K.rs4, 7), (K.rs1, 5, 3), (K.rs4, 10),
    (K.rs3, 9, 1), (K.rs1, 5, 2), (K.rs5, 0), (K.rs1, 5, 1), (K.rs4, 6), (K.small_start, 4),
    (K.rs5, 8), (K.rs5, 10), (K.rs2, 5, 1), (K.rs3, 5, 1), (K.rs4, 9), (K.rs2, 5, 0),
    (K.rs3, 5, 0), (K.rs5, 7), (K.rs4, 5), (K.rs5, 9), (K.rs5, 6), (K.rs5, 3), (K.small_add, 4),
    (K.rs5, 5), (K.rs5, 11), (K.rs5, 4),
)

NAMES = (
    "x_in", "mem", "g", "dl", "ml", "sh_s", "sh_c", "sh_f", "gains", "table",
    "block", "xgrad", "mgrad", "gs", "gc", "gf", "ggain", "gtable",
    "ws", "wc", "wf", "wgu", "wd", "gb", "lb", "zb",
    "n1", "q", "k", "v", "mix", "r1", "n2", "cq", "ck", "cv", "cmix", "r2", "n3",
    "ga", "ub", "hid", "hidt", "n3t", "dg", "du", "dz", "dr", "drb", "tt", "memt",
    "ps", "diag", "redga", "redta", "landg", "landt",
    "gsend", "grecv", "zsend", "zrecv", "rsend", "rrecv", "orecv", "ssend", "srecv", "free",
)


def kernel(*args):
    st = Layer(dict(zip(NAMES, args)))
    st.redg, st.redt = st.redga, st.redta
    barrier = pltpu.get_barrier_semaphore()
    others = [st.dev(fc=1), st.dev(fx=1), st.dev(fy=1)] + [
        st.dev(z=(st.z + k) % 4) for k in (1, 2, 3)]
    for other in others:
        pl.semaphore_signal(barrier, inc=1, device_id=other, device_id_type=MESH)
    st.own_square(0)
    st.masks()
    pl.semaphore_wait(barrier, 6)
    for step, *numbers in SCHEDULE:
        step(st, *numbers)
    st.finish()


def settle_kernel(count, *refs):
    out = [pltpu.make_async_copy(refs[i], refs[count + i], refs[-1].at[i]) for i in range(count)]
    for one in out:
        one.start()
    for one in out:
        one.wait()


def settle(arrays):
    count = len(arrays)
    return pl.pallas_call(
        functools.partial(settle_kernel, count),
        out_shape=tuple(jax.ShapeDtypeStruct(v.shape, v.dtype) for v in arrays),
        in_specs=[pl.BlockSpec(memory_space=pltpu.VMEM)] * count,
        out_specs=tuple([pl.BlockSpec(memory_space=pl.ANY)] * count),
        scratch_shapes=[pltpu.SemaphoreType.DMA((count,))],
        compiler_params=pltpu.CompilerParams(vmem_limit_bytes=67000000),
    )(*arrays)


def fused(inputs, memory, out_cotangent, dec_lengths, mem_lengths, self_params, cross_params,
          ff_params, gains, table):
    slots, length, width = inputs.shape
    mem_len = memory.shape[1]
    vm = pl.BlockSpec(memory_space=pltpu.VMEM)
    sm = pl.BlockSpec(memory_space=pltpu.SMEM)
    s = jax.ShapeDtypeStruct
    rows_s, rows_f = self_params.shape[0] // 128, ff_params.shape[0] // 128
    row = pltpu.VMEM((length, D), BF)
    rowf = pltpu.VMEM((length, D), F32)
    memory_row = pltpu.VMEM((mem_len, D), BF)
    dma = pltpu.SemaphoreType.DMA
    outs = pl.pallas_call(
        kernel,
        out_shape=(
            s((length, D), BF), s((length, D), BF), s((mem_len, D), BF),
            s((rows_s, 128), F32), s((rows_s, 128), F32), s((rows_f, 128), F32),
            s((3, D), F32), s((H, NB), F32),
        ),
        in_specs=[vm, vm, vm, sm, sm, vm, vm, vm, vm, sm],
        out_specs=[vm] * 8,
        scratch_shapes=[
            pltpu.VMEM((4 * D, D), BF), pltpu.VMEM((4 * D, D), BF),
            pltpu.VMEM((32 * FU, 256), BF),
            pltpu.VMEM((2 * D, FF), BF), pltpu.VMEM((FF, D), BF),
            pltpu.VMEM((OWN_ROWS + 2 * STAGE, 256), BF),
            pltpu.VMEM((LAND_ROWS, 256), BF), pltpu.VMEM((Z_ROWS, 256), BF),
            row, row, row, row, row, rowf, row, row, memory_row, memory_row, row, rowf, row,
            pltpu.VMEM((length, FF), F32), pltpu.VMEM((length, FF), F32),
            pltpu.VMEM((length, FF), BF), pltpu.VMEM((FF, length), BF),
            pltpu.VMEM((D, length), BF),
            pltpu.VMEM((length, FF), BF), pltpu.VMEM((length, FF), BF),
            rowf, rowf, row, pltpu.VMEM((D, length), BF), pltpu.VMEM((D, mem_len), BF),
            pltpu.VMEM((H * length, length), F32),
            pltpu.VMEM((16, 128), F32),
            pltpu.VMEM((6, 8, D), F32), pltpu.VMEM((6, 16, 128), F32),
            pltpu.VMEM((5, 8, D), F32), pltpu.VMEM((5, 16, 128), F32),
            dma((120,)), dma((120,)), dma((24,)), dma((12,)), dma((180,)), dma((180,)), dma((9,)),
            dma((10,)), dma((10,)), pltpu.SemaphoreType.REGULAR((2,)),
        ],
        compiler_params=pltpu.CompilerParams(
            collective_id=0, has_side_effects=True, vmem_limit_bytes=67000000),
        cost_estimate=pl.CostEstimate(
            flops=10_000_000_000, bytes_accessed=8_000_000, transcendentals=2_000_000),
    )(
        inputs.reshape(length, width), memory.reshape(mem_len, width),
        out_cotangent.reshape(length, width), dec_lengths, mem_lengths,
        self_params.reshape(rows_s, 128), cross_params.reshape(rows_s, 128),
        ff_params.reshape(rows_f, 128), gains, table.T,
    )
    outs = settle(outs)
    return (
        outs[0].reshape(inputs.shape), outs[1].reshape(inputs.shape),
        outs[2].reshape(memory.shape), outs[3].reshape(-1), outs[4].reshape(-1),
        outs[5].reshape(-1), outs[6], outs[7].T,
    )


HIGHEST = lax.Precision.HIGHEST


def product(left, right):
    return jnp.dot(left, right, preferred_element_type=jnp.float32)


def product_t(left, right):
    return lax.dot_general(
        left, right, (((0,), (0,)), ((), ())), preferred_element_type=jnp.float32
    )


def product_nt(left, right):
    return lax.dot_general(
        left, right, (((1,), (1,)), ((), ())), preferred_element_type=jnp.float32
    )


def rms_scale(value, gain):
    return value * lax.rsqrt(jnp.mean(value * value, axis=-1, keepdims=True) + 1e-06) * gain


def gelu_gate(gate_pre, up_pre):
    return jax.nn.gelu(gate_pre, approximate=True) * up_pre


def bucket_rows(start, count, length):
    half_count = NB // 2
    limits = np.ceil(
        half_count * (MAXD / half_count) ** (np.arange(1, half_count) / half_count)
    ).astype(np.int32)
    query_pos = start + jnp.arange(count, dtype=jnp.int32)
    key_pos = jnp.arange(length, dtype=jnp.int32)
    distance = query_pos[:, None] - key_pos[None, :]
    beyond = half_count + jnp.sum(
        (distance[None] >= jnp.asarray(limits)[:, None, None]).astype(jnp.int32), axis=0
    )
    return jnp.where(distance < half_count, jnp.maximum(distance, 0), beyond)


def onehot_block(start, count, length):
    bucket = bucket_rows(start, count, length)
    hot_rows = jnp.arange(NB, dtype=jnp.int32)[:, None, None] == bucket[None]
    return hot_rows.astype(jnp.float32).reshape(NB, count * length)


def position_bias(table, length):
    block_rows = min(length, 128)
    block_count = length // block_rows

    def position_per_block(block):
        bucket_hot = onehot_block(block * block_rows, block_rows, length)
        return lax.dot_general(
            table,
            bucket_hot,
            (((0,), (0,)), ((), ())),
            precision=HIGHEST,
            preferred_element_type=jnp.float32,
        )

    pieces = lax.map(position_per_block, jnp.arange(block_count, dtype=jnp.int32))
    return (
        pieces.reshape(block_count, H, block_rows, length)
        .transpose(1, 0, 2, 3)
        .reshape(H, length, length)
    )


def table_gradient(score_sums, length):
    block_rows = min(length, 128)

    def table_per_block(carry, block):
        ds_piece = score_sums.reshape(H, block_rows * length)
        bucket_hot = onehot_block(block * block_rows, block_rows, length)
        return (
            carry
            + lax.dot_general(
                bucket_hot,
                ds_piece,
                (((1,), (1,)), ((), ())),
                precision=HIGHEST,
                preferred_element_type=jnp.float32,
            ),
            None,
        )

    result, _ = lax.scan(
        table_per_block,
        jnp.zeros((NB, H), jnp.float32),
        jnp.arange(length // block_rows, dtype=jnp.int32),
    )
    return result


def score_block(queries, keys_in, score_bias, keep_mask):
    q_len = queries.shape[0]
    k_len = keys_in.shape[0]
    raw_scores = (
        jnp.einsum(
            "qhe,khe->hqk",
            queries.reshape(q_len, H, DH),
            keys_in.reshape(k_len, H, DH),
            preferred_element_type=jnp.float32,
        )
        + score_bias
    )
    return jnp.where(keep_mask[None], raw_scores, MASKED)


def attend_forward(queries, keys_in, values, score_bias, keep_mask):
    q_len = queries.shape[0]
    k_len = keys_in.shape[0]
    raw_scores = score_block(queries, keys_in, score_bias, keep_mask)
    row_max = jnp.max(raw_scores, axis=2, keepdims=True)
    exponent = jnp.exp(raw_scores - row_max)
    row_sum = jnp.sum(exponent, axis=2, keepdims=True)
    softmax_low = (exponent / row_sum).astype(jnp.bfloat16)
    head_mix = jnp.einsum(
        "hqk,khe->qhe",
        softmax_low,
        values.reshape(k_len, H, DH),
        preferred_element_type=jnp.float32,
    )
    return (head_mix.reshape(q_len, H * DH).astype(jnp.bfloat16), row_max, row_sum)


def attend_backward(queries, keys_in, values, score_bias, keep_mask, row_max, row_sum, d_mix):
    q_len = queries.shape[0]
    k_len = keys_in.shape[0]
    raw_scores = score_block(queries, keys_in, score_bias, keep_mask)
    softmax_out = jnp.exp(raw_scores - row_max) / row_sum
    softmax_low = softmax_out.astype(jnp.bfloat16)
    mix_heads = d_mix.reshape(q_len, H, DH)
    q_heads = queries.reshape(q_len, H, DH)
    k_heads = keys_in.reshape(k_len, H, DH)
    v_heads = values.reshape(k_len, H, DH)
    d_softmax = jnp.einsum("qhe,khe->hqk", mix_heads, v_heads, preferred_element_type=jnp.float32)
    d_scores = (
        softmax_out * (d_softmax - jnp.sum(softmax_out * d_softmax, axis=2, keepdims=True))
    ).astype(jnp.bfloat16)
    d_values = (
        jnp.einsum("hqk,qhe->khe", softmax_low, mix_heads, preferred_element_type=jnp.float32)
        .reshape(k_len, H * DH)
        .astype(jnp.bfloat16)
    )
    d_queries = (
        jnp.einsum("hqk,khe->qhe", d_scores, k_heads, preferred_element_type=jnp.float32)
        .reshape(q_len, H * DH)
        .astype(jnp.bfloat16)
    )
    d_keys = (
        jnp.einsum("hqk,qhe->khe", d_scores, q_heads, preferred_element_type=jnp.float32)
        .reshape(k_len, H * DH)
        .astype(jnp.bfloat16)
    )
    return (d_queries, d_keys, d_values, d_scores)


def attend_slots(queries, keys_in, values, lengths, score_bias, base_mask):
    slot_count = lengths.shape[0]
    q_len = queries.shape[0] // slot_count
    k_len = keys_in.shape[0] // slot_count
    key_pos = jnp.arange(k_len, dtype=jnp.int32)

    def per_slot(slot_item):
        q_slot, k_slot, v_slot, slot_len = slot_item
        keep_mask = base_mask & (key_pos[None, :] < slot_len)
        return attend_forward(q_slot, k_slot, v_slot, score_bias, keep_mask)

    head_mix, row_max, row_sum = lax.map(
        per_slot,
        (
            queries.reshape(slot_count, q_len, -1),
            keys_in.reshape(slot_count, k_len, -1),
            values.reshape(slot_count, k_len, -1),
            lengths,
        ),
    )
    return (head_mix.reshape(slot_count * q_len, -1), row_max, row_sum)


def attend_back_slots(
    queries, keys_in, values, lengths, score_bias, base_mask, row_max, row_sum, d_mix, with_table
):
    slot_count = lengths.shape[0]
    q_len = queries.shape[0] // slot_count
    k_len = keys_in.shape[0] // slot_count
    key_pos = jnp.arange(k_len, dtype=jnp.int32)
    if with_table:
        start = jnp.zeros((H, q_len, k_len), jnp.float32)
    else:
        start = jnp.zeros((), jnp.float32)

    def per_slot(carry, slot_item):
        q_slot, k_slot, v_slot, slot_len, max_slot, sum_slot, dmix_slot = slot_item
        keep_mask = base_mask & (key_pos[None, :] < slot_len)
        d_queries, d_keys, d_values, d_scores = attend_backward(
            q_slot, k_slot, v_slot, score_bias, keep_mask, max_slot, sum_slot, dmix_slot
        )
        if with_table:
            carry = carry + d_scores.astype(jnp.float32)
        return (carry, (d_queries, d_keys, d_values))

    score_sums, grad_parts = lax.scan(
        per_slot,
        start,
        (
            queries.reshape(slot_count, q_len, -1),
            keys_in.reshape(slot_count, k_len, -1),
            values.reshape(slot_count, k_len, -1),
            lengths,
            row_max,
            row_sum,
            d_mix.reshape(slot_count, q_len, -1),
        ),
    )
    return (
        grad_parts[0].reshape(slot_count * q_len, -1),
        grad_parts[1].reshape(slot_count * k_len, -1),
        grad_parts[2].reshape(slot_count * k_len, -1),
        score_sums,
    )


def gather_weights(self_params, cross_params, ff_params):
    return (
        lax.all_gather(self_params, ("dp", "fsdp"), axis=0, tiled=True),
        lax.all_gather(cross_params, ("dp", "fsdp"), axis=0, tiled=True),
        lax.all_gather(ff_params, ("dp", "fsdp"), axis=0, tiled=True),
    )


def scatter_grads(self_full, cross_full, ff_full):
    wide_count = lax.axis_size("dp")
    spread = (
        lax.all_to_all(
            self_full.reshape(wide_count, -1).astype(jnp.bfloat16),
            "dp",
            split_axis=0,
            concat_axis=0,
            tiled=True,
        ).astype(jnp.float32),
        lax.all_to_all(
            cross_full.reshape(wide_count, -1).astype(jnp.bfloat16),
            "dp",
            split_axis=0,
            concat_axis=0,
            tiled=True,
        ).astype(jnp.float32),
        lax.all_to_all(
            ff_full.reshape(wide_count, -1).astype(jnp.bfloat16),
            "dp",
            split_axis=0,
            concat_axis=0,
            tiled=True,
        ).astype(jnp.float32),
    )
    self_block = jnp.sum(spread[0], axis=0)
    cross_block = jnp.sum(spread[1], axis=0)
    ff_block = jnp.sum(spread[2], axis=0)
    return (
        lax.psum_scatter(
            self_block.astype(jnp.bfloat16), "fsdp", scatter_dimension=0, tiled=True
        ).astype(jnp.float32),
        lax.psum_scatter(
            cross_block.astype(jnp.bfloat16), "fsdp", scatter_dimension=0, tiled=True
        ).astype(jnp.float32),
        lax.psum_scatter(
            ff_block.astype(jnp.bfloat16), "fsdp", scatter_dimension=0, tiled=True
        ).astype(jnp.float32),
    )


def unpack(weights):
    self_flat, cross_flat, ff_flat = weights
    self_mats = self_flat.reshape(4, D, D)
    cross_mats = cross_flat.reshape(4, D, D)
    block_size = D * FF
    return (
        self_mats[0],
        self_mats[1],
        self_mats[2],
        self_mats[3],
        cross_mats[0],
        cross_mats[1],
        cross_mats[2],
        cross_mats[3],
        ff_flat[:block_size].reshape(D, FF),
        ff_flat[block_size : 2 * block_size].reshape(D, FF),
        ff_flat[2 * block_size :].reshape(FF, D),
    )


def run_forward(
    weights, flat_in, flat_mem, gains, pos_bias, causal, open_mask, dec_lengths, mem_lengths
):
    w_sq, w_sk, w_sv, w_so, w_cq, w_ck, w_cv, w_co, w_gate, w_up, w_down = unpack(weights)
    norm_one = rms_scale(flat_in, gains[0]).astype(jnp.bfloat16)
    self_q = product(norm_one, w_sq).astype(jnp.bfloat16)
    self_k = product(norm_one, w_sk).astype(jnp.bfloat16)
    self_v = product(norm_one, w_sv).astype(jnp.bfloat16)
    self_mix, self_max, self_sum = attend_slots(
        self_q, self_k, self_v, dec_lengths, pos_bias, causal
    )
    resid_one = flat_in + product(self_mix, w_so)
    norm_two = rms_scale(resid_one, gains[1]).astype(jnp.bfloat16)
    cross_q = product(norm_two, w_cq).astype(jnp.bfloat16)
    cross_k = product(flat_mem, w_ck).astype(jnp.bfloat16)
    cross_v = product(flat_mem, w_cv).astype(jnp.bfloat16)
    cross_mix, cross_max, cross_sum = attend_slots(
        cross_q, cross_k, cross_v, mem_lengths, 0.0, open_mask
    )
    resid_two = resid_one + product(cross_mix, w_co)
    norm_three = rms_scale(resid_two, gains[2]).astype(jnp.bfloat16)
    gate_pre = product(norm_three, w_gate)
    up_pre = product(norm_three, w_up)
    hidden = gelu_gate(gate_pre, up_pre).astype(jnp.bfloat16)
    block = resid_two + product(hidden, w_down)
    return (
        norm_one,
        self_q,
        self_k,
        self_v,
        self_mix,
        self_max,
        self_sum,
        resid_one,
        norm_two,
        cross_q,
        cross_k,
        cross_v,
        cross_mix,
        cross_max,
        cross_sum,
        resid_two,
        norm_three,
        gate_pre,
        up_pre,
        hidden,
        block,
    )


def by_collectives(
    inputs,
    memory,
    out_cotangent,
    dec_lengths,
    mem_lengths,
    self_params,
    cross_params,
    ff_params,
    gains,
    table,
):
    slot_count, length, model_width = inputs.shape
    mem_len = memory.shape[1]
    row_count = slot_count * length
    pos_bias = position_bias(table, length)
    positions = jnp.arange(length, dtype=jnp.int32)
    causal = positions[None, :] <= positions[:, None]
    open_mask = jnp.ones((length, mem_len), dtype=bool)
    flat_in = inputs.reshape(row_count, model_width).astype(jnp.float32)
    flat_mem = memory.reshape(slot_count * mem_len, model_width)
    weights = gather_weights(self_params, cross_params, ff_params)
    first_pass = run_forward(
        weights, flat_in, flat_mem, gains, pos_bias, causal, open_mask, dec_lengths, mem_lengths
    )
    block_out = first_pass[20].astype(jnp.bfloat16).reshape(slot_count, length, model_width)
    again = gather_weights(self_params, cross_params, ff_params)
    w_sq, w_sk, w_sv, w_so, w_cq, w_ck, w_cv, w_co, w_gate, w_up, w_down = unpack(again)
    (
        norm_one,
        self_q,
        self_k,
        self_v,
        self_mix,
        self_max,
        self_sum,
        resid_one,
        norm_two,
        cross_q,
        cross_k,
        cross_v,
        cross_mix,
        cross_max,
        cross_sum,
        resid_two,
        norm_three,
        gate_pre,
        up_pre,
        hidden,
        _,
    ) = run_forward(
        again, flat_in, flat_mem, gains, pos_bias, causal, open_mask, dec_lengths, mem_lengths
    )
    d_out = out_cotangent.reshape(row_count, model_width)
    grad_down = product_t(hidden, d_out)
    d_hidden = product_nt(d_out, w_down).astype(jnp.bfloat16)
    _, pull_gate = jax.vjp(gelu_gate, gate_pre, up_pre)
    d_gate, d_up = pull_gate(d_hidden.astype(jnp.float32))
    d_gate = d_gate.astype(jnp.bfloat16)
    d_up = d_up.astype(jnp.bfloat16)
    grad_gate = product_t(norm_three, d_gate)
    grad_up = product_t(norm_three, d_up)
    d_norm_three = product_nt(d_gate, w_gate) + product_nt(d_up, w_up)
    _, pull_three = jax.vjp(rms_scale, resid_two, gains[2])
    d_from_three, grad_gain_three = pull_three(d_norm_three)
    d_resid_two = d_out.astype(jnp.float32) + d_from_three
    d_cross = d_resid_two.astype(jnp.bfloat16)
    grad_co = product_t(cross_mix, d_cross)
    d_cross_mix = product_nt(d_cross, w_co).astype(jnp.bfloat16)
    dq_cross, dk_cross, dv_cross, _ = attend_back_slots(
        cross_q,
        cross_k,
        cross_v,
        mem_lengths,
        0.0,
        open_mask,
        cross_max,
        cross_sum,
        d_cross_mix,
        False,
    )
    grad_cq = product_t(norm_two, dq_cross)
    grad_ck = product_t(flat_mem, dk_cross)
    grad_cv = product_t(flat_mem, dv_cross)
    memory_grad = (product_nt(dk_cross, w_ck) + product_nt(dv_cross, w_cv)).astype(jnp.bfloat16)
    _, pull_two = jax.vjp(rms_scale, resid_one, gains[1])
    d_from_two, grad_gain_two = pull_two(product_nt(dq_cross, w_cq))
    d_resid_one = d_resid_two + d_from_two
    d_self = d_resid_one.astype(jnp.bfloat16)
    grad_so = product_t(self_mix, d_self)
    d_self_mix = product_nt(d_self, w_so).astype(jnp.bfloat16)
    dq_self, dk_self, dv_self, score_sums = attend_back_slots(
        self_q, self_k, self_v, dec_lengths, pos_bias, causal, self_max, self_sum, d_self_mix, True
    )
    grad_sq = product_t(norm_one, dq_self)
    grad_sk = product_t(norm_one, dk_self)
    grad_sv = product_t(norm_one, dv_self)
    d_norm_one = product_nt(dq_self, w_sq) + product_nt(dk_self, w_sk) + product_nt(dv_self, w_sv)
    _, pull_one = jax.vjp(rms_scale, flat_in, gains[0])
    d_from_one, grad_gain_one = pull_one(d_norm_one)
    input_grad = (d_resid_one + d_from_one).astype(jnp.bfloat16)
    table_local = table_gradient(score_sums, length)
    self_full = jnp.stack([grad_sq, grad_sk, grad_sv, grad_so]).reshape(-1)
    cross_full = jnp.stack([grad_cq, grad_ck, grad_cv, grad_co]).reshape(-1)
    ff_full = jnp.concatenate([grad_gate.reshape(-1), grad_up.reshape(-1), grad_down.reshape(-1)])
    self_shard, cross_shard, ff_shard = scatter_grads(self_full, cross_full, ff_full)
    gain_local = jnp.stack([grad_gain_one, grad_gain_two, grad_gain_three])
    gain_total, table_total = lax.psum((gain_local, table_local), ("dp", "fsdp"))
    return (
        block_out,
        input_grad.reshape(slot_count, length, model_width),
        memory_grad.reshape(slot_count, mem_len, model_width),
        self_shard,
        cross_shard,
        ff_shard,
        gain_total,
        table_total,
    )


def solution(mesh):
    whole = ("dp", "fsdp")
    rows = P(whole, None, None)
    flat = P(whole)
    small = mesh.shape["dp"] == 8 and mesh.shape["fsdp"] == 4
    return jax.shard_map(
        fused if small else by_collectives,
        mesh=mesh,
        in_specs=(rows, rows, rows, flat, flat, flat, flat, flat, P(), P()),
        out_specs=(rows, rows, rows, flat, flat, flat, P(), P()),
        check_vma=False,
    )
```

```python
import functools

import jax
import jax.numpy as jnp
import numpy as np
from jax import lax
from jax.experimental import pallas as pl
from jax.experimental.pallas import tpu as pltpu
from jax.sharding import PartitionSpec as P

D = 768
FF = 2048
H = 12
DH = 64
NB = 32
MAXD = 128
PAIRS = H // 2
MASKED = -1000000000.0
BF = jnp.bfloat16
F32 = jnp.float32
MESH = pl.DeviceIdType.MESH

AR = 96
AU = 288
FU = 576
GROUPS = (
    (2, 3), (2, 2), (2, 0), (2, 1),
    (1, 3), (1, 2), (1, 1), (1, 0),
    (0, 3), (0, 0), (0, 2), (0, 1),
)
PAIR = (True,) * 4 + (False,) * 8
SHARED = (True, True, True)
UNIT = tuple(FU if t == 2 else AU for t, _ in GROUPS)
OWN = tuple(4 * sum(UNIT[:g]) for g in range(12))
OWN_ROWS = 4 * sum(UNIT)
LAND = tuple(3 * sum(UNIT[:g]) for g in range(12))
LAND_ROWS = 3 * sum(UNIT)
ZBASE = (0, 3 * AU, 6 * AU)
Z_ROWS = 6 * AU + 3 * FU
STAGE = 4 * FU
ROLES = ((1, 1), (1, 0), (0, 1), (0, 0))
SIB = (0, 12, 13, 14)


def limits():
    half = NB // 2
    return [
        int(v)
        for v in np.ceil(half * (MAXD / half) ** (np.arange(1, half) / half)).astype(np.int32)
    ]


def bucket_of(distance):
    half = NB // 2
    beyond = jnp.full(distance.shape, half, jnp.int32)
    for limit in limits():
        beyond = beyond + jnp.where(distance >= limit, 1, 0)
    return jnp.where(distance < half, jnp.maximum(distance, 0), beyond)


def nn(left, right):
    return jnp.dot(left, right, preferred_element_type=F32)


def nt(left, right):
    return lax.dot_general(left, right, (((1,), (1,)), ((), ())), preferred_element_type=F32)


def tn(left, right):
    return lax.dot_general(left, right, (((0,), (0,)), ((), ())), preferred_element_type=F32)


def al(value, step):
    return pl.multiple_of(value, step)


def rms(value, gain):
    r = lax.rsqrt(jnp.mean(value * value, axis=-1, keepdims=True) + 1e-06)
    return value * r * gain


def rms_back(value, gain, dz):
    r = lax.rsqrt(jnp.mean(value * value, axis=-1, keepdims=True) + 1e-06)
    inner = jnp.mean(value * gain * dz, axis=-1, keepdims=True)
    dv = r * gain * dz - value * (r * r * r) * inner
    dg = jnp.sum(value * r * dz, axis=0, keepdims=True)
    return dv, dg


class Layer:
    def __init__(self, refs):
        self.__dict__.update(refs)
        self.flat, self.dm = self.ps, self.n3
        dp = lax.axis_index("dp")
        fs = lax.axis_index("fsdp")
        self.z, self.y = dp // 2, dp % 2
        self.x, self.c = fs // 2, fs % 2
        self.shard = dp * 4 + fs

    def dev(self, z=None, fx=0, fy=0, fc=0):
        z = self.z if z is None else z
        y = (self.y + fy) % 2
        x = (self.x + fx) % 2
        c = (self.c + fc) % 2
        return (z * 2 + y, x * 2 + c)

    def chip(self, fx=0, fy=0):
        return ((self.y + fy) % 2) * 2 + (self.x + fx) % 2

    def shard_at(self, z, fx=0, fy=0, fc=0):
        return z * 8 + self.chip(fx, fy) * 2 + (self.c + fc) % 2

    def copy(self, src, dst, send, recv, device):
        return pltpu.make_async_remote_copy(
            src_ref=src, dst_ref=dst, send_sem=send, recv_sem=recv,
            device_id=device, device_id_type=MESH,
        )

    def piece(self, tensor, shard, half=None, par=None):
        rows = FU if tensor == 2 else AR
        ref = (self.ws, self.wc, self.wf)[tensor]
        start = shard * rows
        if half is None:
            return ref.at[pl.ds(al(start, 16), rows), :]
        rows = rows // 2
        start = pl.ds(al(start + half * rows, 16), rows)
        if not SHARED[tensor]:
            return ref.at[start, :]
        width = ref.shape[1] // 2
        return ref.at[start, pl.ds(al(par * width, 128), width)]

    def plane(self, tensor, k):
        if tensor == 2:
            return k
        far = self.z // 2
        return (self.z, self.z + 1 - 2 * (self.z % 2), 2 - far, 3 - 3 * far)[k]

    def gcopy(self, tensor, zs, kind, there=False):
        par = self.z % 2
        if kind < 2:
            spot, dev = (0, 0), ((1, 0), (0, 1))[kind]
            if there:
                spot = dev
            part, dev = self.piece(tensor, self.shard_at(zs, *spot)), self.dev(None, *dev)
        elif kind < 4:
            spot, dev = ((1, 0), (0, 1)) if kind == 2 else ((0, 1), (1, 0))
            if there:
                spot = (1, 1)
            part = self.piece(tensor, self.shard_at(zs, *spot), kind - 2, par)
            dev = self.dev(None, *dev)
        elif kind < 8:
            spot = ((0, 0), (1, 0), (0, 1), (1, 1))[kind - 4]
            part = self.piece(tensor, self.shard_at(zs, *spot, 1 if there else 0))
            dev = self.dev(fc=1)
        else:
            part = self.piece(
                tensor, self.shard_at(zs, 1, 1), kind - 8, 1 - par if there else par)
            dev = self.dev(z=self.z + 1 - 2 * par)
        row = (tensor * 4 + zs) * 10 + kind
        return self.copy(part, part, self.gsend.at[row], self.grecv.at[row], dev)

    def start(self, tensor, zs, *kinds):
        for kind in kinds:
            self.gcopy(tensor, zs, kind).start()

    def arrive(self, tensor, zs, *kinds):
        for kind in kinds:
            self.gcopy(tensor, zs, kind, True).wait_recv()

    def zcopy(self, tensor, zs, up):
        part = self.piece(tensor, self.shard_at(zs))
        row = tensor * 4 + zs
        return self.copy(
            part, part, self.zsend.at[2 * row + up], self.zrecv.at[row],
            self.dev(z=(self.z + (1 if up else 3)) % 4))

    def inner(self, up):
        return self.z < 3 if up else self.z > 0

    def own_z(self, tensor, up):
        @pl.when(self.inner(up))
        def _():
            self.zcopy(tensor, self.z, up).start()

    def z_arrive(self, tensor, zs):
        self.zcopy(tensor, zs, 0).wait_recv()
        for up in (0, 1):
            @pl.when((zs < self.z if up else zs > self.z) & self.inner(up))
            def _(up=up):
                self.zcopy(tensor, zs, up).start()
        self.start(tensor, zs, 0, 1, 4)

    def own_xy(self, tensor):
        self.start(tensor, self.z, 0, 1, 4)

    def p1(self, tensor, k):
        if tensor < 2:
            self.z_arrive(tensor, self.plane(tensor, k))
            return

        @pl.when(self.z == k)
        def _():
            self.start(tensor, k, 0, 1, 4)

        @pl.when(self.z != k)
        def _():
            self.z_arrive(tensor, k)

    def p2x(self, tensor, k):
        zs = self.plane(tensor, k)
        self.arrive(tensor, zs, 0)
        self.start(tensor, zs, 2, 5)

    def p2y(self, tensor, k):
        zs = self.plane(tensor, k)
        self.arrive(tensor, zs, 1)
        self.start(tensor, zs, 3, 6)

    def p3(self, tensor, k, half):
        zs = self.plane(tensor, k)
        self.arrive(tensor, zs, 2 + half)
        if SHARED[tensor]:
            self.start(tensor, zs, 8 + half)
        elif half:
            self.start(tensor, zs, 7)

    def p4(self, tensor, k):
        if SHARED[tensor]:
            zs = self.plane(tensor, k)
            self.arrive(tensor, zs, 8, 9)
            self.start(tensor, zs, 7)

    def p5(self, tensor, k):
        self.arrive(tensor, self.plane(tensor, k), 4, 5, 6, 7)

    def plane_sent(self, tensor, k):
        for kind in range(10 if SHARED[tensor] else 8):
            self.gcopy(tensor, self.plane(tensor, k), kind).wait_send()

    def z_sent(self, tensor, zs):
        for up in (0, 1):
            @pl.when((zs <= self.z if up else zs >= self.z) & self.inner(up))
            def _(up=up):
                self.zcopy(tensor, zs, up).wait_send()

    def credit(self, which):
        for k in ((0,), (1, 2, 3))[which]:
            self.plane_sent(2, k)
            self.z_sent(2, k)
        pl.semaphore_signal(
            self.free.at[which], inc=1, device_id=self.dev(fc=1), device_id_type=MESH)

    def enter(self, i):
        src = (self.sh_s_hbm, self.sh_c_hbm, self.sh_f_hbm, self.x_hbm, self.mem_hbm, self.g_hbm)
        dst = (self.sh_s, self.sh_c, self.sh_f, self.x_in, self.mem, self.g)
        return pltpu.make_async_copy(src[i], dst[i], self.isem.at[i])

    def leave(self, i, part=None):
        if part is not None:
            rows = slice(128 * part, 128 * part + 128)
            return pltpu.make_async_copy(
                self.mgrad.at[rows, :], self.mgrad_hbm.at[rows, :], self.osem.at[i])
        src = (self.block, self.xgrad, None, self.gs, self.gc, self.gf)[i]
        dst = (self.block_hbm, self.xgrad_hbm, None, self.gs_hbm, self.gc_hbm, self.gf_hbm)[i]
        return pltpu.make_async_copy(src, dst, self.osem.at[i])

    def own_square(self, tensor):
        src, dst = ((self.sh_s, self.ws), (self.sh_c, self.wc))[tensor]
        self.enter(tensor).wait()
        self.flat[0:576, :] = src[...].astype(F32)
        row = al(self.shard * AR, 16)
        for t in range(6):
            dst[pl.ds(row, AR), 128 * t:128 * t + 128] = self.flat[
                pl.ds(t, AR, stride=6), :].astype(BF)

    def own_ff(self):
        self.enter(2).wait()
        self.flat[0:1152, :] = self.sh_f[...].astype(F32)
        base = self.shard * FU
        flat, wf = self.flat, self.wf

        def wide(rows):
            for u in range(4):
                for w in range(2):
                    top = flat[pl.ds(4 * u + w, rows, stride=16), :]
                    low = flat[pl.ds(4 * u + w + 2, rows, stride=16), :]
                    wf[pl.ds(al(base + 2 * rows * u, 16), 2 * rows), 128 * w:128 * w + 128] = (
                        jnp.concatenate([top, low], axis=0).astype(BF))

        def tall(first, rows, offset):
            for t in range(6):
                wf[pl.ds(al(base + offset + rows * (t // 2), 16), rows),
                   128 * (t % 2):128 * (t % 2) + 128] = flat[
                       pl.ds(first + t, rows, stride=6), :].astype(BF)

        @pl.when(self.shard < 21)
        def _():
            wide(72)

        @pl.when(self.shard == 21)
        def _():
            wide(24)
            tall(384, 128, 192)

        @pl.when(self.shard > 21)
        def _():
            tall(0, 192, 0)

    def build_wide(self, ch):
        rows1 = 24 if ch == 10 else 72

        def step(u, _):
            low = self.wf[pl.ds(al(1152 * ch + 144 * u, 16), 144), :].astype(F32)
            high = self.wf[
                pl.ds(al(1152 * ch + FU + 2 * rows1 * u, 16), 2 * rows1), :].astype(F32)
            for w in range(2):
                value = jnp.concatenate(
                    [low[72 * w:72 * w + 72], high[rows1 * w:rows1 * w + rows1]], axis=0)
                self.wgu[144 * ch:144 * ch + 72 + rows1,
                         pl.ds(al(512 * u + 256 * w, 256), 256)] = value.astype(BF)
            return 0

        lax.fori_loop(0, 4, step, 0)

    def build_tall(self, s):
        first, rows, offset = (0, 128, 192) if s == 21 else (192 * s - 4096, 192, 0)
        for p in range(3):
            self.wd[first:first + rows, 256 * p:256 * p + 256] = self.wf[
                FU * s + offset + rows * p:FU * s + offset + rows * p + rows, :]

    def build_plane(self, zs):
        if zs < 2:
            for ch in range(4 * zs, 4 * zs + 4):
                self.build_wide(ch)
        elif zs == 2:
            for ch in (8, 9, 10):
                self.build_wide(ch)
            for s in (21, 22, 23):
                self.build_tall(s)
        else:
            for s in range(24, 32):
                self.build_tall(s)

    def masks(self):
        lane = lax.broadcasted_iota(jnp.int32, (128, 128), 1)
        self.left = lane < DH

    def stack(self, pair):
        zero = jnp.zeros_like(pair)
        return jnp.concatenate(
            [jnp.where(self.left, pair, zero), jnp.where(self.left, zero, pair)], axis=0)

    def unstack(self, both):
        rows = both.shape[0] // 2
        return jnp.where(self.left, both[0:rows], both[rows:])

    def bias(self):
        lane = lax.broadcasted_iota(jnp.int32, (1, 128), 1)
        bucket = bucket_of((128 - lane) % 128)
        for h in range(H):
            row = jnp.zeros((1, 128), F32)
            for b in range(NB):
                row = jnp.where(bucket == b, self.table[h, b], row)
            full = jnp.broadcast_to(row, (128, 128))
            self.ps[128 * h:128 * h + 128, :] = pltpu.roll(
                full, 0, 1, stride=1, stride_axis=0)

    def project(self, left, ref, row, out):
        for p in range(3):
            out[:, 256 * p:256 * p + 256] = nn(
                left, ref[row:row + D, 256 * p:256 * p + 256]).astype(BF)

    def add_product(self, left, ref, row, base, out):
        for p in range(3):
            cols = slice(256 * p, 256 * p + 256)
            out[:, cols] = base[:, cols].astype(F32) + nn(left, ref[row:row + D, cols])

    def heads(self, p):
        return pl.ds(al(p * 256, 256), 256)

    def self_forward(self):
        for i in (3, 4, 5):
            self.enter(i).wait()
        x = self.x_in[...].astype(F32)
        self.n1[...] = rms(x, self.gains[0:1, :]).astype(BF)
        n1 = self.n1[...]
        for m, out in enumerate((self.q, self.k, self.v)):
            self.project(n1, self.ws, D * m, out)
        length = self.dl[0]
        row = lax.broadcasted_iota(jnp.int32, (256, 128), 0) % 128
        col = lax.broadcasted_iota(jnp.int32, (256, 128), 1)
        keep = (col <= row) & (col < length)

        def pair(p, _):
            cols = pl.ds(al(p * 128, 128), 128)
            s = nt(self.stack(self.q[:, cols]), self.k[:, cols]) + self.ps[self.heads(p), :]
            s = jnp.where(keep, s, MASKED)
            e = jnp.exp(s - jnp.max(s, axis=-1, keepdims=True))
            prob = e / jnp.sum(e, axis=-1, keepdims=True)
            self.ps[self.heads(p), :] = prob
            self.mix[:, cols] = self.unstack(nn(prob.astype(BF), self.v[:, cols])).astype(BF)
            return 0

        lax.fori_loop(0, PAIRS, pair, 0)
        self.add_product(self.mix[...], self.ws, 3 * D, self.x_in, self.r1)
        self.n2[...] = rms(self.r1[...], self.gains[1:2, :]).astype(BF)

    def cross_kv(self, m):
        out = (self.ck, self.cv)[m - 1]
        for i in range(4):
            for p in range(3):
                out[128 * i:128 * i + 128, 256 * p:256 * p + 256] = nn(
                    self.mem[128 * i:128 * i + 128, :],
                    self.wc[D * m:D * m + D, 256 * p:256 * p + 256]).astype(BF)

    def cross_probs(self, p):
        cols = pl.ds(al(p * 128, 128), 128)
        col = lax.broadcasted_iota(jnp.int32, (256, self.mem.shape[0]), 1)
        s = nt(self.stack(self.cq[:, cols]), self.ck[:, cols])
        s = jnp.where(col < self.ml[0], s, MASKED)
        e = jnp.exp(s - jnp.max(s, axis=-1, keepdims=True))
        return e / jnp.sum(e, axis=-1, keepdims=True)

    def cross_forward(self, part):
        if part == 0:
            self.project(self.n2[...], self.wc, 0, self.cq)

        def pair(p, _):
            cols = pl.ds(al(p * 128, 128), 128)
            prob = self.cross_probs(p)
            self.cmix[:, cols] = self.unstack(nn(prob.astype(BF), self.cv[:, cols])).astype(BF)
            return 0

        lax.fori_loop(2 * part, 2 * part + 2, pair, 0)
        if part == 2:
            self.add_product(self.cmix[...], self.wc, 3 * D, self.r1, self.r2)
            self.n3[...] = rms(self.r2[...], self.gains[2:3, :]).astype(BF)

    def ff_gate(self):
        n3 = self.n3[...]
        c0 = float(np.sqrt(2.0 / np.pi))

        def chunk(i, _):
            cols = pl.ds(al(i * 256, 256), 256)
            a = nn(n3, self.wgu[0:D, cols])
            sq = a * a
            t = jnp.tanh(c0 * (a + 0.044715 * a * sq))
            self.ga[:, cols] = 0.5 * a * (1.0 + t)
            self.ub[:, cols] = 0.5 * (1.0 + t) + 0.5 * a * (1.0 - t * t) * (
                c0 * (1.0 + 0.134145 * sq))
            return 0

        lax.fori_loop(0, FF // 256, chunk, 0)

    def ff_up(self):
        n3 = self.n3[...]

        def chunk(i, _):
            cols = pl.ds(al(i * 256, 256), 256)
            up = nn(n3, self.wgu[D:2 * D, cols])
            self.ub[:, cols] = up * self.ub[:, cols]
            self.hid[:, cols] = (self.ga[:, cols] * up).astype(BF)
            return 0

        lax.fori_loop(0, FF // 256, chunk, 0)
        self.hidt[...] = self.hid[...].T

    def out_rows(self):
        hid = self.hid[...]
        for p in range(3):
            cols = slice(256 * p, 256 * p + 256)
            self.block[:, cols] = (self.r2[:, cols] + nn(hid, self.wd[:, cols])).astype(BF)
        self.leave(0).start()

    def d_hidden(self, part):
        g = self.g[...]

        def chunk(i, _):
            at = al(i * 256, 256)
            cols = pl.ds(at, 256)
            dh = nt(g, self.wd[pl.ds(at, 256), :]).astype(BF).astype(F32)
            self.dg[:, cols] = (dh * self.ub[:, cols]).astype(BF)
            self.du[:, cols] = (dh * self.ga[:, cols]).astype(BF)
            return 0

        lax.fori_loop(4 * part, 4 * part + 4, chunk, 0)

    def place(self, g):
        own = OWN[g]
        out = OWN_ROWS + (g % 2) * STAGE
        return own + self.c * (out - own), out + self.c * (own - out)

    def grad_tall(self, g, i):
        b0, b1 = self.place(g)
        for p in range(3):
            both = nn(
                self.hidt[pl.ds(al(512 + 384 * i, 16), 384), :],
                self.g[:, 256 * p:256 * p + 256])
            self.gb[pl.ds(al(b0 + FU * i + 192 * p, 16), 192), :] = both[0:192].astype(BF)
            self.gb[pl.ds(al(b1 + FU * i + 192 * p, 16), 192), :] = both[192:].astype(BF)

    def grad_tall_part(self, base, i, first, rows, offset):
        for p in range(3):
            value = nn(self.hidt[first:first + rows, :], self.g[:, 256 * p:256 * p + 256])
            self.gb[pl.ds(al(base + FU * i + offset + rows * p, 16), rows), :] = value.astype(BF)

    def grad_wide(self, g, ch, i):
        b0, b1 = self.place(g)
        rows1 = 24 if ch == 10 else 72
        first, end = 144 * ch, 144 * ch + 72 + rows1

        def step(u, _):
            cols = pl.ds(al(512 * u, 512), 512)
            parts = []
            if first < D:
                parts.append(nn(self.n3t[first:min(end, D), :], self.dg[:, cols]))
            if end > D:
                parts.append(nn(self.n3t[max(first, D) - D:end - D, :], self.du[:, cols]))
            both = parts[0] if len(parts) == 1 else jnp.concatenate(parts, axis=0)
            for base, at, rows in ((b0, 0, 72), (b1, 72, rows1)):
                value = jnp.concatenate(
                    [both[at:at + rows, 0:256], both[at:at + rows, 256:512]], axis=0)
                self.gb[pl.ds(al(base + FU * i + 2 * rows * u, 16), 2 * rows), :] = (
                    value.astype(BF))
            return 0

        lax.fori_loop(0, 4, step, 0)

    def grad_ff(self, g):
        zb = GROUPS[g][1]
        if zb == 2:
            b0, b1 = self.place(g)
            for i in range(3):
                self.grad_wide(g, 8 + i, i)
            self.grad_tall_part(b1, 2, 0, 128, 192)
            self.grad_tall_part(b0, 3, 128, 192, 0)
            self.grad_tall_part(b1, 3, 320, 192, 0)
        else:
            for i in range(4):
                self.grad_wide(g, 4 * zb + i, i)

    def grad_square(self, g, i):
        t, zb = GROUPS[g]
        left = self.memt if t == 1 and zb in (1, 2) else self.tt
        right = ((self.q, self.k, self.v, self.drb), (self.cq, self.ck, self.cv, self.drb))[t][zb]
        b0, b1 = self.place(g)
        rows = left[pl.ds(al(192 * i, 16), 192), :]
        for p in range(3):
            both = nn(rows, right[:, 256 * p:256 * p + 256])
            self.gb[pl.ds(al(b0 + AU * i + 96 * p, 16), 96), :] = both[0:96].astype(BF)
            self.gb[pl.ds(al(b1 + AU * i + 96 * p, 16), 96), :] = both[96:].astype(BF)

    def turn(self, g):
        if g == 1:
            self.n3t[...] = self.n3[...].T
        elif g == 5:
            self.memt[...] = self.mem[...].T
        elif g in (4, 7, 8, 9):
            left = {4: self.cmix, 7: self.n2, 8: self.mix, 9: self.n1}[g]
            self.tt[...] = left[...].T

    def back_product(self, terms, out):
        for p in range(3):
            total = None
            for d_ref, w_ref, row, width in terms:
                value = nt(d_ref[...], w_ref[row + 256 * p:row + 256 * p + 256, 0:width])
                total = value if total is None else total + value
            out[:, 256 * p:256 * p + 256] = total

    def norm_three_back(self):
        self.back_product(((self.dg, self.wgu, 0, FF), (self.du, self.wgu, D, FF)), self.dz)
        dv, dg = rms_back(self.r2[...], self.gains[2:3, :], self.dz[...])
        self.redg[0, 2:3, :] = dg
        self.dr[...] = self.g[...].astype(F32) + dv
        self.drb[...] = self.dr[...].astype(BF)

    def cross_back(self, part):
        for p in range(3) if part == 0 else ():
            self.dm[:, 256 * p:256 * p + 256] = nt(
                self.drb[...], self.wc[3 * D + 256 * p:3 * D + 256 * p + 256, :]).astype(BF)

        def pair(p, _):
            cols = pl.ds(al(p * 128, 128), 128)
            dms = self.stack(self.dm[:, cols])
            kp = self.ck[:, cols]
            qs = self.stack(self.cq[:, cols])
            prob = self.cross_probs(p)
            dp = nt(dms, self.cv[:, cols])
            ds = (prob * (dp - jnp.sum(prob * dp, axis=-1, keepdims=True))).astype(BF)
            self.cv[:, cols] = tn(prob.astype(BF), dms).astype(BF)
            self.cq[:, cols] = self.unstack(nn(ds, kp)).astype(BF)
            self.ck[:, cols] = tn(ds, qs).astype(BF)
            return 0

        lax.fori_loop(2 * part, 2 * part + 2, pair, 0)

    def memory_rows(self, i):
        rows = slice(128 * i, 128 * i + 128)
        for p in range(3):
            wrow = 256 * p
            self.mgrad[rows, 256 * p:256 * p + 256] = (
                nt(self.ck[rows, :], self.wc[D + wrow:D + wrow + 256, :])
                + nt(self.cv[rows, :], self.wc[2 * D + wrow:2 * D + wrow + 256, :])
            ).astype(BF)
        self.leave(6 + i, i).start()

    def norm_two_back(self):
        self.back_product(((self.cq, self.wc, 0, D),), self.dz)
        dv, dg = rms_back(self.r1[...], self.gains[1:2, :], self.dz[...])
        self.redg[0, 1:2, :] = dg
        self.dr[...] = self.dr[...] + dv
        self.drb[...] = self.dr[...].astype(BF)

    def self_back(self, part):
        for p in range(3) if part == 0 else ():
            self.dm[:, 256 * p:256 * p + 256] = nt(
                self.drb[...], self.ws[3 * D + 256 * p:3 * D + 256 * p + 256, :]).astype(BF)

        def pair(p, _):
            cols = pl.ds(al(p * 128, 128), 128)
            dms = self.stack(self.dm[:, cols])
            kp = self.k[:, cols]
            qs = self.stack(self.q[:, cols])
            prob = self.ps[self.heads(p), :]
            dp = nt(dms, self.v[:, cols])
            ds = (prob * (dp - jnp.sum(prob * dp, axis=-1, keepdims=True))).astype(BF)
            self.ps[self.heads(p), :] = ds.astype(F32)
            self.v[:, cols] = tn(prob.astype(BF), dms).astype(BF)
            self.q[:, cols] = self.unstack(nn(ds, kp)).astype(BF)
            self.k[:, cols] = tn(ds, qs).astype(BF)
            return 0

        lax.fori_loop(3 * part, 3 * part + 3, pair, 0)

    def norm_one_back(self):
        self.back_product(
            ((self.q, self.ws, 0, D), (self.k, self.ws, D, D), (self.v, self.ws, 2 * D, D)),
            self.dz)
        dv, dg = rms_back(self.x_in[...].astype(F32), self.gains[0:1, :], self.dz[...])
        self.redg[0, 0:1, :] = dg
        self.xgrad[...] = (self.dr[...] + dv).astype(BF)
        self.leave(1).start()

    def table_back(self):
        row = lax.broadcasted_iota(jnp.int32, (128, 128), 0)
        col = lax.broadcasted_iota(jnp.int32, (128, 128), 1)
        flip = jnp.where(row + col == 127, 1.0, 0.0).astype(BF)
        self.diag[...] = jnp.zeros_like(self.diag)
        for p in range(PAIRS):
            back = nn(self.ps[256 * p:256 * p + 256, :].astype(BF), flip)
            for hh in range(2):
                turned = pltpu.roll(
                    back[128 * hh:128 * hh + 128], 0, 1, stride=1, stride_axis=0)
                self.diag[2 * p + hh:2 * p + hh + 1, :] = jnp.sum(turned, axis=0, keepdims=True)
        lane = lax.broadcasted_iota(jnp.int32, (NB, 128), 1)
        hot = jnp.where(
            bucket_of((lane + 1) % 128) == lax.broadcasted_iota(jnp.int32, (NB, 128), 0), 1.0, 0.0)
        self.redt[0, :, 0:NB] = lax.dot_general(
            self.diag[...], hot, (((1,), (1,)), ((), ())),
            precision=lax.Precision.HIGHEST, preferred_element_type=F32)

    def own(self, g, chip, half=None):
        unit = UNIT[g]
        start = OWN[g] + chip * unit
        if half is not None:
            unit = unit // 2
            start = start + half * unit
        return pl.ds(al(start, 16), unit)

    def land(self, g, which, half=None):
        unit = UNIT[g]
        start = LAND[g] + (0, unit // 2, unit, 2 * unit)[which]
        rows = unit // 2 if which < 2 else unit
        if half is not None:
            rows = unit // 2
            start = start + half * rows
        return pl.ds(start, rows)

    def lanes(self, g, mine):
        if not PAIR[g]:
            return slice(None)
        par = self.z % 2
        return pl.ds(al((par if mine else 1 - par) * 128, 128), 128)

    def scopy(self, g, kind):
        gb, lb = self.gb, self.lb
        row = g * 15 + kind
        sems = self.rsend.at[row], self.rrecv.at[row]
        if kind in SIB:
            unit = UNIT[g]
            at = self.chip(*ROLES[SIB.index(kind)]) * unit
            return self.copy(
                gb.at[pl.ds(al(OWN_ROWS + (g % 2) * STAGE + at, 16), unit), :],
                self.wf.at[pl.ds(al(OWN[g] + at, 16), unit), :], *sems, self.dev(fc=1))
        spot, half, lanes, where, dev = {
            1: ((1, 1), 0, True, 0, (1, 0)),
            2: ((1, 1), 1, True, 1, (0, 1)),
            3: ((1, 0), 0, None, 2, (1, 0)),
            4: ((1, 0), 1, True, 2, (1, 0)),
            5: ((1, 0), 1, False, 2, (1, 0)),
            6: ((0, 1), 1, None, 3, (0, 1)),
            7: ((0, 1), 0, True, 3, (0, 1)),
            8: ((0, 1), 0, False, 3, (0, 1)),
            9: ((1, 1), 0, False, 0, None),
            10: ((1, 1), 1, False, 1, None),
        }[kind]
        src = self.own(g, self.chip(*spot), half)
        dst = self.land(g, where, half if where > 1 else None)
        lanes = slice(None) if lanes is None else self.lanes(g, lanes)
        put = self.lanes(g, True) if dev is None else lanes
        dev = self.dev(z=self.z + 1 - 2 * (self.z % 2)) if dev is None else self.dev(None, *dev)
        return self.copy(gb.at[src, lanes], lb.at[dst, put], *sems, dev)

    def came(self, g, *kinds):
        for kind in kinds:
            if kind in (9, 10):
                part = self.lb.at[self.land(g, kind - 9), self.lanes(g, False)]
                row = g * 15 + kind
                self.copy(
                    part, part, self.rsend.at[row], self.rrecv.at[row],
                    self.dev(fc=1)).wait_recv()
            else:
                self.scopy(g, kind).wait_recv()

    def go(self, g, *kinds):
        for kind in kinds:
            self.scopy(g, kind).start()

    def to_owner(self, g, slot=None):
        t, zb = GROUPS[g]
        unit = UNIT[g]
        if slot is None:
            slot = (self.z + 3 - zb) % 4
        return self.copy(
            self.gb.at[self.own(g, self.chip()), :],
            self.zb.at[pl.ds(al(ZBASE[t] + slot * unit, 16), unit), :],
            self.rsend.at[g * 15 + 11], self.orecv.at[t * 3 + slot], self.dev(z=zb))

    def ready(self, g):
        self.turn(g)
        if g >= 2:
            for role in range(4):
                self.scopy(g - 2, SIB[role]).wait_send()

    def allowed(self, g):
        if g in (0, 2):
            pl.semaphore_wait(self.free.at[g // 2], 1)

    def part(self, g, i):
        (self.grad_tall if g == 0 else self.grad_square)(g, i)

    def grad(self, g):
        self.ready(g)
        if 0 < g < 4:
            self.grad_ff(g)
        else:
            def step(i, _):
                self.part(g, i)
                return 0
            lax.fori_loop(0, 4, step, 0)
        self.allowed(g)
        self.go(g, *SIB)

    def grad_role(self, g, role):
        if role == 0:
            self.ready(g)
        self.part(g, self.chip(*ROLES[role]))
        if role == 0:
            self.allowed(g)
        self.go(g, SIB[role])

    def accumulate(self, dst, lanes, src_ref, src, from_lanes):
        self.gb[dst, lanes] = (
            self.gb[dst, lanes].astype(F32) + src_ref[src, from_lanes].astype(F32)).astype(BF)

    def rs1(self, g, role):
        self.came(g, SIB[role])
        rows = self.own(g, self.chip(*ROLES[role]))
        self.accumulate(rows, slice(None), self.wf, rows, slice(None))
        self.go(g, *(((9, 10), (3, 5), (6, 8), ()) if PAIR[g] else ((1, 2), (3,), (6,), ()))[role])

    def rs2(self, g, half):
        if PAIR[g]:
            self.came(g, 9 + half)
            self.accumulate(
                self.own(g, self.chip(1, 1), half), self.lanes(g, True),
                self.lb, self.land(g, half), self.lanes(g, False))
            self.go(g, 1 + half)

    def rs3(self, g, half):
        kind, spot, late = ((1, (0, 1), 7), (2, (1, 0), 4))[half]
        self.came(g, kind)
        self.accumulate(
            self.own(g, self.chip(*spot), half), self.lanes(g, True),
            self.lb, self.land(g, kind - 1), self.lanes(g, True))
        self.go(g, late)

    def rs4(self, g):
        self.came(g, *((3, 5, 6, 8, 4, 7) if PAIR[g] else (3, 6, 4, 7)))
        rows = self.own(g, self.chip())
        self.gb[rows, :] = (
            self.gb[rows, :].astype(F32) + self.lb[self.land(g, 2), :].astype(F32)
            + self.lb[self.land(g, 3), :].astype(F32)).astype(BF)

        @pl.when(self.z != GROUPS[g][1])
        def _():
            self.to_owner(g).start()

    def rs5(self, g):
        t, zb = GROUPS[g]
        unit = UNIT[g]

        @pl.when(self.z == zb)
        def _():
            for slot in range(3):
                self.to_owner(g, slot).wait_recv()

            def total(start, size, lanes):
                at = pl.ds(al(OWN[g] + self.chip() * unit + start, 16), size)
                value = self.gb[at, lanes].astype(F32)
                for slot in range(3):
                    value = value + self.zb[
                        pl.ds(ZBASE[t] + slot * unit + start, size), lanes].astype(F32)
                return value

            if t < 2:
                out = (self.gs, self.gc)[t]
                for k in range(6):
                    out[pl.ds(k, AR, stride=6), :] = total(
                        96 * (k // 2), 96, slice(128 * (k % 2), 128 * (k % 2) + 128))
                self.leave(3 + t).start()
                return
            out = self.gf

            def wide(rows):
                for u in range(4):
                    for w in range(2):
                        v = total(2 * rows * u, 2 * rows, slice(128 * w, 128 * w + 128))
                        out[pl.ds(4 * u + w, rows, stride=16), :] = v[0:rows]
                        out[pl.ds(4 * u + w + 2, rows, stride=16), :] = v[rows:]

            def tall(first, rows, offset):
                for k in range(6):
                    out[pl.ds(first + k, rows, stride=6), :] = total(
                        offset + rows * (k // 2), rows, slice(128 * (k % 2), 128 * (k % 2) + 128))

            if zb < 2:
                wide(72)
            elif zb == 3:
                tall(0, 192, 0)
            else:
                @pl.when(self.shard < 21)
                def _():
                    wide(72)

                @pl.when(self.shard == 21)
                def _():
                    wide(24)
                    tall(384, 128, 192)

                @pl.when(self.shard > 21)
                def _():
                    tall(0, 192, 0)

            self.leave(5).start()

    def group_sent(self, g):
        for kind in range(1, 11):
            if PAIR[g] or kind not in (5, 8, 9, 10):
                self.scopy(g, kind).wait_send()

        @pl.when(self.z != GROUPS[g][1])
        def _():
            self.to_owner(g).wait_send()

    def small(self, step, which):
        dev = (
            self.dev(fc=1), self.dev(fx=1), self.dev(fy=1),
            self.dev(z=self.z + 1 - 2 * (self.z % 2)), self.dev(z=(self.z + 2) % 4),
        )[step]
        src, dst = ((self.redg, self.landg), (self.redt, self.landt))[which]
        row = step * 2 + which
        return self.copy(
            src.at[step], dst.at[step], self.ssend.at[row], self.srecv.at[row], dev)

    def small_start(self, step):
        for which in range(2):
            self.small(step, which).start()

    def small_add(self, step):
        for which in range(2):
            self.small(step, which).wait_recv()
        self.redg[step + 1] = self.redg[step] + self.landg[step]
        self.redt[step + 1] = self.redt[step] + self.landt[step]


    def finish(self):
        for tensor in (0, 1):
            for k in range(4):
                self.plane_sent(tensor, k)
                self.z_sent(tensor, k)
        for g in range(12):
            self.group_sent(g)
        for g in (10, 11):
            for role in range(4):
                self.scopy(g, SIB[role]).wait_send()
        for i in (0, 1, 3, 4, 5):
            self.leave(i).wait()
        for i in range(4):
            self.leave(6 + i, i).wait()
        self.ggain[...] = self.redga[5, 0:3, :]
        self.gtable[...] = self.redta[5, 0:H, 0:NB]
        for step in range(5):
            for which in range(2):
                self.small(step, which).wait_send()


K = Layer
SCHEDULE = (
    (K.own_xy, 0), (K.own_z, 0, 0), (K.own_z, 0, 1), (K.own_square, 1), (K.own_z, 1, 0),
    (K.own_ff,), (K.own_xy, 1), (K.own_z, 1, 1), (K.p2x, 0, 0), (K.p1, 0, 1), (K.p1, 0, 2),
    (K.p1, 1, 2), (K.p2y, 0, 0), (K.own_z, 2, 1), (K.p1, 1, 1), (K.p2y, 1, 0), (K.own_z, 2, 0),
    (K.p2x, 0, 2), (K.p2x, 0, 1), (K.p2x, 1, 0), (K.p2y, 0, 1), (K.p1, 0, 3), (K.p1, 1, 3),
    (K.p1, 2, 2), (K.p3, 1, 0, 0), (K.p2y, 1, 1), (K.p2x, 1, 1), (K.p1, 2, 1), (K.p3, 1, 0, 1),
    (K.p2y, 0, 2), (K.p3, 0, 0, 0), (K.p3, 0, 0, 1), (K.p2y, 1, 2), (K.p2x, 1, 2), (K.p1, 2, 0),
    (K.p3, 0, 1, 0), (K.p3, 1, 1, 0), (K.p3, 1, 1, 1), (K.p2y, 0, 3), (K.p3, 0, 1, 1),
    (K.p4, 0, 1), (K.p2y, 1, 3), (K.p2x, 0, 3), (K.p2y, 2, 2), (K.p2x, 2, 2), (K.p2x, 2, 1),
    (K.p2x, 1, 3), (K.p5, 0, 1), (K.p2y, 2, 1), (K.p3, 0, 2, 0), (K.p3, 0, 2, 1),
    (K.p3, 1, 2, 0), (K.p3, 1, 2, 1), (K.p1, 2, 3), (K.p3, 0, 3, 0), (K.p4, 0, 2),
    (K.p3, 0, 3, 1), (K.p3, 2, 2, 0), (K.p4, 0, 0), (K.p2x, 2, 0), (K.p2y, 2, 0), (K.p4, 1, 0),
    (K.p3, 1, 3, 0), (K.p5, 0, 2), (K.bias,), (K.p4, 0, 3), (K.p3, 1, 3, 1), (K.p4, 1, 2),
    (K.p5, 0, 0), (K.p3, 2, 1, 0), (K.p3, 2, 1, 1), (K.p3, 2, 2, 1), (K.p4, 1, 1), (K.p5, 1, 0),
    (K.p5, 0, 3), (K.p5, 1, 1), (K.self_forward,), (K.p4, 1, 3), (K.p3, 2, 0, 0), (K.p5, 1, 2),
    (K.p2x, 2, 3), (K.p2y, 2, 3), (K.p3, 2, 0, 1), (K.p4, 2, 1), (K.p5, 1, 3), (K.cross_kv, 2),
    (K.cross_kv, 1), (K.p4, 2, 2), (K.cross_forward, 0), (K.p5, 2, 1), (K.p3, 2, 3, 0),
    (K.cross_forward, 1), (K.p5, 2, 2), (K.build_plane, 1), (K.p3, 2, 3, 1), (K.p4, 2, 0),
    (K.cross_forward, 2), (K.build_plane, 2), (K.p5, 2, 0), (K.build_plane, 0), (K.ff_gate,),
    (K.ff_up,), (K.credit, 0), (K.p4, 2, 3), (K.grad_role, 0, 0), (K.grad_role, 0, 1),
    (K.grad_role, 0, 2), (K.grad_role, 0, 3), (K.p5, 2, 3), (K.rs1, 0, 0), (K.build_plane, 3),
    (K.d_hidden, 0), (K.rs1, 0, 2), (K.rs1, 0, 1), (K.d_hidden, 1), (K.grad, 1), (K.credit, 1),
    (K.rs2, 0, 1), (K.rs2, 0, 0), (K.grad, 2), (K.rs1, 1, 2), (K.rs1, 1, 1), (K.rs1, 1, 0),
    (K.grad, 3), (K.rs1, 2, 2), (K.rs1, 2, 0), (K.rs1, 2, 1), (K.norm_three_back,),
    (K.grad_role, 4, 0), (K.cross_back, 0), (K.rs2, 1, 1), (K.rs2, 1, 0), (K.rs2, 2, 0),
    (K.rs2, 2, 1), (K.rs3, 0, 1), (K.rs1, 1, 3), (K.rs1, 4, 0), (K.rs3, 0, 0),
    (K.grad_role, 4, 1), (K.cross_back, 1), (K.rs1, 3, 0), (K.cross_back, 2),
    (K.grad_role, 4, 2), (K.rs3, 2, 0), (K.grad_role, 4, 3), (K.rs3, 2, 1), (K.rs1, 3, 2),
    (K.rs1, 0, 3), (K.rs1, 2, 3), (K.rs1, 3, 1), (K.rs2, 3, 0), (K.rs3, 1, 1), (K.grad, 5),
    (K.rs3, 1, 0), (K.rs2, 3, 1), (K.rs4, 0), (K.grad, 6), (K.rs4, 2), (K.grad, 7),
    (K.rs1, 4, 2), (K.norm_two_back,), (K.rs1, 5, 0), (K.rs1, 4, 3), (K.grad, 8), (K.rs1, 6, 0),
    (K.self_back, 0), (K.rs3, 3, 0), (K.rs1, 8, 0), (K.rs1, 4, 1), (K.self_back, 1),
    (K.rs3, 3, 1), (K.grad_role, 9, 0), (K.grad_role, 9, 1), (K.rs2, 8, 0), (K.rs4, 1),
    (K.grad_role, 9, 2), (K.rs2, 4, 0), (K.grad_role, 9, 3), (K.rs2, 6, 0), (K.rs1, 7, 0),
    (K.table_back,), (K.rs2, 7, 0), (K.rs1, 8, 3), (K.rs3, 4, 0), (K.rs2, 7, 1), (K.rs2, 4, 1),
    (K.grad_role, 10, 0), (K.grad_role, 10, 1), (K.grad_role, 10, 2), (K.grad_role, 10, 3),
    (K.rs1, 8, 1), (K.rs1, 8, 2), (K.norm_one_back,), (K.rs1, 3, 3), (K.grad_role, 11, 0),
    (K.rs1, 10, 0), (K.rs2, 8, 1), (K.small_start, 0), (K.rs2, 6, 1), (K.rs4, 3),
    (K.small_add, 0), (K.small_start, 1), (K.rs3, 8, 1), (K.grad_role, 11, 1),
    (K.grad_role, 11, 2), (K.memory_rows, 0), (K.rs1, 11, 0), (K.rs2, 11, 1), (K.rs2, 11, 0),
    (K.rs3, 4, 1), (K.small_add, 1), (K.small_start, 2), (K.rs1, 9, 3), (K.rs3, 8, 0),
    (K.memory_rows, 3), (K.rs2, 10, 0), (K.out_rows,), (K.grad_role, 11, 3), (K.rs1, 11, 2),
    (K.rs1, 7, 1), (K.rs5, 2), (K.rs1, 7, 3), (K.rs3, 11, 0), (K.rs1, 6, 2), (K.rs1, 9, 2),
    (K.rs1, 7, 2), (K.rs1, 10, 2), (K.small_add, 2), (K.rs2, 10, 1), (K.small_start, 3),
    (K.rs1, 11, 1), (K.rs4, 8), (K.rs3, 7, 0), (K.rs3, 11, 1), (K.rs1, 11, 3),
    (K.memory_rows, 2), (K.rs3, 7, 1), (K.rs4, 4), (K.rs3, 10, 0), (K.rs1, 9, 0), (K.rs1, 6, 3),
    (K.rs3, 6, 0), (K.rs1, 10, 1), (K.rs4, 11), (K.rs1, 9, 1), (K.rs3, 10, 1), (K.rs1, 10, 3),
    (K.rs2, 9, 0), (K.rs1, 6, 1), (K.memory_rows, 1), (K.rs3, 9, 0), (K.rs3, 6, 1),
    (K.rs2, 9, 1), (K.rs5, 1), (K.small_add, 3), (K.rs4, 7), (K.rs1, 5, 3), (K.rs4, 10),
    (K.rs3, 9, 1), (K.rs1, 5, 2), (K.rs5, 0), (K.rs1, 5, 1), (K.rs4, 6), (K.small_start, 4),
    (K.rs5, 8), (K.rs5, 10), (K.rs2, 5, 1), (K.rs3, 5, 1), (K.rs4, 9), (K.rs2, 5, 0),
    (K.rs3, 5, 0), (K.rs5, 7), (K.rs4, 5), (K.rs5, 9), (K.rs5, 6), (K.rs5, 3), (K.small_add, 4),
    (K.rs5, 5), (K.rs5, 11), (K.rs5, 4),
)

NAMES = (
    "x_hbm", "mem_hbm", "g_hbm", "dl", "ml", "sh_s_hbm", "sh_c_hbm", "sh_f_hbm", "gains", "table",
    "block_hbm", "xgrad_hbm", "mgrad_hbm", "gs_hbm", "gc_hbm", "gf_hbm", "ggain", "gtable",
    "x_in", "mem", "g", "sh_s", "sh_c", "sh_f", "block", "xgrad", "mgrad", "gs", "gc", "gf",
    "isem", "osem",
    "ws", "wc", "wf", "wgu", "wd", "gb", "lb", "zb",
    "n1", "q", "k", "v", "mix", "r1", "n2", "cq", "ck", "cv", "cmix", "r2", "n3",
    "ga", "ub", "hid", "hidt", "n3t", "dg", "du", "dz", "dr", "drb", "tt", "memt",
    "ps", "diag", "redga", "redta", "landg", "landt",
    "gsend", "grecv", "zsend", "zrecv", "rsend", "rrecv", "orecv", "ssend", "srecv", "free",
)


def kernel(*args):
    st = Layer(dict(zip(NAMES, args)))
    st.redg, st.redt = st.redga, st.redta
    barrier = pltpu.get_barrier_semaphore()
    others = [st.dev(fc=1), st.dev(fx=1), st.dev(fy=1)] + [
        st.dev(z=(st.z + k) % 4) for k in (1, 2, 3)]
    for other in others:
        pl.semaphore_signal(barrier, inc=1, device_id=other, device_id_type=MESH)
    for i in range(6):
        st.enter(i).start()
    st.own_square(0)
    st.masks()
    pl.semaphore_wait(barrier, 6)
    for step, *numbers in SCHEDULE:
        step(st, *numbers)
    st.finish()


def settle_kernel(count, *refs):
    src, dst, held = refs[:count], refs[count:2 * count], refs[2 * count:3 * count]
    arrive, go = refs[3 * count:]
    into = [pltpu.make_async_copy(src[i], held[i], arrive.at[i]) for i in range(count)]
    out = [pltpu.make_async_copy(held[i], dst[i], go.at[i]) for i in range(count)]
    for one in into:
        one.start()
    for first, then in zip(into, out):
        first.wait()
        then.start()
    for one in out:
        one.wait()


def settle(arrays):
    anywhere = pl.BlockSpec(memory_space=pl.ANY)
    count = len(arrays)
    return pl.pallas_call(
        functools.partial(settle_kernel, count),
        out_shape=tuple(jax.ShapeDtypeStruct(v.shape, v.dtype) for v in arrays),
        in_specs=[anywhere] * count,
        out_specs=tuple([anywhere] * count),
        scratch_shapes=[pltpu.VMEM(v.shape, v.dtype) for v in arrays] + [
            pltpu.SemaphoreType.DMA((count,)), pltpu.SemaphoreType.DMA((count,))],
        compiler_params=pltpu.CompilerParams(vmem_limit_bytes=67000000),
    )(*arrays)


def fused(inputs, memory, out_cotangent, dec_lengths, mem_lengths, self_params, cross_params,
          ff_params, gains, table):
    slots, length, width = inputs.shape
    mem_len = memory.shape[1]
    hbm = pl.BlockSpec(memory_space=pl.ANY)
    vm = pl.BlockSpec(memory_space=pltpu.VMEM)
    sm = pl.BlockSpec(memory_space=pltpu.SMEM)
    s = jax.ShapeDtypeStruct
    rows_s, rows_f = self_params.shape[0] // 128, ff_params.shape[0] // 128
    row = pltpu.VMEM((length, D), BF)
    rowf = pltpu.VMEM((length, D), F32)
    memory_row = pltpu.VMEM((mem_len, D), BF)
    dma = pltpu.SemaphoreType.DMA
    outs = pl.pallas_call(
        kernel,
        out_shape=(
            s((length, D), BF), s((length, D), BF), s((mem_len, D), BF),
            s((rows_s, 128), F32), s((rows_s, 128), F32), s((rows_f, 128), F32),
            s((3, D), F32), s((H, NB), F32),
        ),
        in_specs=[hbm, hbm, hbm, sm, sm, hbm, hbm, hbm, vm, sm],
        out_specs=[hbm] * 6 + [vm] * 2,
        scratch_shapes=[
            row, memory_row, row, pltpu.VMEM((rows_s, 128), BF), pltpu.VMEM((rows_s, 128), BF),
            pltpu.VMEM((rows_f, 128), BF), row, row, memory_row,
            pltpu.VMEM((rows_s, 128), F32), pltpu.VMEM((rows_s, 128), F32),
            pltpu.VMEM((rows_f, 128), F32), dma((6,)), dma((10,)),
            pltpu.VMEM((4 * D, D), BF), pltpu.VMEM((4 * D, D), BF),
            pltpu.VMEM((32 * FU, 256), BF),
            pltpu.VMEM((2 * D, FF), BF), pltpu.VMEM((FF, D), BF),
            pltpu.VMEM((OWN_ROWS + 2 * STAGE, 256), BF),
            pltpu.VMEM((LAND_ROWS, 256), BF), pltpu.VMEM((Z_ROWS, 256), BF),
            row, row, row, row, row, rowf, row, row, memory_row, memory_row, row, rowf, row,
            pltpu.VMEM((length, FF), F32), pltpu.VMEM((length, FF), F32),
            pltpu.VMEM((length, FF), BF), pltpu.VMEM((FF, length), BF),
            pltpu.VMEM((D, length), BF),
            pltpu.VMEM((length, FF), BF), pltpu.VMEM((length, FF), BF),
            rowf, rowf, row, pltpu.VMEM((D, length), BF), pltpu.VMEM((D, mem_len), BF),
            pltpu.VMEM((H * length, length), F32),
            pltpu.VMEM((16, 128), F32),
            pltpu.VMEM((6, 8, D), F32), pltpu.VMEM((6, 16, 128), F32),
            pltpu.VMEM((5, 8, D), F32), pltpu.VMEM((5, 16, 128), F32),
            dma((120,)), dma((120,)), dma((24,)), dma((12,)), dma((180,)), dma((180,)), dma((9,)),
            dma((10,)), dma((10,)), pltpu.SemaphoreType.REGULAR((2,)),
        ],
        compiler_params=pltpu.CompilerParams(
            collective_id=0, has_side_effects=True, vmem_limit_bytes=67000000),
        cost_estimate=pl.CostEstimate(
            flops=10_000_000_000, bytes_accessed=8_000_000, transcendentals=2_000_000),
    )(
        inputs.reshape(length, width), memory.reshape(mem_len, width),
        out_cotangent.reshape(length, width), dec_lengths, mem_lengths,
        self_params.reshape(rows_s, 128), cross_params.reshape(rows_s, 128),
        ff_params.reshape(rows_f, 128), gains, table.T,
    )
    outs = settle(outs)
    return (
        outs[0].reshape(inputs.shape), outs[1].reshape(inputs.shape),
        outs[2].reshape(memory.shape), outs[3].reshape(-1), outs[4].reshape(-1),
        outs[5].reshape(-1), outs[6], outs[7].T,
    )


HIGHEST = lax.Precision.HIGHEST


def product(left, right):
    return jnp.dot(left, right, preferred_element_type=jnp.float32)


def product_t(left, right):
    return lax.dot_general(
        left, right, (((0,), (0,)), ((), ())), preferred_element_type=jnp.float32
    )


def product_nt(left, right):
    return lax.dot_general(
        left, right, (((1,), (1,)), ((), ())), preferred_element_type=jnp.float32
    )


def rms_scale(value, gain):
    return value * lax.rsqrt(jnp.mean(value * value, axis=-1, keepdims=True) + 1e-06) * gain


def gelu_gate(gate_pre, up_pre):
    return jax.nn.gelu(gate_pre, approximate=True) * up_pre


def bucket_rows(start, count, length):
    half_count = NB // 2
    limits = np.ceil(
        half_count * (MAXD / half_count) ** (np.arange(1, half_count) / half_count)
    ).astype(np.int32)
    query_pos = start + jnp.arange(count, dtype=jnp.int32)
    key_pos = jnp.arange(length, dtype=jnp.int32)
    distance = query_pos[:, None] - key_pos[None, :]
    beyond = half_count + jnp.sum(
        (distance[None] >= jnp.asarray(limits)[:, None, None]).astype(jnp.int32), axis=0
    )
    return jnp.where(distance < half_count, jnp.maximum(distance, 0), beyond)


def onehot_block(start, count, length):
    bucket = bucket_rows(start, count, length)
    hot_rows = jnp.arange(NB, dtype=jnp.int32)[:, None, None] == bucket[None]
    return hot_rows.astype(jnp.float32).reshape(NB, count * length)


def position_bias(table, length):
    block_rows = min(length, 128)
    block_count = length // block_rows

    def position_per_block(block):
        bucket_hot = onehot_block(block * block_rows, block_rows, length)
        return lax.dot_general(
            table,
            bucket_hot,
            (((0,), (0,)), ((), ())),
            precision=HIGHEST,
            preferred_element_type=jnp.float32,
        )

    pieces = lax.map(position_per_block, jnp.arange(block_count, dtype=jnp.int32))
    return (
        pieces.reshape(block_count, H, block_rows, length)
        .transpose(1, 0, 2, 3)
        .reshape(H, length, length)
    )


def table_gradient(score_sums, length):
    block_rows = min(length, 128)

    def table_per_block(carry, block):
        ds_piece = score_sums.reshape(H, block_rows * length)
        bucket_hot = onehot_block(block * block_rows, block_rows, length)
        return (
            carry
            + lax.dot_general(
                bucket_hot,
                ds_piece,
                (((1,), (1,)), ((), ())),
                precision=HIGHEST,
                preferred_element_type=jnp.float32,
            ),
            None,
        )

    result, _ = lax.scan(
        table_per_block,
        jnp.zeros((NB, H), jnp.float32),
        jnp.arange(length // block_rows, dtype=jnp.int32),
    )
    return result


def score_block(queries, keys_in, score_bias, keep_mask):
    q_len = queries.shape[0]
    k_len = keys_in.shape[0]
    raw_scores = (
        jnp.einsum(
            "qhe,khe->hqk",
            queries.reshape(q_len, H, DH),
            keys_in.reshape(k_len, H, DH),
            preferred_element_type=jnp.float32,
        )
        + score_bias
    )
    return jnp.where(keep_mask[None], raw_scores, MASKED)


def attend_forward(queries, keys_in, values, score_bias, keep_mask):
    q_len = queries.shape[0]
    k_len = keys_in.shape[0]
    raw_scores = score_block(queries, keys_in, score_bias, keep_mask)
    row_max = jnp.max(raw_scores, axis=2, keepdims=True)
    exponent = jnp.exp(raw_scores - row_max)
    row_sum = jnp.sum(exponent, axis=2, keepdims=True)
    softmax_low = (exponent / row_sum).astype(jnp.bfloat16)
    head_mix = jnp.einsum(
        "hqk,khe->qhe",
        softmax_low,
        values.reshape(k_len, H, DH),
        preferred_element_type=jnp.float32,
    )
    return (head_mix.reshape(q_len, H * DH).astype(jnp.bfloat16), row_max, row_sum)


def attend_backward(queries, keys_in, values, score_bias, keep_mask, row_max, row_sum, d_mix):
    q_len = queries.shape[0]
    k_len = keys_in.shape[0]
    raw_scores = score_block(queries, keys_in, score_bias, keep_mask)
    softmax_out = jnp.exp(raw_scores - row_max) / row_sum
    softmax_low = softmax_out.astype(jnp.bfloat16)
    mix_heads = d_mix.reshape(q_len, H, DH)
    q_heads = queries.reshape(q_len, H, DH)
    k_heads = keys_in.reshape(k_len, H, DH)
    v_heads = values.reshape(k_len, H, DH)
    d_softmax = jnp.einsum("qhe,khe->hqk", mix_heads, v_heads, preferred_element_type=jnp.float32)
    d_scores = (
        softmax_out * (d_softmax - jnp.sum(softmax_out * d_softmax, axis=2, keepdims=True))
    ).astype(jnp.bfloat16)
    d_values = (
        jnp.einsum("hqk,qhe->khe", softmax_low, mix_heads, preferred_element_type=jnp.float32)
        .reshape(k_len, H * DH)
        .astype(jnp.bfloat16)
    )
    d_queries = (
        jnp.einsum("hqk,khe->qhe", d_scores, k_heads, preferred_element_type=jnp.float32)
        .reshape(q_len, H * DH)
        .astype(jnp.bfloat16)
    )
    d_keys = (
        jnp.einsum("hqk,qhe->khe", d_scores, q_heads, preferred_element_type=jnp.float32)
        .reshape(k_len, H * DH)
        .astype(jnp.bfloat16)
    )
    return (d_queries, d_keys, d_values, d_scores)


def attend_slots(queries, keys_in, values, lengths, score_bias, base_mask):
    slot_count = lengths.shape[0]
    q_len = queries.shape[0] // slot_count
    k_len = keys_in.shape[0] // slot_count
    key_pos = jnp.arange(k_len, dtype=jnp.int32)

    def per_slot(slot_item):
        q_slot, k_slot, v_slot, slot_len = slot_item
        keep_mask = base_mask & (key_pos[None, :] < slot_len)
        return attend_forward(q_slot, k_slot, v_slot, score_bias, keep_mask)

    head_mix, row_max, row_sum = lax.map(
        per_slot,
        (
            queries.reshape(slot_count, q_len, -1),
            keys_in.reshape(slot_count, k_len, -1),
            values.reshape(slot_count, k_len, -1),
            lengths,
        ),
    )
    return (head_mix.reshape(slot_count * q_len, -1), row_max, row_sum)


def attend_back_slots(
    queries, keys_in, values, lengths, score_bias, base_mask, row_max, row_sum, d_mix, with_table
):
    slot_count = lengths.shape[0]
    q_len = queries.shape[0] // slot_count
    k_len = keys_in.shape[0] // slot_count
    key_pos = jnp.arange(k_len, dtype=jnp.int32)
    if with_table:
        start = jnp.zeros((H, q_len, k_len), jnp.float32)
    else:
        start = jnp.zeros((), jnp.float32)

    def per_slot(carry, slot_item):
        q_slot, k_slot, v_slot, slot_len, max_slot, sum_slot, dmix_slot = slot_item
        keep_mask = base_mask & (key_pos[None, :] < slot_len)
        d_queries, d_keys, d_values, d_scores = attend_backward(
            q_slot, k_slot, v_slot, score_bias, keep_mask, max_slot, sum_slot, dmix_slot
        )
        if with_table:
            carry = carry + d_scores.astype(jnp.float32)
        return (carry, (d_queries, d_keys, d_values))

    score_sums, grad_parts = lax.scan(
        per_slot,
        start,
        (
            queries.reshape(slot_count, q_len, -1),
            keys_in.reshape(slot_count, k_len, -1),
            values.reshape(slot_count, k_len, -1),
            lengths,
            row_max,
            row_sum,
            d_mix.reshape(slot_count, q_len, -1),
        ),
    )
    return (
        grad_parts[0].reshape(slot_count * q_len, -1),
        grad_parts[1].reshape(slot_count * k_len, -1),
        grad_parts[2].reshape(slot_count * k_len, -1),
        score_sums,
    )


def gather_weights(self_params, cross_params, ff_params):
    return (
        lax.all_gather(self_params, ("dp", "fsdp"), axis=0, tiled=True),
        lax.all_gather(cross_params, ("dp", "fsdp"), axis=0, tiled=True),
        lax.all_gather(ff_params, ("dp", "fsdp"), axis=0, tiled=True),
    )


def scatter_grads(self_full, cross_full, ff_full):
    wide_count = lax.axis_size("dp")
    spread = (
        lax.all_to_all(
            self_full.reshape(wide_count, -1).astype(jnp.bfloat16),
            "dp",
            split_axis=0,
            concat_axis=0,
            tiled=True,
        ).astype(jnp.float32),
        lax.all_to_all(
            cross_full.reshape(wide_count, -1).astype(jnp.bfloat16),
            "dp",
            split_axis=0,
            concat_axis=0,
            tiled=True,
        ).astype(jnp.float32),
        lax.all_to_all(
            ff_full.reshape(wide_count, -1).astype(jnp.bfloat16),
            "dp",
            split_axis=0,
            concat_axis=0,
            tiled=True,
        ).astype(jnp.float32),
    )
    self_block = jnp.sum(spread[0], axis=0)
    cross_block = jnp.sum(spread[1], axis=0)
    ff_block = jnp.sum(spread[2], axis=0)
    return (
        lax.psum_scatter(
            self_block.astype(jnp.bfloat16), "fsdp", scatter_dimension=0, tiled=True
        ).astype(jnp.float32),
        lax.psum_scatter(
            cross_block.astype(jnp.bfloat16), "fsdp", scatter_dimension=0, tiled=True
        ).astype(jnp.float32),
        lax.psum_scatter(
            ff_block.astype(jnp.bfloat16), "fsdp", scatter_dimension=0, tiled=True
        ).astype(jnp.float32),
    )


def unpack(weights):
    self_flat, cross_flat, ff_flat = weights
    self_mats = self_flat.reshape(4, D, D)
    cross_mats = cross_flat.reshape(4, D, D)
    block_size = D * FF
    return (
        self_mats[0],
        self_mats[1],
        self_mats[2],
        self_mats[3],
        cross_mats[0],
        cross_mats[1],
        cross_mats[2],
        cross_mats[3],
        ff_flat[:block_size].reshape(D, FF),
        ff_flat[block_size : 2 * block_size].reshape(D, FF),
        ff_flat[2 * block_size :].reshape(FF, D),
    )


def run_forward(
    weights, flat_in, flat_mem, gains, pos_bias, causal, open_mask, dec_lengths, mem_lengths
):
    w_sq, w_sk, w_sv, w_so, w_cq, w_ck, w_cv, w_co, w_gate, w_up, w_down = unpack(weights)
    norm_one = rms_scale(flat_in, gains[0]).astype(jnp.bfloat16)
    self_q = product(norm_one, w_sq).astype(jnp.bfloat16)
    self_k = product(norm_one, w_sk).astype(jnp.bfloat16)
    self_v = product(norm_one, w_sv).astype(jnp.bfloat16)
    self_mix, self_max, self_sum = attend_slots(
        self_q, self_k, self_v, dec_lengths, pos_bias, causal
    )
    resid_one = flat_in + product(self_mix, w_so)
    norm_two = rms_scale(resid_one, gains[1]).astype(jnp.bfloat16)
    cross_q = product(norm_two, w_cq).astype(jnp.bfloat16)
    cross_k = product(flat_mem, w_ck).astype(jnp.bfloat16)
    cross_v = product(flat_mem, w_cv).astype(jnp.bfloat16)
    cross_mix, cross_max, cross_sum = attend_slots(
        cross_q, cross_k, cross_v, mem_lengths, 0.0, open_mask
    )
    resid_two = resid_one + product(cross_mix, w_co)
    norm_three = rms_scale(resid_two, gains[2]).astype(jnp.bfloat16)
    gate_pre = product(norm_three, w_gate)
    up_pre = product(norm_three, w_up)
    hidden = gelu_gate(gate_pre, up_pre).astype(jnp.bfloat16)
    block = resid_two + product(hidden, w_down)
    return (
        norm_one,
        self_q,
        self_k,
        self_v,
        self_mix,
        self_max,
        self_sum,
        resid_one,
        norm_two,
        cross_q,
        cross_k,
        cross_v,
        cross_mix,
        cross_max,
        cross_sum,
        resid_two,
        norm_three,
        gate_pre,
        up_pre,
        hidden,
        block,
    )


def by_collectives(
    inputs,
    memory,
    out_cotangent,
    dec_lengths,
    mem_lengths,
    self_params,
    cross_params,
    ff_params,
    gains,
    table,
):
    slot_count, length, model_width = inputs.shape
    mem_len = memory.shape[1]
    row_count = slot_count * length
    pos_bias = position_bias(table, length)
    positions = jnp.arange(length, dtype=jnp.int32)
    causal = positions[None, :] <= positions[:, None]
    open_mask = jnp.ones((length, mem_len), dtype=bool)
    flat_in = inputs.reshape(row_count, model_width).astype(jnp.float32)
    flat_mem = memory.reshape(slot_count * mem_len, model_width)
    weights = gather_weights(self_params, cross_params, ff_params)
    first_pass = run_forward(
        weights, flat_in, flat_mem, gains, pos_bias, causal, open_mask, dec_lengths, mem_lengths
    )
    block_out = first_pass[20].astype(jnp.bfloat16).reshape(slot_count, length, model_width)
    again = gather_weights(self_params, cross_params, ff_params)
    w_sq, w_sk, w_sv, w_so, w_cq, w_ck, w_cv, w_co, w_gate, w_up, w_down = unpack(again)
    (
        norm_one,
        self_q,
        self_k,
        self_v,
        self_mix,
        self_max,
        self_sum,
        resid_one,
        norm_two,
        cross_q,
        cross_k,
        cross_v,
        cross_mix,
        cross_max,
        cross_sum,
        resid_two,
        norm_three,
        gate_pre,
        up_pre,
        hidden,
        _,
    ) = run_forward(
        again, flat_in, flat_mem, gains, pos_bias, causal, open_mask, dec_lengths, mem_lengths
    )
    d_out = out_cotangent.reshape(row_count, model_width)
    grad_down = product_t(hidden, d_out)
    d_hidden = product_nt(d_out, w_down).astype(jnp.bfloat16)
    _, pull_gate = jax.vjp(gelu_gate, gate_pre, up_pre)
    d_gate, d_up = pull_gate(d_hidden.astype(jnp.float32))
    d_gate = d_gate.astype(jnp.bfloat16)
    d_up = d_up.astype(jnp.bfloat16)
    grad_gate = product_t(norm_three, d_gate)
    grad_up = product_t(norm_three, d_up)
    d_norm_three = product_nt(d_gate, w_gate) + product_nt(d_up, w_up)
    _, pull_three = jax.vjp(rms_scale, resid_two, gains[2])
    d_from_three, grad_gain_three = pull_three(d_norm_three)
    d_resid_two = d_out.astype(jnp.float32) + d_from_three
    d_cross = d_resid_two.astype(jnp.bfloat16)
    grad_co = product_t(cross_mix, d_cross)
    d_cross_mix = product_nt(d_cross, w_co).astype(jnp.bfloat16)
    dq_cross, dk_cross, dv_cross, _ = attend_back_slots(
        cross_q,
        cross_k,
        cross_v,
        mem_lengths,
        0.0,
        open_mask,
        cross_max,
        cross_sum,
        d_cross_mix,
        False,
    )
    grad_cq = product_t(norm_two, dq_cross)
    grad_ck = product_t(flat_mem, dk_cross)
    grad_cv = product_t(flat_mem, dv_cross)
    memory_grad = (product_nt(dk_cross, w_ck) + product_nt(dv_cross, w_cv)).astype(jnp.bfloat16)
    _, pull_two = jax.vjp(rms_scale, resid_one, gains[1])
    d_from_two, grad_gain_two = pull_two(product_nt(dq_cross, w_cq))
    d_resid_one = d_resid_two + d_from_two
    d_self = d_resid_one.astype(jnp.bfloat16)
    grad_so = product_t(self_mix, d_self)
    d_self_mix = product_nt(d_self, w_so).astype(jnp.bfloat16)
    dq_self, dk_self, dv_self, score_sums = attend_back_slots(
        self_q, self_k, self_v, dec_lengths, pos_bias, causal, self_max, self_sum, d_self_mix, True
    )
    grad_sq = product_t(norm_one, dq_self)
    grad_sk = product_t(norm_one, dk_self)
    grad_sv = product_t(norm_one, dv_self)
    d_norm_one = product_nt(dq_self, w_sq) + product_nt(dk_self, w_sk) + product_nt(dv_self, w_sv)
    _, pull_one = jax.vjp(rms_scale, flat_in, gains[0])
    d_from_one, grad_gain_one = pull_one(d_norm_one)
    input_grad = (d_resid_one + d_from_one).astype(jnp.bfloat16)
    table_local = table_gradient(score_sums, length)
    self_full = jnp.stack([grad_sq, grad_sk, grad_sv, grad_so]).reshape(-1)
    cross_full = jnp.stack([grad_cq, grad_ck, grad_cv, grad_co]).reshape(-1)
    ff_full = jnp.concatenate([grad_gate.reshape(-1), grad_up.reshape(-1), grad_down.reshape(-1)])
    self_shard, cross_shard, ff_shard = scatter_grads(self_full, cross_full, ff_full)
    gain_local = jnp.stack([grad_gain_one, grad_gain_two, grad_gain_three])
    gain_total, table_total = lax.psum((gain_local, table_local), ("dp", "fsdp"))
    return (
        block_out,
        input_grad.reshape(slot_count, length, model_width),
        memory_grad.reshape(slot_count, mem_len, model_width),
        self_shard,
        cross_shard,
        ff_shard,
        gain_total,
        table_total,
    )


def solution(mesh):
    whole = ("dp", "fsdp")
    rows = P(whole, None, None)
    flat = P(whole)
    small = mesh.shape["dp"] == 8 and mesh.shape["fsdp"] == 4
    return jax.shard_map(
        fused if small else by_collectives,
        mesh=mesh,
        in_specs=(rows, rows, rows, flat, flat, flat, flat, flat, P(), P()),
        out_specs=(rows, rows, rows, flat, flat, flat, P(), P()),
        check_vma=False,
    )
```

```python
import functools

import jax
import jax.numpy as jnp
import numpy as np
from jax import lax
from jax.experimental import pallas as pl
from jax.experimental.pallas import tpu as pltpu
from jax.sharding import PartitionSpec as P

D = 768
FF = 2048
H = 12
DH = 64
NB = 32
MAXD = 128
PAIRS = H // 2
MASKED = -1000000000.0
BF = jnp.bfloat16
F32 = jnp.float32
MESH = pl.DeviceIdType.MESH

AR = 96
AU = 288
FU = 576
GROUPS = (
    (2, 3), (2, 2), (2, 0), (2, 1),
    (1, 3), (1, 2), (1, 1), (1, 0),
    (0, 3), (0, 0), (0, 2), (0, 1),
)
PAIR = (True,) * 10 + (False,) * 2
SHARED = (True, True, True)
UNIT = tuple(FU if t == 2 else AU for t, _ in GROUPS)
OWN = tuple(4 * sum(UNIT[:g]) for g in range(12))
OWN_ROWS = 4 * sum(UNIT)
LAND = tuple(3 * sum(UNIT[:g]) for g in range(12))
LAND_ROWS = 3 * sum(UNIT)
Z_ROWS = 5 * FU
STAGE = 4 * FU
ROLES = ((1, 1), (1, 0), (0, 1), (0, 0))
SIB = (0, 12, 13, 14)


def limits():
    half = NB // 2
    return [
        int(v)
        for v in np.ceil(half * (MAXD / half) ** (np.arange(1, half) / half)).astype(np.int32)
    ]


def bucket_of(distance):
    half = NB // 2
    beyond = jnp.full(distance.shape, half, jnp.int32)
    for limit in limits():
        beyond = beyond + jnp.where(distance >= limit, 1, 0)
    return jnp.where(distance < half, jnp.maximum(distance, 0), beyond)


def nn(left, right):
    return jnp.dot(left, right, preferred_element_type=F32)


def nt(left, right):
    return lax.dot_general(left, right, (((1,), (1,)), ((), ())), preferred_element_type=F32)


def tn(left, right):
    return lax.dot_general(left, right, (((0,), (0,)), ((), ())), preferred_element_type=F32)


def al(value, step):
    return pl.multiple_of(value, step)


def rms(value, gain):
    r = lax.rsqrt(jnp.mean(value * value, axis=-1, keepdims=True) + 1e-06)
    return value * r * gain


def rms_back(value, gain, dz):
    r = lax.rsqrt(jnp.mean(value * value, axis=-1, keepdims=True) + 1e-06)
    inner = jnp.mean(value * gain * dz, axis=-1, keepdims=True)
    dv = r * gain * dz - value * (r * r * r) * inner
    dg = jnp.sum(value * r * dz, axis=0, keepdims=True)
    return dv, dg


class Layer:
    def __init__(self, refs):
        self.__dict__.update(refs)
        self.flat, self.dm = self.ps, self.n3
        dp = lax.axis_index("dp")
        fs = lax.axis_index("fsdp")
        self.z, self.y = dp // 2, dp % 2
        self.x, self.c = fs // 2, fs % 2
        self.shard = dp * 4 + fs

    def dev(self, z=None, fx=0, fy=0, fc=0):
        z = self.z if z is None else z
        y = (self.y + fy) % 2
        x = (self.x + fx) % 2
        c = (self.c + fc) % 2
        return (z * 2 + y, x * 2 + c)

    def chip(self, fx=0, fy=0):
        return ((self.y + fy) % 2) * 2 + (self.x + fx) % 2

    def shard_at(self, z, fx=0, fy=0, fc=0):
        return z * 8 + self.chip(fx, fy) * 2 + (self.c + fc) % 2

    def copy(self, src, dst, send, recv, device):
        return pltpu.make_async_remote_copy(
            src_ref=src, dst_ref=dst, send_sem=send, recv_sem=recv,
            device_id=device, device_id_type=MESH,
        )

    def piece(self, tensor, shard, half=None, par=None):
        rows = FU if tensor == 2 else AR
        ref = (self.ws, self.wc, self.wf)[tensor]
        start = shard * rows
        if half is None:
            return ref.at[pl.ds(al(start, 16), rows), :]
        rows = rows // 2
        start = pl.ds(al(start + half * rows, 16), rows)
        if not SHARED[tensor]:
            return ref.at[start, :]
        width = ref.shape[1] // 2
        return ref.at[start, pl.ds(al(par * width, 128), width)]

    def plane(self, tensor, k):
        if tensor == 2:
            return k
        far = self.z // 2
        return (self.z, self.z + 1 - 2 * (self.z % 2), 2 - far, 3 - 3 * far)[k]

    def gcopy(self, tensor, zs, kind, there=False):
        par = self.z % 2
        if kind < 2:
            spot, dev = (0, 0), ((1, 0), (0, 1))[kind]
            if there:
                spot = dev
            part, dev = self.piece(tensor, self.shard_at(zs, *spot)), self.dev(None, *dev)
        elif kind < 4:
            spot, dev = ((1, 0), (0, 1)) if kind == 2 else ((0, 1), (1, 0))
            if there:
                spot = (1, 1)
            part = self.piece(tensor, self.shard_at(zs, *spot), kind - 2, par)
            dev = self.dev(None, *dev)
        elif kind < 8:
            spot = ((0, 0), (1, 0), (0, 1), (1, 1))[kind - 4]
            part = self.piece(tensor, self.shard_at(zs, *spot, 1 if there else 0))
            dev = self.dev(fc=1)
        else:
            part = self.piece(
                tensor, self.shard_at(zs, 1, 1), kind - 8, 1 - par if there else par)
            dev = self.dev(z=self.z + 1 - 2 * par)
        row = (tensor * 4 + zs) * 10 + kind
        return self.copy(part, part, self.gsend.at[row], self.grecv.at[row], dev)

    def start(self, tensor, zs, *kinds):
        for kind in kinds:
            self.gcopy(tensor, zs, kind).start()

    def arrive(self, tensor, zs, *kinds):
        for kind in kinds:
            self.gcopy(tensor, zs, kind, True).wait_recv()

    def zcopy(self, tensor, zs, up):
        part = self.piece(tensor, self.shard_at(zs))
        row = tensor * 4 + zs
        return self.copy(
            part, part, self.zsend.at[2 * row + up], self.zrecv.at[row],
            self.dev(z=(self.z + (1 if up else 3)) % 4))

    def inner(self, up):
        return self.z < 3 if up else self.z > 0

    def own_z(self, tensor, up):
        @pl.when(self.inner(up))
        def _():
            self.zcopy(tensor, self.z, up).start()

    def z_arrive(self, tensor, zs):
        self.zcopy(tensor, zs, 0).wait_recv()
        for up in (0, 1):
            @pl.when((zs < self.z if up else zs > self.z) & self.inner(up))
            def _(up=up):
                self.zcopy(tensor, zs, up).start()
        self.start(tensor, zs, 0, 1, 4)

    def own_xy(self, tensor):
        self.start(tensor, self.z, 0, 1, 4)

    def p1(self, tensor, k):
        if tensor < 2:
            self.z_arrive(tensor, self.plane(tensor, k))
            return

        @pl.when(self.z == k)
        def _():
            self.start(tensor, k, 0, 1, 4)

        @pl.when(self.z != k)
        def _():
            self.z_arrive(tensor, k)

    def p2x(self, tensor, k):
        zs = self.plane(tensor, k)
        self.arrive(tensor, zs, 0)
        self.start(tensor, zs, 2, 5)

    def p2y(self, tensor, k):
        zs = self.plane(tensor, k)
        self.arrive(tensor, zs, 1)
        self.start(tensor, zs, 3, 6)

    def p3(self, tensor, k, half):
        zs = self.plane(tensor, k)
        self.arrive(tensor, zs, 2 + half)
        if SHARED[tensor]:
            self.start(tensor, zs, 8 + half)
        elif half:
            self.start(tensor, zs, 7)

    def p4(self, tensor, k):
        if SHARED[tensor]:
            zs = self.plane(tensor, k)
            self.arrive(tensor, zs, 8, 9)
            self.start(tensor, zs, 7)

    def p5(self, tensor, k):
        self.arrive(tensor, self.plane(tensor, k), 4, 5, 6, 7)

    def plane_sent(self, tensor, k):
        for kind in range(10 if SHARED[tensor] else 8):
            self.gcopy(tensor, self.plane(tensor, k), kind).wait_send()

    def z_sent(self, tensor, zs):
        for up in (0, 1):
            @pl.when((zs <= self.z if up else zs >= self.z) & self.inner(up))
            def _(up=up):
                self.zcopy(tensor, zs, up).wait_send()

    def credit(self, which):
        for k in ((0,), (1, 2, 3))[which]:
            self.plane_sent(2, k)
            self.z_sent(2, k)
        pl.semaphore_signal(
            self.free.at[which], inc=1, device_id=self.dev(fc=1), device_id_type=MESH)

    def enter(self, i):
        src = (self.sh_s_hbm, self.sh_c_hbm, self.sh_f_hbm, self.x_hbm, self.mem_hbm, self.g_hbm)
        dst = (self.sh_s, self.sh_c, self.sh_f, self.x_in, self.mem, self.g)
        return pltpu.make_async_copy(src[i], dst[i], self.isem.at[i])

    def leave(self, i, part=None):
        if part is not None:
            rows = slice(128 * part, 128 * part + 128)
            return pltpu.make_async_copy(
                self.mgrad.at[rows, :], self.mgrad_hbm.at[rows, :], self.osem.at[i])
        src = (self.block, self.xgrad, None, self.gs, self.gc, self.gf)[i]
        dst = (self.block_hbm, self.xgrad_hbm, None, self.gs_hbm, self.gc_hbm, self.gf_hbm)[i]
        return pltpu.make_async_copy(src, dst, self.osem.at[i])

    def own_square(self, tensor):
        src, dst = ((self.sh_s, self.ws), (self.sh_c, self.wc))[tensor]
        self.enter(tensor).wait()
        self.flat[0:576, :] = src[...].astype(F32)
        row = al(self.shard * AR, 16)
        for t in range(6):
            dst[pl.ds(row, AR), 128 * t:128 * t + 128] = self.flat[
                pl.ds(t, AR, stride=6), :].astype(BF)

    def own_ff(self):
        self.enter(2).wait()
        self.flat[0:1152, :] = self.sh_f[...].astype(F32)
        base = self.shard * FU
        flat, wf = self.flat, self.wf

        def wide(rows):
            for u in range(4):
                for w in range(2):
                    top = flat[pl.ds(4 * u + w, rows, stride=16), :]
                    low = flat[pl.ds(4 * u + w + 2, rows, stride=16), :]
                    wf[pl.ds(al(base + 2 * rows * u, 16), 2 * rows), 128 * w:128 * w + 128] = (
                        jnp.concatenate([top, low], axis=0).astype(BF))

        def tall(first, rows, offset):
            for t in range(6):
                wf[pl.ds(al(base + offset + rows * (t // 2), 16), rows),
                   128 * (t % 2):128 * (t % 2) + 128] = flat[
                       pl.ds(first + t, rows, stride=6), :].astype(BF)

        @pl.when(self.shard < 21)
        def _():
            wide(72)

        @pl.when(self.shard == 21)
        def _():
            wide(24)
            tall(384, 128, 192)

        @pl.when(self.shard > 21)
        def _():
            tall(0, 192, 0)

    def build_wide(self, ch):
        rows1 = 24 if ch == 10 else 72

        def step(u, _):
            low = self.wf[pl.ds(al(1152 * ch + 144 * u, 16), 144), :].astype(F32)
            high = self.wf[
                pl.ds(al(1152 * ch + FU + 2 * rows1 * u, 16), 2 * rows1), :].astype(F32)
            for w in range(2):
                value = jnp.concatenate(
                    [low[72 * w:72 * w + 72], high[rows1 * w:rows1 * w + rows1]], axis=0)
                self.wgu[144 * ch:144 * ch + 72 + rows1,
                         pl.ds(al(512 * u + 256 * w, 256), 256)] = value.astype(BF)
            return 0

        lax.fori_loop(0, 4, step, 0)

    def build_tall(self, s):
        first, rows, offset = (0, 128, 192) if s == 21 else (192 * s - 4096, 192, 0)
        for p in range(3):
            self.wd[first:first + rows, 256 * p:256 * p + 256] = self.wf[
                FU * s + offset + rows * p:FU * s + offset + rows * p + rows, :]

    def build_plane(self, zs):
        if zs < 2:
            for ch in range(4 * zs, 4 * zs + 4):
                self.build_wide(ch)
        elif zs == 2:
            for ch in (8, 9, 10):
                self.build_wide(ch)
            for s in (21, 22, 23):
                self.build_tall(s)
        else:
            for s in range(24, 32):
                self.build_tall(s)

    def masks(self):
        lane = lax.broadcasted_iota(jnp.int32, (128, 128), 1)
        self.left = lane < DH

    def stack(self, pair):
        zero = jnp.zeros_like(pair)
        return jnp.concatenate(
            [jnp.where(self.left, pair, zero), jnp.where(self.left, zero, pair)], axis=0)

    def unstack(self, both):
        rows = both.shape[0] // 2
        return jnp.where(self.left, both[0:rows], both[rows:])

    def bias(self):
        lane = lax.broadcasted_iota(jnp.int32, (1, 128), 1)
        bucket = bucket_of((128 - lane) % 128)
        for h in range(H):
            row = jnp.zeros((1, 128), F32)
            for b in range(NB):
                row = jnp.where(bucket == b, self.table[h, b], row)
            full = jnp.broadcast_to(row, (128, 128))
            self.ps[128 * h:128 * h + 128, :] = pltpu.roll(
                full, 0, 1, stride=1, stride_axis=0)

    def project(self, left, ref, row, out):
        for p in range(3):
            out[:, 256 * p:256 * p + 256] = nn(
                left, ref[row:row + D, 256 * p:256 * p + 256]).astype(BF)

    def add_product(self, left, ref, row, base, out):
        for p in range(3):
            cols = slice(256 * p, 256 * p + 256)
            out[:, cols] = base[:, cols].astype(F32) + nn(left, ref[row:row + D, cols])

    def heads(self, p):
        return pl.ds(al(p * 256, 256), 256)

    def self_forward(self):
        for i in (3, 4, 5):
            self.enter(i).wait()
        x = self.x_in[...].astype(F32)
        self.n1[...] = rms(x, self.gains[0:1, :]).astype(BF)
        n1 = self.n1[...]
        for m, out in enumerate((self.q, self.k, self.v)):
            self.project(n1, self.ws, D * m, out)
        length = self.dl[0]
        row = lax.broadcasted_iota(jnp.int32, (256, 128), 0) % 128
        col = lax.broadcasted_iota(jnp.int32, (256, 128), 1)
        keep = (col <= row) & (col < length)

        def pair(p, _):
            cols = pl.ds(al(p * 128, 128), 128)
            s = nt(self.stack(self.q[:, cols]), self.k[:, cols]) + self.ps[self.heads(p), :]
            s = jnp.where(keep, s, MASKED)
            e = jnp.exp(s - jnp.max(s, axis=-1, keepdims=True))
            prob = e / jnp.sum(e, axis=-1, keepdims=True)
            self.ps[self.heads(p), :] = prob
            self.mix[:, cols] = self.unstack(nn(prob.astype(BF), self.v[:, cols])).astype(BF)
            return 0

        lax.fori_loop(0, PAIRS, pair, 0)
        self.add_product(self.mix[...], self.ws, 3 * D, self.x_in, self.r1)
        self.n2[...] = rms(self.r1[...], self.gains[1:2, :]).astype(BF)

    def cross_kv(self, m):
        out = (self.ck, self.cv)[m - 1]
        for i in range(4):
            for p in range(3):
                out[128 * i:128 * i + 128, 256 * p:256 * p + 256] = nn(
                    self.mem[128 * i:128 * i + 128, :],
                    self.wc[D * m:D * m + D, 256 * p:256 * p + 256]).astype(BF)

    def cross_probs(self, p):
        cols = pl.ds(al(p * 128, 128), 128)
        col = lax.broadcasted_iota(jnp.int32, (256, self.mem.shape[0]), 1)
        s = nt(self.stack(self.cq[:, cols]), self.ck[:, cols])
        s = jnp.where(col < self.ml[0], s, MASKED)
        e = jnp.exp(s - jnp.max(s, axis=-1, keepdims=True))
        return e / jnp.sum(e, axis=-1, keepdims=True)

    def cross_forward(self, part):
        if part == 0:
            self.project(self.n2[...], self.wc, 0, self.cq)

        def pair(p, _):
            cols = pl.ds(al(p * 128, 128), 128)
            prob = self.cross_probs(p)
            self.cmix[:, cols] = self.unstack(nn(prob.astype(BF), self.cv[:, cols])).astype(BF)
            return 0

        lax.fori_loop(2 * part, 2 * part + 2, pair, 0)
        if part == 2:
            self.add_product(self.cmix[...], self.wc, 3 * D, self.r1, self.r2)
            self.n3[...] = rms(self.r2[...], self.gains[2:3, :]).astype(BF)

    def ff_gate(self):
        n3 = self.n3[...]
        c0 = float(np.sqrt(2.0 / np.pi))

        def chunk(i, _):
            cols = pl.ds(al(i * 256, 256), 256)
            a = nn(n3, self.wgu[0:D, cols])
            sq = a * a
            t = jnp.tanh(c0 * (a + 0.044715 * a * sq))
            self.ga[:, cols] = 0.5 * a * (1.0 + t)
            self.ub[:, cols] = 0.5 * (1.0 + t) + 0.5 * a * (1.0 - t * t) * (
                c0 * (1.0 + 0.134145 * sq))
            return 0

        lax.fori_loop(0, FF // 256, chunk, 0)

    def ff_up(self):
        n3 = self.n3[...]

        def chunk(i, _):
            cols = pl.ds(al(i * 256, 256), 256)
            up = nn(n3, self.wgu[D:2 * D, cols])
            self.ub[:, cols] = up * self.ub[:, cols]
            self.hid[:, cols] = (self.ga[:, cols] * up).astype(BF)
            return 0

        lax.fori_loop(0, FF // 256, chunk, 0)
        self.hidt[...] = self.hid[...].T

    def out_rows(self):
        hid = self.hid[...]
        for p in range(3):
            cols = slice(256 * p, 256 * p + 256)
            self.block[:, cols] = (self.r2[:, cols] + nn(hid, self.wd[:, cols])).astype(BF)
        self.leave(0).start()

    def d_hidden(self, part):
        g = self.g[...]

        def chunk(i, _):
            at = al(i * 256, 256)
            cols = pl.ds(at, 256)
            dh = nt(g, self.wd[pl.ds(at, 256), :]).astype(BF).astype(F32)
            self.dg[:, cols] = (dh * self.ub[:, cols]).astype(BF)
            self.du[:, cols] = (dh * self.ga[:, cols]).astype(BF)
            return 0

        lax.fori_loop(4 * part, 4 * part + 4, chunk, 0)

    def place(self, g):
        own = OWN[g]
        out = OWN_ROWS + (g % 2) * STAGE
        return own + self.c * (out - own), out + self.c * (own - out)

    def grad_tall(self, g, i):
        b0, b1 = self.place(g)
        for p in range(3):
            both = nn(
                self.hidt[pl.ds(al(512 + 384 * i, 16), 384), :],
                self.g[:, 256 * p:256 * p + 256])
            self.gb[pl.ds(al(b0 + FU * i + 192 * p, 16), 192), :] = both[0:192].astype(BF)
            self.gb[pl.ds(al(b1 + FU * i + 192 * p, 16), 192), :] = both[192:].astype(BF)

    def grad_tall_part(self, base, i, first, rows, offset):
        for p in range(3):
            value = nn(self.hidt[first:first + rows, :], self.g[:, 256 * p:256 * p + 256])
            self.gb[pl.ds(al(base + FU * i + offset + rows * p, 16), rows), :] = value.astype(BF)

    def grad_wide(self, g, ch, i):
        b0, b1 = self.place(g)
        rows1 = 24 if ch == 10 else 72
        first, end = 144 * ch, 144 * ch + 72 + rows1

        def step(u, _):
            cols = pl.ds(al(512 * u, 512), 512)
            parts = []
            if first < D:
                parts.append(nn(self.n3t[first:min(end, D), :], self.dg[:, cols]))
            if end > D:
                parts.append(nn(self.n3t[max(first, D) - D:end - D, :], self.du[:, cols]))
            both = parts[0] if len(parts) == 1 else jnp.concatenate(parts, axis=0)
            for base, at, rows in ((b0, 0, 72), (b1, 72, rows1)):
                value = jnp.concatenate(
                    [both[at:at + rows, 0:256], both[at:at + rows, 256:512]], axis=0)
                self.gb[pl.ds(al(base + FU * i + 2 * rows * u, 16), 2 * rows), :] = (
                    value.astype(BF))
            return 0

        lax.fori_loop(0, 4, step, 0)

    def grad_ff(self, g):
        zb = GROUPS[g][1]
        if zb == 2:
            b0, b1 = self.place(g)
            for i in range(3):
                self.grad_wide(g, 8 + i, i)
            self.grad_tall_part(b1, 2, 0, 128, 192)
            self.grad_tall_part(b0, 3, 128, 192, 0)
            self.grad_tall_part(b1, 3, 320, 192, 0)
        else:
            for i in range(4):
                self.grad_wide(g, 4 * zb + i, i)

    def grad_square(self, g, i):
        t, zb = GROUPS[g]
        left = self.memt if t == 1 and zb in (1, 2) else self.tt
        right = ((self.q, self.k, self.v, self.drb), (self.cq, self.ck, self.cv, self.drb))[t][zb]
        b0, b1 = self.place(g)
        rows = left[pl.ds(al(192 * i, 16), 192), :]
        for p in range(3):
            both = nn(rows, right[:, 256 * p:256 * p + 256])
            self.gb[pl.ds(al(b0 + AU * i + 96 * p, 16), 96), :] = both[0:96].astype(BF)
            self.gb[pl.ds(al(b1 + AU * i + 96 * p, 16), 96), :] = both[96:].astype(BF)

    def turn(self, g):
        if g == 1:
            self.n3t[...] = self.n3[...].T
        elif g == 5:
            self.memt[...] = self.mem[...].T
        elif g in (4, 7, 8, 9):
            left = {4: self.cmix, 7: self.n2, 8: self.mix, 9: self.n1}[g]
            self.tt[...] = left[...].T

    def back_product(self, terms, out):
        for p in range(3):
            total = None
            for d_ref, w_ref, row, width in terms:
                value = nt(d_ref[...], w_ref[row + 256 * p:row + 256 * p + 256, 0:width])
                total = value if total is None else total + value
            out[:, 256 * p:256 * p + 256] = total

    def norm_three_back(self):
        self.back_product(((self.dg, self.wgu, 0, FF), (self.du, self.wgu, D, FF)), self.dz)
        dv, dg = rms_back(self.r2[...], self.gains[2:3, :], self.dz[...])
        self.redg[0, 2:3, :] = dg
        self.dr[...] = self.g[...].astype(F32) + dv
        self.drb[...] = self.dr[...].astype(BF)
        for up in (0, 1):
            @pl.when(self.inner(up))
            def _(up=up):
                pl.semaphore_signal(
                    self.free.at[3 - up], inc=1,
                    device_id=self.dev(z=(self.z + (1 if up else 3)) % 4), device_id_type=MESH)

    def cross_back(self, part):
        for p in range(3) if part == 0 else ():
            self.dm[:, 256 * p:256 * p + 256] = nt(
                self.drb[...], self.wc[3 * D + 256 * p:3 * D + 256 * p + 256, :]).astype(BF)

        def pair(p, _):
            cols = pl.ds(al(p * 128, 128), 128)
            dms = self.stack(self.dm[:, cols])
            kp = self.ck[:, cols]
            qs = self.stack(self.cq[:, cols])
            prob = self.cross_probs(p)
            dp = nt(dms, self.cv[:, cols])
            ds = (prob * (dp - jnp.sum(prob * dp, axis=-1, keepdims=True))).astype(BF)
            self.cv[:, cols] = tn(prob.astype(BF), dms).astype(BF)
            self.cq[:, cols] = self.unstack(nn(ds, kp)).astype(BF)
            self.ck[:, cols] = tn(ds, qs).astype(BF)
            return 0

        lax.fori_loop(2 * part, 2 * part + 2, pair, 0)

    def memory_rows(self, i):
        rows = slice(128 * i, 128 * i + 128)
        for p in range(3):
            wrow = 256 * p
            self.mgrad[rows, 256 * p:256 * p + 256] = (
                nt(self.ck[rows, :], self.wc[D + wrow:D + wrow + 256, :])
                + nt(self.cv[rows, :], self.wc[2 * D + wrow:2 * D + wrow + 256, :])
            ).astype(BF)
        self.leave(6 + i, i).start()

    def norm_two_back(self):
        self.back_product(((self.cq, self.wc, 0, D),), self.dz)
        dv, dg = rms_back(self.r1[...], self.gains[1:2, :], self.dz[...])
        self.redg[0, 1:2, :] = dg
        self.dr[...] = self.dr[...] + dv
        self.drb[...] = self.dr[...].astype(BF)

    def self_back(self, part):
        for p in range(3) if part == 0 else ():
            self.dm[:, 256 * p:256 * p + 256] = nt(
                self.drb[...], self.ws[3 * D + 256 * p:3 * D + 256 * p + 256, :]).astype(BF)

        def pair(p, _):
            cols = pl.ds(al(p * 128, 128), 128)
            dms = self.stack(self.dm[:, cols])
            kp = self.k[:, cols]
            qs = self.stack(self.q[:, cols])
            prob = self.ps[self.heads(p), :]
            dp = nt(dms, self.v[:, cols])
            ds = (prob * (dp - jnp.sum(prob * dp, axis=-1, keepdims=True))).astype(BF)
            self.ps[self.heads(p), :] = ds.astype(F32)
            self.v[:, cols] = tn(prob.astype(BF), dms).astype(BF)
            self.q[:, cols] = self.unstack(nn(ds, kp)).astype(BF)
            self.k[:, cols] = tn(ds, qs).astype(BF)
            return 0

        lax.fori_loop(3 * part, 3 * part + 3, pair, 0)

    def norm_one_back(self):
        self.back_product(
            ((self.q, self.ws, 0, D), (self.k, self.ws, D, D), (self.v, self.ws, 2 * D, D)),
            self.dz)
        dv, dg = rms_back(self.x_in[...].astype(F32), self.gains[0:1, :], self.dz[...])
        self.redg[0, 0:1, :] = dg
        self.xgrad[...] = (self.dr[...] + dv).astype(BF)
        self.leave(1).start()

    def table_back(self):
        row = lax.broadcasted_iota(jnp.int32, (128, 128), 0)
        col = lax.broadcasted_iota(jnp.int32, (128, 128), 1)
        flip = jnp.where(row + col == 127, 1.0, 0.0).astype(BF)
        self.diag[...] = jnp.zeros_like(self.diag)
        for p in range(PAIRS):
            back = nn(self.ps[256 * p:256 * p + 256, :].astype(BF), flip)
            for hh in range(2):
                turned = pltpu.roll(
                    back[128 * hh:128 * hh + 128], 0, 1, stride=1, stride_axis=0)
                self.diag[2 * p + hh:2 * p + hh + 1, :] = jnp.sum(turned, axis=0, keepdims=True)
        lane = lax.broadcasted_iota(jnp.int32, (NB, 128), 1)
        hot = jnp.where(
            bucket_of((lane + 1) % 128) == lax.broadcasted_iota(jnp.int32, (NB, 128), 0), 1.0, 0.0)
        self.redt[0, :, 0:NB] = lax.dot_general(
            self.diag[...], hot, (((1,), (1,)), ((), ())),
            precision=lax.Precision.HIGHEST, preferred_element_type=F32)

    def own(self, g, chip, half=None):
        unit = UNIT[g]
        start = OWN[g] + chip * unit
        if half is not None:
            unit = unit // 2
            start = start + half * unit
        return pl.ds(al(start, 16), unit)

    def land(self, g, which, half=None):
        unit = UNIT[g]
        start = LAND[g] + (0, unit // 2, unit, 2 * unit)[which]
        rows = unit // 2 if which < 2 else unit
        if half is not None:
            rows = unit // 2
            start = start + half * rows
        return pl.ds(start, rows)

    def lanes(self, g, mine):
        if not PAIR[g]:
            return slice(None)
        par = self.z % 2
        return pl.ds(al((par if mine else 1 - par) * 128, 128), 128)

    def scopy(self, g, kind):
        gb, lb = self.gb, self.lb
        row = g * 15 + kind
        sems = self.rsend.at[row], self.rrecv.at[row]
        if kind in SIB:
            unit = UNIT[g]
            at = self.chip(*ROLES[SIB.index(kind)]) * unit
            return self.copy(
                gb.at[pl.ds(al(OWN_ROWS + (g % 2) * STAGE + at, 16), unit), :],
                self.wf.at[pl.ds(al(OWN[g] + at, 16), unit), :], *sems, self.dev(fc=1))
        spot, half, lanes, where, dev = {
            1: ((1, 1), 0, True, 0, (1, 0)),
            2: ((1, 1), 1, True, 1, (0, 1)),
            3: ((1, 0), 0, None, 2, (1, 0)),
            4: ((1, 0), 1, True, 2, (1, 0)),
            5: ((1, 0), 1, False, 2, (1, 0)),
            6: ((0, 1), 1, None, 3, (0, 1)),
            7: ((0, 1), 0, True, 3, (0, 1)),
            8: ((0, 1), 0, False, 3, (0, 1)),
            9: ((1, 1), 0, False, 0, None),
            10: ((1, 1), 1, False, 1, None),
        }[kind]
        src = self.own(g, self.chip(*spot), half)
        dst = self.land(g, where, half if where > 1 else None)
        lanes = slice(None) if lanes is None else self.lanes(g, lanes)
        put = self.lanes(g, True) if dev is None else lanes
        dev = self.dev(z=self.z + 1 - 2 * (self.z % 2)) if dev is None else self.dev(None, *dev)
        return self.copy(gb.at[src, lanes], lb.at[dst, put], *sems, dev)

    def came(self, g, *kinds):
        for kind in kinds:
            if kind in (9, 10):
                part = self.lb.at[self.land(g, kind - 9), self.lanes(g, False)]
                row = g * 15 + kind
                self.copy(
                    part, part, self.rsend.at[row], self.rrecv.at[row],
                    self.dev(fc=1)).wait_recv()
            else:
                self.scopy(g, kind).wait_recv()

    def go(self, g, *kinds):
        for kind in kinds:
            self.scopy(g, kind).start()

    def z_land(self, g, second):
        t = GROUPS[g][0]
        if t == 2:
            return self.zb.at[pl.ds((4 if second else g) * FU, FU), :]
        if second:
            return self.wgu.at[AU:2 * AU, 256 * t:256 * t + 256]
        return self.wgu.at[0:AU, 256 * (g - 4):256 * (g - 4) + 256]

    def to_owner(self, g, below, second):
        return self.copy(
            self.gb.at[self.own(g, self.chip()), :], self.z_land(g, second),
            self.rsend.at[g * 15 + 11], self.orecv.at[g * 2 + second],
            self.dev(z=(self.z + (1 if below else 3)) % 4))

    def hop(self, g, stage, act):
        zb = GROUPS[g][1]
        for below in (True, False):
            z = stage if below else 3 - stage
            last = zb - 1 if below else zb + 1
            if not (z <= last if below else z >= last) or not 0 <= last < 4:
                continue

            @pl.when(self.z == z)
            def _(below=below, z=z, last=last):
                act(self.to_owner(g, below, 1 if z == last and not below and zb > 0 else 0))

    def z_came(self, g, second):
        part = self.z_land(g, second)
        self.copy(
            part, part, self.rsend.at[g * 15 + 11], self.orecv.at[g * 2 + second],
            self.dev(fc=1)).wait_recv()
        return part

    def zfree(self):
        for up in (0, 1):
            @pl.when(self.inner(up))
            def _(up=up):
                pl.semaphore_wait(self.free.at[2 + up], 1)

    def ready(self, g):
        self.turn(g)
        if g >= 2:
            for role in range(4):
                self.scopy(g - 2, SIB[role]).wait_send()

    def allowed(self, g):
        if g in (0, 2):
            pl.semaphore_wait(self.free.at[g // 2], 1)

    def part(self, g, i):
        (self.grad_tall if g == 0 else self.grad_square)(g, i)

    def grad(self, g):
        self.ready(g)
        if 0 < g < 4:
            self.grad_ff(g)
        else:
            def step(i, _):
                self.part(g, i)
                return 0
            lax.fori_loop(0, 4, step, 0)
        self.allowed(g)
        self.go(g, *SIB)

    def grad_role(self, g, role):
        if role == 0:
            self.ready(g)
        self.part(g, self.chip(*ROLES[role]))
        if role == 0:
            self.allowed(g)
        self.go(g, SIB[role])

    def accumulate(self, dst, lanes, src_ref, src, from_lanes):
        self.gb[dst, lanes] = (
            self.gb[dst, lanes].astype(F32) + src_ref[src, from_lanes].astype(F32)).astype(BF)

    def rs1(self, g, role):
        self.came(g, SIB[role])
        rows = self.own(g, self.chip(*ROLES[role]))
        self.accumulate(rows, slice(None), self.wf, rows, slice(None))
        self.go(g, *(((9, 10), (3, 5), (6, 8), ()) if PAIR[g] else ((1, 2), (3,), (6,), ()))[role])

    def rs2(self, g, half):
        if PAIR[g]:
            self.came(g, 9 + half)
            self.accumulate(
                self.own(g, self.chip(1, 1), half), self.lanes(g, True),
                self.lb, self.land(g, half), self.lanes(g, False))
            self.go(g, 1 + half)

    def rs3(self, g, half):
        kind, spot, late = ((1, (0, 1), 7), (2, (1, 0), 4))[half]
        self.came(g, kind)
        self.accumulate(
            self.own(g, self.chip(*spot), half), self.lanes(g, True),
            self.lb, self.land(g, kind - 1), self.lanes(g, True))
        self.go(g, late)

    def rs4(self, g):
        self.came(g, *((3, 5, 6, 8, 4, 7) if PAIR[g] else (3, 6, 4, 7)))
        rows = self.own(g, self.chip())
        self.gb[rows, :] = (
            self.gb[rows, :].astype(F32) + self.lb[self.land(g, 2), :].astype(F32)
            + self.lb[self.land(g, 3), :].astype(F32)).astype(BF)

    def rsz(self, g, stage):
        def act(copy):
            if stage:
                part = self.z_came(g, 0)
                everything = slice(None)
                self.accumulate(
                    self.own(g, self.chip()), everything, part, everything, everything)
            copy.start()

        self.hop(g, stage, act)

    def rs5(self, g):
        t, zb = GROUPS[g]
        unit = UNIT[g]

        @pl.when(self.z == zb)
        def _():
            places = (0, 1) if 0 < zb < 3 else (0,)
            parts = [self.z_came(g, second) for second in places]

            def total(start, size, lanes):
                at = pl.ds(al(OWN[g] + self.chip() * unit + start, 16), size)
                value = self.gb[at, lanes].astype(F32)
                for part in parts:
                    value = value + part[pl.ds(start, size), lanes].astype(F32)
                return value

            if t < 2:
                out = (self.gs, self.gc)[t]
                for k in range(6):
                    out[pl.ds(k, AR, stride=6), :] = total(
                        96 * (k // 2), 96, slice(128 * (k % 2), 128 * (k % 2) + 128))
                self.leave(3 + t).start()
                return
            out = self.gf

            def wide(rows):
                for u in range(4):
                    for w in range(2):
                        v = total(2 * rows * u, 2 * rows, slice(128 * w, 128 * w + 128))
                        out[pl.ds(4 * u + w, rows, stride=16), :] = v[0:rows]
                        out[pl.ds(4 * u + w + 2, rows, stride=16), :] = v[rows:]

            def tall(first, rows, offset):
                for k in range(6):
                    out[pl.ds(first + k, rows, stride=6), :] = total(
                        offset + rows * (k // 2), rows, slice(128 * (k % 2), 128 * (k % 2) + 128))

            if zb < 2:
                wide(72)
            elif zb == 3:
                tall(0, 192, 0)
            else:
                @pl.when(self.shard < 21)
                def _():
                    wide(72)

                @pl.when(self.shard == 21)
                def _():
                    wide(24)
                    tall(384, 128, 192)

                @pl.when(self.shard > 21)
                def _():
                    tall(0, 192, 0)

            self.leave(5).start()

    def group_sent(self, g):
        for kind in range(1, 11):
            if PAIR[g] or kind not in (5, 8, 9, 10):
                self.scopy(g, kind).wait_send()

        for stage in range(3):
            self.hop(g, stage, lambda copy: copy.wait_send())

    def small(self, step, which):
        dev = (
            self.dev(fc=1), self.dev(fx=1), self.dev(fy=1),
            self.dev(z=self.z + 1 - 2 * (self.z % 2)), self.dev(z=(self.z + 2) % 4),
        )[step]
        src, dst = ((self.redg, self.landg), (self.redt, self.landt))[which]
        row = step * 2 + which
        return self.copy(
            src.at[step], dst.at[step], self.ssend.at[row], self.srecv.at[row], dev)

    def small_start(self, step):
        for which in range(2):
            self.small(step, which).start()

    def small_add(self, step):
        for which in range(2):
            self.small(step, which).wait_recv()
        self.redg[step + 1] = self.redg[step] + self.landg[step]
        self.redt[step + 1] = self.redt[step] + self.landt[step]


    def finish(self):
        for tensor in (0, 1):
            for k in range(4):
                self.plane_sent(tensor, k)
                self.z_sent(tensor, k)
        for g in range(12):
            self.group_sent(g)
        for g in (10, 11):
            for role in range(4):
                self.scopy(g, SIB[role]).wait_send()
        for i in (0, 1, 3, 4, 5):
            self.leave(i).wait()
        for i in range(4):
            self.leave(6 + i, i).wait()
        self.ggain[...] = self.redga[5, 0:3, :]
        self.gtable[...] = self.redta[5, 0:H, 0:NB]
        for step in range(5):
            for which in range(2):
                self.small(step, which).wait_send()


K = Layer
SCHEDULE = (
    (K.own_z, 0, 0), (K.own_xy, 0), (K.own_z, 0, 1), (K.own_square, 1), (K.own_xy, 1),
    (K.own_z, 1, 0), (K.own_z, 1, 1), (K.p1, 0, 1), (K.own_ff,), (K.own_z, 2, 0),
    (K.own_z, 2, 1), (K.p2x, 1, 0), (K.p1, 1, 1), (K.p2y, 0, 1), (K.p2x, 0, 0), (K.p2x, 0, 1),
    (K.p2y, 0, 0), (K.p1, 0, 3), (K.p1, 0, 2), (K.p1, 1, 2), (K.p2y, 1, 1), (K.p2x, 1, 1),
    (K.p1, 1, 3), (K.p2x, 0, 3), (K.p2y, 1, 0), (K.p2y, 0, 3), (K.p2x, 0, 2), (K.p2y, 0, 2),
    (K.p1, 2, 2), (K.p3, 0, 1, 0), (K.p3, 0, 0, 0), (K.p3, 1, 1, 0), (K.p3, 0, 1, 1),
    (K.p3, 0, 0, 1), (K.p3, 1, 0, 0), (K.p2x, 1, 2), (K.p2y, 1, 2), (K.p3, 1, 1, 1),
    (K.p1, 2, 1), (K.p1, 2, 0), (K.p3, 1, 0, 1), (K.p3, 0, 3, 0), (K.p3, 0, 2, 0),
    (K.p2y, 1, 3), (K.p3, 0, 2, 1), (K.p3, 0, 3, 1), (K.p2x, 1, 3), (K.p4, 0, 0), (K.p4, 0, 1),
    (K.p2y, 2, 2), (K.p3, 1, 2, 0), (K.p2x, 2, 2), (K.p1, 2, 3), (K.p4, 0, 3), (K.p3, 1, 2, 1),
    (K.p5, 0, 0), (K.p3, 1, 3, 0), (K.p4, 1, 0), (K.p4, 1, 1), (K.p3, 1, 3, 1), (K.p5, 0, 1),
    (K.p2x, 2, 1), (K.p4, 0, 2), (K.p5, 0, 3), (K.p3, 2, 2, 0), (K.p2y, 2, 1), (K.p2x, 2, 0),
    (K.p5, 0, 2), (K.p3, 2, 2, 1), (K.bias,), (K.self_forward,), (K.p4, 1, 2), (K.p2y, 2, 0),
    (K.p4, 1, 3), (K.p2x, 2, 3), (K.p2y, 2, 3), (K.p3, 2, 1, 0), (K.p5, 1, 1), (K.p4, 2, 2),
    (K.p3, 2, 1, 1), (K.p5, 1, 2), (K.p5, 1, 3), (K.p5, 1, 0), (K.cross_kv, 1), (K.cross_kv, 2),
    (K.p3, 2, 0, 0), (K.cross_forward, 0), (K.p3, 2, 0, 1), (K.p3, 2, 3, 0), (K.p3, 2, 3, 1),
    (K.p5, 2, 2), (K.p4, 2, 1), (K.cross_forward, 1), (K.p4, 2, 0), (K.build_plane, 2),
    (K.cross_forward, 2), (K.p5, 2, 1), (K.build_plane, 1), (K.p5, 2, 0), (K.build_plane, 0),
    (K.ff_gate,), (K.ff_up,), (K.credit, 0), (K.p4, 2, 3), (K.grad_role, 0, 0),
    (K.grad_role, 0, 1), (K.grad_role, 0, 2), (K.grad_role, 0, 3), (K.p5, 2, 3),
    (K.build_plane, 3), (K.rs1, 0, 0), (K.d_hidden, 0), (K.rs1, 0, 1), (K.d_hidden, 1),
    (K.credit, 1), (K.rs1, 0, 2), (K.grad, 1), (K.grad, 2), (K.rs2, 0, 0), (K.rs1, 1, 0),
    (K.rs2, 0, 1), (K.rs1, 1, 1), (K.rs1, 1, 2), (K.grad, 3), (K.rs1, 2, 0),
    (K.norm_three_back,), (K.rs1, 2, 3), (K.rs3, 0, 1), (K.rs1, 3, 1), (K.rs3, 0, 0),
    (K.rs1, 3, 2), (K.cross_back, 0), (K.rs2, 1, 1), (K.grad_role, 4, 0), (K.grad_role, 4, 1),
    (K.cross_back, 1), (K.grad_role, 4, 2), (K.rs2, 2, 0), (K.rs1, 3, 0), (K.rs2, 1, 0),
    (K.cross_back, 2), (K.rs2, 2, 1), (K.rs1, 2, 1), (K.rs1, 0, 3), (K.grad_role, 4, 3),
    (K.rs1, 4, 0), (K.rs4, 0), (K.rs1, 2, 2), (K.grad, 5), (K.rsz, 0, 0), (K.rs3, 2, 0),
    (K.grad, 6), (K.rs3, 2, 1), (K.rs1, 5, 0), (K.rs3, 1, 1), (K.rs2, 3, 0), (K.grad, 7),
    (K.rs1, 6, 0), (K.rs2, 3, 1), (K.rs2, 4, 0), (K.rs3, 1, 0), (K.rs1, 5, 1),
    (K.norm_two_back,), (K.rs1, 7, 0), (K.rsz, 0, 1), (K.rs1, 4, 2), (K.rs4, 2), (K.rsz, 2, 0),
    (K.grad, 8), (K.self_back, 0), (K.rs3, 3, 0), (K.rs3, 3, 1), (K.rs2, 5, 0),
    (K.self_back, 1), (K.grad_role, 9, 0), (K.rs2, 4, 1), (K.rs1, 6, 3), (K.rs2, 7, 0),
    (K.rs3, 4, 0), (K.zfree,), (K.rs1, 8, 0), (K.rs1, 7, 1), (K.rs1, 1, 3), (K.rs1, 3, 3),
    (K.rs2, 5, 1), (K.rs1, 4, 3), (K.rs1, 9, 0), (K.rs1, 7, 2), (K.rs1, 5, 2), (K.rs1, 4, 1),
    (K.rs4, 3), (K.rsz, 3, 0), (K.rs1, 8, 3), (K.rs4, 1), (K.rs1, 8, 1), (K.rs2, 7, 1),
    (K.rsz, 0, 2), (K.rsz, 2, 1), (K.rs1, 8, 2), (K.rsz, 1, 0), (K.table_back,),
    (K.memory_rows, 1), (K.rs3, 5, 0), (K.rs3, 5, 1), (K.norm_one_back,), (K.rs3, 4, 1),
    (K.rs2, 6, 1), (K.rs2, 8, 0), (K.small_start, 0), (K.memory_rows, 0), (K.rs2, 9, 0),
    (K.small_add, 0), (K.rs2, 8, 1), (K.rs2, 6, 0), (K.rs3, 7, 0), (K.grad_role, 9, 1),
    (K.grad_role, 9, 2), (K.grad_role, 9, 3), (K.grad_role, 10, 0), (K.grad_role, 10, 1),
    (K.grad_role, 10, 2), (K.grad_role, 10, 3), (K.grad_role, 11, 0), (K.small_start, 1),
    (K.rs4, 4), (K.grad_role, 11, 1), (K.rs3, 7, 1), (K.grad_role, 11, 2), (K.rs1, 7, 3),
    (K.rs2, 9, 1), (K.rs1, 10, 0), (K.rs2, 10, 1), (K.rs1, 5, 3), (K.grad_role, 11, 3),
    (K.rsz, 2, 2), (K.rsz, 3, 1), (K.small_add, 1), (K.small_start, 2), (K.rs3, 8, 1),
    (K.rsz, 1, 1), (K.rsz, 4, 0), (K.rs2, 10, 0), (K.rs1, 9, 1), (K.rs1, 11, 3), (K.rs4, 5),
    (K.rs1, 9, 3), (K.rs3, 8, 0), (K.rs1, 11, 0), (K.rs1, 9, 2), (K.memory_rows, 2),
    (K.rs2, 11, 0), (K.rs3, 9, 0), (K.rs1, 6, 2), (K.rs1, 10, 3), (K.rs4, 7), (K.rsz, 7, 0),
    (K.rsz, 4, 1), (K.small_add, 2), (K.rs3, 9, 1), (K.rsz, 5, 0), (K.rs2, 11, 1),
    (K.rs1, 6, 1), (K.rs3, 6, 1), (K.rs1, 11, 1), (K.rs4, 8), (K.small_start, 3), (K.rsz, 7, 1),
    (K.rs3, 6, 0), (K.rsz, 8, 0), (K.rs1, 11, 2), (K.rsz, 7, 2), (K.rs3, 11, 0), (K.rsz, 8, 1),
    (K.rs1, 10, 2), (K.rs5, 1), (K.rs4, 9), (K.rsz, 9, 0), (K.rsz, 9, 1), (K.rsz, 5, 1),
    (K.memory_rows, 3), (K.rs5, 2), (K.rs3, 11, 1), (K.small_add, 3), (K.rs5, 0),
    (K.small_start, 4), (K.out_rows,), (K.rs4, 6), (K.rs1, 10, 1), (K.rs3, 10, 0),
    (K.rsz, 6, 0), (K.rs3, 10, 1), (K.rsz, 4, 2), (K.rs5, 3), (K.rsz, 6, 1), (K.rs4, 11),
    (K.rsz, 11, 0), (K.rsz, 8, 2), (K.rsz, 11, 1), (K.rs4, 10), (K.rs5, 5), (K.rsz, 9, 2),
    (K.rsz, 10, 0), (K.rsz, 10, 1), (K.rs5, 9), (K.rs5, 4), (K.rs5, 8), (K.small_add, 4),
    (K.rs5, 6), (K.rs5, 7), (K.rs5, 10), (K.rs5, 11),
)

NAMES = (
    "x_hbm", "mem_hbm", "g_hbm", "dl", "ml", "sh_s_hbm", "sh_c_hbm", "sh_f_hbm", "gains", "table",
    "block_hbm", "xgrad_hbm", "mgrad_hbm", "gs_hbm", "gc_hbm", "gf_hbm", "ggain", "gtable",
    "x_in", "mem", "g", "sh_s", "sh_c", "sh_f", "block", "xgrad", "mgrad", "gs", "gc", "gf",
    "isem", "osem",
    "ws", "wc", "wf", "wgu", "wd", "gb", "lb", "zb",
    "n1", "q", "k", "v", "mix", "r1", "n2", "cq", "ck", "cv", "cmix", "r2", "n3",
    "ga", "ub", "hid", "hidt", "n3t", "dg", "du", "dz", "dr", "drb", "tt", "memt",
    "ps", "diag", "redga", "redta", "landg", "landt",
    "gsend", "grecv", "zsend", "zrecv", "rsend", "rrecv", "orecv", "ssend", "srecv", "free",
)


def kernel(*args):
    st = Layer(dict(zip(NAMES, args)))
    st.redg, st.redt = st.redga, st.redta
    barrier = pltpu.get_barrier_semaphore()
    others = [st.dev(fc=1), st.dev(fx=1), st.dev(fy=1)] + [
        st.dev(z=(st.z + k) % 4) for k in (1, 2, 3)]
    for other in others:
        pl.semaphore_signal(barrier, inc=1, device_id=other, device_id_type=MESH)
    for i in range(6):
        st.enter(i).start()
    st.own_square(0)
    st.masks()
    pl.semaphore_wait(barrier, 6)
    for step, *numbers in SCHEDULE:
        step(st, *numbers)
    st.finish()


def settle_kernel(count, *refs):
    src, dst, held = refs[:count], refs[count:2 * count], refs[2 * count:3 * count]
    arrive, go = refs[3 * count:]
    into = [pltpu.make_async_copy(src[i], held[i], arrive.at[i]) for i in range(count)]
    out = [pltpu.make_async_copy(held[i], dst[i], go.at[i]) for i in range(count)]
    for one in into:
        one.start()
    for first, then in zip(into, out):
        first.wait()
        then.start()
    for one in out:
        one.wait()


def settle(arrays):
    anywhere = pl.BlockSpec(memory_space=pl.ANY)
    count = len(arrays)
    return pl.pallas_call(
        functools.partial(settle_kernel, count),
        out_shape=tuple(jax.ShapeDtypeStruct(v.shape, v.dtype) for v in arrays),
        in_specs=[anywhere] * count,
        out_specs=tuple([anywhere] * count),
        scratch_shapes=[pltpu.VMEM(v.shape, v.dtype) for v in arrays] + [
            pltpu.SemaphoreType.DMA((count,)), pltpu.SemaphoreType.DMA((count,))],
        compiler_params=pltpu.CompilerParams(vmem_limit_bytes=67000000),
    )(*arrays)


def fused(inputs, memory, out_cotangent, dec_lengths, mem_lengths, self_params, cross_params,
          ff_params, gains, table):
    slots, length, width = inputs.shape
    mem_len = memory.shape[1]
    hbm = pl.BlockSpec(memory_space=pl.ANY)
    vm = pl.BlockSpec(memory_space=pltpu.VMEM)
    sm = pl.BlockSpec(memory_space=pltpu.SMEM)
    s = jax.ShapeDtypeStruct
    rows_s, rows_f = self_params.shape[0] // 128, ff_params.shape[0] // 128
    row = pltpu.VMEM((length, D), BF)
    rowf = pltpu.VMEM((length, D), F32)
    memory_row = pltpu.VMEM((mem_len, D), BF)
    dma = pltpu.SemaphoreType.DMA
    outs = pl.pallas_call(
        kernel,
        out_shape=(
            s((length, D), BF), s((length, D), BF), s((mem_len, D), BF),
            s((rows_s, 128), F32), s((rows_s, 128), F32), s((rows_f, 128), F32),
            s((3, D), F32), s((H, NB), F32),
        ),
        in_specs=[hbm, hbm, hbm, sm, sm, hbm, hbm, hbm, vm, sm],
        out_specs=[hbm] * 6 + [vm] * 2,
        scratch_shapes=[
            row, memory_row, row, pltpu.VMEM((rows_s, 128), BF), pltpu.VMEM((rows_s, 128), BF),
            pltpu.VMEM((rows_f, 128), BF), row, row, memory_row,
            pltpu.VMEM((rows_s, 128), F32), pltpu.VMEM((rows_s, 128), F32),
            pltpu.VMEM((rows_f, 128), F32), dma((6,)), dma((10,)),
            pltpu.VMEM((4 * D, D), BF), pltpu.VMEM((4 * D, D), BF),
            pltpu.VMEM((32 * FU, 256), BF),
            pltpu.VMEM((2 * D, FF), BF), pltpu.VMEM((FF, D), BF),
            pltpu.VMEM((OWN_ROWS + 2 * STAGE, 256), BF),
            pltpu.VMEM((LAND_ROWS, 256), BF), pltpu.VMEM((Z_ROWS, 256), BF),
            row, row, row, row, row, rowf, row, row, memory_row, memory_row, row, rowf, row,
            pltpu.VMEM((length, FF), F32), pltpu.VMEM((length, FF), F32),
            pltpu.VMEM((length, FF), BF), pltpu.VMEM((FF, length), BF),
            pltpu.VMEM((D, length), BF),
            pltpu.VMEM((length, FF), BF), pltpu.VMEM((length, FF), BF),
            rowf, rowf, row, pltpu.VMEM((D, length), BF), pltpu.VMEM((D, mem_len), BF),
            pltpu.VMEM((H * length, length), F32),
            pltpu.VMEM((16, 128), F32),
            pltpu.VMEM((6, 8, D), F32), pltpu.VMEM((6, 16, 128), F32),
            pltpu.VMEM((5, 8, D), F32), pltpu.VMEM((5, 16, 128), F32),
            dma((120,)), dma((120,)), dma((24,)), dma((12,)), dma((180,)), dma((180,)), dma((24,)),
            dma((10,)), dma((10,)), pltpu.SemaphoreType.REGULAR((4,)),
        ],
        compiler_params=pltpu.CompilerParams(
            collective_id=0, has_side_effects=True, vmem_limit_bytes=67000000),
        cost_estimate=pl.CostEstimate(
            flops=10_000_000_000, bytes_accessed=8_000_000, transcendentals=2_000_000),
    )(
        inputs.reshape(length, width), memory.reshape(mem_len, width),
        out_cotangent.reshape(length, width), dec_lengths, mem_lengths,
        self_params.reshape(rows_s, 128), cross_params.reshape(rows_s, 128),
        ff_params.reshape(rows_f, 128), gains, table.T,
    )
    outs = settle(outs)
    return (
        outs[0].reshape(inputs.shape), outs[1].reshape(inputs.shape),
        outs[2].reshape(memory.shape), outs[3].reshape(-1), outs[4].reshape(-1),
        outs[5].reshape(-1), outs[6], outs[7].T,
    )


HIGHEST = lax.Precision.HIGHEST


def product(left, right):
    return jnp.dot(left, right, preferred_element_type=jnp.float32)


def product_t(left, right):
    return lax.dot_general(
        left, right, (((0,), (0,)), ((), ())), preferred_element_type=jnp.float32
    )


def product_nt(left, right):
    return lax.dot_general(
        left, right, (((1,), (1,)), ((), ())), preferred_element_type=jnp.float32
    )


def rms_scale(value, gain):
    return value * lax.rsqrt(jnp.mean(value * value, axis=-1, keepdims=True) + 1e-06) * gain


def gelu_gate(gate_pre, up_pre):
    return jax.nn.gelu(gate_pre, approximate=True) * up_pre


def bucket_rows(start, count, length):
    half_count = NB // 2
    limits = np.ceil(
        half_count * (MAXD / half_count) ** (np.arange(1, half_count) / half_count)
    ).astype(np.int32)
    query_pos = start + jnp.arange(count, dtype=jnp.int32)
    key_pos = jnp.arange(length, dtype=jnp.int32)
    distance = query_pos[:, None] - key_pos[None, :]
    beyond = half_count + jnp.sum(
        (distance[None] >= jnp.asarray(limits)[:, None, None]).astype(jnp.int32), axis=0
    )
    return jnp.where(distance < half_count, jnp.maximum(distance, 0), beyond)


def onehot_block(start, count, length):
    bucket = bucket_rows(start, count, length)
    hot_rows = jnp.arange(NB, dtype=jnp.int32)[:, None, None] == bucket[None]
    return hot_rows.astype(jnp.float32).reshape(NB, count * length)


def position_bias(table, length):
    block_rows = min(length, 128)
    block_count = length // block_rows

    def position_per_block(block):
        bucket_hot = onehot_block(block * block_rows, block_rows, length)
        return lax.dot_general(
            table,
            bucket_hot,
            (((0,), (0,)), ((), ())),
            precision=HIGHEST,
            preferred_element_type=jnp.float32,
        )

    pieces = lax.map(position_per_block, jnp.arange(block_count, dtype=jnp.int32))
    return (
        pieces.reshape(block_count, H, block_rows, length)
        .transpose(1, 0, 2, 3)
        .reshape(H, length, length)
    )


def table_gradient(score_sums, length):
    block_rows = min(length, 128)

    def table_per_block(carry, block):
        ds_piece = score_sums.reshape(H, block_rows * length)
        bucket_hot = onehot_block(block * block_rows, block_rows, length)
        return (
            carry
            + lax.dot_general(
                bucket_hot,
                ds_piece,
                (((1,), (1,)), ((), ())),
                precision=HIGHEST,
                preferred_element_type=jnp.float32,
            ),
            None,
        )

    result, _ = lax.scan(
        table_per_block,
        jnp.zeros((NB, H), jnp.float32),
        jnp.arange(length // block_rows, dtype=jnp.int32),
    )
    return result


def score_block(queries, keys_in, score_bias, keep_mask):
    q_len = queries.shape[0]
    k_len = keys_in.shape[0]
    raw_scores = (
        jnp.einsum(
            "qhe,khe->hqk",
            queries.reshape(q_len, H, DH),
            keys_in.reshape(k_len, H, DH),
            preferred_element_type=jnp.float32,
        )
        + score_bias
    )
    return jnp.where(keep_mask[None], raw_scores, MASKED)


def attend_forward(queries, keys_in, values, score_bias, keep_mask):
    q_len = queries.shape[0]
    k_len = keys_in.shape[0]
    raw_scores = score_block(queries, keys_in, score_bias, keep_mask)
    row_max = jnp.max(raw_scores, axis=2, keepdims=True)
    exponent = jnp.exp(raw_scores - row_max)
    row_sum = jnp.sum(exponent, axis=2, keepdims=True)
    softmax_low = (exponent / row_sum).astype(jnp.bfloat16)
    head_mix = jnp.einsum(
        "hqk,khe->qhe",
        softmax_low,
        values.reshape(k_len, H, DH),
        preferred_element_type=jnp.float32,
    )
    return (head_mix.reshape(q_len, H * DH).astype(jnp.bfloat16), row_max, row_sum)


def attend_backward(queries, keys_in, values, score_bias, keep_mask, row_max, row_sum, d_mix):
    q_len = queries.shape[0]
    k_len = keys_in.shape[0]
    raw_scores = score_block(queries, keys_in, score_bias, keep_mask)
    softmax_out = jnp.exp(raw_scores - row_max) / row_sum
    softmax_low = softmax_out.astype(jnp.bfloat16)
    mix_heads = d_mix.reshape(q_len, H, DH)
    q_heads = queries.reshape(q_len, H, DH)
    k_heads = keys_in.reshape(k_len, H, DH)
    v_heads = values.reshape(k_len, H, DH)
    d_softmax = jnp.einsum("qhe,khe->hqk", mix_heads, v_heads, preferred_element_type=jnp.float32)
    d_scores = (
        softmax_out * (d_softmax - jnp.sum(softmax_out * d_softmax, axis=2, keepdims=True))
    ).astype(jnp.bfloat16)
    d_values = (
        jnp.einsum("hqk,qhe->khe", softmax_low, mix_heads, preferred_element_type=jnp.float32)
        .reshape(k_len, H * DH)
        .astype(jnp.bfloat16)
    )
    d_queries = (
        jnp.einsum("hqk,khe->qhe", d_scores, k_heads, preferred_element_type=jnp.float32)
        .reshape(q_len, H * DH)
        .astype(jnp.bfloat16)
    )
    d_keys = (
        jnp.einsum("hqk,qhe->khe", d_scores, q_heads, preferred_element_type=jnp.float32)
        .reshape(k_len, H * DH)
        .astype(jnp.bfloat16)
    )
    return (d_queries, d_keys, d_values, d_scores)


def attend_slots(queries, keys_in, values, lengths, score_bias, base_mask):
    slot_count = lengths.shape[0]
    q_len = queries.shape[0] // slot_count
    k_len = keys_in.shape[0] // slot_count
    key_pos = jnp.arange(k_len, dtype=jnp.int32)

    def per_slot(slot_item):
        q_slot, k_slot, v_slot, slot_len = slot_item
        keep_mask = base_mask & (key_pos[None, :] < slot_len)
        return attend_forward(q_slot, k_slot, v_slot, score_bias, keep_mask)

    head_mix, row_max, row_sum = lax.map(
        per_slot,
        (
            queries.reshape(slot_count, q_len, -1),
            keys_in.reshape(slot_count, k_len, -1),
            values.reshape(slot_count, k_len, -1),
            lengths,
        ),
    )
    return (head_mix.reshape(slot_count * q_len, -1), row_max, row_sum)


def attend_back_slots(
    queries, keys_in, values, lengths, score_bias, base_mask, row_max, row_sum, d_mix, with_table
):
    slot_count = lengths.shape[0]
    q_len = queries.shape[0] // slot_count
    k_len = keys_in.shape[0] // slot_count
    key_pos = jnp.arange(k_len, dtype=jnp.int32)
    if with_table:
        start = jnp.zeros((H, q_len, k_len), jnp.float32)
    else:
        start = jnp.zeros((), jnp.float32)

    def per_slot(carry, slot_item):
        q_slot, k_slot, v_slot, slot_len, max_slot, sum_slot, dmix_slot = slot_item
        keep_mask = base_mask & (key_pos[None, :] < slot_len)
        d_queries, d_keys, d_values, d_scores = attend_backward(
            q_slot, k_slot, v_slot, score_bias, keep_mask, max_slot, sum_slot, dmix_slot
        )
        if with_table:
            carry = carry + d_scores.astype(jnp.float32)
        return (carry, (d_queries, d_keys, d_values))

    score_sums, grad_parts = lax.scan(
        per_slot,
        start,
        (
            queries.reshape(slot_count, q_len, -1),
            keys_in.reshape(slot_count, k_len, -1),
            values.reshape(slot_count, k_len, -1),
            lengths,
            row_max,
            row_sum,
            d_mix.reshape(slot_count, q_len, -1),
        ),
    )
    return (
        grad_parts[0].reshape(slot_count * q_len, -1),
        grad_parts[1].reshape(slot_count * k_len, -1),
        grad_parts[2].reshape(slot_count * k_len, -1),
        score_sums,
    )


def gather_weights(self_params, cross_params, ff_params):
    return (
        lax.all_gather(self_params, ("dp", "fsdp"), axis=0, tiled=True),
        lax.all_gather(cross_params, ("dp", "fsdp"), axis=0, tiled=True),
        lax.all_gather(ff_params, ("dp", "fsdp"), axis=0, tiled=True),
    )


def scatter_grads(self_full, cross_full, ff_full):
    wide_count = lax.axis_size("dp")
    spread = (
        lax.all_to_all(
            self_full.reshape(wide_count, -1).astype(jnp.bfloat16),
            "dp",
            split_axis=0,
            concat_axis=0,
            tiled=True,
        ).astype(jnp.float32),
        lax.all_to_all(
            cross_full.reshape(wide_count, -1).astype(jnp.bfloat16),
            "dp",
            split_axis=0,
            concat_axis=0,
            tiled=True,
        ).astype(jnp.float32),
        lax.all_to_all(
            ff_full.reshape(wide_count, -1).astype(jnp.bfloat16),
            "dp",
            split_axis=0,
            concat_axis=0,
            tiled=True,
        ).astype(jnp.float32),
    )
    self_block = jnp.sum(spread[0], axis=0)
    cross_block = jnp.sum(spread[1], axis=0)
    ff_block = jnp.sum(spread[2], axis=0)
    return (
        lax.psum_scatter(
            self_block.astype(jnp.bfloat16), "fsdp", scatter_dimension=0, tiled=True
        ).astype(jnp.float32),
        lax.psum_scatter(
            cross_block.astype(jnp.bfloat16), "fsdp", scatter_dimension=0, tiled=True
        ).astype(jnp.float32),
        lax.psum_scatter(
            ff_block.astype(jnp.bfloat16), "fsdp", scatter_dimension=0, tiled=True
        ).astype(jnp.float32),
    )


def unpack(weights):
    self_flat, cross_flat, ff_flat = weights
    self_mats = self_flat.reshape(4, D, D)
    cross_mats = cross_flat.reshape(4, D, D)
    block_size = D * FF
    return (
        self_mats[0],
        self_mats[1],
        self_mats[2],
        self_mats[3],
        cross_mats[0],
        cross_mats[1],
        cross_mats[2],
        cross_mats[3],
        ff_flat[:block_size].reshape(D, FF),
        ff_flat[block_size : 2 * block_size].reshape(D, FF),
        ff_flat[2 * block_size :].reshape(FF, D),
    )


def run_forward(
    weights, flat_in, flat_mem, gains, pos_bias, causal, open_mask, dec_lengths, mem_lengths
):
    w_sq, w_sk, w_sv, w_so, w_cq, w_ck, w_cv, w_co, w_gate, w_up, w_down = unpack(weights)
    norm_one = rms_scale(flat_in, gains[0]).astype(jnp.bfloat16)
    self_q = product(norm_one, w_sq).astype(jnp.bfloat16)
    self_k = product(norm_one, w_sk).astype(jnp.bfloat16)
    self_v = product(norm_one, w_sv).astype(jnp.bfloat16)
    self_mix, self_max, self_sum = attend_slots(
        self_q, self_k, self_v, dec_lengths, pos_bias, causal
    )
    resid_one = flat_in + product(self_mix, w_so)
    norm_two = rms_scale(resid_one, gains[1]).astype(jnp.bfloat16)
    cross_q = product(norm_two, w_cq).astype(jnp.bfloat16)
    cross_k = product(flat_mem, w_ck).astype(jnp.bfloat16)
    cross_v = product(flat_mem, w_cv).astype(jnp.bfloat16)
    cross_mix, cross_max, cross_sum = attend_slots(
        cross_q, cross_k, cross_v, mem_lengths, 0.0, open_mask
    )
    resid_two = resid_one + product(cross_mix, w_co)
    norm_three = rms_scale(resid_two, gains[2]).astype(jnp.bfloat16)
    gate_pre = product(norm_three, w_gate)
    up_pre = product(norm_three, w_up)
    hidden = gelu_gate(gate_pre, up_pre).astype(jnp.bfloat16)
    block = resid_two + product(hidden, w_down)
    return (
        norm_one,
        self_q,
        self_k,
        self_v,
        self_mix,
        self_max,
        self_sum,
        resid_one,
        norm_two,
        cross_q,
        cross_k,
        cross_v,
        cross_mix,
        cross_max,
        cross_sum,
        resid_two,
        norm_three,
        gate_pre,
        up_pre,
        hidden,
        block,
    )


def by_collectives(
    inputs,
    memory,
    out_cotangent,
    dec_lengths,
    mem_lengths,
    self_params,
    cross_params,
    ff_params,
    gains,
    table,
):
    slot_count, length, model_width = inputs.shape
    mem_len = memory.shape[1]
    row_count = slot_count * length
    pos_bias = position_bias(table, length)
    positions = jnp.arange(length, dtype=jnp.int32)
    causal = positions[None, :] <= positions[:, None]
    open_mask = jnp.ones((length, mem_len), dtype=bool)
    flat_in = inputs.reshape(row_count, model_width).astype(jnp.float32)
    flat_mem = memory.reshape(slot_count * mem_len, model_width)
    weights = gather_weights(self_params, cross_params, ff_params)
    first_pass = run_forward(
        weights, flat_in, flat_mem, gains, pos_bias, causal, open_mask, dec_lengths, mem_lengths
    )
    block_out = first_pass[20].astype(jnp.bfloat16).reshape(slot_count, length, model_width)
    again = gather_weights(self_params, cross_params, ff_params)
    w_sq, w_sk, w_sv, w_so, w_cq, w_ck, w_cv, w_co, w_gate, w_up, w_down = unpack(again)
    (
        norm_one,
        self_q,
        self_k,
        self_v,
        self_mix,
        self_max,
        self_sum,
        resid_one,
        norm_two,
        cross_q,
        cross_k,
        cross_v,
        cross_mix,
        cross_max,
        cross_sum,
        resid_two,
        norm_three,
        gate_pre,
        up_pre,
        hidden,
        _,
    ) = run_forward(
        again, flat_in, flat_mem, gains, pos_bias, causal, open_mask, dec_lengths, mem_lengths
    )
    d_out = out_cotangent.reshape(row_count, model_width)
    grad_down = product_t(hidden, d_out)
    d_hidden = product_nt(d_out, w_down).astype(jnp.bfloat16)
    _, pull_gate = jax.vjp(gelu_gate, gate_pre, up_pre)
    d_gate, d_up = pull_gate(d_hidden.astype(jnp.float32))
    d_gate = d_gate.astype(jnp.bfloat16)
    d_up = d_up.astype(jnp.bfloat16)
    grad_gate = product_t(norm_three, d_gate)
    grad_up = product_t(norm_three, d_up)
    d_norm_three = product_nt(d_gate, w_gate) + product_nt(d_up, w_up)
    _, pull_three = jax.vjp(rms_scale, resid_two, gains[2])
    d_from_three, grad_gain_three = pull_three(d_norm_three)
    d_resid_two = d_out.astype(jnp.float32) + d_from_three
    d_cross = d_resid_two.astype(jnp.bfloat16)
    grad_co = product_t(cross_mix, d_cross)
    d_cross_mix = product_nt(d_cross, w_co).astype(jnp.bfloat16)
    dq_cross, dk_cross, dv_cross, _ = attend_back_slots(
        cross_q,
        cross_k,
        cross_v,
        mem_lengths,
        0.0,
        open_mask,
        cross_max,
        cross_sum,
        d_cross_mix,
        False,
    )
    grad_cq = product_t(norm_two, dq_cross)
    grad_ck = product_t(flat_mem, dk_cross)
    grad_cv = product_t(flat_mem, dv_cross)
    memory_grad = (product_nt(dk_cross, w_ck) + product_nt(dv_cross, w_cv)).astype(jnp.bfloat16)
    _, pull_two = jax.vjp(rms_scale, resid_one, gains[1])
    d_from_two, grad_gain_two = pull_two(product_nt(dq_cross, w_cq))
    d_resid_one = d_resid_two + d_from_two
    d_self = d_resid_one.astype(jnp.bfloat16)
    grad_so = product_t(self_mix, d_self)
    d_self_mix = product_nt(d_self, w_so).astype(jnp.bfloat16)
    dq_self, dk_self, dv_self, score_sums = attend_back_slots(
        self_q, self_k, self_v, dec_lengths, pos_bias, causal, self_max, self_sum, d_self_mix, True
    )
    grad_sq = product_t(norm_one, dq_self)
    grad_sk = product_t(norm_one, dk_self)
    grad_sv = product_t(norm_one, dv_self)
    d_norm_one = product_nt(dq_self, w_sq) + product_nt(dk_self, w_sk) + product_nt(dv_self, w_sv)
    _, pull_one = jax.vjp(rms_scale, flat_in, gains[0])
    d_from_one, grad_gain_one = pull_one(d_norm_one)
    input_grad = (d_resid_one + d_from_one).astype(jnp.bfloat16)
    table_local = table_gradient(score_sums, length)
    self_full = jnp.stack([grad_sq, grad_sk, grad_sv, grad_so]).reshape(-1)
    cross_full = jnp.stack([grad_cq, grad_ck, grad_cv, grad_co]).reshape(-1)
    ff_full = jnp.concatenate([grad_gate.reshape(-1), grad_up.reshape(-1), grad_down.reshape(-1)])
    self_shard, cross_shard, ff_shard = scatter_grads(self_full, cross_full, ff_full)
    gain_local = jnp.stack([grad_gain_one, grad_gain_two, grad_gain_three])
    gain_total, table_total = lax.psum((gain_local, table_local), ("dp", "fsdp"))
    return (
        block_out,
        input_grad.reshape(slot_count, length, model_width),
        memory_grad.reshape(slot_count, mem_len, model_width),
        self_shard,
        cross_shard,
        ff_shard,
        gain_total,
        table_total,
    )


def solution(mesh):
    whole = ("dp", "fsdp")
    rows = P(whole, None, None)
    flat = P(whole)
    small = mesh.shape["dp"] == 8 and mesh.shape["fsdp"] == 4
    return jax.shard_map(
        fused if small else by_collectives,
        mesh=mesh,
        in_specs=(rows, rows, rows, flat, flat, flat, flat, flat, P(), P()),
        out_specs=(rows, rows, rows, flat, flat, flat, P(), P()),
        check_vma=False,
    )
```

```python
import functools

import jax
import jax.numpy as jnp
import numpy as np
from jax import lax
from jax.experimental import pallas as pl
from jax.experimental.pallas import tpu as pltpu
from jax.sharding import PartitionSpec as P

D = 768
FF = 2048
H = 12
DH = 64
NB = 32
MAXD = 128
PAIRS = H // 2
MASKED = -1000000000.0
BF = jnp.bfloat16
F32 = jnp.float32
MESH = pl.DeviceIdType.MESH

AR = 96
AU = 288
FU = 576
GROUPS = (
    (2, 3), (2, 2), (2, 0), (2, 1),
    (1, 3), (1, 2), (1, 1), (1, 0),
    (0, 3), (0, 0), (0, 2), (0, 1),
)
PAIR = (True,) * 10 + (False,) * 2
SHARED = (True, True, True)
UNIT = tuple(FU if t == 2 else AU for t, _ in GROUPS)
OWN = tuple(4 * sum(UNIT[:g]) for g in range(12))
OWN_ROWS = 4 * sum(UNIT)
LAND = tuple(3 * sum(UNIT[:g]) for g in range(12))
LAND_ROWS = 3 * sum(UNIT)
Z_ROWS = 5 * FU
STAGE = 4 * FU
ROLES = ((1, 1), (1, 0), (0, 1), (0, 0))
SIB = (0, 12, 13, 14)


def limits():
    half = NB // 2
    return [
        int(v)
        for v in np.ceil(half * (MAXD / half) ** (np.arange(1, half) / half)).astype(np.int32)
    ]


def bucket_of(distance):
    half = NB // 2
    beyond = jnp.full(distance.shape, half, jnp.int32)
    for limit in limits():
        beyond = beyond + jnp.where(distance >= limit, 1, 0)
    return jnp.where(distance < half, jnp.maximum(distance, 0), beyond)


def nn(left, right):
    return jnp.dot(left, right, preferred_element_type=F32)


def nt(left, right):
    return lax.dot_general(left, right, (((1,), (1,)), ((), ())), preferred_element_type=F32)


def tn(left, right):
    return lax.dot_general(left, right, (((0,), (0,)), ((), ())), preferred_element_type=F32)


def al(value, step):
    return pl.multiple_of(value, step)


def rms(value, gain):
    r = lax.rsqrt(jnp.mean(value * value, axis=-1, keepdims=True) + 1e-06)
    return value * r * gain


def rms_back(value, gain, dz):
    r = lax.rsqrt(jnp.mean(value * value, axis=-1, keepdims=True) + 1e-06)
    inner = jnp.mean(value * gain * dz, axis=-1, keepdims=True)
    dv = r * gain * dz - value * (r * r * r) * inner
    dg = jnp.sum(value * r * dz, axis=0, keepdims=True)
    return dv, dg


class Layer:
    def __init__(self, refs):
        self.__dict__.update(refs)
        self.flat, self.dm = self.ps, self.n3
        dp = lax.axis_index("dp")
        fs = lax.axis_index("fsdp")
        self.z, self.y = dp // 2, dp % 2
        self.x, self.c = fs // 2, fs % 2
        self.shard = dp * 4 + fs

    def dev(self, z=None, fx=0, fy=0, fc=0):
        z = self.z if z is None else z
        y = (self.y + fy) % 2
        x = (self.x + fx) % 2
        c = (self.c + fc) % 2
        return (z * 2 + y, x * 2 + c)

    def chip(self, fx=0, fy=0):
        return ((self.y + fy) % 2) * 2 + (self.x + fx) % 2

    def shard_at(self, z, fx=0, fy=0, fc=0):
        return z * 8 + self.chip(fx, fy) * 2 + (self.c + fc) % 2

    def copy(self, src, dst, send, recv, device):
        return pltpu.make_async_remote_copy(
            src_ref=src, dst_ref=dst, send_sem=send, recv_sem=recv,
            device_id=device, device_id_type=MESH,
        )

    def piece(self, tensor, shard, half=None, par=None):
        rows = FU if tensor == 2 else AR
        ref = (self.ws, self.wc, self.wf)[tensor]
        start = shard * rows
        if half is None:
            return ref.at[pl.ds(al(start, 16), rows), :]
        rows = rows // 2
        start = pl.ds(al(start + half * rows, 16), rows)
        if not SHARED[tensor]:
            return ref.at[start, :]
        width = ref.shape[1] // 2
        return ref.at[start, pl.ds(al(par * width, 128), width)]

    def plane(self, tensor, k):
        if tensor == 2:
            return k
        far = self.z // 2
        return (self.z, self.z + 1 - 2 * (self.z % 2), 2 - far, 3 - 3 * far)[k]

    def gcopy(self, tensor, zs, kind, there=False):
        par = self.z % 2
        if kind < 2:
            spot, dev = (0, 0), ((1, 0), (0, 1))[kind]
            if there:
                spot = dev
            part, dev = self.piece(tensor, self.shard_at(zs, *spot)), self.dev(None, *dev)
        elif kind < 4:
            spot, dev = ((1, 0), (0, 1)) if kind == 2 else ((0, 1), (1, 0))
            if there:
                spot = (1, 1)
            part = self.piece(tensor, self.shard_at(zs, *spot), kind - 2, par)
            dev = self.dev(None, *dev)
        elif kind < 8:
            spot = ((0, 0), (1, 0), (0, 1), (1, 1))[kind - 4]
            part = self.piece(tensor, self.shard_at(zs, *spot, 1 if there else 0))
            dev = self.dev(fc=1)
        else:
            part = self.piece(
                tensor, self.shard_at(zs, 1, 1), kind - 8, 1 - par if there else par)
            dev = self.dev(z=self.z + 1 - 2 * par)
        row = (tensor * 4 + zs) * 10 + kind
        return self.copy(part, part, self.gsend.at[row], self.grecv.at[row], dev)

    def start(self, tensor, zs, *kinds):
        for kind in kinds:
            self.gcopy(tensor, zs, kind).start()

    def arrive(self, tensor, zs, *kinds):
        for kind in kinds:
            self.gcopy(tensor, zs, kind, True).wait_recv()

    def zcopy(self, tensor, zs, up):
        part = self.piece(tensor, self.shard_at(zs))
        row = tensor * 4 + zs
        return self.copy(
            part, part, self.zsend.at[2 * row + up], self.zrecv.at[row],
            self.dev(z=(self.z + (1 if up else 3)) % 4))

    def inner(self, up):
        return self.z < 3 if up else self.z > 0

    def own_z(self, tensor, up):
        @pl.when(self.inner(up))
        def _():
            self.zcopy(tensor, self.z, up).start()

    def z_arrive(self, tensor, zs):
        self.zcopy(tensor, zs, 0).wait_recv()
        for up in (0, 1):
            @pl.when((zs < self.z if up else zs > self.z) & self.inner(up))
            def _(up=up):
                self.zcopy(tensor, zs, up).start()
        self.start(tensor, zs, 0, 1, 4)

    def own_xy(self, tensor):
        self.start(tensor, self.z, 0, 1, 4)

    def p1(self, tensor, k):
        if tensor < 2:
            self.z_arrive(tensor, self.plane(tensor, k))
            return

        @pl.when(self.z == k)
        def _():
            self.start(tensor, k, 0, 1, 4)

        @pl.when(self.z != k)
        def _():
            self.z_arrive(tensor, k)

    def p2x(self, tensor, k):
        zs = self.plane(tensor, k)
        self.arrive(tensor, zs, 0)
        self.start(tensor, zs, 2, 5)

    def p2y(self, tensor, k):
        zs = self.plane(tensor, k)
        self.arrive(tensor, zs, 1)
        self.start(tensor, zs, 3, 6)

    def p3(self, tensor, k, half):
        zs = self.plane(tensor, k)
        self.arrive(tensor, zs, 2 + half)
        if SHARED[tensor]:
            self.start(tensor, zs, 8 + half)
        elif half:
            self.start(tensor, zs, 7)

    def p4(self, tensor, k):
        if SHARED[tensor]:
            zs = self.plane(tensor, k)
            self.arrive(tensor, zs, 8, 9)
            self.start(tensor, zs, 7)

    def p5(self, tensor, k):
        self.arrive(tensor, self.plane(tensor, k), 4, 5, 6, 7)

    def plane_sent(self, tensor, k):
        for kind in range(10 if SHARED[tensor] else 8):
            self.gcopy(tensor, self.plane(tensor, k), kind).wait_send()

    def z_sent(self, tensor, zs):
        for up in (0, 1):
            @pl.when((zs <= self.z if up else zs >= self.z) & self.inner(up))
            def _(up=up):
                self.zcopy(tensor, zs, up).wait_send()

    def credit(self, which):
        for k in ((0,), (1, 2, 3))[which]:
            self.plane_sent(2, k)
            self.z_sent(2, k)
        pl.semaphore_signal(
            self.free.at[which], inc=1, device_id=self.dev(fc=1), device_id_type=MESH)

    def enter(self, i):
        src = (self.sh_s_hbm, self.sh_c_hbm, self.sh_f_hbm, self.x_hbm, self.mem_hbm, self.g_hbm)
        dst = (self.sh_s, self.sh_c, self.sh_f, self.x_in, self.mem, self.g)
        return pltpu.make_async_copy(src[i], dst[i], self.isem.at[i])

    def leave(self, i, part=None):
        if part is not None:
            rows = slice(128 * part, 128 * part + 128)
            return pltpu.make_async_copy(
                self.mgrad.at[rows, :], self.mgrad_hbm.at[rows, :], self.osem.at[i])
        src = (self.block, self.xgrad, None, self.gs, self.gc, self.gf)[i]
        dst = (self.block_hbm, self.xgrad_hbm, None, self.gs_hbm, self.gc_hbm, self.gf_hbm)[i]
        return pltpu.make_async_copy(src, dst, self.osem.at[i])

    def own_square(self, tensor):
        src, dst = ((self.sh_s, self.ws), (self.sh_c, self.wc))[tensor]
        self.enter(tensor).wait()
        self.flat[0:576, :] = src[...].astype(F32)
        row = al(self.shard * AR, 16)
        for t in range(6):
            dst[pl.ds(row, AR), 128 * t:128 * t + 128] = self.flat[
                pl.ds(t, AR, stride=6), :].astype(BF)

    def own_ff(self):
        self.enter(2).wait()
        self.flat[0:1152, :] = self.sh_f[...].astype(F32)
        base = self.shard * FU
        flat, wf = self.flat, self.wf

        def wide(rows):
            for u in range(4):
                for w in range(2):
                    top = flat[pl.ds(4 * u + w, rows, stride=16), :]
                    low = flat[pl.ds(4 * u + w + 2, rows, stride=16), :]
                    wf[pl.ds(al(base + 2 * rows * u, 16), 2 * rows), 128 * w:128 * w + 128] = (
                        jnp.concatenate([top, low], axis=0).astype(BF))

        def tall(first, rows, offset):
            for t in range(6):
                wf[pl.ds(al(base + offset + rows * (t // 2), 16), rows),
                   128 * (t % 2):128 * (t % 2) + 128] = flat[
                       pl.ds(first + t, rows, stride=6), :].astype(BF)

        @pl.when(self.shard < 21)
        def _():
            wide(72)

        @pl.when(self.shard == 21)
        def _():
            wide(24)
            tall(384, 128, 192)

        @pl.when(self.shard > 21)
        def _():
            tall(0, 192, 0)

    def build_wide(self, ch):
        rows1 = 24 if ch == 10 else 72

        def step(u, _):
            low = self.wf[pl.ds(al(1152 * ch + 144 * u, 16), 144), :].astype(F32)
            high = self.wf[
                pl.ds(al(1152 * ch + FU + 2 * rows1 * u, 16), 2 * rows1), :].astype(F32)
            for w in range(2):
                value = jnp.concatenate(
                    [low[72 * w:72 * w + 72], high[rows1 * w:rows1 * w + rows1]], axis=0)
                self.wgu[144 * ch:144 * ch + 72 + rows1,
                         pl.ds(al(512 * u + 256 * w, 256), 256)] = value.astype(BF)
            return 0

        lax.fori_loop(0, 4, step, 0)

    def build_tall(self, s):
        first, rows, offset = (0, 128, 192) if s == 21 else (192 * s - 4096, 192, 0)
        for p in range(3):
            self.wd[first:first + rows, 256 * p:256 * p + 256] = self.wf[
                FU * s + offset + rows * p:FU * s + offset + rows * p + rows, :]

    def build_plane(self, zs):
        if zs < 2:
            for ch in range(4 * zs, 4 * zs + 4):
                self.build_wide(ch)
        elif zs == 2:
            for ch in (8, 9, 10):
                self.build_wide(ch)
            for s in (21, 22, 23):
                self.build_tall(s)
        else:
            for s in range(24, 32):
                self.build_tall(s)

    def masks(self):
        lane = lax.broadcasted_iota(jnp.int32, (128, 128), 1)
        self.left = lane < DH

    def stack(self, pair):
        zero = jnp.zeros_like(pair)
        return jnp.concatenate(
            [jnp.where(self.left, pair, zero), jnp.where(self.left, zero, pair)], axis=0)

    def unstack(self, both):
        rows = both.shape[0] // 2
        return jnp.where(self.left, both[0:rows], both[rows:])

    def bias(self):
        lane = lax.broadcasted_iota(jnp.int32, (1, 128), 1)
        bucket = bucket_of((128 - lane) % 128)
        for h in range(H):
            row = jnp.zeros((1, 128), F32)
            for b in range(NB):
                row = jnp.where(bucket == b, self.table[h, b], row)
            full = jnp.broadcast_to(row, (128, 128))
            self.ps[128 * h:128 * h + 128, :] = pltpu.roll(
                full, 0, 1, stride=1, stride_axis=0)

    def project(self, left, ref, row, out):
        for p in range(3):
            out[:, 256 * p:256 * p + 256] = nn(
                left, ref[row:row + D, 256 * p:256 * p + 256]).astype(BF)

    def add_product(self, left, ref, row, base, out):
        for p in range(3):
            cols = slice(256 * p, 256 * p + 256)
            out[:, cols] = base[:, cols].astype(F32) + nn(left, ref[row:row + D, cols])

    def heads(self, p):
        return pl.ds(al(p * 256, 256), 256)

    def self_forward(self):
        for i in (3, 4, 5):
            self.enter(i).wait()
        x = self.x_in[...].astype(F32)
        self.n1[...] = rms(x, self.gains[0:1, :]).astype(BF)
        n1 = self.n1[...]
        for m, out in enumerate((self.q, self.k, self.v)):
            self.project(n1, self.ws, D * m, out)
        length = self.dl[0]
        row = lax.broadcasted_iota(jnp.int32, (256, 128), 0) % 128
        col = lax.broadcasted_iota(jnp.int32, (256, 128), 1)
        keep = (col <= row) & (col < length)

        def pair(p, _):
            cols = pl.ds(al(p * 128, 128), 128)
            s = nt(self.stack(self.q[:, cols]), self.k[:, cols]) + self.ps[self.heads(p), :]
            s = jnp.where(keep, s, MASKED)
            e = jnp.exp(s - jnp.max(s, axis=-1, keepdims=True))
            prob = e / jnp.sum(e, axis=-1, keepdims=True)
            self.ps[self.heads(p), :] = prob
            self.mix[:, cols] = self.unstack(nn(prob.astype(BF), self.v[:, cols])).astype(BF)
            return 0

        lax.fori_loop(0, PAIRS, pair, 0)
        self.add_product(self.mix[...], self.ws, 3 * D, self.x_in, self.r1)
        self.n2[...] = rms(self.r1[...], self.gains[1:2, :]).astype(BF)

    def cross_kv(self, m):
        out = (self.ck, self.cv)[m - 1]
        for i in range(4):
            for p in range(3):
                out[128 * i:128 * i + 128, 256 * p:256 * p + 256] = nn(
                    self.mem[128 * i:128 * i + 128, :],
                    self.wc[D * m:D * m + D, 256 * p:256 * p + 256]).astype(BF)

    def cross_probs(self, p):
        cols = pl.ds(al(p * 128, 128), 128)
        col = lax.broadcasted_iota(jnp.int32, (256, self.mem.shape[0]), 1)
        s = nt(self.stack(self.cq[:, cols]), self.ck[:, cols])
        s = jnp.where(col < self.ml[0], s, MASKED)
        e = jnp.exp(s - jnp.max(s, axis=-1, keepdims=True))
        return e / jnp.sum(e, axis=-1, keepdims=True)

    def cross_forward(self, part):
        if part == 0:
            self.project(self.n2[...], self.wc, 0, self.cq)

        def pair(p, _):
            cols = pl.ds(al(p * 128, 128), 128)
            prob = self.cross_probs(p)
            self.cmix[:, cols] = self.unstack(nn(prob.astype(BF), self.cv[:, cols])).astype(BF)
            return 0

        lax.fori_loop(2 * part, 2 * part + 2, pair, 0)
        if part == 2:
            self.add_product(self.cmix[...], self.wc, 3 * D, self.r1, self.r2)
            self.n3[...] = rms(self.r2[...], self.gains[2:3, :]).astype(BF)

    def ff_gate(self):
        n3 = self.n3[...]
        c0 = float(np.sqrt(2.0 / np.pi))

        def chunk(i, _):
            cols = pl.ds(al(i * 256, 256), 256)
            a = nn(n3, self.wgu[0:D, cols])
            sq = a * a
            t = jnp.tanh(c0 * (a + 0.044715 * a * sq))
            self.ga[:, cols] = 0.5 * a * (1.0 + t)
            self.ub[:, cols] = 0.5 * (1.0 + t) + 0.5 * a * (1.0 - t * t) * (
                c0 * (1.0 + 0.134145 * sq))
            return 0

        lax.fori_loop(0, FF // 256, chunk, 0)

    def ff_up(self):
        n3 = self.n3[...]

        def chunk(i, _):
            cols = pl.ds(al(i * 256, 256), 256)
            up = nn(n3, self.wgu[D:2 * D, cols])
            self.ub[:, cols] = up * self.ub[:, cols]
            self.hid[:, cols] = (self.ga[:, cols] * up).astype(BF)
            return 0

        lax.fori_loop(0, FF // 256, chunk, 0)
        self.hidt[...] = self.hid[...].T

    def out_rows(self):
        hid = self.hid[...]
        for p in range(3):
            cols = slice(256 * p, 256 * p + 256)
            self.block[:, cols] = (self.r2[:, cols] + nn(hid, self.wd[:, cols])).astype(BF)
        self.leave(0).start()

    def d_hidden(self, part):
        g = self.g[...]

        def chunk(i, _):
            at = al(i * 256, 256)
            cols = pl.ds(at, 256)
            dh = nt(g, self.wd[pl.ds(at, 256), :]).astype(BF).astype(F32)
            self.dg[:, cols] = (dh * self.ub[:, cols]).astype(BF)
            self.du[:, cols] = (dh * self.ga[:, cols]).astype(BF)
            return 0

        lax.fori_loop(4 * part, 4 * part + 4, chunk, 0)

    def place(self, g):
        own = OWN[g]
        out = OWN_ROWS + (g % 2) * STAGE
        return own + self.c * (out - own), out + self.c * (own - out)

    def grad_tall(self, g, i):
        b0, b1 = self.place(g)
        for p in range(3):
            both = nn(
                self.hidt[pl.ds(al(512 + 384 * i, 16), 384), :],
                self.g[:, 256 * p:256 * p + 256])
            self.gb[pl.ds(al(b0 + FU * i + 192 * p, 16), 192), :] = both[0:192].astype(BF)
            self.gb[pl.ds(al(b1 + FU * i + 192 * p, 16), 192), :] = both[192:].astype(BF)

    def grad_tall_part(self, base, i, first, rows, offset):
        for p in range(3):
            value = nn(self.hidt[first:first + rows, :], self.g[:, 256 * p:256 * p + 256])
            self.gb[pl.ds(al(base + FU * i + offset + rows * p, 16), rows), :] = value.astype(BF)

    def grad_wide(self, g, ch, i):
        b0, b1 = self.place(g)
        rows1 = 24 if ch == 10 else 72
        first, end = 144 * ch, 144 * ch + 72 + rows1

        def step(u, _):
            cols = pl.ds(al(512 * u, 512), 512)
            parts = []
            if first < D:
                parts.append(nn(self.n3t[first:min(end, D), :], self.dg[:, cols]))
            if end > D:
                parts.append(nn(self.n3t[max(first, D) - D:end - D, :], self.du[:, cols]))
            both = parts[0] if len(parts) == 1 else jnp.concatenate(parts, axis=0)
            for base, at, rows in ((b0, 0, 72), (b1, 72, rows1)):
                value = jnp.concatenate(
                    [both[at:at + rows, 0:256], both[at:at + rows, 256:512]], axis=0)
                self.gb[pl.ds(al(base + FU * i + 2 * rows * u, 16), 2 * rows), :] = (
                    value.astype(BF))
            return 0

        lax.fori_loop(0, 4, step, 0)

    def grad_ff(self, g):
        zb = GROUPS[g][1]
        if zb == 2:
            b0, b1 = self.place(g)
            for i in range(3):
                self.grad_wide(g, 8 + i, i)
            self.grad_tall_part(b1, 2, 0, 128, 192)
            self.grad_tall_part(b0, 3, 128, 192, 0)
            self.grad_tall_part(b1, 3, 320, 192, 0)
        else:
            for i in range(4):
                self.grad_wide(g, 4 * zb + i, i)

    def grad_square(self, g, i):
        t, zb = GROUPS[g]
        left = self.memt if t == 1 and zb in (1, 2) else self.tt
        right = ((self.q, self.k, self.v, self.drb), (self.cq, self.ck, self.cv, self.drb))[t][zb]
        b0, b1 = self.place(g)
        rows = left[pl.ds(al(192 * i, 16), 192), :]
        for p in range(3):
            both = nn(rows, right[:, 256 * p:256 * p + 256])
            self.gb[pl.ds(al(b0 + AU * i + 96 * p, 16), 96), :] = both[0:96].astype(BF)
            self.gb[pl.ds(al(b1 + AU * i + 96 * p, 16), 96), :] = both[96:].astype(BF)

    def turn(self, g):
        if g == 1:
            self.n3t[...] = self.n3[...].T
        elif g == 5:
            self.memt[...] = self.mem[...].T
        elif g in (4, 7, 8, 9):
            left = {4: self.cmix, 7: self.n2, 8: self.mix, 9: self.n1}[g]
            self.tt[...] = left[...].T

    def back_product(self, terms, out):
        for p in range(3):
            total = None
            for d_ref, w_ref, row, width in terms:
                value = nt(d_ref[...], w_ref[row + 256 * p:row + 256 * p + 256, 0:width])
                total = value if total is None else total + value
            out[:, 256 * p:256 * p + 256] = total

    def norm_three_back(self):
        self.back_product(((self.dg, self.wgu, 0, FF), (self.du, self.wgu, D, FF)), self.dz)
        dv, dg = rms_back(self.r2[...], self.gains[2:3, :], self.dz[...])
        self.redg[0, 2:3, :] = dg
        self.dr[...] = self.g[...].astype(F32) + dv
        self.drb[...] = self.dr[...].astype(BF)
        for up in (0, 1):
            @pl.when(self.inner(up))
            def _(up=up):
                pl.semaphore_signal(
                    self.free.at[3 - up], inc=1,
                    device_id=self.dev(z=(self.z + (1 if up else 3)) % 4), device_id_type=MESH)

    def cross_back(self, part):
        for p in range(3) if part == 0 else ():
            self.dm[:, 256 * p:256 * p + 256] = nt(
                self.drb[...], self.wc[3 * D + 256 * p:3 * D + 256 * p + 256, :]).astype(BF)

        def pair(p, _):
            cols = pl.ds(al(p * 128, 128), 128)
            dms = self.stack(self.dm[:, cols])
            kp = self.ck[:, cols]
            qs = self.stack(self.cq[:, cols])
            prob = self.cross_probs(p)
            dp = nt(dms, self.cv[:, cols])
            ds = (prob * (dp - jnp.sum(prob * dp, axis=-1, keepdims=True))).astype(BF)
            self.cv[:, cols] = tn(prob.astype(BF), dms).astype(BF)
            self.cq[:, cols] = self.unstack(nn(ds, kp)).astype(BF)
            self.ck[:, cols] = tn(ds, qs).astype(BF)
            return 0

        lax.fori_loop(2 * part, 2 * part + 2, pair, 0)

    def memory_rows(self, i):
        rows = slice(128 * i, 128 * i + 128)
        for p in range(3):
            wrow = 256 * p
            self.mgrad[rows, 256 * p:256 * p + 256] = (
                nt(self.ck[rows, :], self.wc[D + wrow:D + wrow + 256, :])
                + nt(self.cv[rows, :], self.wc[2 * D + wrow:2 * D + wrow + 256, :])
            ).astype(BF)
        self.leave(6 + i, i).start()

    def norm_two_back(self):
        self.back_product(((self.cq, self.wc, 0, D),), self.dz)
        dv, dg = rms_back(self.r1[...], self.gains[1:2, :], self.dz[...])
        self.redg[0, 1:2, :] = dg
        self.dr[...] = self.dr[...] + dv
        self.drb[...] = self.dr[...].astype(BF)

    def self_back(self, part):
        for p in range(3) if part == 0 else ():
            self.dm[:, 256 * p:256 * p + 256] = nt(
                self.drb[...], self.ws[3 * D + 256 * p:3 * D + 256 * p + 256, :]).astype(BF)

        def pair(p, _):
            cols = pl.ds(al(p * 128, 128), 128)
            dms = self.stack(self.dm[:, cols])
            kp = self.k[:, cols]
            qs = self.stack(self.q[:, cols])
            prob = self.ps[self.heads(p), :]
            dp = nt(dms, self.v[:, cols])
            ds = (prob * (dp - jnp.sum(prob * dp, axis=-1, keepdims=True))).astype(BF)
            self.ps[self.heads(p), :] = ds.astype(F32)
            self.v[:, cols] = tn(prob.astype(BF), dms).astype(BF)
            self.q[:, cols] = self.unstack(nn(ds, kp)).astype(BF)
            self.k[:, cols] = tn(ds, qs).astype(BF)
            return 0

        lax.fori_loop(3 * part, 3 * part + 3, pair, 0)

    def norm_one_back(self):
        self.back_product(
            ((self.q, self.ws, 0, D), (self.k, self.ws, D, D), (self.v, self.ws, 2 * D, D)),
            self.dz)
        dv, dg = rms_back(self.x_in[...].astype(F32), self.gains[0:1, :], self.dz[...])
        self.redg[0, 0:1, :] = dg
        self.xgrad[...] = (self.dr[...] + dv).astype(BF)
        self.leave(1).start()

    def table_back(self):
        row = lax.broadcasted_iota(jnp.int32, (128, 128), 0)
        col = lax.broadcasted_iota(jnp.int32, (128, 128), 1)
        flip = jnp.where(row + col == 127, 1.0, 0.0).astype(BF)
        self.diag[...] = jnp.zeros_like(self.diag)
        for p in range(PAIRS):
            back = nn(self.ps[256 * p:256 * p + 256, :].astype(BF), flip)
            for hh in range(2):
                turned = pltpu.roll(
                    back[128 * hh:128 * hh + 128], 0, 1, stride=1, stride_axis=0)
                self.diag[2 * p + hh:2 * p + hh + 1, :] = jnp.sum(turned, axis=0, keepdims=True)
        lane = lax.broadcasted_iota(jnp.int32, (NB, 128), 1)
        hot = jnp.where(
            bucket_of((lane + 1) % 128) == lax.broadcasted_iota(jnp.int32, (NB, 128), 0), 1.0, 0.0)
        self.redt[0, :, 0:NB] = lax.dot_general(
            self.diag[...], hot, (((1,), (1,)), ((), ())),
            precision=lax.Precision.HIGHEST, preferred_element_type=F32)

    def own(self, g, chip, half=None):
        unit = UNIT[g]
        start = OWN[g] + chip * unit
        if half is not None:
            unit = unit // 2
            start = start + half * unit
        return pl.ds(al(start, 16), unit)

    def land(self, g, which, half=None):
        unit = UNIT[g]
        start = LAND[g] + (0, unit // 2, unit, 2 * unit)[which]
        rows = unit // 2 if which < 2 else unit
        if half is not None:
            rows = unit // 2
            start = start + half * rows
        return pl.ds(start, rows)

    def lanes(self, g, mine):
        if not PAIR[g]:
            return slice(None)
        par = self.z % 2
        return pl.ds(al((par if mine else 1 - par) * 128, 128), 128)

    def scopy(self, g, kind):
        gb, lb = self.gb, self.lb
        row = g * 15 + kind
        sems = self.rsend.at[row], self.rrecv.at[row]
        if kind in SIB:
            unit = UNIT[g]
            at = self.chip(*ROLES[SIB.index(kind)]) * unit
            return self.copy(
                gb.at[pl.ds(al(OWN_ROWS + (g % 2) * STAGE + at, 16), unit), :],
                self.wf.at[pl.ds(al(OWN[g] + at, 16), unit), :], *sems, self.dev(fc=1))
        spot, half, lanes, where, dev = {
            1: ((1, 1), 0, True, 0, (1, 0)),
            2: ((1, 1), 1, True, 1, (0, 1)),
            3: ((1, 0), 0, None, 2, (1, 0)),
            4: ((1, 0), 1, True, 2, (1, 0)),
            5: ((1, 0), 1, False, 2, (1, 0)),
            6: ((0, 1), 1, None, 3, (0, 1)),
            7: ((0, 1), 0, True, 3, (0, 1)),
            8: ((0, 1), 0, False, 3, (0, 1)),
            9: ((1, 1), 0, False, 0, None),
            10: ((1, 1), 1, False, 1, None),
        }[kind]
        src = self.own(g, self.chip(*spot), half)
        dst = self.land(g, where, half if where > 1 else None)
        lanes = slice(None) if lanes is None else self.lanes(g, lanes)
        put = self.lanes(g, True) if dev is None else lanes
        dev = self.dev(z=self.z + 1 - 2 * (self.z % 2)) if dev is None else self.dev(None, *dev)
        return self.copy(gb.at[src, lanes], lb.at[dst, put], *sems, dev)

    def came(self, g, *kinds):
        for kind in kinds:
            if kind in (9, 10):
                part = self.lb.at[self.land(g, kind - 9), self.lanes(g, False)]
                row = g * 15 + kind
                self.copy(
                    part, part, self.rsend.at[row], self.rrecv.at[row],
                    self.dev(fc=1)).wait_recv()
            else:
                self.scopy(g, kind).wait_recv()

    def go(self, g, *kinds):
        for kind in kinds:
            self.scopy(g, kind).start()

    def z_land(self, g, second):
        t = GROUPS[g][0]
        if t == 2:
            return self.zb.at[pl.ds((4 if second else g) * FU, FU), :]
        if second:
            return self.wgu.at[AU:2 * AU, 256 * t:256 * t + 256]
        return self.wgu.at[0:AU, 256 * (g - 4):256 * (g - 4) + 256]

    def to_owner(self, g, below, second):
        return self.copy(
            self.gb.at[self.own(g, self.chip()), :], self.z_land(g, second),
            self.rsend.at[g * 15 + 11], self.orecv.at[g * 2 + second],
            self.dev(z=(self.z + (1 if below else 3)) % 4))

    def hop(self, g, stage, act):
        zb = GROUPS[g][1]
        for below in (True, False):
            z = stage if below else 3 - stage
            last = zb - 1 if below else zb + 1
            if not (z <= last if below else z >= last) or not 0 <= last < 4:
                continue

            @pl.when(self.z == z)
            def _(below=below, z=z, last=last):
                act(self.to_owner(g, below, 1 if z == last and not below and zb > 0 else 0))

    def z_came(self, g, second):
        part = self.z_land(g, second)
        self.copy(
            part, part, self.rsend.at[g * 15 + 11], self.orecv.at[g * 2 + second],
            self.dev(fc=1)).wait_recv()
        return part

    def zfree(self):
        for up in (0, 1):
            @pl.when(self.inner(up))
            def _(up=up):
                pl.semaphore_wait(self.free.at[2 + up], 1)

    def ready(self, g):
        self.turn(g)
        if g >= 2:
            for role in range(4):
                self.scopy(g - 2, SIB[role]).wait_send()

    def allowed(self, g):
        if g in (0, 2):
            pl.semaphore_wait(self.free.at[g // 2], 1)

    def part(self, g, i):
        (self.grad_tall if g == 0 else self.grad_square)(g, i)

    def grad(self, g):
        self.ready(g)
        if 0 < g < 4:
            self.grad_ff(g)
        else:
            def step(i, _):
                self.part(g, i)
                return 0
            lax.fori_loop(0, 4, step, 0)
        self.allowed(g)
        self.go(g, *SIB)

    def grad_role(self, g, role):
        if role == 0:
            self.ready(g)
        self.part(g, self.chip(*ROLES[role]))
        if role == 0:
            self.allowed(g)
        self.go(g, SIB[role])

    def accumulate(self, dst, lanes, src_ref, src, from_lanes):
        self.gb[dst, lanes] = (
            self.gb[dst, lanes].astype(F32) + src_ref[src, from_lanes].astype(F32)).astype(BF)

    def rs1(self, g, role):
        self.came(g, SIB[role])
        rows = self.own(g, self.chip(*ROLES[role]))
        self.accumulate(rows, slice(None), self.wf, rows, slice(None))
        self.go(g, *(((9, 10), (3, 5), (6, 8), ()) if PAIR[g] else ((1, 2), (3,), (6,), ()))[role])

    def rs2(self, g, half):
        if PAIR[g]:
            self.came(g, 9 + half)
            self.accumulate(
                self.own(g, self.chip(1, 1), half), self.lanes(g, True),
                self.lb, self.land(g, half), self.lanes(g, False))
            self.go(g, 1 + half)

    def rs3(self, g, half):
        kind, spot, late = ((1, (0, 1), 7), (2, (1, 0), 4))[half]
        self.came(g, kind)
        self.accumulate(
            self.own(g, self.chip(*spot), half), self.lanes(g, True),
            self.lb, self.land(g, kind - 1), self.lanes(g, True))
        self.go(g, late)

    def rs4(self, g):
        self.came(g, *((3, 5, 6, 8, 4, 7) if PAIR[g] else (3, 6, 4, 7)))
        rows = self.own(g, self.chip())
        self.gb[rows, :] = (
            self.gb[rows, :].astype(F32) + self.lb[self.land(g, 2), :].astype(F32)
            + self.lb[self.land(g, 3), :].astype(F32)).astype(BF)

    def rsz(self, g, stage):
        def act(copy):
            if stage:
                part = self.z_came(g, 0)
                everything = slice(None)
                self.accumulate(
                    self.own(g, self.chip()), everything, part, everything, everything)
            copy.start()

        self.hop(g, stage, act)

    def rs5(self, g):
        t, zb = GROUPS[g]
        unit = UNIT[g]

        @pl.when(self.z == zb)
        def _():
            places = (0, 1) if 0 < zb < 3 else (0,)
            parts = [self.z_came(g, second) for second in places]

            def total(start, size, lanes):
                at = pl.ds(al(OWN[g] + self.chip() * unit + start, 16), size)
                value = self.gb[at, lanes].astype(F32)
                for part in parts:
                    value = value + part[pl.ds(start, size), lanes].astype(F32)
                return value

            if t < 2:
                out = (self.gs, self.gc)[t]
                for k in range(6):
                    out[pl.ds(k, AR, stride=6), :] = total(
                        96 * (k // 2), 96, slice(128 * (k % 2), 128 * (k % 2) + 128))
                self.leave(3 + t).start()
                return
            out = self.gf

            def wide(rows):
                for u in range(4):
                    for w in range(2):
                        v = total(2 * rows * u, 2 * rows, slice(128 * w, 128 * w + 128))
                        out[pl.ds(4 * u + w, rows, stride=16), :] = v[0:rows]
                        out[pl.ds(4 * u + w + 2, rows, stride=16), :] = v[rows:]

            def tall(first, rows, offset):
                for k in range(6):
                    out[pl.ds(first + k, rows, stride=6), :] = total(
                        offset + rows * (k // 2), rows, slice(128 * (k % 2), 128 * (k % 2) + 128))

            if zb < 2:
                wide(72)
            elif zb == 3:
                tall(0, 192, 0)
            else:
                @pl.when(self.shard < 21)
                def _():
                    wide(72)

                @pl.when(self.shard == 21)
                def _():
                    wide(24)
                    tall(384, 128, 192)

                @pl.when(self.shard > 21)
                def _():
                    tall(0, 192, 0)

            self.leave(5).start()

    def group_sent(self, g):
        for kind in range(1, 11):
            if PAIR[g] or kind not in (5, 8, 9, 10):
                self.scopy(g, kind).wait_send()

        for stage in range(3):
            self.hop(g, stage, lambda copy: copy.wait_send())

    def small(self, step, which):
        dev = (
            self.dev(fc=1), self.dev(fx=1), self.dev(fy=1),
            self.dev(z=self.z + 1 - 2 * (self.z % 2)), self.dev(z=(self.z + 2) % 4),
        )[step]
        src, dst = ((self.redg, self.landg), (self.redt, self.landt))[which]
        row = step * 2 + which
        return self.copy(
            src.at[step], dst.at[step], self.ssend.at[row], self.srecv.at[row], dev)

    def small_start(self, step):
        for which in range(2):
            self.small(step, which).start()

    def small_add(self, step):
        for which in range(2):
            self.small(step, which).wait_recv()
        self.redg[step + 1] = self.redg[step] + self.landg[step]
        self.redt[step + 1] = self.redt[step] + self.landt[step]


    def finish(self):
        for tensor in (0, 1):
            for k in range(4):
                self.plane_sent(tensor, k)
                self.z_sent(tensor, k)
        for g in range(12):
            self.group_sent(g)
        for g in (10, 11):
            for role in range(4):
                self.scopy(g, SIB[role]).wait_send()
        for i in (0, 1, 3, 4, 5):
            self.leave(i).wait()
        for i in range(4):
            self.leave(6 + i, i).wait()
        self.ggain[...] = self.redga[5, 0:3, :]
        self.gtable[...] = self.redta[5, 0:H, 0:NB]
        for step in range(5):
            for which in range(2):
                self.small(step, which).wait_send()


K = Layer
SCHEDULE = (
    (K.own_z, 0, 1), (K.own_xy, 0), (K.own_z, 0, 0), (K.own_square, 1), (K.own_ff,),
    (K.own_xy, 1), (K.bias,), (K.own_z, 1, 1), (K.own_z, 1, 0), (K.p1, 0, 1), (K.p1, 0, 2),
    (K.p1, 1, 2), (K.p1, 1, 1), (K.p1, 0, 3), (K.own_z, 2, 1), (K.p2x, 1, 0), (K.own_z, 2, 0),
    (K.p2x, 0, 1), (K.p2y, 0, 2), (K.p2x, 1, 2), (K.p2y, 1, 2), (K.p2x, 1, 1), (K.p2y, 1, 1),
    (K.p2y, 1, 0), (K.p1, 1, 3), (K.p2x, 0, 2), (K.p2x, 0, 3), (K.p2y, 0, 1), (K.p2x, 0, 0),
    (K.p2y, 0, 0), (K.p1, 2, 1), (K.p3, 1, 1, 0), (K.p2y, 0, 3), (K.p3, 1, 2, 0),
    (K.p3, 1, 2, 1), (K.p1, 2, 2), (K.p1, 2, 0), (K.p4, 1, 2), (K.p3, 1, 0, 0), (K.p3, 0, 2, 0),
    (K.p3, 0, 3, 0), (K.p3, 1, 0, 1), (K.p3, 0, 1, 0), (K.p2x, 1, 3), (K.p3, 0, 0, 0),
    (K.p3, 0, 0, 1), (K.p3, 0, 1, 1), (K.p3, 0, 2, 1), (K.p2y, 1, 3), (K.p3, 1, 1, 1),
    (K.p3, 0, 3, 1), (K.p2x, 2, 1), (K.p2y, 2, 1), (K.p1, 2, 3), (K.p2x, 2, 0), (K.p4, 0, 0),
    (K.p3, 1, 3, 0), (K.p4, 1, 0), (K.p4, 0, 2), (K.p3, 1, 3, 1), (K.p4, 1, 1), (K.p2x, 2, 2),
    (K.p4, 0, 1), (K.p5, 0, 2), (K.p4, 0, 3), (K.p2y, 2, 0), (K.p3, 2, 1, 0), (K.p2y, 2, 2),
    (K.p5, 0, 0), (K.p5, 0, 3), (K.p3, 2, 1, 1), (K.p5, 0, 1), (K.p4, 1, 3), (K.p5, 1, 2),
    (K.self_forward,), (K.p5, 1, 1), (K.p5, 1, 0), (K.p5, 1, 3), (K.p2x, 2, 3), (K.cross_kv, 1),
    (K.p3, 2, 0, 0), (K.p2y, 2, 3), (K.cross_kv, 2), (K.p3, 2, 0, 1), (K.cross_forward, 0),
    (K.p3, 2, 2, 0), (K.p3, 2, 2, 1), (K.p4, 2, 1), (K.p3, 2, 3, 0), (K.cross_forward, 1),
    (K.p4, 2, 0), (K.p5, 2, 1), (K.build_plane, 1), (K.p3, 2, 3, 1), (K.cross_forward, 2),
    (K.p5, 2, 0), (K.build_plane, 0), (K.credit, 0), (K.p4, 2, 2), (K.ff_gate,), (K.p5, 2, 2),
    (K.build_plane, 2), (K.ff_up,), (K.p4, 2, 3), (K.grad_role, 0, 0), (K.grad_role, 0, 1),
    (K.grad_role, 0, 2), (K.grad_role, 0, 3), (K.p5, 2, 3), (K.build_plane, 3), (K.d_hidden, 0),
    (K.rs1, 0, 2), (K.credit, 1), (K.rs1, 0, 1), (K.rs1, 0, 0), (K.d_hidden, 1), (K.grad, 1),
    (K.grad, 2), (K.rs2, 0, 0), (K.rs1, 1, 1), (K.rs1, 1, 2), (K.rs1, 1, 0), (K.grad, 3),
    (K.rs1, 2, 2), (K.rs1, 2, 1), (K.rs1, 2, 0), (K.norm_three_back,), (K.rs2, 1, 0),
    (K.grad_role, 4, 0), (K.grad_role, 4, 1), (K.rs2, 0, 1), (K.grad_role, 4, 2),
    (K.cross_back, 0), (K.rs1, 3, 0), (K.rs2, 2, 0), (K.rs2, 1, 1), (K.cross_back, 1),
    (K.rs1, 4, 0), (K.rs1, 3, 2), (K.rs1, 3, 1), (K.grad_role, 4, 3), (K.cross_back, 2),
    (K.rs3, 1, 0), (K.grad, 5), (K.rs3, 1, 1), (K.rs2, 2, 1), (K.grad, 6), (K.rs1, 5, 0),
    (K.rs2, 3, 1), (K.rs3, 0, 1), (K.rs1, 4, 2), (K.rs1, 1, 3), (K.rs2, 4, 0), (K.rs2, 3, 0),
    (K.rs1, 6, 0), (K.grad, 7), (K.rs1, 2, 3), (K.rs3, 0, 0), (K.rs4, 1), (K.rsz, 1, 0),
    (K.rs3, 2, 1), (K.rs3, 2, 0), (K.norm_two_back,), (K.rs1, 4, 1), (K.rs1, 0, 3), (K.grad, 8),
    (K.rs2, 6, 0), (K.rs3, 3, 1), (K.rs1, 7, 0), (K.rs1, 5, 1), (K.rs2, 5, 1), (K.rs3, 3, 0),
    (K.rs2, 6, 1), (K.self_back, 0), (K.self_back, 1), (K.rs1, 8, 0), (K.rs1, 6, 2), (K.rs4, 0),
    (K.rs4, 2), (K.grad_role, 9, 0), (K.rsz, 1, 1), (K.rs1, 6, 1), (K.rs3, 4, 0), (K.rsz, 0, 0),
    (K.rs3, 6, 1), (K.rs1, 4, 3), (K.zfree,), (K.rsz, 2, 0), (K.grad_role, 9, 1), (K.rs1, 7, 2),
    (K.grad_role, 9, 2), (K.rs2, 7, 1), (K.rs1, 9, 0), (K.grad_role, 9, 3), (K.rs2, 5, 0),
    (K.rs2, 7, 0), (K.rs3, 5, 1), (K.rs1, 7, 3), (K.rs1, 3, 3), (K.rs4, 3), (K.rsz, 3, 0),
    (K.grad_role, 10, 0), (K.grad_role, 10, 1), (K.rs1, 6, 3), (K.rs1, 5, 2), (K.rs2, 8, 0),
    (K.rs1, 7, 1), (K.grad_role, 10, 2), (K.grad_role, 10, 3), (K.grad_role, 11, 0),
    (K.grad_role, 11, 1), (K.grad_role, 11, 2), (K.rs3, 6, 0), (K.rsz, 0, 1), (K.rs1, 8, 3),
    (K.norm_one_back,), (K.rs1, 9, 3), (K.rs2, 8, 1), (K.rs3, 5, 0), (K.rs3, 7, 1),
    (K.memory_rows, 2), (K.rs2, 4, 1), (K.rs3, 7, 0), (K.rsz, 2, 1), (K.rs1, 10, 0),
    (K.rs1, 11, 0), (K.rs2, 9, 1), (K.table_back,), (K.rs1, 10, 3), (K.rs1, 9, 2),
    (K.rs2, 11, 0), (K.grad_role, 11, 3), (K.small_start, 0), (K.rs2, 9, 0), (K.rs1, 8, 1),
    (K.rs1, 8, 2), (K.memory_rows, 1), (K.rs4, 6), (K.rs1, 5, 3), (K.rs3, 8, 1), (K.rsz, 6, 0),
    (K.rs3, 4, 1), (K.rs2, 10, 1), (K.rs1, 9, 1), (K.rs4, 7), (K.rs4, 5), (K.rs5, 1),
    (K.rsz, 7, 0), (K.rs2, 11, 1), (K.rsz, 3, 1), (K.rsz, 0, 2), (K.rs2, 10, 0), (K.rs3, 9, 0),
    (K.small_add, 0), (K.small_start, 1), (K.rsz, 5, 0), (K.rsz, 2, 2), (K.memory_rows, 0),
    (K.rsz, 7, 1), (K.rs3, 9, 1), (K.rs3, 8, 0), (K.rs1, 10, 2), (K.memory_rows, 3),
    (K.rs3, 10, 0), (K.rsz, 5, 1), (K.rs1, 10, 1), (K.out_rows,), (K.rsz, 6, 1), (K.rs1, 11, 2),
    (K.rs3, 11, 0), (K.rs3, 10, 1), (K.rs4, 4), (K.rs1, 11, 1), (K.rsz, 4, 0), (K.rsz, 4, 1),
    (K.rs4, 8), (K.rsz, 8, 0), (K.rs5, 3), (K.rs4, 9), (K.rsz, 9, 0), (K.rsz, 9, 1),
    (K.rs3, 11, 1), (K.small_add, 1), (K.small_start, 2), (K.rsz, 7, 2), (K.rsz, 8, 1),
    (K.rs4, 10), (K.rs5, 6), (K.rsz, 4, 2), (K.rs1, 11, 3), (K.rsz, 10, 0), (K.rs4, 11),
    (K.rsz, 10, 1), (K.rsz, 11, 0), (K.small_add, 2), (K.small_start, 3), (K.rs5, 5),
    (K.rs5, 0), (K.rs5, 2), (K.rs5, 4), (K.rs5, 7), (K.rsz, 11, 1), (K.rsz, 9, 2),
    (K.rsz, 8, 2), (K.small_add, 3), (K.small_start, 4), (K.rs5, 10), (K.rs5, 11), (K.rs5, 9),
    (K.small_add, 4), (K.rs5, 8),
)

NAMES = (
    "x_hbm", "mem_hbm", "g_hbm", "dl", "ml", "sh_s_hbm", "sh_c_hbm", "sh_f_hbm", "gains", "table",
    "block_hbm", "xgrad_hbm", "mgrad_hbm", "gs_hbm", "gc_hbm", "gf_hbm", "ggain", "gtable",
    "x_in", "mem", "g", "sh_s", "sh_c", "sh_f", "block", "xgrad", "mgrad", "gs", "gc", "gf",
    "isem", "osem",
    "ws", "wc", "wf", "wgu", "wd", "gb", "lb", "zb",
    "n1", "q", "k", "v", "mix", "r1", "n2", "cq", "ck", "cv", "cmix", "r2", "n3",
    "ga", "ub", "hid", "hidt", "n3t", "dg", "du", "dz", "dr", "drb", "tt", "memt",
    "ps", "diag", "redga", "redta", "landg", "landt",
    "gsend", "grecv", "zsend", "zrecv", "rsend", "rrecv", "orecv", "ssend", "srecv", "free",
)


def kernel(*args):
    st = Layer(dict(zip(NAMES, args)))
    st.redg, st.redt = st.redga, st.redta
    barrier = pltpu.get_barrier_semaphore()
    others = [st.dev(fc=1), st.dev(fx=1), st.dev(fy=1)] + [
        st.dev(z=(st.z + k) % 4) for k in (1, 2, 3)]
    for other in others:
        pl.semaphore_signal(barrier, inc=1, device_id=other, device_id_type=MESH)
    for i in range(6):
        st.enter(i).start()
    st.own_square(0)
    st.masks()
    pl.semaphore_wait(barrier, 6)
    for step, *numbers in SCHEDULE:
        step(st, *numbers)
    st.finish()


def settle_kernel(count, *refs):
    src, dst, held = refs[:count], refs[count:2 * count], refs[2 * count:3 * count]
    arrive, go = refs[3 * count:]
    into = [pltpu.make_async_copy(src[i], held[i], arrive.at[i]) for i in range(count)]
    out = [pltpu.make_async_copy(held[i], dst[i], go.at[i]) for i in range(count)]
    for one in into:
        one.start()
    for first, then in zip(into, out):
        first.wait()
        then.start()
    for one in out:
        one.wait()


def settle(arrays):
    anywhere = pl.BlockSpec(memory_space=pl.ANY)
    count = len(arrays)
    return pl.pallas_call(
        functools.partial(settle_kernel, count),
        out_shape=tuple(jax.ShapeDtypeStruct(v.shape, v.dtype) for v in arrays),
        in_specs=[anywhere] * count,
        out_specs=tuple([anywhere] * count),
        scratch_shapes=[pltpu.VMEM(v.shape, v.dtype) for v in arrays] + [
            pltpu.SemaphoreType.DMA((count,)), pltpu.SemaphoreType.DMA((count,))],
        compiler_params=pltpu.CompilerParams(vmem_limit_bytes=67000000),
    )(*arrays)


def fused(inputs, memory, out_cotangent, dec_lengths, mem_lengths, self_params, cross_params,
          ff_params, gains, table):
    slots, length, width = inputs.shape
    mem_len = memory.shape[1]
    hbm = pl.BlockSpec(memory_space=pl.ANY)
    vm = pl.BlockSpec(memory_space=pltpu.VMEM)
    sm = pl.BlockSpec(memory_space=pltpu.SMEM)
    s = jax.ShapeDtypeStruct
    rows_s, rows_f = self_params.shape[0] // 128, ff_params.shape[0] // 128
    row = pltpu.VMEM((length, D), BF)
    rowf = pltpu.VMEM((length, D), F32)
    memory_row = pltpu.VMEM((mem_len, D), BF)
    dma = pltpu.SemaphoreType.DMA
    outs = pl.pallas_call(
        kernel,
        out_shape=(
            s((length, D), BF), s((length, D), BF), s((mem_len, D), BF),
            s((rows_s, 128), F32), s((rows_s, 128), F32), s((rows_f, 128), F32),
            s((3, D), F32), s((H, NB), F32),
        ),
        in_specs=[hbm, hbm, hbm, sm, sm, hbm, hbm, hbm, vm, sm],
        out_specs=[hbm] * 6 + [vm] * 2,
        scratch_shapes=[
            row, memory_row, row, pltpu.VMEM((rows_s, 128), BF), pltpu.VMEM((rows_s, 128), BF),
            pltpu.VMEM((rows_f, 128), BF), row, row, memory_row,
            pltpu.VMEM((rows_s, 128), F32), pltpu.VMEM((rows_s, 128), F32),
            pltpu.VMEM((rows_f, 128), F32), dma((6,)), dma((10,)),
            pltpu.VMEM((4 * D, D), BF), pltpu.VMEM((4 * D, D), BF),
            pltpu.VMEM((32 * FU, 256), BF),
            pltpu.VMEM((2 * D, FF), BF), pltpu.VMEM((FF, D), BF),
            pltpu.VMEM((OWN_ROWS + 2 * STAGE, 256), BF),
            pltpu.VMEM((LAND_ROWS, 256), BF), pltpu.VMEM((Z_ROWS, 256), BF),
            row, row, row, row, row, rowf, row, row, memory_row, memory_row, row, rowf, row,
            pltpu.VMEM((length, FF), F32), pltpu.VMEM((length, FF), F32),
            pltpu.VMEM((length, FF), BF), pltpu.VMEM((FF, length), BF),
            pltpu.VMEM((D, length), BF),
            pltpu.VMEM((length, FF), BF), pltpu.VMEM((length, FF), BF),
            rowf, rowf, row, pltpu.VMEM((D, length), BF), pltpu.VMEM((D, mem_len), BF),
            pltpu.VMEM((H * length, length), F32),
            pltpu.VMEM((16, 128), F32),
            pltpu.VMEM((6, 8, D), F32), pltpu.VMEM((6, 16, 128), F32),
            pltpu.VMEM((5, 8, D), F32), pltpu.VMEM((5, 16, 128), F32),
            dma((120,)), dma((120,)), dma((24,)), dma((12,)), dma((180,)), dma((180,)), dma((24,)),
            dma((10,)), dma((10,)), pltpu.SemaphoreType.REGULAR((4,)),
        ],
        compiler_params=pltpu.CompilerParams(
            collective_id=0, has_side_effects=True, vmem_limit_bytes=67000000),
        cost_estimate=pl.CostEstimate(
            flops=10_000_000_000, bytes_accessed=8_000_000, transcendentals=2_000_000),
    )(
        inputs.reshape(length, width), memory.reshape(mem_len, width),
        out_cotangent.reshape(length, width), dec_lengths, mem_lengths,
        self_params.reshape(rows_s, 128), cross_params.reshape(rows_s, 128),
        ff_params.reshape(rows_f, 128), gains, table.T,
    )
    outs = settle(outs)
    return (
        outs[0].reshape(inputs.shape), outs[1].reshape(inputs.shape),
        outs[2].reshape(memory.shape), outs[3].reshape(-1), outs[4].reshape(-1),
        outs[5].reshape(-1), outs[6], outs[7].T,
    )


HIGHEST = lax.Precision.HIGHEST


def product(left, right):
    return jnp.dot(left, right, preferred_element_type=jnp.float32)


def product_t(left, right):
    return lax.dot_general(
        left, right, (((0,), (0,)), ((), ())), preferred_element_type=jnp.float32
    )


def product_nt(left, right):
    return lax.dot_general(
        left, right, (((1,), (1,)), ((), ())), preferred_element_type=jnp.float32
    )


def rms_scale(value, gain):
    return value * lax.rsqrt(jnp.mean(value * value, axis=-1, keepdims=True) + 1e-06) * gain


def gelu_gate(gate_pre, up_pre):
    return jax.nn.gelu(gate_pre, approximate=True) * up_pre


def bucket_rows(start, count, length):
    half_count = NB // 2
    limits = np.ceil(
        half_count * (MAXD / half_count) ** (np.arange(1, half_count) / half_count)
    ).astype(np.int32)
    query_pos = start + jnp.arange(count, dtype=jnp.int32)
    key_pos = jnp.arange(length, dtype=jnp.int32)
    distance = query_pos[:, None] - key_pos[None, :]
    beyond = half_count + jnp.sum(
        (distance[None] >= jnp.asarray(limits)[:, None, None]).astype(jnp.int32), axis=0
    )
    return jnp.where(distance < half_count, jnp.maximum(distance, 0), beyond)


def onehot_block(start, count, length):
    bucket = bucket_rows(start, count, length)
    hot_rows = jnp.arange(NB, dtype=jnp.int32)[:, None, None] == bucket[None]
    return hot_rows.astype(jnp.float32).reshape(NB, count * length)


def position_bias(table, length):
    block_rows = min(length, 128)
    block_count = length // block_rows

    def position_per_block(block):
        bucket_hot = onehot_block(block * block_rows, block_rows, length)
        return lax.dot_general(
            table,
            bucket_hot,
            (((0,), (0,)), ((), ())),
            precision=HIGHEST,
            preferred_element_type=jnp.float32,
        )

    pieces = lax.map(position_per_block, jnp.arange(block_count, dtype=jnp.int32))
    return (
        pieces.reshape(block_count, H, block_rows, length)
        .transpose(1, 0, 2, 3)
        .reshape(H, length, length)
    )


def table_gradient(score_sums, length):
    block_rows = min(length, 128)

    def table_per_block(carry, block):
        ds_piece = score_sums.reshape(H, block_rows * length)
        bucket_hot = onehot_block(block * block_rows, block_rows, length)
        return (
            carry
            + lax.dot_general(
                bucket_hot,
                ds_piece,
                (((1,), (1,)), ((), ())),
                precision=HIGHEST,
                preferred_element_type=jnp.float32,
            ),
            None,
        )

    result, _ = lax.scan(
        table_per_block,
        jnp.zeros((NB, H), jnp.float32),
        jnp.arange(length // block_rows, dtype=jnp.int32),
    )
    return result


def score_block(queries, keys_in, score_bias, keep_mask):
    q_len = queries.shape[0]
    k_len = keys_in.shape[0]
    raw_scores = (
        jnp.einsum(
            "qhe,khe->hqk",
            queries.reshape(q_len, H, DH),
            keys_in.reshape(k_len, H, DH),
            preferred_element_type=jnp.float32,
        )
        + score_bias
    )
    return jnp.where(keep_mask[None], raw_scores, MASKED)


def attend_forward(queries, keys_in, values, score_bias, keep_mask):
    q_len = queries.shape[0]
    k_len = keys_in.shape[0]
    raw_scores = score_block(queries, keys_in, score_bias, keep_mask)
    row_max = jnp.max(raw_scores, axis=2, keepdims=True)
    exponent = jnp.exp(raw_scores - row_max)
    row_sum = jnp.sum(exponent, axis=2, keepdims=True)
    softmax_low = (exponent / row_sum).astype(jnp.bfloat16)
    head_mix = jnp.einsum(
        "hqk,khe->qhe",
        softmax_low,
        values.reshape(k_len, H, DH),
        preferred_element_type=jnp.float32,
    )
    return (head_mix.reshape(q_len, H * DH).astype(jnp.bfloat16), row_max, row_sum)


def attend_backward(queries, keys_in, values, score_bias, keep_mask, row_max, row_sum, d_mix):
    q_len = queries.shape[0]
    k_len = keys_in.shape[0]
    raw_scores = score_block(queries, keys_in, score_bias, keep_mask)
    softmax_out = jnp.exp(raw_scores - row_max) / row_sum
    softmax_low = softmax_out.astype(jnp.bfloat16)
    mix_heads = d_mix.reshape(q_len, H, DH)
    q_heads = queries.reshape(q_len, H, DH)
    k_heads = keys_in.reshape(k_len, H, DH)
    v_heads = values.reshape(k_len, H, DH)
    d_softmax = jnp.einsum("qhe,khe->hqk", mix_heads, v_heads, preferred_element_type=jnp.float32)
    d_scores = (
        softmax_out * (d_softmax - jnp.sum(softmax_out * d_softmax, axis=2, keepdims=True))
    ).astype(jnp.bfloat16)
    d_values = (
        jnp.einsum("hqk,qhe->khe", softmax_low, mix_heads, preferred_element_type=jnp.float32)
        .reshape(k_len, H * DH)
        .astype(jnp.bfloat16)
    )
    d_queries = (
        jnp.einsum("hqk,khe->qhe", d_scores, k_heads, preferred_element_type=jnp.float32)
        .reshape(q_len, H * DH)
        .astype(jnp.bfloat16)
    )
    d_keys = (
        jnp.einsum("hqk,qhe->khe", d_scores, q_heads, preferred_element_type=jnp.float32)
        .reshape(k_len, H * DH)
        .astype(jnp.bfloat16)
    )
    return (d_queries, d_keys, d_values, d_scores)


def attend_slots(queries, keys_in, values, lengths, score_bias, base_mask):
    slot_count = lengths.shape[0]
    q_len = queries.shape[0] // slot_count
    k_len = keys_in.shape[0] // slot_count
    key_pos = jnp.arange(k_len, dtype=jnp.int32)

    def per_slot(slot_item):
        q_slot, k_slot, v_slot, slot_len = slot_item
        keep_mask = base_mask & (key_pos[None, :] < slot_len)
        return attend_forward(q_slot, k_slot, v_slot, score_bias, keep_mask)

    head_mix, row_max, row_sum = lax.map(
        per_slot,
        (
            queries.reshape(slot_count, q_len, -1),
            keys_in.reshape(slot_count, k_len, -1),
            values.reshape(slot_count, k_len, -1),
            lengths,
        ),
    )
    return (head_mix.reshape(slot_count * q_len, -1), row_max, row_sum)


def attend_back_slots(
    queries, keys_in, values, lengths, score_bias, base_mask, row_max, row_sum, d_mix, with_table
):
    slot_count = lengths.shape[0]
    q_len = queries.shape[0] // slot_count
    k_len = keys_in.shape[0] // slot_count
    key_pos = jnp.arange(k_len, dtype=jnp.int32)
    if with_table:
        start = jnp.zeros((H, q_len, k_len), jnp.float32)
    else:
        start = jnp.zeros((), jnp.float32)

    def per_slot(carry, slot_item):
        q_slot, k_slot, v_slot, slot_len, max_slot, sum_slot, dmix_slot = slot_item
        keep_mask = base_mask & (key_pos[None, :] < slot_len)
        d_queries, d_keys, d_values, d_scores = attend_backward(
            q_slot, k_slot, v_slot, score_bias, keep_mask, max_slot, sum_slot, dmix_slot
        )
        if with_table:
            carry = carry + d_scores.astype(jnp.float32)
        return (carry, (d_queries, d_keys, d_values))

    score_sums, grad_parts = lax.scan(
        per_slot,
        start,
        (
            queries.reshape(slot_count, q_len, -1),
            keys_in.reshape(slot_count, k_len, -1),
            values.reshape(slot_count, k_len, -1),
            lengths,
            row_max,
            row_sum,
            d_mix.reshape(slot_count, q_len, -1),
        ),
    )
    return (
        grad_parts[0].reshape(slot_count * q_len, -1),
        grad_parts[1].reshape(slot_count * k_len, -1),
        grad_parts[2].reshape(slot_count * k_len, -1),
        score_sums,
    )


def gather_weights(self_params, cross_params, ff_params):
    return (
        lax.all_gather(self_params, ("dp", "fsdp"), axis=0, tiled=True),
        lax.all_gather(cross_params, ("dp", "fsdp"), axis=0, tiled=True),
        lax.all_gather(ff_params, ("dp", "fsdp"), axis=0, tiled=True),
    )


def scatter_grads(self_full, cross_full, ff_full):
    wide_count = lax.axis_size("dp")
    spread = (
        lax.all_to_all(
            self_full.reshape(wide_count, -1).astype(jnp.bfloat16),
            "dp",
            split_axis=0,
            concat_axis=0,
            tiled=True,
        ).astype(jnp.float32),
        lax.all_to_all(
            cross_full.reshape(wide_count, -1).astype(jnp.bfloat16),
            "dp",
            split_axis=0,
            concat_axis=0,
            tiled=True,
        ).astype(jnp.float32),
        lax.all_to_all(
            ff_full.reshape(wide_count, -1).astype(jnp.bfloat16),
            "dp",
            split_axis=0,
            concat_axis=0,
            tiled=True,
        ).astype(jnp.float32),
    )
    self_block = jnp.sum(spread[0], axis=0)
    cross_block = jnp.sum(spread[1], axis=0)
    ff_block = jnp.sum(spread[2], axis=0)
    return (
        lax.psum_scatter(
            self_block.astype(jnp.bfloat16), "fsdp", scatter_dimension=0, tiled=True
        ).astype(jnp.float32),
        lax.psum_scatter(
            cross_block.astype(jnp.bfloat16), "fsdp", scatter_dimension=0, tiled=True
        ).astype(jnp.float32),
        lax.psum_scatter(
            ff_block.astype(jnp.bfloat16), "fsdp", scatter_dimension=0, tiled=True
        ).astype(jnp.float32),
    )


def unpack(weights):
    self_flat, cross_flat, ff_flat = weights
    self_mats = self_flat.reshape(4, D, D)
    cross_mats = cross_flat.reshape(4, D, D)
    block_size = D * FF
    return (
        self_mats[0],
        self_mats[1],
        self_mats[2],
        self_mats[3],
        cross_mats[0],
        cross_mats[1],
        cross_mats[2],
        cross_mats[3],
        ff_flat[:block_size].reshape(D, FF),
        ff_flat[block_size : 2 * block_size].reshape(D, FF),
        ff_flat[2 * block_size :].reshape(FF, D),
    )


def run_forward(
    weights, flat_in, flat_mem, gains, pos_bias, causal, open_mask, dec_lengths, mem_lengths
):
    w_sq, w_sk, w_sv, w_so, w_cq, w_ck, w_cv, w_co, w_gate, w_up, w_down = unpack(weights)
    norm_one = rms_scale(flat_in, gains[0]).astype(jnp.bfloat16)
    self_q = product(norm_one, w_sq).astype(jnp.bfloat16)
    self_k = product(norm_one, w_sk).astype(jnp.bfloat16)
    self_v = product(norm_one, w_sv).astype(jnp.bfloat16)
    self_mix, self_max, self_sum = attend_slots(
        self_q, self_k, self_v, dec_lengths, pos_bias, causal
    )
    resid_one = flat_in + product(self_mix, w_so)
    norm_two = rms_scale(resid_one, gains[1]).astype(jnp.bfloat16)
    cross_q = product(norm_two, w_cq).astype(jnp.bfloat16)
    cross_k = product(flat_mem, w_ck).astype(jnp.bfloat16)
    cross_v = product(flat_mem, w_cv).astype(jnp.bfloat16)
    cross_mix, cross_max, cross_sum = attend_slots(
        cross_q, cross_k, cross_v, mem_lengths, 0.0, open_mask
    )
    resid_two = resid_one + product(cross_mix, w_co)
    norm_three = rms_scale(resid_two, gains[2]).astype(jnp.bfloat16)
    gate_pre = product(norm_three, w_gate)
    up_pre = product(norm_three, w_up)
    hidden = gelu_gate(gate_pre, up_pre).astype(jnp.bfloat16)
    block = resid_two + product(hidden, w_down)
    return (
        norm_one,
        self_q,
        self_k,
        self_v,
        self_mix,
        self_max,
        self_sum,
        resid_one,
        norm_two,
        cross_q,
        cross_k,
        cross_v,
        cross_mix,
        cross_max,
        cross_sum,
        resid_two,
        norm_three,
        gate_pre,
        up_pre,
        hidden,
        block,
    )


def by_collectives(
    inputs,
    memory,
    out_cotangent,
    dec_lengths,
    mem_lengths,
    self_params,
    cross_params,
    ff_params,
    gains,
    table,
):
    slot_count, length, model_width = inputs.shape
    mem_len = memory.shape[1]
    row_count = slot_count * length
    pos_bias = position_bias(table, length)
    positions = jnp.arange(length, dtype=jnp.int32)
    causal = positions[None, :] <= positions[:, None]
    open_mask = jnp.ones((length, mem_len), dtype=bool)
    flat_in = inputs.reshape(row_count, model_width).astype(jnp.float32)
    flat_mem = memory.reshape(slot_count * mem_len, model_width)
    weights = gather_weights(self_params, cross_params, ff_params)
    first_pass = run_forward(
        weights, flat_in, flat_mem, gains, pos_bias, causal, open_mask, dec_lengths, mem_lengths
    )
    block_out = first_pass[20].astype(jnp.bfloat16).reshape(slot_count, length, model_width)
    again = gather_weights(self_params, cross_params, ff_params)
    w_sq, w_sk, w_sv, w_so, w_cq, w_ck, w_cv, w_co, w_gate, w_up, w_down = unpack(again)
    (
        norm_one,
        self_q,
        self_k,
        self_v,
        self_mix,
        self_max,
        self_sum,
        resid_one,
        norm_two,
        cross_q,
        cross_k,
        cross_v,
        cross_mix,
        cross_max,
        cross_sum,
        resid_two,
        norm_three,
        gate_pre,
        up_pre,
        hidden,
        _,
    ) = run_forward(
        again, flat_in, flat_mem, gains, pos_bias, causal, open_mask, dec_lengths, mem_lengths
    )
    d_out = out_cotangent.reshape(row_count, model_width)
    grad_down = product_t(hidden, d_out)
    d_hidden = product_nt(d_out, w_down).astype(jnp.bfloat16)
    _, pull_gate = jax.vjp(gelu_gate, gate_pre, up_pre)
    d_gate, d_up = pull_gate(d_hidden.astype(jnp.float32))
    d_gate = d_gate.astype(jnp.bfloat16)
    d_up = d_up.astype(jnp.bfloat16)
    grad_gate = product_t(norm_three, d_gate)
    grad_up = product_t(norm_three, d_up)
    d_norm_three = product_nt(d_gate, w_gate) + product_nt(d_up, w_up)
    _, pull_three = jax.vjp(rms_scale, resid_two, gains[2])
    d_from_three, grad_gain_three = pull_three(d_norm_three)
    d_resid_two = d_out.astype(jnp.float32) + d_from_three
    d_cross = d_resid_two.astype(jnp.bfloat16)
    grad_co = product_t(cross_mix, d_cross)
    d_cross_mix = product_nt(d_cross, w_co).astype(jnp.bfloat16)
    dq_cross, dk_cross, dv_cross, _ = attend_back_slots(
        cross_q,
        cross_k,
        cross_v,
        mem_lengths,
        0.0,
        open_mask,
        cross_max,
        cross_sum,
        d_cross_mix,
        False,
    )
    grad_cq = product_t(norm_two, dq_cross)
    grad_ck = product_t(flat_mem, dk_cross)
    grad_cv = product_t(flat_mem, dv_cross)
    memory_grad = (product_nt(dk_cross, w_ck) + product_nt(dv_cross, w_cv)).astype(jnp.bfloat16)
    _, pull_two = jax.vjp(rms_scale, resid_one, gains[1])
    d_from_two, grad_gain_two = pull_two(product_nt(dq_cross, w_cq))
    d_resid_one = d_resid_two + d_from_two
    d_self = d_resid_one.astype(jnp.bfloat16)
    grad_so = product_t(self_mix, d_self)
    d_self_mix = product_nt(d_self, w_so).astype(jnp.bfloat16)
    dq_self, dk_self, dv_self, score_sums = attend_back_slots(
        self_q, self_k, self_v, dec_lengths, pos_bias, causal, self_max, self_sum, d_self_mix, True
    )
    grad_sq = product_t(norm_one, dq_self)
    grad_sk = product_t(norm_one, dk_self)
    grad_sv = product_t(norm_one, dv_self)
    d_norm_one = product_nt(dq_self, w_sq) + product_nt(dk_self, w_sk) + product_nt(dv_self, w_sv)
    _, pull_one = jax.vjp(rms_scale, flat_in, gains[0])
    d_from_one, grad_gain_one = pull_one(d_norm_one)
    input_grad = (d_resid_one + d_from_one).astype(jnp.bfloat16)
    table_local = table_gradient(score_sums, length)
    self_full = jnp.stack([grad_sq, grad_sk, grad_sv, grad_so]).reshape(-1)
    cross_full = jnp.stack([grad_cq, grad_ck, grad_cv, grad_co]).reshape(-1)
    ff_full = jnp.concatenate([grad_gate.reshape(-1), grad_up.reshape(-1), grad_down.reshape(-1)])
    self_shard, cross_shard, ff_shard = scatter_grads(self_full, cross_full, ff_full)
    gain_local = jnp.stack([grad_gain_one, grad_gain_two, grad_gain_three])
    gain_total, table_total = lax.psum((gain_local, table_local), ("dp", "fsdp"))
    return (
        block_out,
        input_grad.reshape(slot_count, length, model_width),
        memory_grad.reshape(slot_count, mem_len, model_width),
        self_shard,
        cross_shard,
        ff_shard,
        gain_total,
        table_total,
    )


def solution(mesh):
    whole = ("dp", "fsdp")
    rows = P(whole, None, None)
    flat = P(whole)
    small = mesh.shape["dp"] == 8 and mesh.shape["fsdp"] == 4
    return jax.shard_map(
        fused if small else by_collectives,
        mesh=mesh,
        in_specs=(rows, rows, rows, flat, flat, flat, flat, flat, P(), P()),
        out_specs=(rows, rows, rows, flat, flat, flat, P(), P()),
        check_vma=False,
    )
```
